32 devices in a mesh: dp: 8 (over z, y), tensor: 4 (over x, core).
Axes of the slice: x: 2, y: 2, z: 4, core: 2. Of those that a mesh axis runs over, the one named last changes fastest.
Arguments:
- tokens: bfloat16 [8, 1024, 2048], P('dp'), may hold values from -6 to 6
- segment_ids: int32 [8, 1024], P('dp'), may hold values from 0 to 7, never falling along the last dimension, each value on 1 to 512 neighbouring positions
- out_grad: bfloat16 [8, 1024, 2048], P('dp'), may hold values from -6 to 6
- attn_norm_gain: float32 [2048], replicated, may hold values from 0.5 to 1.5
- attn_norm_bias: float32 [2048], replicated, may hold values from -1.75 to 1.75
- mlp_norm_gain: float32 [2048], replicated, may hold values from 0.5 to 1.5
- mlp_norm_bias: float32 [2048], replicated, may hold values from -1.75 to 1.75
- qkv_weight: float32 [2048, 8, 3, 256], P('dp', 'tensor'), may hold values from -0.1875 to 0.1875
- qv_bias: float32 [8, 2, 256], P('tensor'), may hold values from -1.75 to 1.75
- key_bias: float32 [8, 64], P('tensor'), may hold values from -3 to 3
- dense_weight: float32 [8, 256, 2048], P('tensor', None, 'dp'), may hold values from -0.75 to 0.75
- dense_bias: float32 [2048], replicated, may hold values from -1.75 to 1.75
- up_weight: float32 [2048, 8192], P('dp', 'tensor'), may hold values from -0.125 to 0.125
- up_bias: float32 [8192], P('tensor'), may hold values from -3 to 3
- down_weight: float32 [8192, 2048], P('tensor', 'dp'), may hold values from -0.0625 to 0.0625
- down_bias: float32 [2048], replicated, may hold values from -1.75 to 1.75
Outputs:
- block_out: bfloat16 [8, 1024, 2048], P('dp')
- input_grad: bfloat16 [8, 1024, 2048], P('dp')
- attn_norm_gain_grad: float32 [2048], replicated
- attn_norm_bias_grad: float32 [2048], replicated
- mlp_norm_gain_grad: float32 [2048], replicated
- mlp_norm_bias_grad: float32 [2048], replicated
- qkv_weight_grad: float32 [2048, 8, 3, 256], P('dp', 'tensor')
- qv_bias_grad: float32 [8, 2, 256], P('tensor')
- key_bias_grad: float32 [8, 64], P('tensor')
- dense_weight_grad: float32 [8, 256, 2048], P('tensor', None, 'dp')
- dense_bias_grad: float32 [2048], replicated
- up_weight_grad: float32 [2048, 8192], P('dp', 'tensor')
- up_bias_grad: float32 [8192], P('tensor')
- down_weight_grad: float32 [8192, 2048], P('tensor', 'dp')
- down_bias_grad: float32 [2048], replicated
The draws below stay inside these ranges and needn't reach their ends.
Inputs may be any that keep to these rules, and one draw needn't show every extreme that they name: `segment_ids`: ids never fall along a sequence; each of the 8 documents of a sequence holds 1 to 512 tokens, one exactly 512.
All inputs are finite; a program needn't handle non-finite values.
Results may differ from the reference program's by a relative error of at most 0.007.
The reference program's roundings to bfloat16 on the way count: a program that leaves them out, or rounds other values in their place, can miss the bound.
Values may be sent and summed in bfloat16 or wider, within the bound.
A program may use at most 256 MiB of HBM per device.

```python
import math
import jax
import jax.numpy as jnp
import numpy as np
from jax import lax

D = 2048
HEADS = 8
HEAD_DIM = 256
ROT = 64
FF = 8192
LEN = 1024
DOCS = 8
SEQS = 8
QBLOCK = 512


def raised(array, key, source, target, blocks, factor):
    def block_of(position):
        return (jnp.arange(array.shape[position]) // (array.shape[position] // blocks)).reshape((-1,) + (1,) * (array.ndim - 1 - position))

    first = jax.random.permutation(key, blocks)[block_of(target)]
    second = (block_of(target) + blocks // 2) % blocks
    return jnp.where((block_of(source) == first) | (block_of(source) == second), factor * array, array)


def block_levels(stream_key, dims, pieces, low, largest):
    gain, own = 1.0, jax.random.fold_in(stream_key, 6)
    for dim, shards_of in pieces:
        draws = jnp.exp(jax.random.uniform(jax.random.fold_in(own, dim), (shards_of,), jnp.float32, low / len(pieces), largest / len(pieces)))
        gain = gain * jnp.repeat(draws, dims[dim] // shards_of).reshape([-1 if axis == dim else 1 for axis in range(len(dims))])
    return gain


def split_up(count, total, bound, lean):
    weights = [(1 << 20) // math.isqrt(rank ** lean) + 1 for rank in range(2, count + 1)]
    rest, holding = total - bound - (count - 1), [1] * (count - 1)
    while rest > 0:
        movable = [i for i in range(count - 1) if holding[i] < bound]
        whole, remaining = sum([weights[i] for i in movable]), rest
        for i in movable:
            addition = min(bound - holding[i], max(1, remaining * weights[i] // whole), rest)
            holding[i] = holding[i] + addition
            rest = rest - addition
    return np.array([bound] + holding)


def ragged(key, amount, total, bound, skew):
    if amount == 2:
        one = jax.random.randint(key, (), max(1, total - bound), min(bound, total - 1) + 1)
        return jnp.stack([one, total - one])
    sizes = jnp.asarray(split_up(amount, total, bound, skew), jnp.int32)
    pairs = (amount - 1) // 2
    giver, taker = sizes[1:1 + 2 * pairs:2], sizes[2:2 + 2 * pairs:2]
    slack = jnp.minimum(giver - 1, bound - taker)
    shifted = jax.random.randint(jax.random.fold_in(key, 1), (pairs,), 0, 1 << 20) % (slack + 1)
    sizes = sizes.at[1:1 + 2 * pairs:2].set(giver - shifted).at[2:2 + 2 * pairs:2].set(taker + shifted)
    return sizes[jax.random.permutation(jax.random.fold_in(key, 2), amount)]


def normal_values(rng, shape, spread, most, cuts=(), kind=jnp.bfloat16):
    array = jax.random.normal(rng, shape, jnp.float32) * spread
    if len(cuts) > 0:
        array = block_levels(rng, shape, cuts, -0.22, 0.18) * array
    return jnp.clip(array, min=-most, max=most).astype(kind)


def bell_draw_with(rng, extent, scale, most, cuts, heavy, kind=jnp.bfloat16):
    entries = scale * jax.random.normal(rng, extent, jnp.float32)
    if cuts:
        entries = entries * block_levels(rng, extent, cuts, -0.22, 0.18)
    return jnp.clip(raised(entries, jax.random.fold_in(rng, 3), *heavy), -most, most).astype(kind)


def setup_inputs(seed: int = 0) -> dict:
    streams_of = jax.random.split(jax.random.key(seed), 17)
    tokens = normal_values(streams_of[0], (SEQS, LEN, D), 1.0, 6.0, ((0, 8),))
    segment_ids = jax.vmap(lambda own: jnp.searchsorted(jnp.cumsum(ragged(own, DOCS, LEN, LEN // 2, 2)), jnp.arange(LEN), side="right"))(jax.random.split(streams_of[1], SEQS)).reshape((SEQS, LEN)).astype(jnp.int32)
    out_grad = bell_draw_with(streams_of[2], (SEQS, LEN, D), 1.0, 6.0, ((0, 8),), (0, 2, 8, 2.0))
    attn_norm_gain = jnp.clip(1.0 + 0.1 * jax.random.normal(streams_of[3], (D,), jnp.float32), 0.5, 1.5)
    attn_norm_bias = normal_values(streams_of[4], (D,), 0.3, 1.75, (), jnp.float32)
    mlp_norm_gain = jnp.clip(1.0 + 0.1 * jax.random.normal(streams_of[5], (D,), jnp.float32), 0.5, 1.5)
    mlp_norm_bias = normal_values(streams_of[6], (D,), 0.3, 1.75, (), jnp.float32)
    qkv_weight = normal_values(streams_of[7], (D, HEADS, 3, HEAD_DIM), (D // 2) ** -0.5, 0.1875, ((0, 8), (1, 4)), jnp.float32)
    qv_bias = normal_values(streams_of[8], (HEADS, 2, HEAD_DIM), 0.3, 1.75, ((0, 4),), jnp.float32)
    key_bias = normal_values(streams_of[9], (HEADS, ROT), 0.5, 3.0, ((0, 4),), jnp.float32)
    dense_weight = normal_values(streams_of[10], (HEADS, HEAD_DIM, D), (D // 32) ** -0.5, 0.75, ((0, 4), (2, 8)), jnp.float32)
    dense_bias = normal_values(streams_of[11], (D,), 0.3, 1.75, (), jnp.float32)
    up_weight = normal_values(streams_of[12], (D, FF), D ** -0.5, 0.125, ((0, 8), (1, 4)), jnp.float32)
    up_bias = normal_values(streams_of[13], (FF,), 0.5, 3.0, ((0, 4),), jnp.float32)
    down_weight = normal_values(streams_of[14], (FF, D), FF ** -0.5, 0.0625, ((0, 4), (1, 8)), jnp.float32)
    down_bias = normal_values(streams_of[15], (D,), 0.3, 1.75, (), jnp.float32)
    return dict(tokens=tokens, segment_ids=segment_ids, out_grad=out_grad, attn_norm_gain=attn_norm_gain, attn_norm_bias=attn_norm_bias, mlp_norm_gain=mlp_norm_gain, mlp_norm_bias=mlp_norm_bias, qkv_weight=qkv_weight, qv_bias=qv_bias, key_bias=key_bias, dense_weight=dense_weight, dense_bias=dense_bias, up_weight=up_weight, up_bias=up_bias, down_weight=down_weight, down_bias=down_bias)


HIGHEST = lax.Precision.HIGHEST

@jax.custom_vjp
def low(v):
    return lax.optimization_barrier(v.astype(jnp.bfloat16)).astype(jnp.float32)

@jax.custom_vjp
def low_back(v):
    return v

def low_keep(v):
    return (low(v), None)

def low_pass(kept, grad):
    return (grad,)

def back_keep(v):
    return (v, None)

def back_low(kept, grad):
    return (low(grad),)
low.defvjp(low_keep, low_pass)
low_back.defvjp(back_keep, back_low)

def layer_norm(values, gain_vec, offset):
    center = values - lax.optimization_barrier(jnp.mean(values, axis=-1, keepdims=True))
    inverse = lax.rsqrt(lax.optimization_barrier(jnp.mean(center * center, axis=-1, keepdims=True)) + 1e-05)
    return center * inverse * gain_vec + offset

def rope_tables(length):
    half_rot = ROT // 2
    frequency = 10000.0 ** (-(jnp.arange(half_rot, dtype=jnp.float32) * 2.0) / ROT)
    angles = jnp.arange(length, dtype=jnp.float32)[:, None] * frequency[None, :]
    cosine = jnp.concatenate([jnp.cos(angles), jnp.cos(angles)], axis=-1)[:, None, :]
    sine_table = jnp.concatenate([jnp.sin(angles), jnp.sin(angles)], axis=-1)[:, None, :]
    return (cosine, sine_table)

def rotate(tensor, cosine, sine_table):
    half_rot = ROT // 2
    rotary_part = tensor[..., :ROT]
    turned = jnp.concatenate([-rotary_part[..., half_rot:], rotary_part[..., :half_rot]], axis=-1)
    return jnp.concatenate([rotary_part * cosine + turned * sine_table, tensor[..., ROT:]], axis=-1)

def attend(queries, key_rows, values, seg_row):
    block_count = LEN // QBLOCK
    q_blocks = queries.reshape(block_count, QBLOCK, HEADS, HEAD_DIM)
    first_rows = jnp.arange(block_count, dtype=jnp.int32) * QBLOCK
    columns = jnp.arange(LEN, dtype=jnp.int32)
    score_scale = HEAD_DIM ** (-0.5)

    def one_block(members):
        q_block, first_row = members
        row_ids = first_row + jnp.arange(QBLOCK, dtype=jnp.int32)
        seg_block = lax.dynamic_slice_in_dim(seg_row, first_row, QBLOCK, 0)
        scores = jnp.einsum('qhd,khd->hqk', q_block, key_rows, precision=HIGHEST) * score_scale
        scores = low_back(scores)
        allowed = (columns[None, :] <= row_ids[:, None]) & (seg_block[:, None] == seg_row[None, :])
        scores = jnp.where(allowed[None], scores, -1e+30)
        probabilities = low(jax.nn.softmax(scores, axis=-1))
        return jnp.einsum('hqk,khd->qhd', probabilities, values, precision=HIGHEST)
    blocks_out = lax.map(jax.checkpoint(one_block), (q_blocks, first_rows))
    return blocks_out.reshape(LEN, HEADS, HEAD_DIM)

def forward(inputs, segments, weights):
    attn_gain, attn_offset, mlp_gain, mlp_offset, qkv_master, qv_offset, key_offset, dense_master, dense_offset, up_master, up_offset, down_master, down_offset = weights
    group_size = inputs.shape[0]
    token_count = group_size * LEN
    flat_in = inputs.reshape(token_count, D)
    attn_in = low(layer_norm(flat_in, attn_gain, attn_offset))
    mlp_in = low(layer_norm(flat_in, mlp_gain, mlp_offset))
    key_full = jnp.concatenate([key_offset, jnp.zeros((HEADS, HEAD_DIM - ROT), jnp.float32)], axis=1)
    offset_full = jnp.stack([qv_offset[:, 0], key_full, qv_offset[:, 1]], axis=1)
    mixed_qkv = jnp.dot(attn_in, low(qkv_master).reshape(D, HEADS * 3 * HEAD_DIM), precision=HIGHEST)
    mixed_qkv = low_back(mixed_qkv + offset_full.reshape(-1))
    mixed_qkv = mixed_qkv.reshape(group_size, LEN, HEADS, 3, HEAD_DIM)
    cosine, sine_table = rope_tables(LEN)
    queries = low(rotate(mixed_qkv[..., 0, :], cosine, sine_table))
    key_rows = low(rotate(mixed_qkv[..., 1, :], cosine, sine_table))
    values = low(mixed_qkv[..., 2, :])
    context = jax.vmap(attend)(queries, key_rows, values, segments)
    context = low_back(low(context)).reshape(token_count, HEADS * HEAD_DIM)
    attn_out = jnp.dot(context, low(dense_master).reshape(HEADS * HEAD_DIM, D), precision=HIGHEST) + dense_offset
    up_pre = low_back(jnp.dot(mlp_in, low(up_master), precision=HIGHEST) + up_offset)
    activation = low(jax.nn.gelu(up_pre, approximate=False))
    mlp_out = jnp.dot(activation, low(down_master), precision=HIGHEST) + down_offset
    return (flat_in + attn_out + mlp_out).reshape(group_size, LEN, D)

def reference(tokens, segment_ids, out_grad, attn_norm_gain, attn_norm_bias, mlp_norm_gain, mlp_norm_bias, qkv_weight, qv_bias, key_bias, dense_weight, dense_bias, up_weight, up_bias, down_weight, down_bias):
    params = (attn_norm_gain, attn_norm_bias, mlp_norm_gain, mlp_norm_bias, qkv_weight, qv_bias, key_bias, dense_weight, dense_bias, up_weight, up_bias, down_weight, down_bias)
    group_size = 4 if SEQS % 4 == 0 else 1
    group_count = SEQS // group_size
    inputs = tokens.astype(jnp.float32).reshape(group_count, group_size, LEN, D)
    segments = segment_ids.reshape(group_count, group_size, LEN)
    cotangents = out_grad.astype(jnp.float32).reshape(group_count, group_size, LEN, D)

    def one_group(totals, members):
        group_in, group_seg, group_grad = members

        def apply_layer(values, *weights):
            return forward(values, group_seg, weights)
        result, pullback = jax.vjp(apply_layer, group_in, *params)
        gradients = pullback(group_grad)
        totals = tuple((total_sum + grad_term for total_sum, grad_term in zip(totals, gradients[1:])))
        return (totals, (result.astype(jnp.bfloat16), gradients[0].astype(jnp.bfloat16)))
    initial = tuple((jnp.zeros_like(weight) for weight in params))
    totals, (outputs, in_grads) = lax.scan(one_group, initial, (inputs, segments, cotangents))
    return (outputs.reshape(SEQS, LEN, D), in_grads.reshape(SEQS, LEN, D), totals[0], totals[1], totals[2], totals[3], totals[4], totals[5], totals[6], totals[7], totals[8], totals[9], totals[10], totals[11], totals[12])
```

```python
import jax
import jax.numpy as jnp
from jax import lax
from jax.experimental import pallas as pl
from jax.experimental.pallas import tpu as pltpu
from jax.sharding import PartitionSpec as P

ROT = 64
PAIR = 2
QBLOCK = 256
DOC_MAX = 512
F = jnp.float32
B = jnp.bfloat16


def dot(left, right, dims, kind):
    return lax.dot_general(left, right, (dims, ((), ())), preferred_element_type=F).astype(kind)


def gelu_slope(pre_act):
    cumulative = 0.5 * (1.0 + lax.erf(pre_act * 0.7071067811865476))
    density = jnp.exp(-0.5 * pre_act * pre_act) * 0.3989422804014327
    return cumulative + pre_act * density


def rope_tables(length):
    half = ROT // 2
    frequency = 10000.0 ** (-(jnp.arange(half, dtype=F) * 2.0) / ROT)
    angles = jnp.arange(length, dtype=F)[:, None] * frequency[None, :]
    cosine, sine = jnp.cos(angles), jnp.sin(angles)
    flat = jnp.zeros((length, 128 - ROT), F)
    zero = jnp.zeros_like(sine)
    return (
        jnp.concatenate([cosine, cosine, flat + 1.0], axis=1),
        jnp.concatenate([-sine, zero, flat], axis=1),
        jnp.concatenate([zero, sine, flat], axis=1),
    )


def turn(rows, cosine, from_above, from_below):
    head = rows[:, :128]
    above = pltpu.roll(head, 128 - ROT // 2, 1)
    below = pltpu.roll(head, ROT // 2, 1)
    turned = head * cosine + above * from_above + below * from_below
    return jnp.concatenate([turned, rows[:, 128:]], axis=1)


def block_mask(seg_col_ref, seg_row_ref, first, low, high):
    rows = first + lax.broadcasted_iota(jnp.int32, (QBLOCK, high - low), 0)
    columns = low + lax.broadcasted_iota(jnp.int32, (QBLOCK, high - low), 1)
    same = seg_col_ref[0, first : first + QBLOCK, :] == seg_row_ref[0, :, low:high]
    return (columns <= rows) & same


def key_range(first):
    return max(0, first - DOC_MAX), first + QBLOCK


def attn_forward(mixed_ref, bias_ref, cos_ref, up_ref, down_ref, col_ref, row_ref, q_ref, k_ref, v_ref, ctx_ref, lse_ref):
    size = q_ref.shape[2]
    length = q_ref.shape[1]
    scale = size ** (-0.5)
    tables = (cos_ref[...], up_ref[...], down_ref[...])
    q_ref[0] = turn(mixed_ref[0, :, :size] + bias_ref[:, :size], *tables).astype(B)
    k_ref[0] = turn(mixed_ref[0, :, size : 2 * size] + bias_ref[:, size : 2 * size], *tables).astype(B)
    v_ref[0] = (mixed_ref[0, :, 2 * size :] + bias_ref[:, 2 * size :]).astype(B)
    for first in range(0, length, QBLOCK):
        low, high = key_range(first)
        scores = dot(q_ref[0, first : first + QBLOCK], k_ref[0, low:high], ((1,), (1,)), F) * scale
        scores = jnp.where(block_mask(col_ref, row_ref, first, low, high), scores, -1e30)
        row_max = jnp.max(scores, axis=1, keepdims=True)
        expo = jnp.exp(scores - row_max)
        total = jnp.sum(expo, axis=1, keepdims=True)
        probs = (expo / total).astype(B)
        ctx_ref[0, first : first + QBLOCK] = dot(probs, v_ref[0, low:high], ((1,), (0,)), B)
        lse_ref[0, first : first + QBLOCK] = row_max + jnp.log(total)


def attn_backward(q_ref, k_ref, v_ref, grad_ref, lse_ref, cos_ref, up_ref, down_ref, col_ref, row_ref, mixed_ref, sum_ref, q_acc, k_acc, v_acc):
    size = q_ref.shape[2]
    length = q_ref.shape[1]
    scale = size ** (-0.5)
    k_acc[...] = jnp.zeros_like(k_acc)
    v_acc[...] = jnp.zeros_like(v_acc)
    for first in range(0, length, QBLOCK):
        low, high = key_range(first)
        here = slice(first, first + QBLOCK)
        scores = dot(q_ref[0, here], k_ref[0, low:high], ((1,), (1,)), F) * scale
        scores = jnp.where(block_mask(col_ref, row_ref, first, low, high), scores, -1e30)
        probs = jnp.exp(scores - lse_ref[0, here])
        v_acc[low:high] += dot(probs.astype(B), grad_ref[0, here], ((0,), (0,)), F)
        prob_grad = dot(grad_ref[0, here], v_ref[0, low:high], ((1,), (1,)), F)
        centred = jnp.sum(probs * prob_grad, axis=1, keepdims=True)
        score_grad = (probs * (prob_grad - centred)).astype(B)
        q_acc[here] = dot(score_grad, k_ref[0, low:high], ((1,), (0,)), F) * scale
        k_acc[low:high] += dot(score_grad, q_ref[0, here], ((0,), (0,)), F) * scale
    tables = (cos_ref[...], -up_ref[...], -down_ref[...])
    q_grad = turn(q_acc[...], *tables).astype(B)
    k_grad = turn(k_acc[...], *tables).astype(B)
    v_grad = v_acc[...].astype(B)
    for number, part in enumerate((q_grad, k_grad, v_grad)):
        mixed_ref[0, :, number * size : (number + 1) * size] = part
        sum_ref[0, :, number * size : (number + 1) * size] = jnp.sum(part.astype(F), axis=0, keepdims=True)


def per_seq(rows, columns):
    return pl.BlockSpec((1, rows, columns), lambda seq: (seq, 0, 0))


def shared(rows, columns):
    return pl.BlockSpec((rows, columns), lambda seq: (0, 0))


def body(
    tokens,
    segment_ids,
    out_grad,
    attn_norm_gain,
    attn_norm_bias,
    mlp_norm_gain,
    mlp_norm_bias,
    qkv_weight,
    qv_bias,
    key_bias,
    dense_weight,
    dense_bias,
    up_weight,
    up_bias,
    down_weight,
    down_bias,
    *,
    groups,
    ways,
):
    length, width = tokens.shape[1:]
    heads, size = qkv_weight.shape[1] // 2, qkv_weight.shape[3]
    part = width // groups
    me = lax.axis_index("dp")
    half = (me // PAIR) % 2
    place = lax.axis_index("tensor")
    core, side = place % 2, place // 2
    spread = [bit for bit in (1 << k for k in reversed(range(groups.bit_length() - 1))) if bit != PAIR]

    def swap(array, bit):
        return lax.ppermute(array, "dp", [(i, i ^ bit) for i in range(groups)])

    def cross(array, bit):
        return lax.ppermute(array, "tensor", [(i, i ^ bit) for i in range(ways)])

    def pick(array, index, axis, count=2):
        rows = array.shape[axis] // count
        return lax.dynamic_slice_in_dim(array, index * rows, rows, axis)

    def join(mine, theirs, index, axis):
        pair = jnp.concatenate([mine, theirs], axis=axis)
        turned = jnp.concatenate([theirs, mine], axis=axis)
        return jnp.where(index == 0, pair, turned)

    order = [0, PAIR]
    for bit in spread:
        order = order + [mask | bit for mask in order]
    inverse = [order.index(mask) for mask in range(groups)]

    def arranged(array):
        return jnp.concatenate(
            [lax.dynamic_slice_in_dim(array, (mask ^ me) * part, part, array.ndim - 1) for mask in order], axis=-1
        )

    def natural(array):
        table = jnp.asarray(inverse, jnp.int32)
        return jnp.concatenate(
            [lax.dynamic_slice_in_dim(array, table[block ^ me] * part, part, array.ndim - 1) for block in range(groups)],
            axis=-1,
        )

    def gather(shard, halves_axis, axis):
        shard = shard.astype(B)
        mine, theirs = pick(shard, half, halves_axis), pick(shard, 1 - half, halves_axis)
        pieces = [jnp.concatenate([mine, swap(theirs, PAIR)], axis=axis)]
        for bit in spread:
            pieces = pieces + [swap(piece, bit) for piece in pieces]
        return jnp.concatenate(pieces, axis=axis)

    def scatter(product, axis, halves_axis):
        count = groups // 2
        sent = swap(product(count, groups, B), spread[-1])
        held = product(0, count, F) + sent.astype(F)
        for bit in reversed(spread[:-1]):
            keep, send = jnp.split(held, 2, axis=axis)
            held = keep + swap(send.astype(B), bit).astype(F)
        keep, send = jnp.split(held, 2, axis=axis)
        return join(keep, swap(send, PAIR), half, halves_axis)

    def share_rows(rows):
        rows = join(rows, cross(rows, 2), side, 0)
        return join(rows, cross(rows, 1), core, 0)

    def own_rows(array, axis):
        return pick(pick(array, core, axis), side, axis)

    def partner_rows(array):
        return share_rows(swap(own_rows(array, 0), PAIR))

    def total_rows(partial):
        held = pick(partial, core, 1).astype(F) + cross(pick(partial, 1 - core, 1), 1).astype(F)
        held = pick(held, side, 1) + cross(pick(held, 1 - side, 1).astype(B), 2).astype(F)
        sent = swap(held[1].astype(B), PAIR).astype(F)
        rows = sent.shape[0]
        sent = jnp.flip(sent.reshape(rows, groups // 2, 2, part), axis=2).reshape(rows, width)
        return held[0] + sent

    own_x, own_g = tokens[0], out_grad[0]
    w_up = gather(up_weight, 1, 0)
    x_other = partner_rows(own_x)
    w_down = gather(down_weight, 0, 1)
    g_other = partner_rows(own_g)
    w_qkv = gather(qkv_weight.reshape(part, 2, -1), 1, 0).reshape(width, -1)
    w_dense = gather(dense_weight.reshape(2 * heads * size, part), 0, 1)

    x_pair = arranged(jnp.concatenate([own_x, x_other], axis=0))
    g_pair = arranged(jnp.concatenate([own_g, g_other], axis=0))
    gains = [arranged(v) for v in (attn_norm_gain, attn_norm_bias, mlp_norm_gain, mlp_norm_bias)]

    def hat(rows):
        rows = rows.astype(F)
        center = rows - jnp.mean(rows, axis=-1, keepdims=True)
        inverse_dev = lax.rsqrt(jnp.mean(center * center, axis=-1, keepdims=True) + 1e-05)
        return center * inverse_dev, inverse_dev

    normed, _ = hat(x_pair)
    attn_in = (normed * gains[0] + gains[1]).astype(B)
    mlp_in = (normed * gains[2] + gains[3]).astype(B)

    up_here = pick(up_bias, half, 0)
    up_pre = dot(mlp_in, w_up, ((1,), (0,)), F) + up_here
    activation = jax.nn.gelu(up_pre, approximate=False).astype(B)
    middle = width // 2

    def columns(array, low, high):
        return array[:, low * part : high * part]

    down_shard = scatter(lambda low, high, kind: dot(activation, columns(g_pair, low, high), ((0,), (0,)), kind), 1, 0)
    pre_grad = (dot(g_pair, w_down, ((1,), (1,)), F) * gelu_slope(up_pre)).astype(B)
    up_shard = scatter(lambda low, high, kind: dot(columns(mlp_in, low, high), pre_grad, ((0,), (0,)), kind), 0, 1)
    up_bias_sum = jnp.sum(pre_grad.astype(F), axis=0)

    seg_other = swap(segment_ids[0], PAIR)
    seg = jnp.stack([segment_ids[0], seg_other])
    seg_col, seg_row = seg[:, :, None], seg[:, None, :]
    qv_here, key_here = pick(qv_bias, half, 0), pick(key_bias, half, 0)
    key_full = jnp.concatenate([key_here, jnp.zeros((heads, size - ROT), F)], axis=1)
    offsets = jnp.stack([qv_here[:, 0], key_full, qv_here[:, 1]], axis=1).reshape(heads, 1, 3 * size)
    mixed = dot(attn_in, w_qkv, ((1,), (0,)), F).reshape(2, length, heads, 3 * size)
    tables = rope_tables(length)
    table_specs = [shared(length, 128)] * 3
    seg_specs = [per_seq(length, 1), per_seq(1, length)]
    context_grad = dot(g_pair, w_dense, ((1,), (1,)), B).reshape(2, length, heads, size)
    contexts, mixed_grads, mixed_sums = [], [], []
    head_shape = jax.ShapeDtypeStruct((2, length, size), B)
    for head in range(heads):
        q, k, v, context, lse = pl.pallas_call(
            attn_forward,
            grid=(2,),
            in_specs=[per_seq(length, 3 * size), shared(1, 3 * size)] + table_specs + seg_specs,
            out_specs=[per_seq(length, size)] * 4 + [per_seq(length, 1)],
            out_shape=[head_shape] * 4 + [jax.ShapeDtypeStruct((2, length, 1), F)],
            name="attn_forward",
        )(mixed[:, :, head], offsets[head], *tables, seg_col, seg_row)
        mixed_grad, mixed_sum = pl.pallas_call(
            attn_backward,
            grid=(2,),
            in_specs=[per_seq(length, size)] * 4 + [per_seq(length, 1)] + table_specs + seg_specs,
            out_specs=[per_seq(length, 3 * size), per_seq(1, 3 * size)],
            out_shape=[
                jax.ShapeDtypeStruct((2, length, 3 * size), B),
                jax.ShapeDtypeStruct((2, 1, 3 * size), F),
            ],
            scratch_shapes=[pltpu.VMEM((length, size), F)] * 3,
            name="attn_backward",
        )(q, k, v, context_grad[:, :, head], lse, *tables, seg_col, seg_row)
        contexts.append(context.reshape(2 * length, size))
        mixed_grads.append(mixed_grad.reshape(2 * length, 3 * size))
        mixed_sums.append(jnp.sum(mixed_sum, axis=(0, 1)))
    context = jnp.concatenate(contexts, axis=1)
    mixed_grad = jnp.concatenate(mixed_grads, axis=1)
    mixed_sum = jnp.stack(mixed_sums).reshape(heads, 3, size)

    qkv_shard = scatter(lambda low, high, kind: dot(columns(attn_in, low, high), mixed_grad, ((0,), (0,)), kind), 0, 1)
    dense_shard = scatter(lambda low, high, kind: dot(context, columns(g_pair, low, high), ((0,), (0,)), kind), 1, 0)

    branch = dot(context, w_dense, ((1,), (0,)), F) + dot(activation, w_down, ((1,), (0,)), F)
    branch_rows = total_rows(branch.astype(B).reshape(2, length, width))
    x_rows, g_rows = own_rows(x_pair[:length], 0), own_rows(g_pair[:length], 0)
    out_rows = (x_rows.astype(F) + branch_rows + arranged(dense_bias) + arranged(down_bias)).astype(B)
    block_out = share_rows(natural(out_rows))

    attn_in_grad = dot(mixed_grad, w_qkv, ((1,), (1,)), F)
    mlp_in_grad = dot(pre_grad, w_up, ((1,), (1,)), F)
    blend = (attn_in_grad * gains[0] + mlp_in_grad * gains[2]).astype(B)
    blend_rows = total_rows(blend.reshape(2, length, width))
    hat_rows, inverse_rows = hat(x_rows)
    inner = (
        blend_rows
        - jnp.mean(blend_rows, axis=-1, keepdims=True)
        - hat_rows * jnp.mean(blend_rows * hat_rows, axis=-1, keepdims=True)
    )
    input_grad = share_rows(natural((g_rows.astype(F) + inner * inverse_rows).astype(B)))

    norm_sums = natural(
        jnp.stack(
            [
                jnp.sum(attn_in_grad * normed, axis=0),
                jnp.sum(attn_in_grad, axis=0),
                jnp.sum(mlp_in_grad * normed, axis=0),
                jnp.sum(mlp_in_grad, axis=0),
            ]
        )
    ).reshape(-1)
    bias_sum = jnp.sum(own_g.astype(F), axis=0)

    def slotted(array):
        zero = jnp.zeros_like(array)
        return join(array, zero, half, 0)

    small = [norm_sums, bias_sum, slotted(up_bias_sum), slotted(mixed_sum).reshape(-1)]
    sizes = [s.shape[0] for s in small]
    flat = jnp.concatenate(small)
    for bit in [1 << k for k in range(groups.bit_length() - 1)]:
        flat = flat + swap(flat, bit)
    ends = [sum(sizes[: i + 1]) for i in range(len(sizes))]
    norms = flat[: ends[0]]
    for bit in [1 << k for k in range(ways.bit_length() - 1)]:
        norms = norms + cross(norms, bit)
    norms = norms.reshape(4, width)
    bias_grad = flat[ends[0] : ends[1]]
    up_bias_grad = flat[ends[1] : ends[2]]
    mixed_bias = flat[ends[2] :].reshape(2 * heads, 3, size)
    qv_grad = jnp.stack([mixed_bias[:, 0], mixed_bias[:, 2]], axis=1)
    key_bias_grad = mixed_bias[:, 1, :ROT]

    return (
        block_out[None],
        input_grad[None],
        norms[0],
        norms[1],
        norms[2],
        norms[3],
        qkv_shard.reshape(qkv_weight.shape),
        qv_grad,
        key_bias_grad,
        dense_shard.reshape(dense_weight.shape),
        bias_grad,
        up_shard,
        up_bias_grad,
        down_shard,
        bias_grad,
    )


def solution(mesh):
    placed = (
        P("dp", None, None),
        P("dp", None),
        P("dp", None, None),
        P(),
        P(),
        P(),
        P(),
        P("dp", "tensor", None, None),
        P("tensor", None, None),
        P("tensor", None),
        P("tensor", None, "dp"),
        P(),
        P("dp", "tensor"),
        P("tensor"),
        P("tensor", "dp"),
        P(),
    )

    def whole(*arrays):
        return body(*arrays, groups=mesh.shape["dp"], ways=mesh.shape["tensor"])

    return jax.shard_map(
        whole,
        mesh=mesh,
        in_specs=placed,
        out_specs=(
            P("dp", None, None),
            P("dp", None, None),
            P(),
            P(),
            P(),
            P(),
            P("dp", "tensor", None, None),
            P("tensor", None, None),
            P("tensor", None),
            P("tensor", None, "dp"),
            P(),
            P("dp", "tensor"),
            P("tensor"),
            P("tensor", "dp"),
            P(),
        ),
        check_vma=False,
    )
```

```python
import functools

import jax
import jax.numpy as jnp
from jax import lax
from jax.experimental import pallas as pl
from jax.experimental.pallas import tpu as pltpu
from jax.sharding import PartitionSpec as P

ROT = 64
PAIR = 2
QBLOCK = 256
DOC_MAX = 512
F = jnp.float32
B = jnp.bfloat16


def dot(left, right, dims, kind):
    return lax.dot_general(left, right, (dims, ((), ())), preferred_element_type=F).astype(kind)


def gelu_slope(pre_act):
    cumulative = 0.5 * (1.0 + lax.erf(pre_act * 0.7071067811865476))
    density = jnp.exp(-0.5 * pre_act * pre_act) * 0.3989422804014327
    return cumulative + pre_act * density


def rope_tables(length):
    half = ROT // 2
    frequency = 10000.0 ** (-(jnp.arange(half, dtype=F) * 2.0) / ROT)
    angles = jnp.arange(length, dtype=F)[:, None] * frequency[None, :]
    cosine, sine = jnp.cos(angles), jnp.sin(angles)
    flat = jnp.zeros((length, 128 - ROT), F)
    zero = jnp.zeros_like(sine)
    return (
        jnp.concatenate([cosine, cosine, flat + 1.0], axis=1),
        jnp.concatenate([-sine, zero, flat], axis=1),
        jnp.concatenate([zero, sine, flat], axis=1),
    )


def turn(rows, cosine, from_above, from_below):
    head = rows[:, :128]
    above = pltpu.roll(head, 128 - ROT // 2, 1)
    below = pltpu.roll(head, ROT // 2, 1)
    turned = head * cosine + above * from_above + below * from_below
    return jnp.concatenate([turned, rows[:, 128:]], axis=1)


def block_mask(seg_col_ref, seg_row_ref, first, low, high):
    rows = first + lax.broadcasted_iota(jnp.int32, (QBLOCK, high - low), 0)
    columns = low + lax.broadcasted_iota(jnp.int32, (QBLOCK, high - low), 1)
    same = seg_col_ref[0, first : first + QBLOCK, :] == seg_row_ref[0, :, low:high]
    return (columns <= rows) & same


def key_range(first):
    return max(0, first - DOC_MAX), first + QBLOCK


def attn_forward(mixed_ref, bias_ref, cos_ref, up_ref, down_ref, col_ref, row_ref, q_ref, k_ref, v_ref, ctx_ref, lse_ref):
    size = q_ref.shape[2]
    length = q_ref.shape[1]
    scale = size ** (-0.5)
    tables = (cos_ref[...], up_ref[...], down_ref[...])
    q_ref[0] = turn(mixed_ref[0, :, :size] + bias_ref[:, :size], *tables).astype(B)
    k_ref[0] = turn(mixed_ref[0, :, size : 2 * size] + bias_ref[:, size : 2 * size], *tables).astype(B)
    v_ref[0] = (mixed_ref[0, :, 2 * size :] + bias_ref[:, 2 * size :]).astype(B)
    for first in range(0, length, QBLOCK):
        low, high = key_range(first)
        scores = dot(q_ref[0, first : first + QBLOCK], k_ref[0, low:high], ((1,), (1,)), F) * scale
        scores = jnp.where(block_mask(col_ref, row_ref, first, low, high), scores, -1e30)
        row_max = jnp.max(scores, axis=1, keepdims=True)
        expo = jnp.exp(scores - row_max)
        total = jnp.sum(expo, axis=1, keepdims=True)
        probs = (expo / total).astype(B)
        ctx_ref[0, first : first + QBLOCK] = dot(probs, v_ref[0, low:high], ((1,), (0,)), B)
        lse_ref[0, first : first + QBLOCK] = row_max + jnp.log(total)


def attn_backward(q_ref, k_ref, v_ref, grad_ref, lse_ref, cos_ref, up_ref, down_ref, col_ref, row_ref, mixed_ref, sum_ref, q_acc, k_acc, v_acc):
    size = q_ref.shape[2]
    length = q_ref.shape[1]
    scale = size ** (-0.5)
    k_acc[...] = jnp.zeros_like(k_acc)
    v_acc[...] = jnp.zeros_like(v_acc)
    for first in range(0, length, QBLOCK):
        low, high = key_range(first)
        here = slice(first, first + QBLOCK)
        scores = dot(q_ref[0, here], k_ref[0, low:high], ((1,), (1,)), F) * scale
        scores = jnp.where(block_mask(col_ref, row_ref, first, low, high), scores, -1e30)
        probs = jnp.exp(scores - lse_ref[0, here])
        v_acc[low:high] += dot(probs.astype(B), grad_ref[0, here], ((0,), (0,)), F)
        prob_grad = dot(grad_ref[0, here], v_ref[0, low:high], ((1,), (1,)), F)
        centred = jnp.sum(probs * prob_grad, axis=1, keepdims=True)
        score_grad = (probs * (prob_grad - centred)).astype(B)
        q_acc[here] = dot(score_grad, k_ref[0, low:high], ((1,), (0,)), F) * scale
        k_acc[low:high] += dot(score_grad, q_ref[0, here], ((0,), (0,)), F) * scale
    tables = (cos_ref[...], -up_ref[...], -down_ref[...])
    q_grad = turn(q_acc[...], *tables).astype(B)
    k_grad = turn(k_acc[...], *tables).astype(B)
    v_grad = v_acc[...].astype(B)
    for number, part in enumerate((q_grad, k_grad, v_grad)):
        mixed_ref[0, :, number * size : (number + 1) * size] = part
        sum_ref[0, :, number * size : (number + 1) * size] = jnp.sum(part.astype(F), axis=0, keepdims=True)


def pre_kernel(g_ref, w_ref, slope_ref, out_ref, sum_ref):
    grad = (dot(g_ref[...], w_ref[...], ((1,), (0,)), F) * slope_ref[...]).astype(B)
    out_ref[...] = grad

    @pl.when(pl.program_id(0) == 0)
    def _():
        sum_ref[...] = jnp.zeros_like(sum_ref)

    sum_ref[...] += jnp.sum(grad.astype(F), axis=0, keepdims=True)


def branch_kernel(ctx_ref, act_ref, dense_ref, down_ref, out_ref):
    width = out_ref.shape[1]
    for low in range(0, width, 512):
        here = slice(low, low + 512)
        out_ref[:, here] = (
            dot(ctx_ref[...], dense_ref[here, :], ((1,), (1,)), F)
            + dot(act_ref[...], down_ref[here, :], ((1,), (1,)), F)
        ).astype(B)


def blend_kernel(part, order_ref, mixed_ref, pre_ref, qkv_ref, up_ref, x_ref, vec_ref, out_ref, sum_ref):
    @pl.when(pl.program_id(0) == 0)
    def _():
        sum_ref[...] = jnp.zeros_like(sum_ref)

    rows = x_ref[...].astype(F)
    mean = jnp.mean(rows, axis=1, keepdims=True)
    center = rows - mean
    inverse = lax.rsqrt(jnp.mean(center * center, axis=1, keepdims=True) + 1e-05)
    for place in range(x_ref.shape[1] // part):
        here = slice(place * part, (place + 1) * part)
        there = pl.ds(pl.multiple_of(order_ref[place] * part, part), part)
        attn_grad = dot(mixed_ref[...], qkv_ref[here, :], ((1,), (1,)), F)
        mlp_grad = dot(pre_ref[...], up_ref[here, :], ((1,), (1,)), F)
        normed = (x_ref[:, here].astype(F) - mean) * inverse
        out_ref[:, here] = (attn_grad * vec_ref[0:1, there] + mlp_grad * vec_ref[2:3, there]).astype(B)
        sum_ref[0:1, there] += jnp.sum(attn_grad * normed, axis=0, keepdims=True)
        sum_ref[1:2, there] += jnp.sum(attn_grad, axis=0, keepdims=True)
        sum_ref[2:3, there] += jnp.sum(mlp_grad * normed, axis=0, keepdims=True)
        sum_ref[3:4, there] += jnp.sum(mlp_grad, axis=0, keepdims=True)


def finish_out(part, place_ref, held_ref, sent_ref, x_ref, vec_ref, out_ref):
    for block in range(x_ref.shape[1] // part):
        here = slice(block * part, (block + 1) * part)
        place, other = place_ref[0, block], place_ref[1, block]
        mine = held_ref[:, pl.ds(pl.multiple_of(place * part, part), part)]
        theirs = sent_ref[:, pl.ds(pl.multiple_of(other * part, part), part)].astype(F)
        bias = vec_ref[4:5, here] + vec_ref[5:6, here]
        out_ref[:, here] = (x_ref[:, here].astype(F) + (mine + theirs) + bias).astype(B)


def finish_grad(part, place_ref, held_ref, sent_ref, x_ref, g_ref, out_ref):
    rows = x_ref[...].astype(F)
    mean = jnp.mean(rows, axis=1, keepdims=True)
    center = rows - mean
    inverse = lax.rsqrt(jnp.mean(center * center, axis=1, keepdims=True) + 1e-05)
    blends = []
    for block in range(x_ref.shape[1] // part):
        place, other = place_ref[0, block], place_ref[1, block]
        mine = held_ref[:, pl.ds(pl.multiple_of(place * part, part), part)]
        theirs = sent_ref[:, pl.ds(pl.multiple_of(other * part, part), part)].astype(F)
        blends.append(mine + theirs)
    blend = jnp.concatenate(blends, axis=1)
    normed = center * inverse
    inner = blend - jnp.mean(blend, axis=1, keepdims=True) - normed * jnp.mean(blend * normed, axis=1, keepdims=True)
    out_ref[...] = (g_ref[...].astype(F) + inner * inverse).astype(B)


def per_seq(rows, columns):
    return pl.BlockSpec((1, rows, columns), lambda seq, *_: (seq, 0, 0))


def shared(rows, columns):
    return pl.BlockSpec((rows, columns), lambda *_: (0, 0))


def tiled(rows, columns):
    return pl.BlockSpec((rows, columns), lambda tile, *_: (tile, 0))


def call(kernel, grid, in_specs, out_specs, out_shape, flops, moved, prefetch=0, aliases=None, scratch=(), name=None):
    return pl.pallas_call(
        kernel,
        grid_spec=pltpu.PrefetchScalarGridSpec(
            num_scalar_prefetch=prefetch, grid=grid, in_specs=in_specs, out_specs=out_specs, scratch_shapes=list(scratch)
        ),
        out_shape=out_shape,
        input_output_aliases=aliases or {},
        cost_estimate=pl.CostEstimate(flops=flops, bytes_accessed=moved, transcendentals=0),
        compiler_params=pltpu.CompilerParams(vmem_limit_bytes=56 * 1024 * 1024),
        name=name,
    )


MESH = pl.DeviceIdType.MESH
CHUNK = 256


def bit_of(index, bit):
    return lax.rem(lax.div(index, bit), 2)


def flip(index, mask):
    bit = 1
    while bit <= mask:
        if mask & bit:
            index = index + bit * (1 - 2 * bit_of(index, bit))
        bit *= 2
    return index


def block_order(groups):
    spread = [bit for bit in (1 << k for k in reversed(range(groups.bit_length() - 1))) if bit != PAIR]
    order = [0, PAIR]
    for bit in spread:
        order = order + [mask | bit for mask in order]
    return spread, order


def stats(rows):
    mean = jnp.mean(rows, axis=1, keepdims=True)
    center = rows - mean
    return mean, lax.rsqrt(jnp.mean(center * center, axis=1, keepdims=True) + 1e-05)


def greet(partners):
    barrier = pltpu.get_barrier_semaphore()
    for axis, index in partners:
        pl.semaphore_signal(barrier, inc=1, device_id={axis: index}, device_id_type=MESH)
    pl.semaphore_wait(barrier, len(partners))


def gather_kernel(
    groups,
    mine_ref,
    theirs_ref,
    x_ref,
    g_ref,
    vec_ref,
    up_bias_ref,
    offset_ref,
    cos_ref,
    above_ref,
    below_ref,
    col_ref,
    row_ref,
    w_out,
    x_other,
    g_other,
    x_rel,
    g_rel,
    mlp_out,
    mixed_out,
    ctx_out,
    act_out,
    slope_out,
    send_out,
    keep_out,
    sum_ref,
    w,
    raw_x,
    raw_g,
    attn_v,
    g_v,
    mlp_v,
    xr_v,
    grad_v,
    send_v,
    q_v,
    k_v,
    v_v,
    cg_v,
    ctx_v,
    mg_v,
    dk_v,
    dv_v,
    act_v,
    slope_v,
    send_sem,
    recv_sem,
    own_sem,
    load_sem,
    rel_sem,
    tile_sem,
    out_sem,
):
    length, width = x_ref.shape
    part = width // groups
    size = q_v.shape[1]
    quarter = length // 4
    me, place = lax.axis_index("dp"), lax.axis_index("tensor")
    core, side = lax.rem(place, 2), lax.div(place, 2)
    pair_to, side_to, core_to = flip(me, PAIR), flip(place, 2), flip(place, 1)
    spread, order = block_order(groups)
    greet([("dp", flip(me, bit)) for bit in [PAIR] + spread] + [("tensor", side_to), ("tensor", core_to)])
    copies = {}

    def remote(key, source, target, axis, index):
        number = len(copies)
        copies[key] = pltpu.make_async_remote_copy(
            src_ref=source,
            dst_ref=target,
            send_sem=send_sem.at[number],
            recv_sem=recv_sem.at[number],
            device_id={axis: index},
            device_id_type=MESH,
        )
        copies[key].start()

    def rows(position):
        return pl.ds(position * part, part)

    def pair_up(group):
        remote(("w", group, 1), theirs_ref.at[group], w.at[group, rows(1)], "dp", pair_to)

    def onward(group, position, level):
        source = mine_ref.at[group] if position == 0 else w.at[group, rows(position)]
        far = position + (2 << level)
        remote(("w", group, far), source, w.at[group, rows(far)], "dp", flip(me, spread[level]))

    def arrive(group, position, ahead=()):
        copies[("w", group, position)].wait_recv()

    spot = pl.ds(pl.multiple_of(core * (2 * quarter) + side * quarter, quarter), quarter)
    pair_rows = pl.ds(pl.multiple_of(core * (2 * quarter), quarter), 2 * quarter)
    levels = len(spread)
    assert levels == 2

    def load(x, g, tile, slot):
        here = pl.ds(pl.multiple_of(tile * CHUNK, CHUNK), CHUNK)
        return (
            pltpu.make_async_copy(x.at[here], raw_x.at[slot], load_sem.at[0, slot]),
            pltpu.make_async_copy(g.at[here], raw_g.at[slot], load_sem.at[1, slot]),
        )

    def normalise(seq, x, g):
        for copy in load(x, g, 0, 0):
            copy.start()

        def one(tile, carry):
            slot = lax.rem(tile, 2)

            @pl.when(tile + 1 < length // CHUNK)
            def _():
                for copy in load(x, g, tile + 1, 1 - slot):
                    copy.start()

            for copy in load(x, g, tile, slot):
                copy.wait()
            here = pl.ds(pl.multiple_of(tile * CHUNK, CHUNK), CHUNK)
            both = pl.ds(pl.multiple_of(seq * length + tile * CHUNK, CHUNK), CHUNK)
            mean, inverse = stats(raw_x[slot].astype(F))
            for position, mask in enumerate(order):
                to = slice(position * part, (position + 1) * part)
                there = pl.ds(pl.multiple_of(flip(me, mask) * part, part), part)
                piece = raw_x[slot, :, there]
                normed = (piece.astype(F) - mean) * inverse
                attn_v[here, to] = (normed * vec_ref[0:1, there] + vec_ref[1:2, there]).astype(B)
                mlp_v[both, to] = (normed * vec_ref[2:3, there] + vec_ref[3:4, there]).astype(B)
                xr_v[here, to] = piece
                g_v[here, to] = raw_g[slot, :, there]
            return carry

        lax.fori_loop(0, length // CHUNK, one, 0)
        both = pl.ds(seq * length, length)
        return [
            pltpu.make_async_copy(xr_v, x_rel.at[both], rel_sem.at[seq, 0]),
            pltpu.make_async_copy(g_v, g_rel.at[both], rel_sem.at[seq, 1]),
            pltpu.make_async_copy(mlp_v.at[both], mlp_out.at[both], rel_sem.at[seq, 2]),
        ]

    def project():
        def one(tile, carry):
            here = pl.ds(pl.multiple_of(tile * CHUNK, CHUNK), CHUNK)
            mixed = dot(attn_v[here], w[0, :, : 3 * size], ((1,), (0,)), F) + offset_ref[...]
            tables = (cos_ref[here], above_ref[here], below_ref[here])
            q_v[here] = turn(mixed[:, :size], *tables).astype(B)
            k_v[here] = turn(mixed[:, size : 2 * size], *tables).astype(B)
            v_v[here] = mixed[:, 2 * size :].astype(B)
            cg_v[here] = dot(g_v[here], w[0, :, 3 * size :], ((1,), (0,)), B)
            return carry

        lax.fori_loop(0, length // CHUNK, one, 0)

    def attend(seq):
        scale = size ** (-0.5)
        dk_v[...] = jnp.zeros_like(dk_v)
        dv_v[...] = jnp.zeros_like(dv_v)
        for first in range(0, length, QBLOCK):
            low, high = key_range(first)
            here, keys = slice(first, first + QBLOCK), slice(low, high)
            scores = dot(q_v[here], k_v[keys], ((1,), (1,)), F) * scale
            row_ids = first + lax.broadcasted_iota(jnp.int32, (QBLOCK, high - low), 0)
            key_ids = low + lax.broadcasted_iota(jnp.int32, (QBLOCK, high - low), 1)
            allowed = (key_ids <= row_ids) & (col_ref[seq, here, :] == row_ref[seq, :, keys])
            scores = jnp.where(allowed, scores, -1e30)
            expo = jnp.exp(scores - jnp.max(scores, axis=1, keepdims=True))
            probs = expo / jnp.sum(expo, axis=1, keepdims=True)
            low_probs = probs.astype(B)
            ctx_v[here] = dot(low_probs, v_v[keys], ((1,), (0,)), B)
            dv_v[keys] += dot(low_probs, cg_v[here], ((0,), (0,)), F)
            prob_grad = dot(cg_v[here], v_v[keys], ((1,), (1,)), F)
            centred = jnp.sum(probs * prob_grad, axis=1, keepdims=True)
            score_grad = (probs * (prob_grad - centred)).astype(B)
            q_grad = dot(score_grad, k_v[keys], ((1,), (0,)), F) * scale
            tables = (cos_ref[here], -above_ref[here], -below_ref[here])
            mg_v[here, :size] = turn(q_grad, *tables).astype(B)
            dk_v[keys] += dot(score_grad, q_v[here], ((0,), (0,)), F) * scale
        for first in range(0, length, QBLOCK):
            here = slice(first, first + QBLOCK)
            tables = (cos_ref[here], -above_ref[here], -below_ref[here])
            mg_v[here, size : 2 * size] = turn(dk_v[here], *tables).astype(B)
            mg_v[here, 2 * size :] = dv_v[here].astype(B)
        sums = jnp.sum(mg_v[...].astype(F), axis=0, keepdims=True)
        if seq == 0:
            sum_ref[...] = sums
        else:
            sum_ref[...] += sums
        both = pl.ds(seq * length, length)
        return [
            pltpu.make_async_copy(mg_v, mixed_out.at[both], rel_sem.at[seq, 3]),
            pltpu.make_async_copy(ctx_v, ctx_out.at[both], rel_sem.at[seq, 4]),
        ]

    def attn_grads(seq, low, high):
        def one(block, carry):
            here = pl.ds(pl.multiple_of(block * CHUNK, CHUNK), CHUNK)
            qkv = dot(attn_v[:, here], mg_v[...], ((0,), (0,)), F)
            dense = dot(g_v[:, here], ctx_v[...], ((0,), (0,)), F)
            if seq == 0:
                grad_v[here, : 3 * size] = qkv
                grad_v[here, 3 * size :] = dense
            else:
                grad_v[here, : 3 * size] += qkv
                grad_v[here, 3 * size :] += dense
            return carry

        lax.fori_loop(low // CHUNK, high // CHUNK, one, 0)

    def up(low, high):
        def store(tile, slot):
            here = pl.ds(pl.multiple_of(tile * CHUNK, CHUNK), CHUNK)
            return (
                pltpu.make_async_copy(act_v.at[slot], act_out.at[here], tile_sem.at[0, slot]),
                pltpu.make_async_copy(slope_v.at[slot], slope_out.at[here], tile_sem.at[1, slot]),
            )

        def one(tile, carry):
            slot = lax.rem(tile, 2)
            here = pl.ds(pl.multiple_of(tile * CHUNK, CHUNK), CHUNK)
            pre = dot(mlp_v[here], w[1], ((1,), (0,)), F) + up_bias_ref[...]

            @pl.when(tile >= low + 2)
            def _():
                for copy in store(tile - 2, slot):
                    copy.wait()

            cumulative = 0.5 * (1.0 + lax.erf(pre * 0.7071067811865476))
            density = jnp.exp(-0.5 * pre * pre) * 0.3989422804014327
            act_v[slot] = (pre * cumulative).astype(B)
            slope_v[slot] = cumulative + pre * density
            for copy in store(tile, slot):
                copy.start()
            return carry

        lax.fori_loop(low, high, one, 0)
        for tile in (high - 2, high - 1):
            for copy in store(tile, tile % 2):
                copy.wait()

    def weights_out(group):
        return pltpu.make_async_copy(w.at[group], w_out.at[group], out_sem.at[group])

    pair_up(0)
    onward(0, 0, 0)
    onward(0, 0, 1)
    own = [pltpu.make_async_copy(mine_ref.at[group], w.at[group, rows(0)], own_sem.at[group]) for group in range(3)]
    for copy in own:
        copy.start()
    first_out = normalise(0, x_ref, g_ref)
    for copy in first_out:
        copy.start()
    arrive(0, 1)
    onward(0, 1, 0)
    onward(0, 1, 1)
    remote("x1", x_ref.at[spot], x_other.at[spot], "dp", pair_to)
    pair_up(1)
    onward(1, 0, 0)
    onward(1, 0, 1)
    arrive(0, 2)
    onward(0, 2, 1)
    remote("g1", g_ref.at[spot], g_other.at[spot], "dp", pair_to)
    arrive(0, 3)
    onward(0, 3, 1)
    copies["x1"].wait_recv()
    remote("x2", x_other.at[spot], x_other.at[spot], "tensor", side_to)
    arrive(1, 1)
    onward(1, 1, 0)
    onward(1, 1, 1)
    pair_up(2)
    onward(2, 0, 0)
    onward(2, 0, 1)
    for position in range(4, 8):
        arrive(0, position)
    for copy in own:
        copy.wait()
    out = [weights_out(0)]
    out[0].start()
    project()
    arrive(1, 2)
    onward(1, 2, 1)
    copies["x2"].wait_recv()
    remote("x3", x_other.at[pair_rows], x_other.at[pair_rows], "tensor", core_to)
    copies["g1"].wait_recv()
    remote("g2", g_other.at[spot], g_other.at[spot], "tensor", side_to)
    second_out = attend(0)
    for copy in second_out:
        copy.start()
    arrive(2, 1)
    onward(2, 1, 0)
    onward(2, 1, 1)
    arrive(1, 3)
    onward(1, 3, 1)
    attn_grads(0, 0, width)
    copies["x3"].wait_recv()
    copies["g2"].wait_recv()
    remote("g3", g_other.at[pair_rows], g_other.at[pair_rows], "tensor", core_to)
    for copy in first_out + second_out:
        copy.wait()
    copies["g3"].wait_recv()
    arrive(2, 2)
    onward(2, 2, 1)
    third_out = normalise(1, x_other, g_other)
    for copy in third_out:
        copy.start()
    project()
    arrive(2, 3)
    onward(2, 3, 1)
    fourth_out = attend(1)
    for copy in fourth_out:
        copy.start()
    attn_grads(1, width // 2, width)
    send_v[...] = grad_v[width // 2 :].astype(B)
    out.append(pltpu.make_async_copy(send_v, send_out, out_sem.at[3]))
    out[-1].start()
    attn_grads(1, 0, width // 2)
    out.append(pltpu.make_async_copy(grad_v.at[pl.ds(0, width // 2)], keep_out, out_sem.at[4]))
    out[-1].start()
    for position in range(4, 8):
        arrive(1, position)
    out.append(weights_out(1))
    out[-1].start()
    up(0, 2 * length // CHUNK)
    for position in range(4, 8):
        arrive(2, position)
    out.append(weights_out(2))
    out[-1].start()
    for copy in third_out + fourth_out + out:
        copy.wait()
    for copy in copies.values():
        copy.wait_send()


def body_narrow(
    tokens,
    segment_ids,
    out_grad,
    attn_norm_gain,
    attn_norm_bias,
    mlp_norm_gain,
    mlp_norm_bias,
    qkv_weight,
    qv_bias,
    key_bias,
    dense_weight,
    dense_bias,
    up_weight,
    up_bias,
    down_weight,
    down_bias,
    *,
    groups,
    ways,
):
    length, width = tokens.shape[1:]
    heads, size = qkv_weight.shape[1] // 2, qkv_weight.shape[3]
    part = width // groups
    me = lax.axis_index("dp")
    half = (me // PAIR) % 2
    place = lax.axis_index("tensor")
    core, side = place % 2, place // 2
    spread = [bit for bit in (1 << k for k in reversed(range(groups.bit_length() - 1))) if bit != PAIR]

    def swap(array, bit):
        return lax.ppermute(array, "dp", [(i, i ^ bit) for i in range(groups)])

    def cross(array, bit):
        return lax.ppermute(array, "tensor", [(i, i ^ bit) for i in range(ways)])

    def pick(array, index, axis, count=2):
        rows = array.shape[axis] // count
        return lax.dynamic_slice_in_dim(array, index * rows, rows, axis)

    def join(mine, theirs, index, axis):
        pair = jnp.concatenate([mine, theirs], axis=axis)
        turned = jnp.concatenate([theirs, mine], axis=axis)
        return jnp.where(index == 0, pair, turned)

    order = [0, PAIR]
    for bit in spread:
        order = order + [mask | bit for mask in order]
    inverse = [order.index(mask) for mask in range(groups)]

    def arranged(array):
        return jnp.concatenate(
            [lax.dynamic_slice_in_dim(array, (mask ^ me) * part, part, array.ndim - 1) for mask in order], axis=-1
        )

    def natural(array):
        table = jnp.asarray(inverse, jnp.int32)
        return jnp.concatenate(
            [lax.dynamic_slice_in_dim(array, table[block ^ me] * part, part, array.ndim - 1) for block in range(groups)],
            axis=-1,
        )

    def gather(shard, halves_axis, axis):
        shard = shard.astype(B)
        mine, theirs = pick(shard, half, halves_axis), pick(shard, 1 - half, halves_axis)
        pieces = [jnp.concatenate([mine, swap(theirs, PAIR)], axis=axis)]
        for bit in spread:
            pieces = pieces + [swap(piece, bit) for piece in pieces]
        return jnp.concatenate(pieces, axis=axis)

    def scatter(product, axis, halves_axis):
        count = groups // 2
        sent = swap(product(count, groups, B), spread[-1])
        held = product(0, count, F) + sent.astype(F)
        for bit in reversed(spread[:-1]):
            keep, send = jnp.split(held, 2, axis=axis)
            held = keep + swap(send.astype(B), bit).astype(F)
        keep, send = jnp.split(held, 2, axis=axis)
        return join(keep, swap(send, PAIR), half, halves_axis)

    def share_rows(rows):
        rows = join(rows, cross(rows, 2), side, 0)
        return join(rows, cross(rows, 1), core, 0)

    def own_rows(array, axis):
        return pick(pick(array, core, axis), side, axis)

    def partner_rows(array):
        return share_rows(swap(own_rows(array, 0), PAIR))

    def total_rows(partial):
        held = pick(partial, core, 1).astype(F) + cross(pick(partial, 1 - core, 1), 1).astype(F)
        held = pick(held, side, 1) + cross(pick(held, 1 - side, 1).astype(B), 2).astype(F)
        sent = swap(held[1].astype(B), PAIR).astype(F)
        rows = sent.shape[0]
        sent = jnp.flip(sent.reshape(rows, groups // 2, 2, part), axis=2).reshape(rows, width)
        return held[0] + sent

    own_x, own_g = tokens[0], out_grad[0]
    w_up = gather(up_weight, 1, 0)
    x_other = partner_rows(own_x)
    w_down = gather(down_weight, 0, 1)
    g_other = partner_rows(own_g)
    w_qkv = gather(qkv_weight.reshape(part, 2, -1), 1, 0).reshape(width, -1)
    w_dense = gather(dense_weight.reshape(2 * heads * size, part), 0, 1)

    x_pair = arranged(jnp.concatenate([own_x, x_other], axis=0))
    g_pair = arranged(jnp.concatenate([own_g, g_other], axis=0))
    gains = [arranged(v) for v in (attn_norm_gain, attn_norm_bias, mlp_norm_gain, mlp_norm_bias)]

    def hat(rows):
        rows = rows.astype(F)
        center = rows - jnp.mean(rows, axis=-1, keepdims=True)
        inverse_dev = lax.rsqrt(jnp.mean(center * center, axis=-1, keepdims=True) + 1e-05)
        return center * inverse_dev, inverse_dev

    normed, _ = hat(x_pair)
    attn_in = (normed * gains[0] + gains[1]).astype(B)
    mlp_in = (normed * gains[2] + gains[3]).astype(B)

    up_here = pick(up_bias, half, 0)
    up_pre = dot(mlp_in, w_up, ((1,), (0,)), F) + up_here
    activation = jax.nn.gelu(up_pre, approximate=False).astype(B)
    middle = width // 2

    def columns(array, low, high):
        return array[:, low * part : high * part]

    down_shard = scatter(lambda low, high, kind: dot(activation, columns(g_pair, low, high), ((0,), (0,)), kind), 1, 0)
    pre_grad = (dot(g_pair, w_down, ((1,), (1,)), F) * gelu_slope(up_pre)).astype(B)
    up_shard = scatter(lambda low, high, kind: dot(columns(mlp_in, low, high), pre_grad, ((0,), (0,)), kind), 0, 1)
    up_bias_sum = jnp.sum(pre_grad.astype(F), axis=0)

    seg_other = swap(segment_ids[0], PAIR)
    seg = jnp.stack([segment_ids[0], seg_other])
    seg_col, seg_row = seg[:, :, None], seg[:, None, :]
    qv_here, key_here = pick(qv_bias, half, 0), pick(key_bias, half, 0)
    key_full = jnp.concatenate([key_here, jnp.zeros((heads, size - ROT), F)], axis=1)
    offsets = jnp.stack([qv_here[:, 0], key_full, qv_here[:, 1]], axis=1).reshape(heads, 1, 3 * size)
    mixed = dot(attn_in, w_qkv, ((1,), (0,)), F).reshape(2, length, heads, 3 * size)
    tables = rope_tables(length)
    table_specs = [shared(length, 128)] * 3
    seg_specs = [per_seq(length, 1), per_seq(1, length)]
    context_grad = dot(g_pair, w_dense, ((1,), (1,)), B).reshape(2, length, heads, size)
    contexts, mixed_grads, mixed_sums = [], [], []
    head_shape = jax.ShapeDtypeStruct((2, length, size), B)
    for head in range(heads):
        q, k, v, context, lse = pl.pallas_call(
            attn_forward,
            grid=(2,),
            in_specs=[per_seq(length, 3 * size), shared(1, 3 * size)] + table_specs + seg_specs,
            out_specs=[per_seq(length, size)] * 4 + [per_seq(length, 1)],
            out_shape=[head_shape] * 4 + [jax.ShapeDtypeStruct((2, length, 1), F)],
            name="attn_forward",
        )(mixed[:, :, head], offsets[head], *tables, seg_col, seg_row)
        mixed_grad, mixed_sum = pl.pallas_call(
            attn_backward,
            grid=(2,),
            in_specs=[per_seq(length, size)] * 4 + [per_seq(length, 1)] + table_specs + seg_specs,
            out_specs=[per_seq(length, 3 * size), per_seq(1, 3 * size)],
            out_shape=[
                jax.ShapeDtypeStruct((2, length, 3 * size), B),
                jax.ShapeDtypeStruct((2, 1, 3 * size), F),
            ],
            scratch_shapes=[pltpu.VMEM((length, size), F)] * 3,
            name="attn_backward",
        )(q, k, v, context_grad[:, :, head], lse, *tables, seg_col, seg_row)
        contexts.append(context.reshape(2 * length, size))
        mixed_grads.append(mixed_grad.reshape(2 * length, 3 * size))
        mixed_sums.append(jnp.sum(mixed_sum, axis=(0, 1)))
    context = jnp.concatenate(contexts, axis=1)
    mixed_grad = jnp.concatenate(mixed_grads, axis=1)
    mixed_sum = jnp.stack(mixed_sums).reshape(heads, 3, size)

    qkv_shard = scatter(lambda low, high, kind: dot(columns(attn_in, low, high), mixed_grad, ((0,), (0,)), kind), 0, 1)
    dense_shard = scatter(lambda low, high, kind: dot(context, columns(g_pair, low, high), ((0,), (0,)), kind), 1, 0)

    branch = dot(context, w_dense, ((1,), (0,)), F) + dot(activation, w_down, ((1,), (0,)), F)
    branch_rows = total_rows(branch.astype(B).reshape(2, length, width))
    x_rows, g_rows = own_rows(x_pair[:length], 0), own_rows(g_pair[:length], 0)
    out_rows = (x_rows.astype(F) + branch_rows + arranged(dense_bias) + arranged(down_bias)).astype(B)
    block_out = share_rows(natural(out_rows))

    attn_in_grad = dot(mixed_grad, w_qkv, ((1,), (1,)), F)
    mlp_in_grad = dot(pre_grad, w_up, ((1,), (1,)), F)
    blend = (attn_in_grad * gains[0] + mlp_in_grad * gains[2]).astype(B)
    blend_rows = total_rows(blend.reshape(2, length, width))
    hat_rows, inverse_rows = hat(x_rows)
    inner = (
        blend_rows
        - jnp.mean(blend_rows, axis=-1, keepdims=True)
        - hat_rows * jnp.mean(blend_rows * hat_rows, axis=-1, keepdims=True)
    )
    input_grad = share_rows(natural((g_rows.astype(F) + inner * inverse_rows).astype(B)))

    norm_sums = natural(
        jnp.stack(
            [
                jnp.sum(attn_in_grad * normed, axis=0),
                jnp.sum(attn_in_grad, axis=0),
                jnp.sum(mlp_in_grad * normed, axis=0),
                jnp.sum(mlp_in_grad, axis=0),
            ]
        )
    ).reshape(-1)
    bias_sum = jnp.sum(own_g.astype(F), axis=0)

    def slotted(array):
        zero = jnp.zeros_like(array)
        return join(array, zero, half, 0)

    small = [norm_sums, bias_sum, slotted(up_bias_sum), slotted(mixed_sum).reshape(-1)]
    sizes = [s.shape[0] for s in small]
    flat = jnp.concatenate(small)
    for bit in [1 << k for k in range(groups.bit_length() - 1)]:
        flat = flat + swap(flat, bit)
    ends = [sum(sizes[: i + 1]) for i in range(len(sizes))]
    norms = flat[: ends[0]]
    for bit in [1 << k for k in range(ways.bit_length() - 1)]:
        norms = norms + cross(norms, bit)
    norms = norms.reshape(4, width)
    bias_grad = flat[ends[0] : ends[1]]
    up_bias_grad = flat[ends[1] : ends[2]]
    mixed_bias = flat[ends[2] :].reshape(2 * heads, 3, size)
    qv_grad = jnp.stack([mixed_bias[:, 0], mixed_bias[:, 2]], axis=1)
    key_bias_grad = mixed_bias[:, 1, :ROT]

    return (
        block_out[None],
        input_grad[None],
        norms[0],
        norms[1],
        norms[2],
        norms[3],
        qkv_shard.reshape(qkv_weight.shape),
        qv_grad,
        key_bias_grad,
        dense_shard.reshape(dense_weight.shape),
        bias_grad,
        up_shard,
        up_bias_grad,
        down_shard,
        bias_grad,
    )


def body(
    tokens,
    segment_ids,
    out_grad,
    attn_norm_gain,
    attn_norm_bias,
    mlp_norm_gain,
    mlp_norm_bias,
    qkv_weight,
    qv_bias,
    key_bias,
    dense_weight,
    dense_bias,
    up_weight,
    up_bias,
    down_weight,
    down_bias,
    *,
    groups,
    ways,
):
    length, width = tokens.shape[1:]
    heads, size = qkv_weight.shape[1] // 2, qkv_weight.shape[3]
    assert heads == 1
    part = width // groups
    hidden = up_weight.shape[1] // 2
    count = 2 * length
    me = lax.axis_index("dp")
    half = (me // PAIR) % 2
    place = lax.axis_index("tensor")
    core, side = place % 2, place // 2
    spread = [bit for bit in (1 << k for k in reversed(range(groups.bit_length() - 1))) if bit != PAIR]
    shape = jax.ShapeDtypeStruct
    last = [me]

    def swap(array, bit):
        return lax.ppermute(array, "dp", [(i, i ^ bit) for i in range(groups)])

    def cross(array, bit):
        return lax.ppermute(array, "tensor", [(i, i ^ bit) for i in range(ways)])

    def pick(array, index, axis, number=2):
        rows = array.shape[axis] // number
        return lax.dynamic_slice_in_dim(array, index * rows, rows, axis)

    def join(mine, theirs, index, axis):
        pair = jnp.concatenate([mine, theirs], axis=axis)
        turned = jnp.concatenate([theirs, mine], axis=axis)
        return jnp.where(index == 0, pair, turned)

    def after(*values):
        held, _ = lax.optimization_barrier((values, last[0]))
        return held

    def done(*values):
        values = lax.optimization_barrier(values)
        last[0] = values
        return values

    order = [0, PAIR]
    for bit in spread:
        order = order + [mask | bit for mask in order]
    inverse = [order.index(mask) for mask in range(groups)]
    held_at = jnp.asarray(inverse, jnp.int32)[jnp.arange(groups) ^ me]
    place_table = jnp.stack([held_at, held_at ^ 1])
    order_table = jnp.asarray(order, jnp.int32) ^ me
    vectors = jnp.stack([attn_norm_gain, attn_norm_bias, mlp_norm_gain, mlp_norm_bias, dense_bias, down_bias])
    step = part

    def scatter(send, keep):
        held = keep + swap(send, spread[-1]).astype(F)
        for bit in reversed(spread[:-1]):
            keep, send = jnp.split(held, 2, axis=0)
            held = keep + swap(send.astype(B), bit).astype(F)
        keep, send = jnp.split(held, 2, axis=0)
        return keep, swap(send, PAIR)

    def share_rows(rows):
        pair = jnp.stack([rows, cross(rows, 2)])
        quad = jnp.stack([pair, cross(pair, 1)])
        quad = jnp.where(side == 0, quad, jnp.concatenate([quad[:, 1:], quad[:, :1]], axis=1))
        quad = jnp.where(core == 0, quad, jnp.concatenate([quad[1:], quad[:1]], axis=0))
        return quad.reshape(length, width)

    def own_rows(array, axis):
        return pick(pick(array, core, axis), side, axis)

    def total_rows(partial):
        partial = partial.reshape(2, length, width)
        near = cross(pick(partial, 1 - core, 1), 1)
        keep = pick(partial, core, 1)
        far = (pick(keep, 1 - side, 1).astype(F) + pick(near, 1 - side, 1).astype(F)).astype(B)
        far = cross(far, 2)
        keep = pick(keep, side, 1).astype(F) + pick(near, side, 1).astype(F)
        sent = swap((keep[1] + far[1].astype(F)).astype(B), PAIR)
        return keep[0] + far[0].astype(F), sent

    own_x, own_g = tokens[0], out_grad[0]

    shards = [
        jnp.concatenate(
            [
                qkv_weight.astype(B).reshape(part, 2, 3 * size),
                dense_weight.astype(B).transpose(2, 0, 1),
            ],
            axis=2,
        ),
        up_weight.astype(B).reshape(part, 2, hidden),
        down_weight.astype(B).reshape(2, hidden, part).transpose(2, 0, 1),
    ]
    mine = jnp.stack([pick(shard, half, 1)[:, 0] for shard in shards])
    theirs = jnp.stack([pick(shard, 1 - half, 1)[:, 0] for shard in shards])

    seg_other = swap(segment_ids[0], PAIR)
    seg = jnp.stack([segment_ids[0], seg_other])
    seg_col, seg_row = seg[:, :, None], seg[:, None, :]
    qv_here, key_here = pick(qv_bias, half, 0), pick(key_bias, half, 0)
    key_full = jnp.concatenate([key_here, jnp.zeros((heads, size - ROT), F)], axis=1)
    offsets = jnp.stack([qv_here[:, 0], key_full, qv_here[:, 1]], axis=1).reshape(1, 3 * size)
    tables = rope_tables(length)
    up_here = pick(up_bias, half, 0)[None]
    columns = hidden
    half_width = width // 2
    vmem, hbm = pl.BlockSpec(memory_space=pltpu.VMEM), pl.BlockSpec(memory_space=pl.ANY)
    (
        weights,
        _,
        _,
        x_pair,
        g_pair,
        mlp_in,
        mixed_grad,
        context,
        activation,
        slope,
        attn_send,
        attn_keep,
        mixed_sum,
    ) = pl.pallas_call(
        functools.partial(gather_kernel, groups),
        in_specs=[hbm] * 4 + [vmem] * 8,
        out_specs=[hbm] * 12 + [vmem],
        out_shape=[
            shape((3, width, columns), B),
            shape((length, width), B),
            shape((length, width), B),
            shape((count, width), B),
            shape((count, width), B),
            shape((count, width), B),
            shape((count, 3 * size), B),
            shape((count, size), B),
            shape((count, hidden), B),
            shape((count, hidden), F),
            shape((half_width, columns), B),
            shape((half_width, columns), F),
            shape((1, 3 * size), F),
        ],
        scratch_shapes=[
            pltpu.VMEM((3, width, columns), B),
            pltpu.VMEM((2, CHUNK, width), B),
            pltpu.VMEM((2, CHUNK, width), B),
            pltpu.VMEM((length, width), B),
            pltpu.VMEM((length, width), B),
            pltpu.VMEM((count, width), B),
            pltpu.VMEM((length, width), B),
            pltpu.VMEM((width, columns), F),
            pltpu.VMEM((half_width, columns), B),
            pltpu.VMEM((length, size), B),
            pltpu.VMEM((length, size), B),
            pltpu.VMEM((length, size), B),
            pltpu.VMEM((length, size), B),
            pltpu.VMEM((length, size), B),
            pltpu.VMEM((length, 3 * size), B),
            pltpu.VMEM((length, size), F),
            pltpu.VMEM((length, size), F),
            pltpu.VMEM((2, CHUNK, hidden), B),
            pltpu.VMEM((2, CHUNK, hidden), F),
            pltpu.SemaphoreType.DMA((27,)),
            pltpu.SemaphoreType.DMA((27,)),
            pltpu.SemaphoreType.DMA((3,)),
            pltpu.SemaphoreType.DMA((2, 2)),
            pltpu.SemaphoreType.DMA((2, 5)),
            pltpu.SemaphoreType.DMA((2, 2)),
            pltpu.SemaphoreType.DMA((5,)),
        ],
        compiler_params=pltpu.CompilerParams(
            collective_id=0, has_side_effects=True, vmem_limit_bytes=67043328
        ),
        cost_estimate=pl.CostEstimate(flops=40 * 10**9, bytes_accessed=10**8, transcendentals=10**7),
        name="gather",
    )(mine, theirs, own_x, own_g, vectors, up_here, offsets, *tables, seg_col, seg_row)
    mixed_sum = mixed_sum.reshape(heads, 3, size)
    w_qkv, w_dense = weights[0, :, : 3 * size], weights[0, :, 3 * size :]
    w_up, w_down = weights[1], weights[2]
    last[0] = attn_send

    near, far = slice(0, width // 2), slice(width // 2, width)

    def partial(pairs, columns, kind):
        return jnp.concatenate([dot(left[:, columns], right, ((0,), (0,)), kind) for left, right in pairs], axis=1)

    def scattered(*pairs):
        (send,) = done(partial(pairs, far, B))
        pairs = [after(*pair) for pair in pairs]
        (keep,) = done(partial(pairs, near, F))
        return scatter(send, keep)

    attn_near, attn_far = scatter(attn_send, attn_keep)

    tile = 512
    tiles = (count // tile,)
    down_near, down_far = scattered((g_pair, activation))
    pre_grad, up_bias_sum = done(
        *call(
            pre_kernel,
            tiles,
            [tiled(tile, width), shared(width, hidden), tiled(tile, hidden)],
            [tiled(tile, hidden), shared(1, hidden)],
            [shape((count, hidden), B), shape((1, hidden), F)],
            2 * count * width * hidden,
            20 * count * hidden,
            name="pre_grad",
        )(g_pair, w_down, slope)
    )
    blend, norm_sums = done(
        *call(
            lambda *refs: blend_kernel(step, *refs),
            tiles,
            [
                tiled(tile, 3 * size),
                tiled(tile, hidden),
                shared(width, 3 * size),
                shared(width, hidden),
                tiled(tile, width),
                shared(6, width),
            ],
            [tiled(tile, width), shared(4, width)],
            [shape((count, width), B), shape((4, width), F)],
            2 * count * width * (hidden + 3 * size),
            20 * count * hidden,
            prefetch=1,
            name="blend",
        )(order_table, mixed_grad, pre_grad, w_qkv, w_up, x_pair, vectors)
    )
    blend_held, blend_sent = total_rows(blend)
    context, activation, w_dense, w_down = after(context, activation, w_dense, w_down)
    (branch,) = done(
        call(
            branch_kernel,
            tiles,
            [tiled(tile, size), tiled(tile, hidden), shared(width, size), shared(width, hidden)],
            tiled(tile, width),
            shape((count, width), B),
            2 * count * width * (hidden + size),
            20 * count * hidden,
            name="branch",
        )(context, activation, w_dense, w_down)
    )
    branch_held, branch_sent = total_rows(branch)
    up_near, up_far = scattered((mlp_in, pre_grad))

    quarter = length // 4
    x_rows, g_rows = own_rows(own_x, 0), own_rows(own_g, 0)
    rows_out = shape((quarter, width), B)
    row_spec = tiled(quarter // 2, width)

    def finished(kernel, name, *operands):
        specs = [row_spec if a.shape[0] == quarter else shared(*a.shape) for a in operands]
        return call(
            lambda *refs: kernel(step, *refs), (2,), specs, row_spec, rows_out, 10 * quarter * width, 10 * quarter * width,
            prefetch=1, name=name,
        )(place_table, *operands)

    input_grad = share_rows(finished(finish_grad, "finish_grad", blend_held, blend_sent, x_rows, g_rows))
    block_out = share_rows(finished(finish_out, "finish_out", branch_held, branch_sent, x_rows, vectors))

    def by_half(near, far):
        return jnp.where(half == 0, jnp.stack([near, far]), jnp.stack([far, near]))

    attn_shard = by_half(attn_near, attn_far)
    qkv_shard = attn_shard[:, :, : 3 * size].transpose(1, 0, 2)
    dense_shard = attn_shard[:, :, 3 * size :].transpose(0, 2, 1)
    up_shard = jnp.where(half == 0, jnp.concatenate([up_near, up_far], 1), jnp.concatenate([up_far, up_near], 1))
    down_shard = by_half(down_near, down_far).transpose(0, 2, 1)

    bias_sum = jnp.sum(own_g.astype(F), axis=0)

    def slotted(array):
        zero = jnp.zeros_like(array)
        return join(array, zero, half, 0)

    small = [norm_sums.reshape(-1), bias_sum, slotted(up_bias_sum[0]), slotted(mixed_sum).reshape(-1)]
    sizes = [s.shape[0] for s in small]
    flat = jnp.concatenate(small)
    for bit in [1 << k for k in range(groups.bit_length() - 1)]:
        flat = flat + swap(flat, bit)
    ends = [sum(sizes[: i + 1]) for i in range(len(sizes))]
    norms = flat[: ends[0]]
    for bit in [1 << k for k in range(ways.bit_length() - 1)]:
        norms = norms + cross(norms, bit)
    norms = norms.reshape(4, width)
    bias_grad = flat[ends[0] : ends[1]]
    up_bias_grad = flat[ends[1] : ends[2]]
    mixed_bias = flat[ends[2] :].reshape(2 * heads, 3, size)
    qv_grad = jnp.stack([mixed_bias[:, 0], mixed_bias[:, 2]], axis=1)
    key_bias_grad = mixed_bias[:, 1, :ROT]

    return (
        block_out[None],
        input_grad[None],
        norms[0],
        norms[1],
        norms[2],
        norms[3],
        qkv_shard.reshape(qkv_weight.shape),
        qv_grad,
        key_bias_grad,
        dense_shard.reshape(dense_weight.shape),
        bias_grad,
        up_shard,
        up_bias_grad,
        down_shard.reshape(down_weight.shape),
        bias_grad,
    )


def solution(mesh):
    placed = (
        P("dp", None, None),
        P("dp", None),
        P("dp", None, None),
        P(),
        P(),
        P(),
        P(),
        P("dp", "tensor", None, None),
        P("tensor", None, None),
        P("tensor", None),
        P("tensor", None, "dp"),
        P(),
        P("dp", "tensor"),
        P("tensor"),
        P("tensor", "dp"),
        P(),
    )

    def whole(*arrays):
        groups, ways = mesh.shape["dp"], mesh.shape["tensor"]
        part = arrays[0].shape[2] // groups
        chosen = body_narrow if part % 128 or groups != 8 else body
        return chosen(*arrays, groups=groups, ways=ways)

    return jax.shard_map(
        whole,
        mesh=mesh,
        in_specs=placed,
        out_specs=(
            P("dp", None, None),
            P("dp", None, None),
            P(),
            P(),
            P(),
            P(),
            P("dp", "tensor", None, None),
            P("tensor", None, None),
            P("tensor", None),
            P("tensor", None, "dp"),
            P(),
            P("dp", "tensor"),
            P("tensor"),
            P("tensor", "dp"),
            P(),
        ),
        check_vma=False,
    )
```

```python
import functools

import jax
import jax.numpy as jnp
from jax import lax
from jax.experimental import pallas as pl
from jax.experimental.pallas import tpu as pltpu
from jax.sharding import PartitionSpec as P

ROT = 64
PAIR = 2
QBLOCK = 256
DOC_MAX = 512
F = jnp.float32
B = jnp.bfloat16


def dot(left, right, dims, kind):
    return lax.dot_general(left, right, (dims, ((), ())), preferred_element_type=F).astype(kind)


def gelu_slope(pre_act):
    cumulative = 0.5 * (1.0 + lax.erf(pre_act * 0.7071067811865476))
    density = jnp.exp(-0.5 * pre_act * pre_act) * 0.3989422804014327
    return cumulative + pre_act * density


def rope_tables(length):
    half = ROT // 2
    frequency = 10000.0 ** (-(jnp.arange(half, dtype=F) * 2.0) / ROT)
    angles = jnp.arange(length, dtype=F)[:, None] * frequency[None, :]
    cosine, sine = jnp.cos(angles), jnp.sin(angles)
    flat = jnp.zeros((length, 128 - ROT), F)
    zero = jnp.zeros_like(sine)
    return (
        jnp.concatenate([cosine, cosine, flat + 1.0], axis=1),
        jnp.concatenate([-sine, zero, flat], axis=1),
        jnp.concatenate([zero, sine, flat], axis=1),
    )


def turn(rows, cosine, from_above, from_below):
    head = rows[:, :128]
    above = pltpu.roll(head, 128 - ROT // 2, 1)
    below = pltpu.roll(head, ROT // 2, 1)
    turned = head * cosine + above * from_above + below * from_below
    return jnp.concatenate([turned, rows[:, 128:]], axis=1)


def block_mask(seg_col_ref, seg_row_ref, first, low, high):
    rows = first + lax.broadcasted_iota(jnp.int32, (QBLOCK, high - low), 0)
    columns = low + lax.broadcasted_iota(jnp.int32, (QBLOCK, high - low), 1)
    same = seg_col_ref[0, first : first + QBLOCK, :] == seg_row_ref[0, :, low:high]
    return (columns <= rows) & same


def key_range(first):
    return max(0, first - DOC_MAX), first + QBLOCK


def attn_forward(mixed_ref, bias_ref, cos_ref, up_ref, down_ref, col_ref, row_ref, q_ref, k_ref, v_ref, ctx_ref, lse_ref):
    size = q_ref.shape[2]
    length = q_ref.shape[1]
    scale = size ** (-0.5)
    tables = (cos_ref[...], up_ref[...], down_ref[...])
    q_ref[0] = turn(mixed_ref[0, :, :size] + bias_ref[:, :size], *tables).astype(B)
    k_ref[0] = turn(mixed_ref[0, :, size : 2 * size] + bias_ref[:, size : 2 * size], *tables).astype(B)
    v_ref[0] = (mixed_ref[0, :, 2 * size :] + bias_ref[:, 2 * size :]).astype(B)
    for first in range(0, length, QBLOCK):
        low, high = key_range(first)
        scores = dot(q_ref[0, first : first + QBLOCK], k_ref[0, low:high], ((1,), (1,)), F) * scale
        scores = jnp.where(block_mask(col_ref, row_ref, first, low, high), scores, -1e30)
        row_max = jnp.max(scores, axis=1, keepdims=True)
        expo = jnp.exp(scores - row_max)
        total = jnp.sum(expo, axis=1, keepdims=True)
        probs = (expo / total).astype(B)
        ctx_ref[0, first : first + QBLOCK] = dot(probs, v_ref[0, low:high], ((1,), (0,)), B)
        lse_ref[0, first : first + QBLOCK] = row_max + jnp.log(total)


def attn_backward(q_ref, k_ref, v_ref, grad_ref, lse_ref, cos_ref, up_ref, down_ref, col_ref, row_ref, mixed_ref, sum_ref, q_acc, k_acc, v_acc):
    size = q_ref.shape[2]
    length = q_ref.shape[1]
    scale = size ** (-0.5)
    k_acc[...] = jnp.zeros_like(k_acc)
    v_acc[...] = jnp.zeros_like(v_acc)
    for first in range(0, length, QBLOCK):
        low, high = key_range(first)
        here = slice(first, first + QBLOCK)
        scores = dot(q_ref[0, here], k_ref[0, low:high], ((1,), (1,)), F) * scale
        scores = jnp.where(block_mask(col_ref, row_ref, first, low, high), scores, -1e30)
        probs = jnp.exp(scores - lse_ref[0, here])
        v_acc[low:high] += dot(probs.astype(B), grad_ref[0, here], ((0,), (0,)), F)
        prob_grad = dot(grad_ref[0, here], v_ref[0, low:high], ((1,), (1,)), F)
        centred = jnp.sum(probs * prob_grad, axis=1, keepdims=True)
        score_grad = (probs * (prob_grad - centred)).astype(B)
        q_acc[here] = dot(score_grad, k_ref[0, low:high], ((1,), (0,)), F) * scale
        k_acc[low:high] += dot(score_grad, q_ref[0, here], ((0,), (0,)), F) * scale
    tables = (cos_ref[...], -up_ref[...], -down_ref[...])
    q_grad = turn(q_acc[...], *tables).astype(B)
    k_grad = turn(k_acc[...], *tables).astype(B)
    v_grad = v_acc[...].astype(B)
    for number, part in enumerate((q_grad, k_grad, v_grad)):
        mixed_ref[0, :, number * size : (number + 1) * size] = part
        sum_ref[0, :, number * size : (number + 1) * size] = jnp.sum(part.astype(F), axis=0, keepdims=True)


def per_seq(rows, columns):
    return pl.BlockSpec((1, rows, columns), lambda seq, *_: (seq, 0, 0))


def shared(rows, columns):
    return pl.BlockSpec((rows, columns), lambda *_: (0, 0))


MESH = pl.DeviceIdType.MESH
CHUNK = 256


def bit_of(index, bit):
    return lax.rem(lax.div(index, bit), 2)


def flip(index, mask):
    bit = 1
    while bit <= mask:
        if mask & bit:
            index = index + bit * (1 - 2 * bit_of(index, bit))
        bit *= 2
    return index


def block_order(groups):
    spread = [bit for bit in (1 << k for k in reversed(range(groups.bit_length() - 1))) if bit != PAIR]
    order = [0, PAIR]
    for bit in spread:
        order = order + [mask | bit for mask in order]
    return spread, order


def stats(rows):
    mean = jnp.mean(rows, axis=1, keepdims=True)
    center = rows - mean
    return mean, lax.rsqrt(jnp.mean(center * center, axis=1, keepdims=True) + 1e-05)


def greet(partners):
    barrier = pltpu.get_barrier_semaphore()
    for axis, index in partners:
        pl.semaphore_signal(barrier, inc=1, device_id={axis: index}, device_id_type=MESH)
    pl.semaphore_wait(barrier, len(partners))


def gather_kernel(
    groups,
    mine_ref,
    theirs_ref,
    x_ref,
    g_ref,
    vec_ref,
    up_bias_ref,
    offset_ref,
    cos_ref,
    above_ref,
    below_ref,
    col_ref,
    row_ref,
    w_out,
    x_other,
    g_other,
    x_rel,
    g_rel,
    mlp_out,
    mixed_out,
    ctx_out,
    act_out,
    slope_out,
    send_out,
    keep_out,
    sum_ref,
    bias_ref,
    w,
    raw_x,
    raw_g,
    attn_v,
    g_v,
    mlp_v,
    xr_v,
    grad_v,
    send_v,
    q_v,
    k_v,
    v_v,
    cg_v,
    ctx_v,
    mg_v,
    dk_v,
    dv_v,
    act_v,
    slope_v,
    send_sem,
    recv_sem,
    own_sem,
    load_sem,
    rel_sem,
    tile_sem,
    out_sem,
):
    length, width = x_ref.shape
    part = width // groups
    size = q_v.shape[1]
    quarter = length // 4
    me, place = lax.axis_index("dp"), lax.axis_index("tensor")
    core, side = lax.rem(place, 2), lax.div(place, 2)
    pair_to, side_to, core_to = flip(me, PAIR), flip(place, 2), flip(place, 1)
    spread, order = block_order(groups)
    greet([("dp", flip(me, bit)) for bit in [PAIR] + spread] + [("tensor", side_to), ("tensor", core_to)])
    copies = {}

    def remote(key, source, target, axis, index):
        number = len(copies)
        copies[key] = pltpu.make_async_remote_copy(
            src_ref=source,
            dst_ref=target,
            send_sem=send_sem.at[number],
            recv_sem=recv_sem.at[number],
            device_id={axis: index},
            device_id_type=MESH,
        )
        copies[key].start()

    def rows(position):
        return pl.ds(position * part, part)

    def pair_up(group):
        remote(("w", group, 1), theirs_ref.at[group], w.at[group, rows(1)], "dp", pair_to)

    def onward(group, position, level):
        source = mine_ref.at[group] if position == 0 else w.at[group, rows(position)]
        far = position + (2 << level)
        remote(("w", group, far), source, w.at[group, rows(far)], "dp", flip(me, spread[level]))

    def arrive(group, position, ahead=()):
        copies[("w", group, position)].wait_recv()

    spot = pl.ds(pl.multiple_of(core * (2 * quarter) + side * quarter, quarter), quarter)
    pair_rows = pl.ds(pl.multiple_of(core * (2 * quarter), quarter), 2 * quarter)
    levels = len(spread)
    assert levels == 2

    def load(x, g, tile, slot):
        here = pl.ds(pl.multiple_of(tile * CHUNK, CHUNK), CHUNK)
        return (
            pltpu.make_async_copy(x.at[here], raw_x.at[slot], load_sem.at[0, slot]),
            pltpu.make_async_copy(g.at[here], raw_g.at[slot], load_sem.at[1, slot]),
        )

    def normalise(seq, x, g):
        for copy in load(x, g, 0, 0):
            copy.start()

        def one(tile, carry):
            slot = lax.rem(tile, 2)

            @pl.when(tile + 1 < length // CHUNK)
            def _():
                for copy in load(x, g, tile + 1, 1 - slot):
                    copy.start()

            for copy in load(x, g, tile, slot):
                copy.wait()
            here = pl.ds(pl.multiple_of(tile * CHUNK, CHUNK), CHUNK)
            both = pl.ds(pl.multiple_of(seq * length + tile * CHUNK, CHUNK), CHUNK)
            mean, inverse = stats(raw_x[slot].astype(F))
            if seq == 0:
                bias_ref[...] += jnp.sum(raw_g[slot].astype(F), axis=0, keepdims=True)
            for position, mask in enumerate(order):
                to = slice(position * part, (position + 1) * part)
                there = pl.ds(pl.multiple_of(flip(me, mask) * part, part), part)
                piece = raw_x[slot, :, there]
                normed = (piece.astype(F) - mean) * inverse
                attn_v[here, to] = (normed * vec_ref[0:1, there] + vec_ref[1:2, there]).astype(B)
                mlp_v[both, to] = (normed * vec_ref[2:3, there] + vec_ref[3:4, there]).astype(B)
                xr_v[here, to] = piece
                g_v[here, to] = raw_g[slot, :, there]
            return carry

        lax.fori_loop(0, length // CHUNK, one, 0)
        both = pl.ds(seq * length, length)
        return [
            pltpu.make_async_copy(xr_v, x_rel.at[both], rel_sem.at[seq, 0]),
            pltpu.make_async_copy(g_v, g_rel.at[both], rel_sem.at[seq, 1]),
            pltpu.make_async_copy(mlp_v.at[both], mlp_out.at[both], rel_sem.at[seq, 2]),
        ]

    def project():
        def one(tile, carry):
            here = pl.ds(pl.multiple_of(tile * CHUNK, CHUNK), CHUNK)
            mixed = dot(attn_v[here], w[0, :, : 3 * size], ((1,), (0,)), F) + offset_ref[...]
            tables = (cos_ref[here], above_ref[here], below_ref[here])
            q_v[here] = turn(mixed[:, :size], *tables).astype(B)
            k_v[here] = turn(mixed[:, size : 2 * size], *tables).astype(B)
            v_v[here] = mixed[:, 2 * size :].astype(B)
            cg_v[here] = dot(g_v[here], w[0, :, 3 * size :], ((1,), (0,)), B)
            return carry

        lax.fori_loop(0, length // CHUNK, one, 0)

    def attend(seq):
        scale = size ** (-0.5)
        dk_v[...] = jnp.zeros_like(dk_v)
        dv_v[...] = jnp.zeros_like(dv_v)
        for first in range(0, length, QBLOCK):
            low, high = key_range(first)
            here, keys = slice(first, first + QBLOCK), slice(low, high)
            scores = dot(q_v[here], k_v[keys], ((1,), (1,)), F) * scale
            row_ids = first + lax.broadcasted_iota(jnp.int32, (QBLOCK, high - low), 0)
            key_ids = low + lax.broadcasted_iota(jnp.int32, (QBLOCK, high - low), 1)
            allowed = (key_ids <= row_ids) & (col_ref[seq, here, :] == row_ref[seq, :, keys])
            scores = jnp.where(allowed, scores, -1e30)
            expo = jnp.exp(scores - jnp.max(scores, axis=1, keepdims=True))
            probs = expo / jnp.sum(expo, axis=1, keepdims=True)
            low_probs = probs.astype(B)
            ctx_v[here] = dot(low_probs, v_v[keys], ((1,), (0,)), B)
            dv_v[keys] += dot(low_probs, cg_v[here], ((0,), (0,)), F)
            prob_grad = dot(cg_v[here], v_v[keys], ((1,), (1,)), F)
            centred = jnp.sum(probs * prob_grad, axis=1, keepdims=True)
            score_grad = (probs * (prob_grad - centred)).astype(B)
            q_grad = dot(score_grad, k_v[keys], ((1,), (0,)), F) * scale
            tables = (cos_ref[here], -above_ref[here], -below_ref[here])
            mg_v[here, :size] = turn(q_grad, *tables).astype(B)
            dk_v[keys] += dot(score_grad, q_v[here], ((0,), (0,)), F) * scale
        for first in range(0, length, QBLOCK):
            here = slice(first, first + QBLOCK)
            tables = (cos_ref[here], -above_ref[here], -below_ref[here])
            mg_v[here, size : 2 * size] = turn(dk_v[here], *tables).astype(B)
            mg_v[here, 2 * size :] = dv_v[here].astype(B)
        sums = jnp.sum(mg_v[...].astype(F), axis=0, keepdims=True)
        if seq == 0:
            sum_ref[...] = sums
        else:
            sum_ref[...] += sums
        both = pl.ds(seq * length, length)
        return [
            pltpu.make_async_copy(mg_v, mixed_out.at[both], rel_sem.at[seq, 3]),
            pltpu.make_async_copy(ctx_v, ctx_out.at[both], rel_sem.at[seq, 4]),
        ]

    def attn_grads(seq, low, high):
        def one(block, carry):
            here = pl.ds(pl.multiple_of(block * CHUNK, CHUNK), CHUNK)
            qkv = dot(attn_v[:, here], mg_v[...], ((0,), (0,)), F)
            dense = dot(g_v[:, here], ctx_v[...], ((0,), (0,)), F)
            if seq == 0:
                grad_v[here, : 3 * size] = qkv
                grad_v[here, 3 * size :] = dense
            else:
                grad_v[here, : 3 * size] += qkv
                grad_v[here, 3 * size :] += dense
            return carry

        lax.fori_loop(low // CHUNK, high // CHUNK, one, 0)

    def up(low, high):
        def store(tile, slot):
            here = pl.ds(pl.multiple_of(tile * CHUNK, CHUNK), CHUNK)
            return (
                pltpu.make_async_copy(act_v.at[slot], act_out.at[here], tile_sem.at[0, slot]),
                pltpu.make_async_copy(slope_v.at[slot], slope_out.at[here], tile_sem.at[1, slot]),
            )

        def one(tile, carry):
            slot = lax.rem(tile, 2)
            here = pl.ds(pl.multiple_of(tile * CHUNK, CHUNK), CHUNK)
            pre = dot(mlp_v[here], w[1], ((1,), (0,)), F) + up_bias_ref[...]

            @pl.when(tile >= low + 2)
            def _():
                for copy in store(tile - 2, slot):
                    copy.wait()

            cumulative = 0.5 * (1.0 + lax.erf(pre * 0.7071067811865476))
            density = jnp.exp(-0.5 * pre * pre) * 0.3989422804014327
            act_v[slot] = (pre * cumulative).astype(B)
            slope_v[slot] = cumulative + pre * density
            for copy in store(tile, slot):
                copy.start()
            return carry

        lax.fori_loop(low, high, one, 0)
        for tile in (high - 2, high - 1):
            for copy in store(tile, tile % 2):
                copy.wait()

    def weights_out(group):
        return pltpu.make_async_copy(w.at[group], w_out.at[group], out_sem.at[group])

    pair_up(0)
    onward(0, 0, 0)
    onward(0, 0, 1)
    own = [pltpu.make_async_copy(mine_ref.at[group], w.at[group, rows(0)], own_sem.at[group]) for group in range(3)]
    for copy in own:
        copy.start()
    bias_ref[...] = jnp.zeros_like(bias_ref)
    first_out = normalise(0, x_ref, g_ref)
    for copy in first_out:
        copy.start()
    arrive(0, 1)
    onward(0, 1, 0)
    onward(0, 1, 1)
    remote("x1", x_ref.at[spot], x_other.at[spot], "dp", pair_to)
    pair_up(1)
    onward(1, 0, 0)
    onward(1, 0, 1)
    arrive(0, 2)
    onward(0, 2, 1)
    remote("g1", g_ref.at[spot], g_other.at[spot], "dp", pair_to)
    arrive(0, 3)
    onward(0, 3, 1)
    copies["x1"].wait_recv()
    remote("x2", x_other.at[spot], x_other.at[spot], "tensor", side_to)
    arrive(1, 1)
    onward(1, 1, 0)
    onward(1, 1, 1)
    pair_up(2)
    onward(2, 0, 0)
    onward(2, 0, 1)
    for position in range(4, 8):
        arrive(0, position)
    for copy in own:
        copy.wait()
    out = [weights_out(0)]
    out[0].start()
    project()
    arrive(1, 2)
    onward(1, 2, 1)
    copies["x2"].wait_recv()
    remote("x3", x_other.at[pair_rows], x_other.at[pair_rows], "tensor", core_to)
    copies["g1"].wait_recv()
    remote("g2", g_other.at[spot], g_other.at[spot], "tensor", side_to)
    second_out = attend(0)
    for copy in second_out:
        copy.start()
    arrive(2, 1)
    onward(2, 1, 0)
    onward(2, 1, 1)
    arrive(1, 3)
    onward(1, 3, 1)
    attn_grads(0, 0, width)
    copies["x3"].wait_recv()
    copies["g2"].wait_recv()
    remote("g3", g_other.at[pair_rows], g_other.at[pair_rows], "tensor", core_to)
    for copy in first_out + second_out:
        copy.wait()
    copies["g3"].wait_recv()
    arrive(2, 2)
    onward(2, 2, 1)
    third_out = normalise(1, x_other, g_other)
    for copy in third_out:
        copy.start()
    project()
    arrive(2, 3)
    onward(2, 3, 1)
    fourth_out = attend(1)
    for copy in fourth_out:
        copy.start()
    attn_grads(1, width // 2, width)
    send_v[...] = grad_v[width // 2 :].astype(B)
    out.append(pltpu.make_async_copy(send_v, send_out, out_sem.at[3]))
    out[-1].start()
    attn_grads(1, 0, width // 2)
    out.append(pltpu.make_async_copy(grad_v.at[pl.ds(0, width // 2)], keep_out, out_sem.at[4]))
    out[-1].start()
    for position in range(4, 8):
        arrive(1, position)
    out.append(weights_out(1))
    out[-1].start()
    up(0, 2 * length // CHUNK)
    for position in range(4, 8):
        arrive(2, position)
    out.append(weights_out(2))
    out[-1].start()
    for copy in third_out + fourth_out + out:
        copy.wait()
    for copy in copies.values():
        copy.wait_send()


def scatter_kernel(
    groups,
    attn_send,
    attn_keep,
    weights,
    x_rel,
    g_rel,
    mlp_in,
    mixed_grad,
    context,
    activation,
    slope,
    x_ref,
    g_ref,
    vec_ref,
    mixed_sum,
    bias_sum,
    block_out,
    input_grad,
    near_out,
    far_out,
    y_recv,
    z_recv,
    c_recv,
    x_recv,
    e_recv,
    small_out,
    w,
    act_v,
    pre_v,
    tile_v,
    col_v,
    slope_t,
    mix_t,
    ctx_v,
    keep_v,
    y_send,
    z_send,
    y_stage,
    c_send,
    c_stage,
    r_stage,
    x_send,
    hold_v,
    mean_v,
    inverse_v,
    e_send,
    sum_v,
    small_v,
    small_recv,
    load_sem,
    tile_sem,
    ys_sem,
    yr_sem,
    zs_sem,
    zr_sem,
    ps_sem,
    pr_sem,
    cs_sem,
    cr_sem,
    xs_sem,
    xr_sem,
    es_sem,
    er_sem,
    fs_sem,
    fr_sem,
    ss_sem,
    sr_sem,
    out_sem,
):
    length, width = x_ref.shape
    part = width // groups
    size = context.shape[1]
    hidden = activation.shape[1]
    quarter = length // 4
    me, place = lax.axis_index("dp"), lax.axis_index("tensor")
    core, side, half = lax.rem(place, 2), lax.div(place, 2), bit_of(me, PAIR)
    pair_to, side_to, core_to = flip(me, PAIR), flip(place, 2), flip(place, 1)
    spread, order = block_order(groups)
    z_to, y_to = [flip(me, bit) for bit in spread]
    greet([("dp", pair_to), ("dp", z_to), ("dp", y_to), ("tensor", side_to), ("tensor", core_to)])

    def remote(source, target, send, recv, axis, index):
        return pltpu.make_async_remote_copy(
            src_ref=source, dst_ref=target, send_sem=send, recv_sem=recv, device_id={axis: index}, device_id_type=MESH
        )

    def span(position, count=1):
        return pl.ds(position * part, count * part)

    def step(index, amount):
        return pl.ds(pl.multiple_of(index * amount, amount), amount)

    def y_copy(group, position):
        source = attn_send if group == 0 else y_send
        here = step(position, part) if not isinstance(position, int) else span(position)
        return remote(
            source.at[here], y_recv.at[group, here], ys_sem.at[group, position], yr_sem.at[group, position], "dp", y_to
        )

    def z_copy(group, position):
        return remote(
            z_send.at[slot_of[group], span(position)],
            z_recv.at[group, span(position)],
            zs_sem.at[group, position],
            zr_sem.at[group, position],
            "dp",
            z_to,
        )

    slot_of = (0, 0, 1)

    def p_copy(group):
        return remote(
            keep_v.at[slot_of[group], span(1)], far_out.at[group], ps_sem.at[group], pr_sem.at[group], "dp", pair_to
        )

    def near_copy(group):
        return pltpu.make_async_copy(keep_v.at[slot_of[group], span(0)], near_out.at[group], out_sem.at[group])

    def staged(source):
        copy = pltpu.make_async_copy(source, y_stage, load_sem.at[6])
        copy.start()
        copy.wait()

    def y_far(group):
        for position in (3, 2):
            y_copy(group, position).wait_recv()
            staged(y_recv.at[group, span(position)])
            total = keep_v[slot_of[group], span(position)] + y_stage[...].astype(F)
            if group == 1:
                z_copy(0, position - 2).wait_send()
            z_send[slot_of[group], span(position - 2)] = total.astype(B)
            z_copy(group, position - 2).start()

    def y_near(group):
        for position in (1, 0):
            y_copy(group, position).wait_recv()
            staged(y_recv.at[group, span(position)])
            keep_v[slot_of[group], span(position)] += y_stage[...].astype(F)

    def z_last(group, position):
        z_copy(group, position).wait_recv()
        staged(z_recv.at[group, span(position)])
        keep_v[slot_of[group], span(position)] += y_stage[...].astype(F)
        if position == 1:
            p_copy(group).start()
        else:
            near_copy(group).start()

    loads = [
        pltpu.make_async_copy(weights.at[2], w.at[2], load_sem.at[0]),
        pltpu.make_async_copy(weights.at[0], w.at[0], load_sem.at[1]),
        pltpu.make_async_copy(weights.at[1], w.at[1], load_sem.at[2]),
        pltpu.make_async_copy(activation, act_v, load_sem.at[3]),
        pltpu.make_async_copy(context, ctx_v, load_sem.at[4]),
        pltpu.make_async_copy(attn_keep, keep_v.at[0], load_sem.at[5]),
    ]
    for copy in loads:
        copy.start()
    for position in (3, 2, 1, 0):
        y_copy(0, position).start()

    small_v[...] = jnp.zeros_like(small_v)

    def pre_load(tile, slot):
        here = step(tile, CHUNK)
        return (
            pltpu.make_async_copy(g_rel.at[here], tile_v.at[step(slot, CHUNK)], tile_sem.at[0, slot]),
            pltpu.make_async_copy(slope.at[here], slope_t.at[slot], tile_sem.at[1, slot]),
        )

    for copy in pre_load(0, 0):
        copy.start()
    sum_v[...] = jnp.zeros_like(sum_v)
    loads[0].wait()

    def pre_tile(tile, carry):
        slot = lax.rem(tile, 2)

        @pl.when(tile + 1 < 2 * length // CHUNK)
        def _():
            for copy in pre_load(tile + 1, 1 - slot):
                copy.start()

        for copy in pre_load(tile, slot):
            copy.wait()
        grad = (dot(tile_v[step(slot, CHUNK)], w[2], ((1,), (0,)), F) * slope_t[slot]).astype(B)
        pre_v[step(tile, CHUNK)] = grad
        sum_v[...] += jnp.sum(grad.astype(F), axis=0, keepdims=True)
        return carry

    lax.fori_loop(0, 2 * length // CHUNK, pre_tile, 0)

    tall = 2 * quarter
    blocks = width // CHUNK

    def c_copy(which, seq, block):
        here = step(block, CHUNK)
        return remote(
            c_send.at[:, here],
            c_recv.at[which, seq, :, here],
            cs_sem.at[which, seq, block],
            cr_sem.at[which, seq, block],
            "tensor",
            core_to,
        )

    def x_copy(which, seq):
        return remote(
            x_send.at[which, seq], x_recv.at[which, seq], xs_sem.at[which, seq], xr_sem.at[which, seq], "tensor", side_to
        )

    def e_copy(which):
        return remote(e_send.at[which], e_recv.at[which], es_sem.at[which], er_sem.at[which], "dp", pair_to)

    def send_tile(which, seq, begin, block_of):
        start = pl.multiple_of(seq * length + (1 - core) * tall, tall)
        begin(start)

        def one(block, carry):
            value = block_of(start, block)
            if (which, seq) != (0, 1):
                before = (0, 1) if seq == 0 and which == 0 else ((0, 0) if seq == 1 else (1, 1))
                c_copy(*before, block).wait_send()
            c_send[:, step(block, CHUNK)] = value.astype(B)
            c_copy(which, seq, block).start()
            return carry

        lax.fori_loop(0, blocks, one, 0)

    def c_load(which, seq, block, slot):
        return pltpu.make_async_copy(c_recv.at[which, seq, :, step(block, CHUNK)], c_stage.at[slot], tile_sem.at[2, slot])

    def keep_tile(which, seq, begin, block_of):
        start = pl.multiple_of(seq * length + core * tall, tall)
        begin(start)
        c_copy(which, seq, 0).wait_recv()
        c_load(which, seq, 0, 0).start()

        def one(block, carry):
            slot = lax.rem(block, 2)
            value = block_of(start, block)

            @pl.when(block + 1 < blocks)
            def _():
                c_copy(which, seq, block + 1).wait_recv()
                c_load(which, seq, block + 1, 1 - slot).start()

            c_load(which, seq, block, slot).wait()
            r_stage[...] = value + c_stage[slot].astype(F)
            here = step(block, CHUNK)
            hold_v[which, seq, :, here] = r_stage[step(side, quarter)]
            x_send[which, seq, :, here] = r_stage[step(1 - side, quarter)].astype(B)
            return carry

        lax.fori_loop(0, blocks, one, 0)
        x_copy(which, seq).start()

    def blend_begin(start):
        copies = (
            pltpu.make_async_copy(x_rel.at[pl.ds(start, tall)], tile_v, tile_sem.at[3, 0]),
            pltpu.make_async_copy(mixed_grad.at[pl.ds(start, tall)], mix_t, tile_sem.at[3, 1]),
        )
        for copy in copies:
            copy.start()
        for copy in copies:
            copy.wait()
        for slot in range(2):
            mean, inverse = stats(tile_v[span_rows(slot)].astype(F))
            mean_v[span_rows(slot)] = jnp.broadcast_to(mean, (CHUNK, 128))
            inverse_v[span_rows(slot)] = jnp.broadcast_to(inverse, (CHUNK, 128))

    def span_rows(slot):
        return pl.ds(slot * CHUNK, CHUNK)

    def natural_block(position):
        result = me
        for level, bit in enumerate([PAIR] + spread):
            flipped = lax.rem(lax.div(position, 1 << level), 2)
            result = result + bit * (1 - 2 * bit_of(me, bit)) * flipped
        return result

    def blend_block(start, block):
        here = step(block, CHUNK)
        there = step(natural_block(block), part)
        attn_grad = dot(mix_t[...], w[0, here, : 3 * size], ((1,), (1,)), F)
        mlp_grad = dot(pre_v[pl.ds(start, tall)], w[1, here, :], ((1,), (1,)), F)
        mean, inverse = mean_v[...], inverse_v[...]
        mean = jnp.concatenate([mean] * (CHUNK // 128), axis=1)
        inverse = jnp.concatenate([inverse] * (CHUNK // 128), axis=1)
        normed = (tile_v[:, here].astype(F) - mean) * inverse
        small_v[0:1, there] += jnp.sum(attn_grad * normed, axis=0, keepdims=True)
        small_v[1:2, there] += jnp.sum(attn_grad, axis=0, keepdims=True)
        small_v[2:3, there] += jnp.sum(mlp_grad * normed, axis=0, keepdims=True)
        small_v[3:4, there] += jnp.sum(mlp_grad, axis=0, keepdims=True)
        return attn_grad * vec_ref[0:1, there] + mlp_grad * vec_ref[2:3, there]

    for copy in loads[1:3]:
        copy.wait()
    send_tile(0, 1, blend_begin, blend_block)
    loads[5].wait()
    y_far(0)
    send_tile(0, 0, blend_begin, blend_block)
    keep_tile(0, 1, blend_begin, blend_block)
    keep_tile(0, 0, blend_begin, blend_block)

    small_v[4:5] = bias_sum[...]
    small_v[5:6, step(half, hidden)] = sum_v[...]
    small_v[6:7, pl.ds(pl.multiple_of(half * (width // 2), width // 2), 3 * size)] = mixed_sum[...]
    rounds = [("dp", flip(me, bit)) for bit in [PAIR] + spread] + [("tensor", side_to), ("tensor", core_to)]

    def small_copy(number):
        return remote(small_v, small_recv.at[number], ss_sem.at[number], sr_sem.at[number], *rounds[number])

    def small_end(number):
        small_copy(number).wait()
        if number < 3:
            small_v[...] += small_recv[number]
        else:
            small_v[0:4] += small_recv[number, 0:4]
        if number + 1 < len(rounds):
            small_copy(number + 1).start()

    small_copy(0).start()

    def product(columns, right, group, positions, sent, old=None):
        count = len(positions)
        base = positions[0]
        sign = positions[1] - positions[0] if count > 1 else 1

        def load(number, slot):
            return pltpu.make_async_copy(
                columns.at[:, step(base + sign * number, part)], col_v.at[slot], tile_sem.at[4, slot]
            )

        load(0, 0).start()

        def one(number, carry):
            slot = lax.rem(number, 2)

            @pl.when(number + 1 < count)
            def _():
                load(number + 1, 1 - slot).start()

            load(number, slot).wait()
            value = dot(col_v[slot], right[...], ((0,), (0,)), F)
            position = base + sign * number
            if sent:
                if old is not None:
                    y_copy(old, position - groups // 2).wait_send()
                y_send[step(position - groups // 2, part)] = value.astype(B)
                y_copy(group, position - groups // 2).start()
            else:
                keep_v[slot_of[group], step(position, part)] = value
            return carry

        lax.fori_loop(0, count, one, 0)

    loads[3].wait()
    product(g_rel, act_v, 2, (7, 6, 5, 4), True)
    small_end(0)
    product(g_rel, act_v, 2, (3, 2, 1, 0), False)
    y_near(0)
    small_end(1)

    loads[4].wait()

    def branch_begin(start):
        pass

    def branch_block(start, block):
        here, rows = step(block, CHUNK), pl.ds(start, tall)
        return dot(ctx_v[rows], w[0, here, 3 * size :], ((1,), (1,)), F) + dot(
            act_v[rows], w[2, here, :], ((1,), (1,)), F
        )

    def read_stage(source):
        copy = pltpu.make_async_copy(source, tile_v.at[pl.ds(0, quarter)], load_sem.at[6])
        copy.start()
        copy.wait()

    def e_start(which):
        x_copy(which, 1).wait_recv()
        read_stage(x_recv.at[which, 1])

        def one(block, carry):
            here = step(block, CHUNK)
            e_send[which, :, here] = (hold_v[which, 1, :, here] + tile_v[0:quarter, here].astype(F)).astype(B)
            return carry

        lax.fori_loop(0, blocks, one, 0)
        e_copy(which).start()

    def gather_own(which):
        x_copy(which, 0).wait_recv()
        read_stage(x_recv.at[which, 0])

        def one(block, carry):
            here = step(block, CHUNK)
            hold_v[which, 0, :, here] += tile_v[0:quarter, here].astype(F)
            return carry

        lax.fori_loop(0, blocks, one, 0)

    def spot(c, s):
        return pl.ds(pl.multiple_of(c * tall + s * quarter, quarter), quarter)

    def position_of(block, shifted=False):
        result = 0
        for level, bit in enumerate([PAIR] + spread):
            mine = bit_of(me, bit)
            if shifted and bit == PAIR:
                mine = 1 - mine
            result = result + (1 << level) * ((1 - mine) if block & bit else mine)
        return result

    def finish(which, out_ref):
        gather_own(which)
        e_copy(which).wait_recv()
        copies = [
            pltpu.make_async_copy(e_recv.at[which], tile_v.at[pl.ds(0, quarter)], load_sem.at[6]),
            pltpu.make_async_copy(x_ref.at[spot(core, side)], tile_v.at[pl.ds(quarter, quarter)], load_sem.at[7]),
        ]
        if which == 0:
            copies.append(pltpu.make_async_copy(g_ref.at[spot(core, side)], x_send.at[0, 0], load_sem.at[8]))
            x_copy(0, 0).wait_send()
        for copy in copies:
            copy.start()
        for copy in copies:
            copy.wait()
        here = pl.ds(which * quarter, quarter)
        if which == 0:
            total_u, total_un = 0.0, 0.0
            mean, inverse = stats(tile_v[quarter:].astype(F))
            for block in range(groups):
                mine = hold_v[0, 0, :, step(position_of(block), part)]
                theirs = tile_v[0:quarter, step(position_of(block, True), part)].astype(F)
                blend = mine + theirs
                normed = (tile_v[quarter:, block * part : (block + 1) * part].astype(F) - mean) * inverse
                hold_v[0, 1, :, block * part : (block + 1) * part] = blend
                total_u = total_u + jnp.sum(blend, axis=1, keepdims=True)
                total_un = total_un + jnp.sum(blend * normed, axis=1, keepdims=True)
            mean_u, mean_un = total_u * (1.0 / width), total_un * (1.0 / width)
            for block in range(groups):
                at = slice(block * part, (block + 1) * part)
                normed = (tile_v[quarter:, at].astype(F) - mean) * inverse
                inner = (hold_v[0, 1, :, at] - mean_u - normed * mean_un) * inverse
                c_send[here, at] = (x_send[0, 0, :, at].astype(F) + inner).astype(B)
        else:
            for block in range(groups):
                at = slice(block * part, (block + 1) * part)
                mine = hold_v[1, 0, :, step(position_of(block), part)]
                theirs = tile_v[0:quarter, step(position_of(block, True), part)].astype(F)
                bias = vec_ref[4:5, at] + vec_ref[5:6, at]
                c_send[here, at] = (tile_v[quarter:, at].astype(F) + (mine + theirs) + bias).astype(B)
        first = remote(
            c_send.at[here], out_ref.at[spot(core, side)], fs_sem.at[which, 0], fr_sem.at[which, 0], "tensor", side_to
        )
        second = remote(
            c_send.at[here], out_ref.at[spot(core, side)], fs_sem.at[which, 1], fr_sem.at[which, 1], "tensor", core_to
        )
        own = pltpu.make_async_copy(c_send.at[here], out_ref.at[spot(core, side)], out_sem.at[3 + which])
        for copy in (first, second, own):
            copy.start()
        return first, second, own

    def finish_end(which, out_ref, copies):
        first, second, own = copies
        first.wait_recv()
        third = remote(
            out_ref.at[spot(core, 1 - side)],
            out_ref.at[spot(core, 1 - side)],
            fs_sem.at[which, 2],
            fr_sem.at[which, 2],
            "tensor",
            core_to,
        )
        third.start()
        return [first.wait_send, second.wait, third.wait, own.wait]

    send_tile(1, 1, branch_begin, branch_block)
    e_start(0)
    small_end(2)
    send_tile(1, 0, branch_begin, branch_block)
    keep_tile(1, 1, branch_begin, branch_block)
    keep_tile(1, 0, branch_begin, branch_block)
    small_end(3)
    y_far(2)
    product(mlp_in, pre_v, 1, (7, 6, 5, 4), True, old=2)
    small_end(4)
    small_out[...] = small_v[...]
    z_last(0, 1)
    z_last(0, 0)
    y_near(2)
    for block in range(blocks):
        c_copy(1, 0, block).wait_send()
    copies_grad = finish(0, input_grad)
    e_start(1)
    p_copy(0).wait_send()
    near_copy(0).wait()
    product(mlp_in, pre_v, 1, (3, 2, 1, 0), False)
    z_last(2, 1)
    y_far(1)
    ends = finish_end(0, input_grad, copies_grad)
    z_last(2, 0)
    copies_out = finish(1, block_out)
    y_near(1)
    z_last(1, 1)
    ends += finish_end(1, block_out, copies_out)
    z_last(1, 0)
    for end in ends:
        end()
    for group in range(3):
        p_copy(group).wait_recv()
        if group:
            p_copy(group).wait_send()
            near_copy(group).wait()
        for position in range(2):
            if group:
                z_copy(group, position).wait_send()
        for position in range(4):
            if group != 2:
                y_copy(group, position).wait_send()
    for which in range(2):
        e_copy(which).wait_send()
        for seq in range(2):
            if (which, seq) != (0, 0):
                x_copy(which, seq).wait_send()


def body_narrow(
    tokens,
    segment_ids,
    out_grad,
    attn_norm_gain,
    attn_norm_bias,
    mlp_norm_gain,
    mlp_norm_bias,
    qkv_weight,
    qv_bias,
    key_bias,
    dense_weight,
    dense_bias,
    up_weight,
    up_bias,
    down_weight,
    down_bias,
    *,
    groups,
    ways,
):
    length, width = tokens.shape[1:]
    heads, size = qkv_weight.shape[1] // 2, qkv_weight.shape[3]
    part = width // groups
    me = lax.axis_index("dp")
    half = (me // PAIR) % 2
    place = lax.axis_index("tensor")
    core, side = place % 2, place // 2
    spread = [bit for bit in (1 << k for k in reversed(range(groups.bit_length() - 1))) if bit != PAIR]

    def swap(array, bit):
        return lax.ppermute(array, "dp", [(i, i ^ bit) for i in range(groups)])

    def cross(array, bit):
        return lax.ppermute(array, "tensor", [(i, i ^ bit) for i in range(ways)])

    def pick(array, index, axis, count=2):
        rows = array.shape[axis] // count
        return lax.dynamic_slice_in_dim(array, index * rows, rows, axis)

    def join(mine, theirs, index, axis):
        pair = jnp.concatenate([mine, theirs], axis=axis)
        turned = jnp.concatenate([theirs, mine], axis=axis)
        return jnp.where(index == 0, pair, turned)

    order = [0, PAIR]
    for bit in spread:
        order = order + [mask | bit for mask in order]
    inverse = [order.index(mask) for mask in range(groups)]

    def arranged(array):
        return jnp.concatenate(
            [lax.dynamic_slice_in_dim(array, (mask ^ me) * part, part, array.ndim - 1) for mask in order], axis=-1
        )

    def natural(array):
        table = jnp.asarray(inverse, jnp.int32)
        return jnp.concatenate(
            [lax.dynamic_slice_in_dim(array, table[block ^ me] * part, part, array.ndim - 1) for block in range(groups)],
            axis=-1,
        )

    def gather(shard, halves_axis, axis):
        shard = shard.astype(B)
        mine, theirs = pick(shard, half, halves_axis), pick(shard, 1 - half, halves_axis)
        pieces = [jnp.concatenate([mine, swap(theirs, PAIR)], axis=axis)]
        for bit in spread:
            pieces = pieces + [swap(piece, bit) for piece in pieces]
        return jnp.concatenate(pieces, axis=axis)

    def scatter(product, axis, halves_axis):
        count = groups // 2
        sent = swap(product(count, groups, B), spread[-1])
        held = product(0, count, F) + sent.astype(F)
        for bit in reversed(spread[:-1]):
            keep, send = jnp.split(held, 2, axis=axis)
            held = keep + swap(send.astype(B), bit).astype(F)
        keep, send = jnp.split(held, 2, axis=axis)
        return join(keep, swap(send, PAIR), half, halves_axis)

    def share_rows(rows):
        rows = join(rows, cross(rows, 2), side, 0)
        return join(rows, cross(rows, 1), core, 0)

    def own_rows(array, axis):
        return pick(pick(array, core, axis), side, axis)

    def partner_rows(array):
        return share_rows(swap(own_rows(array, 0), PAIR))

    def total_rows(partial):
        held = pick(partial, core, 1).astype(F) + cross(pick(partial, 1 - core, 1), 1).astype(F)
        held = pick(held, side, 1) + cross(pick(held, 1 - side, 1).astype(B), 2).astype(F)
        sent = swap(held[1].astype(B), PAIR).astype(F)
        rows = sent.shape[0]
        sent = jnp.flip(sent.reshape(rows, groups // 2, 2, part), axis=2).reshape(rows, width)
        return held[0] + sent

    own_x, own_g = tokens[0], out_grad[0]
    w_up = gather(up_weight, 1, 0)
    x_other = partner_rows(own_x)
    w_down = gather(down_weight, 0, 1)
    g_other = partner_rows(own_g)
    w_qkv = gather(qkv_weight.reshape(part, 2, -1), 1, 0).reshape(width, -1)
    w_dense = gather(dense_weight.reshape(2 * heads * size, part), 0, 1)

    x_pair = arranged(jnp.concatenate([own_x, x_other], axis=0))
    g_pair = arranged(jnp.concatenate([own_g, g_other], axis=0))
    gains = [arranged(v) for v in (attn_norm_gain, attn_norm_bias, mlp_norm_gain, mlp_norm_bias)]

    def hat(rows):
        rows = rows.astype(F)
        center = rows - jnp.mean(rows, axis=-1, keepdims=True)
        inverse_dev = lax.rsqrt(jnp.mean(center * center, axis=-1, keepdims=True) + 1e-05)
        return center * inverse_dev, inverse_dev

    normed, _ = hat(x_pair)
    attn_in = (normed * gains[0] + gains[1]).astype(B)
    mlp_in = (normed * gains[2] + gains[3]).astype(B)

    up_here = pick(up_bias, half, 0)
    up_pre = dot(mlp_in, w_up, ((1,), (0,)), F) + up_here
    activation = jax.nn.gelu(up_pre, approximate=False).astype(B)
    middle = width // 2

    def columns(array, low, high):
        return array[:, low * part : high * part]

    down_shard = scatter(lambda low, high, kind: dot(activation, columns(g_pair, low, high), ((0,), (0,)), kind), 1, 0)
    pre_grad = (dot(g_pair, w_down, ((1,), (1,)), F) * gelu_slope(up_pre)).astype(B)
    up_shard = scatter(lambda low, high, kind: dot(columns(mlp_in, low, high), pre_grad, ((0,), (0,)), kind), 0, 1)
    up_bias_sum = jnp.sum(pre_grad.astype(F), axis=0)

    seg_other = swap(segment_ids[0], PAIR)
    seg = jnp.stack([segment_ids[0], seg_other])
    seg_col, seg_row = seg[:, :, None], seg[:, None, :]
    qv_here, key_here = pick(qv_bias, half, 0), pick(key_bias, half, 0)
    key_full = jnp.concatenate([key_here, jnp.zeros((heads, size - ROT), F)], axis=1)
    offsets = jnp.stack([qv_here[:, 0], key_full, qv_here[:, 1]], axis=1).reshape(heads, 1, 3 * size)
    mixed = dot(attn_in, w_qkv, ((1,), (0,)), F).reshape(2, length, heads, 3 * size)
    tables = rope_tables(length)
    table_specs = [shared(length, 128)] * 3
    seg_specs = [per_seq(length, 1), per_seq(1, length)]
    context_grad = dot(g_pair, w_dense, ((1,), (1,)), B).reshape(2, length, heads, size)
    contexts, mixed_grads, mixed_sums = [], [], []
    head_shape = jax.ShapeDtypeStruct((2, length, size), B)
    for head in range(heads):
        q, k, v, context, lse = pl.pallas_call(
            attn_forward,
            grid=(2,),
            in_specs=[per_seq(length, 3 * size), shared(1, 3 * size)] + table_specs + seg_specs,
            out_specs=[per_seq(length, size)] * 4 + [per_seq(length, 1)],
            out_shape=[head_shape] * 4 + [jax.ShapeDtypeStruct((2, length, 1), F)],
            name="attn_forward",
        )(mixed[:, :, head], offsets[head], *tables, seg_col, seg_row)
        mixed_grad, mixed_sum = pl.pallas_call(
            attn_backward,
            grid=(2,),
            in_specs=[per_seq(length, size)] * 4 + [per_seq(length, 1)] + table_specs + seg_specs,
            out_specs=[per_seq(length, 3 * size), per_seq(1, 3 * size)],
            out_shape=[
                jax.ShapeDtypeStruct((2, length, 3 * size), B),
                jax.ShapeDtypeStruct((2, 1, 3 * size), F),
            ],
            scratch_shapes=[pltpu.VMEM((length, size), F)] * 3,
            name="attn_backward",
        )(q, k, v, context_grad[:, :, head], lse, *tables, seg_col, seg_row)
        contexts.append(context.reshape(2 * length, size))
        mixed_grads.append(mixed_grad.reshape(2 * length, 3 * size))
        mixed_sums.append(jnp.sum(mixed_sum, axis=(0, 1)))
    context = jnp.concatenate(contexts, axis=1)
    mixed_grad = jnp.concatenate(mixed_grads, axis=1)
    mixed_sum = jnp.stack(mixed_sums).reshape(heads, 3, size)

    qkv_shard = scatter(lambda low, high, kind: dot(columns(attn_in, low, high), mixed_grad, ((0,), (0,)), kind), 0, 1)
    dense_shard = scatter(lambda low, high, kind: dot(context, columns(g_pair, low, high), ((0,), (0,)), kind), 1, 0)

    branch = dot(context, w_dense, ((1,), (0,)), F) + dot(activation, w_down, ((1,), (0,)), F)
    branch_rows = total_rows(branch.astype(B).reshape(2, length, width))
    x_rows, g_rows = own_rows(x_pair[:length], 0), own_rows(g_pair[:length], 0)
    out_rows = (x_rows.astype(F) + branch_rows + arranged(dense_bias) + arranged(down_bias)).astype(B)
    block_out = share_rows(natural(out_rows))

    attn_in_grad = dot(mixed_grad, w_qkv, ((1,), (1,)), F)
    mlp_in_grad = dot(pre_grad, w_up, ((1,), (1,)), F)
    blend = (attn_in_grad * gains[0] + mlp_in_grad * gains[2]).astype(B)
    blend_rows = total_rows(blend.reshape(2, length, width))
    hat_rows, inverse_rows = hat(x_rows)
    inner = (
        blend_rows
        - jnp.mean(blend_rows, axis=-1, keepdims=True)
        - hat_rows * jnp.mean(blend_rows * hat_rows, axis=-1, keepdims=True)
    )
    input_grad = share_rows(natural((g_rows.astype(F) + inner * inverse_rows).astype(B)))

    norm_sums = natural(
        jnp.stack(
            [
                jnp.sum(attn_in_grad * normed, axis=0),
                jnp.sum(attn_in_grad, axis=0),
                jnp.sum(mlp_in_grad * normed, axis=0),
                jnp.sum(mlp_in_grad, axis=0),
            ]
        )
    ).reshape(-1)
    bias_sum = jnp.sum(own_g.astype(F), axis=0)

    def slotted(array):
        zero = jnp.zeros_like(array)
        return join(array, zero, half, 0)

    small = [norm_sums, bias_sum, slotted(up_bias_sum), slotted(mixed_sum).reshape(-1)]
    sizes = [s.shape[0] for s in small]
    flat = jnp.concatenate(small)
    for bit in [1 << k for k in range(groups.bit_length() - 1)]:
        flat = flat + swap(flat, bit)
    ends = [sum(sizes[: i + 1]) for i in range(len(sizes))]
    norms = flat[: ends[0]]
    for bit in [1 << k for k in range(ways.bit_length() - 1)]:
        norms = norms + cross(norms, bit)
    norms = norms.reshape(4, width)
    bias_grad = flat[ends[0] : ends[1]]
    up_bias_grad = flat[ends[1] : ends[2]]
    mixed_bias = flat[ends[2] :].reshape(2 * heads, 3, size)
    qv_grad = jnp.stack([mixed_bias[:, 0], mixed_bias[:, 2]], axis=1)
    key_bias_grad = mixed_bias[:, 1, :ROT]

    return (
        block_out[None],
        input_grad[None],
        norms[0],
        norms[1],
        norms[2],
        norms[3],
        qkv_shard.reshape(qkv_weight.shape),
        qv_grad,
        key_bias_grad,
        dense_shard.reshape(dense_weight.shape),
        bias_grad,
        up_shard,
        up_bias_grad,
        down_shard,
        bias_grad,
    )


def body(
    tokens,
    segment_ids,
    out_grad,
    attn_norm_gain,
    attn_norm_bias,
    mlp_norm_gain,
    mlp_norm_bias,
    qkv_weight,
    qv_bias,
    key_bias,
    dense_weight,
    dense_bias,
    up_weight,
    up_bias,
    down_weight,
    down_bias,
    *,
    groups,
    ways,
):
    length, width = tokens.shape[1:]
    heads, size = qkv_weight.shape[1] // 2, qkv_weight.shape[3]
    assert heads == 1 and ways == 4
    part = width // groups
    hidden = up_weight.shape[1] // 2
    count = 2 * length
    me = lax.axis_index("dp")
    half = (me // PAIR) % 2
    shape = jax.ShapeDtypeStruct

    def swap(array, bit):
        return lax.ppermute(array, "dp", [(i, i ^ bit) for i in range(groups)])

    def pick(array, index, axis):
        rows = array.shape[axis] // 2
        return lax.dynamic_slice_in_dim(array, index * rows, rows, axis)

    vectors = jnp.stack([attn_norm_gain, attn_norm_bias, mlp_norm_gain, mlp_norm_bias, dense_bias, down_bias])
    own_x, own_g = tokens[0], out_grad[0]

    shards = [
        jnp.concatenate(
            [
                qkv_weight.astype(B).reshape(part, 2, 3 * size),
                dense_weight.astype(B).transpose(2, 0, 1),
            ],
            axis=2,
        ),
        up_weight.astype(B).reshape(part, 2, hidden),
        down_weight.astype(B).reshape(2, hidden, part).transpose(2, 0, 1),
    ]
    mine = jnp.stack([pick(shard, half, 1)[:, 0] for shard in shards])
    theirs = jnp.stack([pick(shard, 1 - half, 1)[:, 0] for shard in shards])

    seg_other = swap(segment_ids[0], PAIR)
    seg = jnp.stack([segment_ids[0], seg_other])
    seg_col, seg_row = seg[:, :, None], seg[:, None, :]
    qv_here, key_here = pick(qv_bias, half, 0), pick(key_bias, half, 0)
    key_full = jnp.concatenate([key_here, jnp.zeros((heads, size - ROT), F)], axis=1)
    offsets = jnp.stack([qv_here[:, 0], key_full, qv_here[:, 1]], axis=1).reshape(1, 3 * size)
    tables = rope_tables(length)
    up_here = pick(up_bias, half, 0)[None]
    columns = hidden
    half_width = width // 2
    vmem, hbm = pl.BlockSpec(memory_space=pltpu.VMEM), pl.BlockSpec(memory_space=pl.ANY)
    (
        weights,
        _,
        _,
        x_pair,
        g_pair,
        mlp_in,
        mixed_grad,
        context,
        activation,
        slope,
        attn_send,
        attn_keep,
        mixed_sum,
        bias_sum,
    ) = pl.pallas_call(
        functools.partial(gather_kernel, groups),
        in_specs=[hbm] * 4 + [vmem] * 8,
        out_specs=[hbm] * 12 + [vmem] * 2,
        out_shape=[
            shape((3, width, columns), B),
            shape((length, width), B),
            shape((length, width), B),
            shape((count, width), B),
            shape((count, width), B),
            shape((count, width), B),
            shape((count, 3 * size), B),
            shape((count, size), B),
            shape((count, hidden), B),
            shape((count, hidden), F),
            shape((half_width, columns), B),
            shape((half_width, columns), F),
            shape((1, 3 * size), F),
            shape((1, width), F),
        ],
        scratch_shapes=[
            pltpu.VMEM((3, width, columns), B),
            pltpu.VMEM((2, CHUNK, width), B),
            pltpu.VMEM((2, CHUNK, width), B),
            pltpu.VMEM((length, width), B),
            pltpu.VMEM((length, width), B),
            pltpu.VMEM((count, width), B),
            pltpu.VMEM((length, width), B),
            pltpu.VMEM((width, columns), F),
            pltpu.VMEM((half_width, columns), B),
            pltpu.VMEM((length, size), B),
            pltpu.VMEM((length, size), B),
            pltpu.VMEM((length, size), B),
            pltpu.VMEM((length, size), B),
            pltpu.VMEM((length, size), B),
            pltpu.VMEM((length, 3 * size), B),
            pltpu.VMEM((length, size), F),
            pltpu.VMEM((length, size), F),
            pltpu.VMEM((2, CHUNK, hidden), B),
            pltpu.VMEM((2, CHUNK, hidden), F),
            pltpu.SemaphoreType.DMA((27,)),
            pltpu.SemaphoreType.DMA((27,)),
            pltpu.SemaphoreType.DMA((3,)),
            pltpu.SemaphoreType.DMA((2, 2)),
            pltpu.SemaphoreType.DMA((2, 5)),
            pltpu.SemaphoreType.DMA((2, 2)),
            pltpu.SemaphoreType.DMA((5,)),
        ],
        compiler_params=pltpu.CompilerParams(
            collective_id=0, has_side_effects=True, vmem_limit_bytes=67043328
        ),
        cost_estimate=pl.CostEstimate(flops=40 * 10**9, bytes_accessed=10**8, transcendentals=10**7),
        name="gather",
    )(mine, theirs, own_x, own_g, vectors, up_here, offsets, *tables, seg_col, seg_row)
    quarter = length // 4
    tall, blocks = 2 * quarter, width // CHUNK
    rows_third = shape((3, part, columns), F)
    dma = pltpu.SemaphoreType.DMA
    block_out, input_grad, near, far, _, _, _, _, _, small = pl.pallas_call(
        functools.partial(scatter_kernel, groups),
        in_specs=[hbm] * 12 + [vmem] * 3,
        out_specs=[hbm] * 9 + [vmem],
        out_shape=[
            shape((length, width), B),
            shape((length, width), B),
            rows_third,
            rows_third,
            shape((3, half_width, columns), B),
            shape((3, half_width // 2, columns), B),
            shape((2, 2, tall, width), B),
            shape((2, 2, quarter, width), B),
            shape((2, quarter, width), B),
            shape((8, width), F),
        ],
        scratch_shapes=[
            pltpu.VMEM((3, width, columns), B),
            pltpu.VMEM((count, hidden), B),
            pltpu.VMEM((count, hidden), B),
            pltpu.VMEM((tall, width), B),
            pltpu.VMEM((2, count, part), B),
            pltpu.VMEM((2, CHUNK, hidden), F),
            pltpu.VMEM((tall, 3 * size), B),
            pltpu.VMEM((count, size), B),
            pltpu.VMEM((2, half_width, columns), F),
            pltpu.VMEM((half_width, columns), B),
            pltpu.VMEM((2, half_width // 2, columns), B),
            pltpu.VMEM((part, columns), B),
            pltpu.VMEM((tall, width), B),
            pltpu.VMEM((2, tall, CHUNK), B),
            pltpu.VMEM((tall, CHUNK), F),
            pltpu.VMEM((2, 2, quarter, width), B),
            pltpu.VMEM((2, 2, quarter, width), F),
            pltpu.VMEM((tall, 128), F),
            pltpu.VMEM((tall, 128), F),
            pltpu.VMEM((2, quarter, width), B),
            pltpu.VMEM((1, hidden), F),
            pltpu.VMEM((8, width), F),
            pltpu.VMEM((5, 8, width), F),
            dma((9,)),
            dma((5, 2)),
            dma((3, 4)),
            dma((3, 4)),
            dma((3, 2)),
            dma((3, 2)),
            dma((3,)),
            dma((3,)),
            dma((2, 2, blocks)),
            dma((2, 2, blocks)),
            dma((2, 2)),
            dma((2, 2)),
            dma((2,)),
            dma((2,)),
            dma((2, 3)),
            dma((2, 3)),
            dma((5,)),
            dma((5,)),
            dma((5,)),
        ],
        compiler_params=pltpu.CompilerParams(
            collective_id=1, has_side_effects=True, vmem_limit_bytes=67043328
        ),
        cost_estimate=pl.CostEstimate(flops=60 * 10**9, bytes_accessed=10**8, transcendentals=10**7),
        name="scatter",
    )(
        attn_send,
        attn_keep,
        weights,
        x_pair,
        g_pair,
        mlp_in,
        mixed_grad,
        context,
        activation,
        slope,
        own_x,
        own_g,
        vectors,
        mixed_sum,
        bias_sum,
    )

    def by_half(group, columns=slice(None)):
        mine, theirs = near[group, :, columns], far[group, :, columns]
        return jnp.where(half == 0, jnp.stack([mine, theirs]), jnp.stack([theirs, mine]))

    qkv_shard = by_half(0, slice(0, 3 * size)).transpose(1, 0, 2)
    dense_shard = by_half(0, slice(3 * size, None)).transpose(0, 2, 1)
    up_shard = jnp.where(half == 0, jnp.concatenate([near[1], far[1]], 1), jnp.concatenate([far[1], near[1]], 1))
    down_shard = by_half(2).transpose(0, 2, 1)
    norms, bias_grad, up_bias_grad = small[0:4], small[4], small[5]
    mixed_bias = small[6].reshape(2, width // 2)[:, : 3 * size].reshape(2, 3, size)
    qv_grad = jnp.stack([mixed_bias[:, 0], mixed_bias[:, 2]], axis=1)
    key_bias_grad = mixed_bias[:, 1, :ROT]

    return (
        block_out[None],
        input_grad[None],
        norms[0],
        norms[1],
        norms[2],
        norms[3],
        qkv_shard.reshape(qkv_weight.shape),
        qv_grad,
        key_bias_grad,
        dense_shard.reshape(dense_weight.shape),
        bias_grad,
        up_shard,
        up_bias_grad,
        down_shard.reshape(down_weight.shape),
        bias_grad,
    )


def solution(mesh):
    placed = (
        P("dp", None, None),
        P("dp", None),
        P("dp", None, None),
        P(),
        P(),
        P(),
        P(),
        P("dp", "tensor", None, None),
        P("tensor", None, None),
        P("tensor", None),
        P("tensor", None, "dp"),
        P(),
        P("dp", "tensor"),
        P("tensor"),
        P("tensor", "dp"),
        P(),
    )

    def whole(*arrays):
        groups, ways = mesh.shape["dp"], mesh.shape["tensor"]
        part = arrays[0].shape[2] // groups
        chosen = body_narrow if part % 128 or groups != 8 else body
        return chosen(*arrays, groups=groups, ways=ways)

    return jax.shard_map(
        whole,
        mesh=mesh,
        in_specs=placed,
        out_specs=(
            P("dp", None, None),
            P("dp", None, None),
            P(),
            P(),
            P(),
            P(),
            P("dp", "tensor", None, None),
            P("tensor", None, None),
            P("tensor", None),
            P("tensor", None, "dp"),
            P(),
            P("dp", "tensor"),
            P("tensor"),
            P("tensor", "dp"),
            P(),
        ),
        check_vma=False,
    )
```

```python
import functools

import jax
import jax.numpy as jnp
from jax import lax
from jax.experimental import pallas as pl
from jax.experimental.pallas import tpu as pltpu
from jax.sharding import PartitionSpec as P

ROT = 64
PAIR = 2
QBLOCK = 256
DOC_MAX = 512
F = jnp.float32
B = jnp.bfloat16


def dot(left, right, dims, kind):
    return lax.dot_general(left, right, (dims, ((), ())), preferred_element_type=F).astype(kind)


def gelu_slope(pre_act):
    cumulative = 0.5 * (1.0 + lax.erf(pre_act * 0.7071067811865476))
    density = jnp.exp(-0.5 * pre_act * pre_act) * 0.3989422804014327
    return cumulative + pre_act * density


def rope_tables(length):
    half = ROT // 2
    frequency = 10000.0 ** (-(jnp.arange(half, dtype=F) * 2.0) / ROT)
    angles = jnp.arange(length, dtype=F)[:, None] * frequency[None, :]
    cosine, sine = jnp.cos(angles), jnp.sin(angles)
    flat = jnp.zeros((length, 128 - ROT), F)
    zero = jnp.zeros_like(sine)
    return (
        jnp.concatenate([cosine, cosine, flat + 1.0], axis=1),
        jnp.concatenate([-sine, zero, flat], axis=1),
        jnp.concatenate([zero, sine, flat], axis=1),
    )


def turn(rows, cosine, from_above, from_below):
    head = rows[:, :128]
    above = pltpu.roll(head, 128 - ROT // 2, 1)
    below = pltpu.roll(head, ROT // 2, 1)
    turned = head * cosine + above * from_above + below * from_below
    return jnp.concatenate([turned, rows[:, 128:]], axis=1)


def block_mask(seg_col_ref, seg_row_ref, first, low, high):
    rows = first + lax.broadcasted_iota(jnp.int32, (QBLOCK, high - low), 0)
    columns = low + lax.broadcasted_iota(jnp.int32, (QBLOCK, high - low), 1)
    same = seg_col_ref[0, first : first + QBLOCK, :] == seg_row_ref[0, :, low:high]
    return (columns <= rows) & same


def key_range(first):
    return max(0, first - DOC_MAX), first + QBLOCK


def attn_forward(mixed_ref, bias_ref, cos_ref, up_ref, down_ref, col_ref, row_ref, q_ref, k_ref, v_ref, ctx_ref, lse_ref):
    size = q_ref.shape[2]
    length = q_ref.shape[1]
    scale = size ** (-0.5)
    tables = (cos_ref[...], up_ref[...], down_ref[...])
    q_ref[0] = turn(mixed_ref[0, :, :size] + bias_ref[:, :size], *tables).astype(B)
    k_ref[0] = turn(mixed_ref[0, :, size : 2 * size] + bias_ref[:, size : 2 * size], *tables).astype(B)
    v_ref[0] = (mixed_ref[0, :, 2 * size :] + bias_ref[:, 2 * size :]).astype(B)
    for first in range(0, length, QBLOCK):
        low, high = key_range(first)
        scores = dot(q_ref[0, first : first + QBLOCK], k_ref[0, low:high], ((1,), (1,)), F) * scale
        scores = jnp.where(block_mask(col_ref, row_ref, first, low, high), scores, -1e30)
        row_max = jnp.max(scores, axis=1, keepdims=True)
        expo = jnp.exp(scores - row_max)
        total = jnp.sum(expo, axis=1, keepdims=True)
        probs = (expo / total).astype(B)
        ctx_ref[0, first : first + QBLOCK] = dot(probs, v_ref[0, low:high], ((1,), (0,)), B)
        lse_ref[0, first : first + QBLOCK] = row_max + jnp.log(total)


def attn_backward(q_ref, k_ref, v_ref, grad_ref, lse_ref, cos_ref, up_ref, down_ref, col_ref, row_ref, mixed_ref, sum_ref, q_acc, k_acc, v_acc):
    size = q_ref.shape[2]
    length = q_ref.shape[1]
    scale = size ** (-0.5)
    k_acc[...] = jnp.zeros_like(k_acc)
    v_acc[...] = jnp.zeros_like(v_acc)
    for first in range(0, length, QBLOCK):
        low, high = key_range(first)
        here = slice(first, first + QBLOCK)
        scores = dot(q_ref[0, here], k_ref[0, low:high], ((1,), (1,)), F) * scale
        scores = jnp.where(block_mask(col_ref, row_ref, first, low, high), scores, -1e30)
        probs = jnp.exp(scores - lse_ref[0, here])
        v_acc[low:high] += dot(probs.astype(B), grad_ref[0, here], ((0,), (0,)), F)
        prob_grad = dot(grad_ref[0, here], v_ref[0, low:high], ((1,), (1,)), F)
        centred = jnp.sum(probs * prob_grad, axis=1, keepdims=True)
        score_grad = (probs * (prob_grad - centred)).astype(B)
        q_acc[here] = dot(score_grad, k_ref[0, low:high], ((1,), (0,)), F) * scale
        k_acc[low:high] += dot(score_grad, q_ref[0, here], ((0,), (0,)), F) * scale
    tables = (cos_ref[...], -up_ref[...], -down_ref[...])
    q_grad = turn(q_acc[...], *tables).astype(B)
    k_grad = turn(k_acc[...], *tables).astype(B)
    v_grad = v_acc[...].astype(B)
    for number, part in enumerate((q_grad, k_grad, v_grad)):
        mixed_ref[0, :, number * size : (number + 1) * size] = part
        sum_ref[0, :, number * size : (number + 1) * size] = jnp.sum(part.astype(F), axis=0, keepdims=True)


def per_seq(rows, columns):
    return pl.BlockSpec((1, rows, columns), lambda seq, *_: (seq, 0, 0))


def shared(rows, columns):
    return pl.BlockSpec((rows, columns), lambda *_: (0, 0))


MESH = pl.DeviceIdType.MESH
CHUNK = 256


def bit_of(index, bit):
    return lax.rem(lax.div(index, bit), 2)


def flip(index, mask):
    bit = 1
    while bit <= mask:
        if mask & bit:
            index = index + bit * (1 - 2 * bit_of(index, bit))
        bit *= 2
    return index


def block_order(groups):
    spread = [bit for bit in (1 << k for k in reversed(range(groups.bit_length() - 1))) if bit != PAIR]
    order = [0, PAIR]
    for bit in spread:
        order = order + [mask | bit for mask in order]
    return spread, order


def stats(rows):
    mean = jnp.mean(rows, axis=1, keepdims=True)
    center = rows - mean
    return mean, lax.rsqrt(jnp.mean(center * center, axis=1, keepdims=True) + 1e-05)


def greet(partners):
    barrier = pltpu.get_barrier_semaphore()
    for axis, index in partners:
        pl.semaphore_signal(barrier, inc=1, device_id={axis: index}, device_id_type=MESH)
    pl.semaphore_wait(barrier, len(partners))


def gather_kernel(
    groups,
    mine_ref,
    theirs_ref,
    x_ref,
    g_ref,
    vec_ref,
    up_bias_ref,
    offset_ref,
    cos_ref,
    above_ref,
    below_ref,
    col_ref,
    row_ref,
    w_out,
    w_relay,
    x_other,
    g_other,
    x_rel,
    g_rel,
    mlp_out,
    mixed_out,
    ctx_out,
    act_out,
    slope_out,
    send_out,
    keep_out,
    sum_ref,
    bias_ref,
    w,
    raw_x,
    raw_g,
    attn_v,
    g_v,
    mlp_v,
    xr_v,
    grad_v,
    send_v,
    q_v,
    k_v,
    v_v,
    cg_v,
    ctx_v,
    mg_v,
    dk_v,
    dv_v,
    act_v,
    slope_v,
    send_sem,
    recv_sem,
    cross_sem,
    two_sem,
    three_sem,
    relay_sem,
    quarter_sem,
    own_sem,
    load_sem,
    rel_sem,
    tile_sem,
    out_sem,
):
    length, width = x_ref.shape
    part = width // groups
    size = q_v.shape[1]
    quarter = length // 4
    me, place = lax.axis_index("dp"), lax.axis_index("tensor")
    core, side = lax.rem(place, 2), lax.div(place, 2)
    pair_to, side_to, core_to = flip(me, PAIR), flip(place, 2), flip(place, 1)
    spread, order = block_order(groups)
    across = PAIR | spread[0]
    inner = bit_of(me, PAIR) != bit_of(me, spread[0])
    greet(
        [("dp", flip(me, mask)) for mask in [PAIR, across] + spread] + [("tensor", side_to), ("tensor", core_to)]
    )
    outer = bit_of(me, PAIR) == bit_of(me, spread[0])
    copies, partial_copies = {}, []

    def remote(key, source, target, axis, index):
        number = len(copies)
        copies[key] = pltpu.make_async_remote_copy(
            src_ref=source,
            dst_ref=target,
            send_sem=send_sem.at[number],
            recv_sem=recv_sem.at[number],
            device_id={axis: index},
            device_id_type=MESH,
        )
        copies[key].start()

    def rows(position):
        return pl.ds(position * part, part)

    def pair_up(group, here=None):
        key = ("w", group, 1)
        if key not in copies:
            number = len(copies)
            copies[key] = pltpu.make_async_remote_copy(
                src_ref=theirs_ref.at[group],
                dst_ref=w.at[group, rows(1)],
                send_sem=send_sem.at[number],
                recv_sem=recv_sem.at[number],
                device_id={"dp": pair_to},
                device_id_type=MESH,
            )
        if here is None:
            copies[key].start()
        else:
            pl.when(here)(copies[key].start)

    def onward(group, position, level):
        source = mine_ref.at[group] if position == 0 else w.at[group, rows(position)]
        far = position + (2 << level)
        remote(("w", group, far), source, w.at[group, rows(far)], "dp", flip(me, spread[level]))

    def partly(here, source, target, send, recv, to):
        copy = pltpu.make_async_remote_copy(
            src_ref=source,
            dst_ref=target,
            send_sem=send,
            recv_sem=recv,
            device_id={"dp": to},
            device_id_type=MESH,
        )
        partial_copies.append((here, copy))
        pl.when(here)(copy.start)
        return copy

    across_to = flip(me, across)

    def straight(group):
        copy = partly(
            inner, theirs_ref.at[group], w.at[group, rows(3)], cross_sem.at[group, 0], three_sem.at[group], across_to
        )
        copies[("w", group, 3)] = copy

    def hand(group, here=None):
        source, sem = mine_ref.at[group], cross_sem.at[group, 1]
        if here is not inner:
            partly(outer, source, w_relay.at[group, rows(0)], sem, relay_sem.at[group, 0], pair_to)
        if here is not outer:
            partly(inner, source, w_relay.at[group, rows(1)], sem, relay_sem.at[group, 1], across_to)

    def relay(group):
        source = w.at[group, rows(1)]
        partly(
            inner, source, w_relay.at[group, rows(2)], cross_sem.at[group, 2], relay_sem.at[group, 2], across_to
        )

    def pass_on(group, *numbers):
        for number in numbers:
            source, target = w_relay.at[group, rows(number)], 3 if number == 2 else 2
            here = pltpu.make_async_remote_copy(
                src_ref=source,
                dst_ref=source,
                send_sem=relay_sem.at[group, number],
                recv_sem=relay_sem.at[group, number],
                device_id={"dp": pair_to},
                device_id_type=MESH,
            )
            pl.when(inner)(here.wait_recv)
            copy = partly(
                inner,
                source,
                w.at[group, rows(target)],
                cross_sem.at[group, 3 + number],
                (three_sem if target == 3 else two_sem).at[group],
                across_to if number == 0 else pair_to,
            )
            copies[("w", group, target)] = copy

    def quarter_to_pair(key, source, target, here, first):
        copy = pltpu.make_async_remote_copy(
            src_ref=source,
            dst_ref=target,
            send_sem=quarter_sem.at[key, 0],
            recv_sem=quarter_sem.at[key, 1],
            device_id={"dp": pair_to},
            device_id_type=MESH,
        )
        pl.when(here)(copy.start)
        if first:
            partial_copies.append((None, copy))
        return copy

    def arrive(group, position, ahead=()):
        copies[("w", group, position)].wait_recv()

    spot = pl.ds(pl.multiple_of(core * (2 * quarter) + side * quarter, quarter), quarter)
    pair_rows = pl.ds(pl.multiple_of(core * (2 * quarter), quarter), 2 * quarter)
    levels = len(spread)
    assert levels == 2

    def load(x, g, tile, slot):
        here = pl.ds(pl.multiple_of(tile * CHUNK, CHUNK), CHUNK)
        return (
            pltpu.make_async_copy(x.at[here], raw_x.at[slot], load_sem.at[0, slot]),
            pltpu.make_async_copy(g.at[here], raw_g.at[slot], load_sem.at[1, slot]),
        )

    def normalise(seq, x, g):
        for copy in load(x, g, 0, 0):
            copy.start()

        def one(tile, carry):
            slot = lax.rem(tile, 2)

            @pl.when(tile + 1 < length // CHUNK)
            def _():
                for copy in load(x, g, tile + 1, 1 - slot):
                    copy.start()

            for copy in load(x, g, tile, slot):
                copy.wait()
            here = pl.ds(pl.multiple_of(tile * CHUNK, CHUNK), CHUNK)
            both = pl.ds(pl.multiple_of(seq * length + tile * CHUNK, CHUNK), CHUNK)
            mean, inverse = stats(raw_x[slot].astype(F))
            if seq == 0:
                bias_ref[...] += jnp.sum(raw_g[slot].astype(F), axis=0, keepdims=True)
            for position, mask in enumerate(order):
                to = slice(position * part, (position + 1) * part)
                there = pl.ds(pl.multiple_of(flip(me, mask) * part, part), part)
                piece = raw_x[slot, :, there]
                normed = (piece.astype(F) - mean) * inverse
                attn_v[here, to] = (normed * vec_ref[0:1, there] + vec_ref[1:2, there]).astype(B)
                mlp_v[both, to] = (normed * vec_ref[2:3, there] + vec_ref[3:4, there]).astype(B)
                xr_v[here, to] = piece
                g_v[here, to] = raw_g[slot, :, there]
            return carry

        lax.fori_loop(0, length // CHUNK, one, 0)
        both = pl.ds(seq * length, length)
        return [
            pltpu.make_async_copy(xr_v, x_rel.at[both], rel_sem.at[seq, 0]),
            pltpu.make_async_copy(g_v, g_rel.at[both], rel_sem.at[seq, 1]),
            pltpu.make_async_copy(mlp_v.at[both], mlp_out.at[both], rel_sem.at[seq, 2]),
        ]

    def project():
        def one(tile, carry):
            here = pl.ds(pl.multiple_of(tile * CHUNK, CHUNK), CHUNK)
            mixed = dot(attn_v[here], w[0, :, : 3 * size], ((1,), (0,)), F) + offset_ref[...]
            tables = (cos_ref[here], above_ref[here], below_ref[here])
            q_v[here] = turn(mixed[:, :size], *tables).astype(B)
            k_v[here] = turn(mixed[:, size : 2 * size], *tables).astype(B)
            v_v[here] = mixed[:, 2 * size :].astype(B)
            cg_v[here] = dot(g_v[here], w[0, :, 3 * size :], ((1,), (0,)), B)
            return carry

        lax.fori_loop(0, length // CHUNK, one, 0)

    def attend(seq):
        scale = size ** (-0.5)
        dk_v[...] = jnp.zeros_like(dk_v)
        dv_v[...] = jnp.zeros_like(dv_v)
        for first in range(0, length, QBLOCK):
            low, high = key_range(first)
            here, keys = slice(first, first + QBLOCK), slice(low, high)
            scores = dot(q_v[here], k_v[keys], ((1,), (1,)), F) * scale
            row_ids = first + lax.broadcasted_iota(jnp.int32, (QBLOCK, high - low), 0)
            key_ids = low + lax.broadcasted_iota(jnp.int32, (QBLOCK, high - low), 1)
            allowed = (key_ids <= row_ids) & (col_ref[seq, here, :] == row_ref[seq, :, keys])
            scores = jnp.where(allowed, scores, -1e30)
            expo = jnp.exp(scores - jnp.max(scores, axis=1, keepdims=True))
            probs = expo / jnp.sum(expo, axis=1, keepdims=True)
            low_probs = probs.astype(B)
            ctx_v[here] = dot(low_probs, v_v[keys], ((1,), (0,)), B)
            dv_v[keys] += dot(low_probs, cg_v[here], ((0,), (0,)), F)
            prob_grad = dot(cg_v[here], v_v[keys], ((1,), (1,)), F)
            centred = jnp.sum(probs * prob_grad, axis=1, keepdims=True)
            score_grad = (probs * (prob_grad - centred)).astype(B)
            q_grad = dot(score_grad, k_v[keys], ((1,), (0,)), F) * scale
            tables = (cos_ref[here], -above_ref[here], -below_ref[here])
            mg_v[here, :size] = turn(q_grad, *tables).astype(B)
            dk_v[keys] += dot(score_grad, q_v[here], ((0,), (0,)), F) * scale
        for first in range(0, length, QBLOCK):
            here = slice(first, first + QBLOCK)
            tables = (cos_ref[here], -above_ref[here], -below_ref[here])
            mg_v[here, size : 2 * size] = turn(dk_v[here], *tables).astype(B)
            mg_v[here, 2 * size :] = dv_v[here].astype(B)
        sums = jnp.sum(mg_v[...].astype(F), axis=0, keepdims=True)
        if seq == 0:
            sum_ref[...] = sums
        else:
            sum_ref[...] += sums
        both = pl.ds(seq * length, length)
        return [
            pltpu.make_async_copy(mg_v, mixed_out.at[both], rel_sem.at[seq, 3]),
            pltpu.make_async_copy(ctx_v, ctx_out.at[both], rel_sem.at[seq, 4]),
        ]

    def attn_grads(seq, low, high):
        def one(block, carry):
            here = pl.ds(pl.multiple_of(block * CHUNK, CHUNK), CHUNK)
            qkv = dot(attn_v[:, here], mg_v[...], ((0,), (0,)), F)
            dense = dot(g_v[:, here], ctx_v[...], ((0,), (0,)), F)
            if seq == 0:
                grad_v[here, : 3 * size] = qkv
                grad_v[here, 3 * size :] = dense
            else:
                grad_v[here, : 3 * size] += qkv
                grad_v[here, 3 * size :] += dense
            return carry

        lax.fori_loop(low // CHUNK, high // CHUNK, one, 0)

    def up(low, high):
        def store(tile, slot):
            here = pl.ds(pl.multiple_of(tile * CHUNK, CHUNK), CHUNK)
            return (
                pltpu.make_async_copy(act_v.at[slot], act_out.at[here], tile_sem.at[0, slot]),
                pltpu.make_async_copy(slope_v.at[slot], slope_out.at[here], tile_sem.at[1, slot]),
            )

        def one(tile, carry):
            slot = lax.rem(tile, 2)
            here = pl.ds(pl.multiple_of(tile * CHUNK, CHUNK), CHUNK)
            pre = dot(mlp_v[here], w[1], ((1,), (0,)), F) + up_bias_ref[...]

            @pl.when(tile >= low + 2)
            def _():
                for copy in store(tile - 2, slot):
                    copy.wait()

            cumulative = 0.5 * (1.0 + lax.erf(pre * 0.7071067811865476))
            density = jnp.exp(-0.5 * pre * pre) * 0.3989422804014327
            act_v[slot] = (pre * cumulative).astype(B)
            slope_v[slot] = cumulative + pre * density
            for copy in store(tile, slot):
                copy.start()
            return carry

        lax.fori_loop(low, high, one, 0)
        for tile in (high - 2, high - 1):
            for copy in store(tile, tile % 2):
                copy.wait()

    def weights_out(group):
        return pltpu.make_async_copy(w.at[group], w_out.at[group], out_sem.at[group])

    def x_to_pair(here, first):
        return quarter_to_pair(0, x_ref.at[spot], x_other.at[spot], here, first)

    def g_to_pair(here, first):
        return quarter_to_pair(1, g_ref.at[spot], g_other.at[spot], here, first)

    pair_up(0)
    straight(0)
    hand(0)
    onward(0, 0, 1)
    x_to_pair(outer, True)
    pair_up(1, outer)
    hand(1, outer)
    g_to_pair(outer, True)
    x_first = x_to_pair(inner, False)
    own = [pltpu.make_async_copy(mine_ref.at[group], w.at[group, rows(0)], own_sem.at[group]) for group in range(3)]
    for copy in own:
        copy.start()
    bias_ref[...] = jnp.zeros_like(bias_ref)
    first_out = normalise(0, x_ref, g_ref)
    for copy in first_out:
        copy.start()
    arrive(0, 1)
    relay(0)
    onward(0, 1, 1)
    pass_on(0, 0, 1)
    straight(1)
    hand(1, inner)
    pair_up(1, inner)
    onward(1, 0, 1)
    pass_on(0, 2)
    arrive(0, 2)
    onward(0, 2, 1)
    arrive(0, 3)
    onward(0, 3, 1)
    g_first = g_to_pair(inner, False)
    x_first.wait_recv()
    remote("x2", x_other.at[spot], x_other.at[spot], "tensor", side_to)
    arrive(1, 1)
    relay(1)
    onward(1, 1, 1)
    pair_up(2, outer)
    hand(2, outer)
    for position in range(4, 8):
        arrive(0, position)
    for copy in own:
        copy.wait()
    out = [weights_out(0)]
    out[0].start()
    project()
    pass_on(1, 0, 1)
    copies["x2"].wait_recv()
    remote("x3", x_other.at[pair_rows], x_other.at[pair_rows], "tensor", core_to)
    pair_up(2, inner)
    straight(2)
    hand(2, inner)
    onward(2, 0, 1)
    second_out = attend(0)
    for copy in second_out:
        copy.start()
    pass_on(1, 2)
    g_first.wait_recv()
    remote("g2", g_other.at[spot], g_other.at[spot], "tensor", side_to)
    arrive(1, 2)
    onward(1, 2, 1)
    arrive(1, 3)
    onward(1, 3, 1)
    attn_grads(0, 0, width)
    arrive(2, 1)
    relay(2)
    onward(2, 1, 1)
    pass_on(2, 0)
    copies["x3"].wait_recv()
    for copy in first_out + second_out:
        copy.wait()
    copies["g2"].wait_recv()
    remote("g3", g_other.at[pair_rows], g_other.at[pair_rows], "tensor", core_to)
    copies["g3"].wait_recv()
    third_out = normalise(1, x_other, g_other)
    for copy in third_out:
        copy.start()
    pass_on(2, 1)
    project()
    pass_on(2, 2)
    arrive(2, 2)
    onward(2, 2, 1)
    fourth_out = attend(1)
    for copy in fourth_out:
        copy.start()
    arrive(2, 3)
    onward(2, 3, 1)
    attn_grads(1, width // 2, width)
    send_v[...] = grad_v[width // 2 :].astype(B)
    out.append(pltpu.make_async_copy(send_v, send_out, out_sem.at[3]))
    out[-1].start()
    attn_grads(1, 0, width // 2)
    out.append(pltpu.make_async_copy(grad_v.at[pl.ds(0, width // 2)], keep_out, out_sem.at[4]))
    out[-1].start()
    for position in range(4, 8):
        arrive(1, position)
    out.append(weights_out(1))
    out[-1].start()
    up(0, 2 * length // CHUNK)
    for position in range(4, 8):
        arrive(2, position)
    out.append(weights_out(2))
    out[-1].start()
    for copy in third_out + fourth_out + out:
        copy.wait()
    for key, copy in copies.items():
        if key[0] != "w" or key[2] not in (2, 3):
            copy.wait_send()
    for here, copy in partial_copies:
        if here is None:
            copy.wait_send()
        else:
            pl.when(here)(copy.wait_send)


SCHEDULE = (
    ("pre", 1),
    ("st", 1, 1),
    ("yf", 0, 3),
    ("kt", 1, 1),
    ("ps", 2),
    ("yf", 0, 2),
    ("st", 0, 1),
    ("yn", 0, 1),
    ("kt", 0, 1),
    ("po", 0, 1),
    ("es", 1),
    ("st", 1, 0),
    ("po", 0, 2),
    ("po", 0, 0),
    ("pk", 2),
    ("kt", 1, 0),
    ("pre", 0),
    ("yf", 2, 3),
    ("st", 0, 0),
    ("yn", 0, 0),
    ("yf", 2, 2),
    ("kt", 0, 0),
    ("sb",),
    ("es", 0),
    ("po", 2, 1),
    ("ps", 1),
    ("se", 0),
    ("zl", 0, 1),
    ("zl", 0, 0),
    ("po", 2, 0),
    ("pk", 1),
    ("yf", 1, 3),
    ("fin", 1),
    ("yn", 2, 0),
    ("se", 1),
    ("yf", 1, 2),
    ("yn", 2, 1),
    ("po", 2, 2),
    ("zl", 2, 1),
    ("fin", 0),
    ("po", 1, 1),
    ("yn", 1, 0),
    ("po", 1, 2),
    ("yn", 1, 1),
    ("po", 1, 0),
    ("se", 2),
    ("zl", 1, 1),
    ("zl", 1, 0),
    ("fe", 1),
    ("fe", 0),
    ("zl", 2, 0),
    ("se", 3),
    ("se", 4),
)


def scatter_kernel(
    groups,
    attn_send,
    attn_keep,
    weights,
    x_rel,
    g_rel,
    mlp_in,
    mixed_grad,
    context,
    activation,
    slope,
    x_ref,
    g_ref,
    vec_ref,
    mixed_sum,
    bias_sum,
    block_out,
    input_grad,
    near_out,
    far_out,
    far_two,
    y_recv,
    z_recv,
    z_relay,
    c_recv,
    x_recv,
    e_recv,
    small_out,
    w,
    act_v,
    pre_v,
    tile_v,
    col_v,
    slope_t,
    mix_t,
    ctx_v,
    keep_v,
    y_send,
    z_send,
    p_send,
    y_stage,
    c_send,
    c_stage,
    r_stage,
    x_send,
    hold_v,
    mean_v,
    inverse_v,
    sum_v,
    small_v,
    small_recv,
    load_sem,
    tile_sem,
    ys_sem,
    yr_sem,
    zs_sem,
    zr_sem,
    zl_sem,
    zf_sem,
    two_sem,
    ps_sem,
    pr_sem,
    cs_sem,
    cr_sem,
    xs_sem,
    xr_sem,
    es_sem,
    er_sem,
    fs_sem,
    fr_sem,
    ss_sem,
    sr_sem,
    out_sem,
):
    length, width = x_ref.shape
    part = width // groups
    size = context.shape[1]
    hidden = activation.shape[1]
    quarter = length // 4
    me, place = lax.axis_index("dp"), lax.axis_index("tensor")
    core, side, half = lax.rem(place, 2), lax.div(place, 2), bit_of(me, PAIR)
    pair_to, side_to, core_to = flip(me, PAIR), flip(place, 2), flip(place, 1)
    spread, order = block_order(groups)
    z_to, y_to = [flip(me, bit) for bit in spread]
    across_to = flip(z_to, PAIR)
    inner = bit_of(me, PAIR) != bit_of(me, spread[0])
    outer = bit_of(me, PAIR) == bit_of(me, spread[0])
    greet([("dp", to) for to in (pair_to, z_to, y_to, across_to)] + [("tensor", side_to), ("tensor", core_to)])

    def remote(source, target, send, recv, axis, index):
        return pltpu.make_async_remote_copy(
            src_ref=source, dst_ref=target, send_sem=send, recv_sem=recv, device_id={axis: index}, device_id_type=MESH
        )

    def span(position, count=1):
        return pl.ds(position * part, count * part)

    def step(index, amount):
        return pl.ds(pl.multiple_of(index * amount, amount), amount)

    def y_copy(group, position):
        source = attn_send if group == 0 else y_send
        here = step(position, part) if not isinstance(position, int) else span(position)
        return remote(
            source.at[here], y_recv.at[group, here], ys_sem.at[group, position], yr_sem.at[group, position], "dp", y_to
        )

    slot_of = (0, 0, 1)

    def z_copy(group, position):
        source, sem = z_send.at[slot_of[group], span(position - 2)], zs_sem.at[group, position - 2]
        onward = (
            remote(source, far_two.at[group], sem, two_sem.at[group], "dp", across_to)
            if position == 3
            else remote(source, z_relay.at[group, span(2)], sem, zl_sem.at[group, 2], "dp", across_to)
        )
        aside = remote(
            source, z_relay.at[group, span(position - 2)], sem, zl_sem.at[group, position - 2], "dp", pair_to
        )
        return onward, aside

    def forward(group, number):
        target = 0 if number == 2 else number
        arrived = remote(
            z_relay.at[group, span(number)],
            z_recv.at[group, span(target)],
            zf_sem.at[group, number],
            zl_sem.at[group, number],
            "dp",
            pair_to,
        )
        return arrived, remote(
            z_relay.at[group, span(number)],
            z_recv.at[group, span(target)],
            zf_sem.at[group, number],
            zr_sem.at[group, target],
            "dp",
            pair_to if number == 2 else across_to,
        )

    def pass_on(group, *numbers):
        @pl.when(inner)
        def _():
            for number in numbers:
                arrived, copy = forward(group, number)
                arrived.wait_recv()
                copy.start()

    def z_arrived(group, position):
        return remote(
            z_relay.at[group, span(position)],
            z_recv.at[group, span(position)],
            zf_sem.at[group, position],
            zr_sem.at[group, position],
            "dp",
            pair_to,
        )

    def p_copy(group):
        return remote(
            p_send.at[slot_of[group]], far_out.at[group], ps_sem.at[group], pr_sem.at[group], "dp", pair_to
        )

    def near_copy(group):
        return pltpu.make_async_copy(keep_v.at[slot_of[group], span(0)], near_out.at[group], out_sem.at[group])

    def staged(source):
        copy = pltpu.make_async_copy(source, y_stage, load_sem.at[6])
        copy.start()
        copy.wait()

    def y_far(group, position):
        if group == 0:
            need(5)
        y_copy(group, position).wait_recv()
        staged(y_recv.at[group, span(position)])
        total = keep_v[slot_of[group], span(position)] + y_stage[...].astype(F)
        onward, aside = z_copy(group, position)
        if group == 1:
            z_copy(0, position)[0].wait_send()
        z_send[slot_of[group], span(position - 2)] = total.astype(B)
        pl.when(inner)(onward.start)
        pl.when(outer)(aside.start)

    def y_near(group, position):
        if group == 0:
            need(5)
        y_copy(group, position).wait_recv()
        staged(y_recv.at[group, span(position)])
        total = keep_v[slot_of[group], span(position)] + y_stage[...].astype(F)
        keep_v[slot_of[group], span(position)] = total
        if position == 1:
            if group == 1:
                p_copy(0).wait_send()

            @pl.when(outer)
            def _():
                p_send[slot_of[group]] = keep_v[slot_of[group], span(1)].astype(B)
                p_copy(group).start()

    def z_last(group, position):
        def add():
            z_arrived(group, position).wait_recv()
            staged(z_recv.at[group, span(position)])
            return keep_v[slot_of[group], span(position)] + y_stage[...].astype(F)

        if position == 1:

            @pl.when(inner)
            def _():
                p_send[slot_of[group]] = add().astype(B)
                p_copy(group).start()

        else:
            keep_v[slot_of[group], span(0)] = add()
            near_copy(group).start()

    loads = [
        pltpu.make_async_copy(weights.at[2], w.at[2], load_sem.at[0]),
        pltpu.make_async_copy(weights.at[0], w.at[0], load_sem.at[1]),
        pltpu.make_async_copy(weights.at[1], w.at[1], load_sem.at[2]),
        pltpu.make_async_copy(activation, act_v, load_sem.at[3]),
        pltpu.make_async_copy(context, ctx_v, load_sem.at[4]),
        pltpu.make_async_copy(attn_keep, keep_v.at[0], load_sem.at[5]),
    ]
    for number in (4, 3, 1, 0, 5, 2):
        loads[number].start()
    loaded = set()

    def need(*numbers):
        for number in numbers:
            if number not in loaded:
                loaded.add(number)
                loads[number].wait()

    for position in (3, 2, 1, 0):
        y_copy(0, position).start()

    small_v[...] = jnp.zeros_like(small_v)

    def pre_load(tile, slot):
        here = step(tile, CHUNK)
        return (
            pltpu.make_async_copy(g_rel.at[here], tile_v.at[step(slot, CHUNK)], tile_sem.at[0, slot]),
            pltpu.make_async_copy(slope.at[here], slope_t.at[slot], tile_sem.at[1, slot]),
        )

    sum_v[...] = jnp.zeros_like(sum_v)

    def pre_tiles(seq):
        need(0)
        low, high = seq * length // CHUNK, (seq + 1) * length // CHUNK
        for copy in pre_load(low, 0):
            copy.start()

        def one(tile, carry):
            slot = lax.rem(tile, 2)

            @pl.when(tile + 1 < high)
            def _():
                for copy in pre_load(tile + 1, 1 - slot):
                    copy.start()

            for copy in pre_load(tile, slot):
                copy.wait()
            grad = (dot(tile_v[step(slot, CHUNK)], w[2], ((1,), (0,)), F) * slope_t[slot]).astype(B)
            pre_v[step(tile, CHUNK)] = grad
            sum_v[...] += jnp.sum(grad.astype(F), axis=0, keepdims=True)
            return carry

        lax.fori_loop(low, high, one, 0)

    tall = 2 * quarter
    blocks = width // CHUNK

    def c_copy(which, seq, block):
        here = step(block, CHUNK)
        return remote(
            c_send.at[:, here],
            c_recv.at[which, seq, :, here],
            cs_sem.at[which, seq, block],
            cr_sem.at[which, seq, block],
            "tensor",
            core_to,
        )

    def x_copy(which, seq):
        return remote(
            x_send.at[which, seq], x_recv.at[which, seq], xs_sem.at[which, seq], xr_sem.at[which, seq], "tensor", side_to
        )

    def e_copy(which):
        return remote(x_send.at[which, 1], e_recv.at[which], es_sem.at[which], er_sem.at[which], "dp", pair_to)

    sent_tiles = []

    def send_tile(which, seq):
        begin, block_of = tile_of[which]
        need(*((1, 2) if which == 0 else (0, 1, 3, 4)))
        start = pl.multiple_of(seq * length + (1 - core) * tall, tall)
        begin(start)

        def one(block, carry):
            value = block_of(start, block)
            if sent_tiles:
                c_copy(*sent_tiles[-1], block).wait_send()
            c_send[:, step(block, CHUNK)] = value.astype(B)
            c_copy(which, seq, block).start()
            return carry

        lax.fori_loop(0, blocks, one, 0)
        sent_tiles.append((which, seq))

    def c_load(which, seq, block, slot):
        return pltpu.make_async_copy(c_recv.at[which, seq, :, step(block, CHUNK)], c_stage.at[slot], tile_sem.at[2, slot])

    def keep_tile(which, seq):
        begin, block_of = tile_of[which]
        start = pl.multiple_of(seq * length + core * tall, tall)
        begin(start)
        c_copy(which, seq, 0).wait_recv()
        c_load(which, seq, 0, 0).start()

        def one(block, carry):
            slot = lax.rem(block, 2)
            value = block_of(start, block)

            @pl.when(block + 1 < blocks)
            def _():
                c_copy(which, seq, block + 1).wait_recv()
                c_load(which, seq, block + 1, 1 - slot).start()

            c_load(which, seq, block, slot).wait()
            r_stage[...] = value + c_stage[slot].astype(F)
            here = step(block, CHUNK)
            hold_v[which, seq, :, here] = r_stage[step(side, quarter)]
            x_send[which, seq, :, here] = r_stage[step(1 - side, quarter)].astype(B)
            return carry

        lax.fori_loop(0, blocks, one, 0)
        x_copy(which, seq).start()

    def blend_begin(start):
        copies = (
            pltpu.make_async_copy(x_rel.at[pl.ds(start, tall)], tile_v, tile_sem.at[3, 0]),
            pltpu.make_async_copy(mixed_grad.at[pl.ds(start, tall)], mix_t, tile_sem.at[3, 1]),
        )
        for copy in copies:
            copy.start()
        for copy in copies:
            copy.wait()
        for slot in range(2):
            mean, inverse = stats(tile_v[span_rows(slot)].astype(F))
            mean_v[span_rows(slot)] = jnp.broadcast_to(mean, (CHUNK, 128))
            inverse_v[span_rows(slot)] = jnp.broadcast_to(inverse, (CHUNK, 128))

    def span_rows(slot):
        return pl.ds(slot * CHUNK, CHUNK)

    def natural_block(position):
        result = me
        for level, bit in enumerate([PAIR] + spread):
            flipped = lax.rem(lax.div(position, 1 << level), 2)
            result = result + bit * (1 - 2 * bit_of(me, bit)) * flipped
        return result

    def blend_block(start, block):
        here = step(block, CHUNK)
        there = step(natural_block(block), part)
        attn_grad = dot(mix_t[...], w[0, here, : 3 * size], ((1,), (1,)), F)
        mlp_grad = dot(pre_v[pl.ds(start, tall)], w[1, here, :], ((1,), (1,)), F)
        mean, inverse = mean_v[...], inverse_v[...]
        mean = jnp.concatenate([mean] * (CHUNK // 128), axis=1)
        inverse = jnp.concatenate([inverse] * (CHUNK // 128), axis=1)
        normed = (tile_v[:, here].astype(F) - mean) * inverse
        small_v[0:1, there] += jnp.sum(attn_grad * normed, axis=0, keepdims=True)
        small_v[1:2, there] += jnp.sum(attn_grad, axis=0, keepdims=True)
        small_v[2:3, there] += jnp.sum(mlp_grad * normed, axis=0, keepdims=True)
        small_v[3:4, there] += jnp.sum(mlp_grad, axis=0, keepdims=True)
        return attn_grad * vec_ref[0:1, there] + mlp_grad * vec_ref[2:3, there]

    def product(columns, right, group, positions, sent, old=None):
        count = len(positions)
        base = positions[0]
        sign = positions[1] - positions[0] if count > 1 else 1

        def load(number, slot):
            return pltpu.make_async_copy(
                columns.at[:, step(base + sign * number, part)], col_v.at[slot], tile_sem.at[4, slot]
            )

        load(0, 0).start()

        def one(number, carry):
            slot = lax.rem(number, 2)

            @pl.when(number + 1 < count)
            def _():
                load(number + 1, 1 - slot).start()

            load(number, slot).wait()
            value = dot(col_v[slot], right[...], ((0,), (0,)), F)
            position = base + sign * number
            if sent:
                if old is not None:
                    y_copy(old, position - groups // 2).wait_send()
                y_send[step(position - groups // 2, part)] = value.astype(B)
                y_copy(group, position - groups // 2).start()
            else:
                keep_v[slot_of[group], step(position, part)] = value
            return carry

        lax.fori_loop(0, count, one, 0)

    def small_begin():
        small_v[4:5] = bias_sum[...]
        small_v[5:6, step(half, hidden)] = sum_v[...]
        small_v[6:7, pl.ds(pl.multiple_of(half * (width // 2), width // 2), 3 * size)] = mixed_sum[...]
        small_copy(0).start()

    rounds = [("dp", flip(me, bit)) for bit in [PAIR] + spread] + [("tensor", side_to), ("tensor", core_to)]

    def small_copy(number):
        return remote(small_v, small_recv.at[number], ss_sem.at[number], sr_sem.at[number], *rounds[number])

    def small_end(number):
        small_copy(number).wait()
        if number < 3:
            small_v[...] += small_recv[number]
        else:
            small_v[0:4] += small_recv[number, 0:4]
        if number + 1 < len(rounds):
            small_copy(number + 1).start()

    def branch_begin(start):
        pass

    def branch_block(start, block):
        here, rows = step(block, CHUNK), pl.ds(start, tall)
        return dot(ctx_v[rows], w[0, here, 3 * size :], ((1,), (1,)), F) + dot(
            act_v[rows], w[2, here, :], ((1,), (1,)), F
        )

    def read_stage(source):
        copy = pltpu.make_async_copy(source, tile_v.at[pl.ds(0, quarter)], load_sem.at[6])
        copy.start()
        copy.wait()

    def e_start(which):
        x_copy(which, 1).wait_recv()
        x_copy(which, 1).wait_send()
        read_stage(x_recv.at[which, 1])

        def one(block, carry):
            here = step(block, CHUNK)
            x_send[which, 1, :, here] = (hold_v[which, 1, :, here] + tile_v[0:quarter, here].astype(F)).astype(B)
            return carry

        lax.fori_loop(0, blocks, one, 0)
        e_copy(which).start()

    def gather_own(which):
        x_copy(which, 0).wait_recv()
        read_stage(x_recv.at[which, 0])

        def one(block, carry):
            here = step(block, CHUNK)
            hold_v[which, 0, :, here] += tile_v[0:quarter, here].astype(F)
            return carry

        lax.fori_loop(0, blocks, one, 0)

    def spot(c, s):
        return pl.ds(pl.multiple_of(c * tall + s * quarter, quarter), quarter)

    def position_of(block, shifted=False):
        result = 0
        for level, bit in enumerate([PAIR] + spread):
            mine = bit_of(me, bit)
            if shifted and bit == PAIR:
                mine = 1 - mine
            result = result + (1 << level) * ((1 - mine) if block & bit else mine)
        return result

    def finish(which, out_ref):
        if len(sent_tiles) == 4:
            sent_tiles.append(None)
            for block in range(blocks):
                c_copy(*sent_tiles[3], block).wait_send()
        gather_own(which)
        e_copy(which).wait_recv()
        copies = [
            pltpu.make_async_copy(e_recv.at[which], tile_v.at[pl.ds(0, quarter)], load_sem.at[6]),
            pltpu.make_async_copy(x_ref.at[spot(core, side)], tile_v.at[pl.ds(quarter, quarter)], load_sem.at[7]),
        ]
        if which == 0:
            copies.append(pltpu.make_async_copy(g_ref.at[spot(core, side)], x_send.at[0, 0], load_sem.at[8]))
            x_copy(0, 0).wait_send()
        for copy in copies:
            copy.start()
        for copy in copies:
            copy.wait()
        here = pl.ds(which * quarter, quarter)
        if which == 0:
            total_u, total_un = 0.0, 0.0
            mean, inverse = stats(tile_v[quarter:].astype(F))
            for block in range(groups):
                mine = hold_v[0, 0, :, step(position_of(block), part)]
                theirs = tile_v[0:quarter, step(position_of(block, True), part)].astype(F)
                blend = mine + theirs
                normed = (tile_v[quarter:, block * part : (block + 1) * part].astype(F) - mean) * inverse
                hold_v[0, 1, :, block * part : (block + 1) * part] = blend
                total_u = total_u + jnp.sum(blend, axis=1, keepdims=True)
                total_un = total_un + jnp.sum(blend * normed, axis=1, keepdims=True)
            mean_u, mean_un = total_u * (1.0 / width), total_un * (1.0 / width)
            for block in range(groups):
                at = slice(block * part, (block + 1) * part)
                normed = (tile_v[quarter:, at].astype(F) - mean) * inverse
                inner = (hold_v[0, 1, :, at] - mean_u - normed * mean_un) * inverse
                c_send[here, at] = (x_send[0, 0, :, at].astype(F) + inner).astype(B)
        else:
            for block in range(groups):
                at = slice(block * part, (block + 1) * part)
                mine = hold_v[1, 0, :, step(position_of(block), part)]
                theirs = tile_v[0:quarter, step(position_of(block, True), part)].astype(F)
                bias = vec_ref[4:5, at] + vec_ref[5:6, at]
                c_send[here, at] = (tile_v[quarter:, at].astype(F) + (mine + theirs) + bias).astype(B)
        first = remote(
            c_send.at[here], out_ref.at[spot(core, side)], fs_sem.at[which, 0], fr_sem.at[which, 0], "tensor", side_to
        )
        second = remote(
            c_send.at[here], out_ref.at[spot(core, side)], fs_sem.at[which, 1], fr_sem.at[which, 1], "tensor", core_to
        )
        own = pltpu.make_async_copy(c_send.at[here], out_ref.at[spot(core, side)], out_sem.at[3 + which])
        for copy in (first, second, own):
            copy.start()
        return first, second, own

    def finish_end(which, out_ref, copies):
        first, second, own = copies
        first.wait_recv()
        third = remote(
            out_ref.at[spot(core, 1 - side)],
            out_ref.at[spot(core, 1 - side)],
            fs_sem.at[which, 2],
            fr_sem.at[which, 2],
            "tensor",
            core_to,
        )
        third.start()
        return [first.wait_send, second.wait, third.wait, own.wait]

    tile_of = ((blend_begin, blend_block), (branch_begin, branch_block))
    outs, finished, ends = (input_grad, block_out), {}, []

    def do_product(group, sent):
        columns, right = ((mlp_in, pre_v), (g_rel, act_v))[group - 1]
        if group == 2:
            need(3)
        if group == 1 and not sent:
            near_copy(0).wait()
        product(columns, right, group, (7, 6, 5, 4) if sent else (3, 2, 1, 0), sent, 2 if sent and group == 1 else None)

    def do_finish(which):
        finished[which] = finish(which, outs[which])

    def do_end(which):
        ends.extend(finish_end(which, outs[which], finished[which]))

    stages = {
        "pre": pre_tiles,
        "st": send_tile,
        "kt": keep_tile,
        "ps": lambda group: do_product(group, True),
        "pk": lambda group: do_product(group, False),
        "yf": y_far,
        "yn": y_near,
        "po": pass_on,
        "zl": z_last,
        "es": e_start,
        "fin": do_finish,
        "fe": do_end,
        "sb": small_begin,
        "se": small_end,
    }
    for name, *numbers in SCHEDULE:
        stages[name](*numbers)
    small_out[...] = small_v[...]
    for end in ends:
        end()
    for group in range(3):
        p_copy(group).wait_recv()
        if group:
            p_copy(group).wait_send()
            near_copy(group).wait()
            for position in (2, 3):
                z_copy(group, position)[0].wait_send()
        for position in range(4):
            if group != 2:
                y_copy(group, position).wait_send()

        @pl.when(inner)
        def _():
            remote(
                p_send.at[0], far_two.at[group], two_sem.at[group], two_sem.at[group], "dp", across_to
            ).wait_recv()
            for number in range(3):
                forward(group, number)[1].wait_send()

    for which in range(2):
        e_copy(which).wait_send()
        if which:
            x_copy(which, 0).wait_send()


def body_narrow(
    tokens,
    segment_ids,
    out_grad,
    attn_norm_gain,
    attn_norm_bias,
    mlp_norm_gain,
    mlp_norm_bias,
    qkv_weight,
    qv_bias,
    key_bias,
    dense_weight,
    dense_bias,
    up_weight,
    up_bias,
    down_weight,
    down_bias,
    *,
    groups,
    ways,
):
    length, width = tokens.shape[1:]
    heads, size = qkv_weight.shape[1] // 2, qkv_weight.shape[3]
    part = width // groups
    me = lax.axis_index("dp")
    half = (me // PAIR) % 2
    place = lax.axis_index("tensor")
    core, side = place % 2, place // 2
    spread = [bit for bit in (1 << k for k in reversed(range(groups.bit_length() - 1))) if bit != PAIR]

    def swap(array, bit):
        return lax.ppermute(array, "dp", [(i, i ^ bit) for i in range(groups)])

    def cross(array, bit):
        return lax.ppermute(array, "tensor", [(i, i ^ bit) for i in range(ways)])

    def pick(array, index, axis, count=2):
        rows = array.shape[axis] // count
        return lax.dynamic_slice_in_dim(array, index * rows, rows, axis)

    def join(mine, theirs, index, axis):
        pair = jnp.concatenate([mine, theirs], axis=axis)
        turned = jnp.concatenate([theirs, mine], axis=axis)
        return jnp.where(index == 0, pair, turned)

    order = [0, PAIR]
    for bit in spread:
        order = order + [mask | bit for mask in order]
    inverse = [order.index(mask) for mask in range(groups)]

    def arranged(array):
        return jnp.concatenate(
            [lax.dynamic_slice_in_dim(array, (mask ^ me) * part, part, array.ndim - 1) for mask in order], axis=-1
        )

    def natural(array):
        table = jnp.asarray(inverse, jnp.int32)
        return jnp.concatenate(
            [lax.dynamic_slice_in_dim(array, table[block ^ me] * part, part, array.ndim - 1) for block in range(groups)],
            axis=-1,
        )

    def gather(shard, halves_axis, axis):
        shard = shard.astype(B)
        mine, theirs = pick(shard, half, halves_axis), pick(shard, 1 - half, halves_axis)
        pieces = [jnp.concatenate([mine, swap(theirs, PAIR)], axis=axis)]
        for bit in spread:
            pieces = pieces + [swap(piece, bit) for piece in pieces]
        return jnp.concatenate(pieces, axis=axis)

    def scatter(product, axis, halves_axis):
        count = groups // 2
        sent = swap(product(count, groups, B), spread[-1])
        held = product(0, count, F) + sent.astype(F)
        for bit in reversed(spread[:-1]):
            keep, send = jnp.split(held, 2, axis=axis)
            held = keep + swap(send.astype(B), bit).astype(F)
        keep, send = jnp.split(held, 2, axis=axis)
        return join(keep, swap(send, PAIR), half, halves_axis)

    def share_rows(rows):
        rows = join(rows, cross(rows, 2), side, 0)
        return join(rows, cross(rows, 1), core, 0)

    def own_rows(array, axis):
        return pick(pick(array, core, axis), side, axis)

    def partner_rows(array):
        return share_rows(swap(own_rows(array, 0), PAIR))

    def total_rows(partial):
        held = pick(partial, core, 1).astype(F) + cross(pick(partial, 1 - core, 1), 1).astype(F)
        held = pick(held, side, 1) + cross(pick(held, 1 - side, 1).astype(B), 2).astype(F)
        sent = swap(held[1].astype(B), PAIR).astype(F)
        rows = sent.shape[0]
        sent = jnp.flip(sent.reshape(rows, groups // 2, 2, part), axis=2).reshape(rows, width)
        return held[0] + sent

    own_x, own_g = tokens[0], out_grad[0]
    w_up = gather(up_weight, 1, 0)
    x_other = partner_rows(own_x)
    w_down = gather(down_weight, 0, 1)
    g_other = partner_rows(own_g)
    w_qkv = gather(qkv_weight.reshape(part, 2, -1), 1, 0).reshape(width, -1)
    w_dense = gather(dense_weight.reshape(2 * heads * size, part), 0, 1)

    x_pair = arranged(jnp.concatenate([own_x, x_other], axis=0))
    g_pair = arranged(jnp.concatenate([own_g, g_other], axis=0))
    gains = [arranged(v) for v in (attn_norm_gain, attn_norm_bias, mlp_norm_gain, mlp_norm_bias)]

    def hat(rows):
        rows = rows.astype(F)
        center = rows - jnp.mean(rows, axis=-1, keepdims=True)
        inverse_dev = lax.rsqrt(jnp.mean(center * center, axis=-1, keepdims=True) + 1e-05)
        return center * inverse_dev, inverse_dev

    normed, _ = hat(x_pair)
    attn_in = (normed * gains[0] + gains[1]).astype(B)
    mlp_in = (normed * gains[2] + gains[3]).astype(B)

    up_here = pick(up_bias, half, 0)
    up_pre = dot(mlp_in, w_up, ((1,), (0,)), F) + up_here
    activation = jax.nn.gelu(up_pre, approximate=False).astype(B)
    middle = width // 2

    def columns(array, low, high):
        return array[:, low * part : high * part]

    down_shard = scatter(lambda low, high, kind: dot(activation, columns(g_pair, low, high), ((0,), (0,)), kind), 1, 0)
    pre_grad = (dot(g_pair, w_down, ((1,), (1,)), F) * gelu_slope(up_pre)).astype(B)
    up_shard = scatter(lambda low, high, kind: dot(columns(mlp_in, low, high), pre_grad, ((0,), (0,)), kind), 0, 1)
    up_bias_sum = jnp.sum(pre_grad.astype(F), axis=0)

    seg_other = swap(segment_ids[0], PAIR)
    seg = jnp.stack([segment_ids[0], seg_other])
    seg_col, seg_row = seg[:, :, None], seg[:, None, :]
    qv_here, key_here = pick(qv_bias, half, 0), pick(key_bias, half, 0)
    key_full = jnp.concatenate([key_here, jnp.zeros((heads, size - ROT), F)], axis=1)
    offsets = jnp.stack([qv_here[:, 0], key_full, qv_here[:, 1]], axis=1).reshape(heads, 1, 3 * size)
    mixed = dot(attn_in, w_qkv, ((1,), (0,)), F).reshape(2, length, heads, 3 * size)
    tables = rope_tables(length)
    table_specs = [shared(length, 128)] * 3
    seg_specs = [per_seq(length, 1), per_seq(1, length)]
    context_grad = dot(g_pair, w_dense, ((1,), (1,)), B).reshape(2, length, heads, size)
    contexts, mixed_grads, mixed_sums = [], [], []
    head_shape = jax.ShapeDtypeStruct((2, length, size), B)
    for head in range(heads):
        q, k, v, context, lse = pl.pallas_call(
            attn_forward,
            grid=(2,),
            in_specs=[per_seq(length, 3 * size), shared(1, 3 * size)] + table_specs + seg_specs,
            out_specs=[per_seq(length, size)] * 4 + [per_seq(length, 1)],
            out_shape=[head_shape] * 4 + [jax.ShapeDtypeStruct((2, length, 1), F)],
            name="attn_forward",
        )(mixed[:, :, head], offsets[head], *tables, seg_col, seg_row)
        mixed_grad, mixed_sum = pl.pallas_call(
            attn_backward,
            grid=(2,),
            in_specs=[per_seq(length, size)] * 4 + [per_seq(length, 1)] + table_specs + seg_specs,
            out_specs=[per_seq(length, 3 * size), per_seq(1, 3 * size)],
            out_shape=[
                jax.ShapeDtypeStruct((2, length, 3 * size), B),
                jax.ShapeDtypeStruct((2, 1, 3 * size), F),
            ],
            scratch_shapes=[pltpu.VMEM((length, size), F)] * 3,
            name="attn_backward",
        )(q, k, v, context_grad[:, :, head], lse, *tables, seg_col, seg_row)
        contexts.append(context.reshape(2 * length, size))
        mixed_grads.append(mixed_grad.reshape(2 * length, 3 * size))
        mixed_sums.append(jnp.sum(mixed_sum, axis=(0, 1)))
    context = jnp.concatenate(contexts, axis=1)
    mixed_grad = jnp.concatenate(mixed_grads, axis=1)
    mixed_sum = jnp.stack(mixed_sums).reshape(heads, 3, size)

    qkv_shard = scatter(lambda low, high, kind: dot(columns(attn_in, low, high), mixed_grad, ((0,), (0,)), kind), 0, 1)
    dense_shard = scatter(lambda low, high, kind: dot(context, columns(g_pair, low, high), ((0,), (0,)), kind), 1, 0)

    branch = dot(context, w_dense, ((1,), (0,)), F) + dot(activation, w_down, ((1,), (0,)), F)
    branch_rows = total_rows(branch.astype(B).reshape(2, length, width))
    x_rows, g_rows = own_rows(x_pair[:length], 0), own_rows(g_pair[:length], 0)
    out_rows = (x_rows.astype(F) + branch_rows + arranged(dense_bias) + arranged(down_bias)).astype(B)
    block_out = share_rows(natural(out_rows))

    attn_in_grad = dot(mixed_grad, w_qkv, ((1,), (1,)), F)
    mlp_in_grad = dot(pre_grad, w_up, ((1,), (1,)), F)
    blend = (attn_in_grad * gains[0] + mlp_in_grad * gains[2]).astype(B)
    blend_rows = total_rows(blend.reshape(2, length, width))
    hat_rows, inverse_rows = hat(x_rows)
    inner = (
        blend_rows
        - jnp.mean(blend_rows, axis=-1, keepdims=True)
        - hat_rows * jnp.mean(blend_rows * hat_rows, axis=-1, keepdims=True)
    )
    input_grad = share_rows(natural((g_rows.astype(F) + inner * inverse_rows).astype(B)))

    norm_sums = natural(
        jnp.stack(
            [
                jnp.sum(attn_in_grad * normed, axis=0),
                jnp.sum(attn_in_grad, axis=0),
                jnp.sum(mlp_in_grad * normed, axis=0),
                jnp.sum(mlp_in_grad, axis=0),
            ]
        )
    ).reshape(-1)
    bias_sum = jnp.sum(own_g.astype(F), axis=0)

    def slotted(array):
        zero = jnp.zeros_like(array)
        return join(array, zero, half, 0)

    small = [norm_sums, bias_sum, slotted(up_bias_sum), slotted(mixed_sum).reshape(-1)]
    sizes = [s.shape[0] for s in small]
    flat = jnp.concatenate(small)
    for bit in [1 << k for k in range(groups.bit_length() - 1)]:
        flat = flat + swap(flat, bit)
    ends = [sum(sizes[: i + 1]) for i in range(len(sizes))]
    norms = flat[: ends[0]]
    for bit in [1 << k for k in range(ways.bit_length() - 1)]:
        norms = norms + cross(norms, bit)
    norms = norms.reshape(4, width)
    bias_grad = flat[ends[0] : ends[1]]
    up_bias_grad = flat[ends[1] : ends[2]]
    mixed_bias = flat[ends[2] :].reshape(2 * heads, 3, size)
    qv_grad = jnp.stack([mixed_bias[:, 0], mixed_bias[:, 2]], axis=1)
    key_bias_grad = mixed_bias[:, 1, :ROT]

    return (
        block_out[None],
        input_grad[None],
        norms[0],
        norms[1],
        norms[2],
        norms[3],
        qkv_shard.reshape(qkv_weight.shape),
        qv_grad,
        key_bias_grad,
        dense_shard.reshape(dense_weight.shape),
        bias_grad,
        up_shard,
        up_bias_grad,
        down_shard,
        bias_grad,
    )


def body(
    tokens,
    segment_ids,
    out_grad,
    attn_norm_gain,
    attn_norm_bias,
    mlp_norm_gain,
    mlp_norm_bias,
    qkv_weight,
    qv_bias,
    key_bias,
    dense_weight,
    dense_bias,
    up_weight,
    up_bias,
    down_weight,
    down_bias,
    *,
    groups,
    ways,
):
    length, width = tokens.shape[1:]
    heads, size = qkv_weight.shape[1] // 2, qkv_weight.shape[3]
    assert heads == 1 and ways == 4
    part = width // groups
    hidden = up_weight.shape[1] // 2
    count = 2 * length
    me = lax.axis_index("dp")
    half = (me // PAIR) % 2
    shape = jax.ShapeDtypeStruct

    def swap(array, bit):
        return lax.ppermute(array, "dp", [(i, i ^ bit) for i in range(groups)])

    def pick(array, index, axis):
        rows = array.shape[axis] // 2
        return lax.dynamic_slice_in_dim(array, index * rows, rows, axis)

    vectors = jnp.stack([attn_norm_gain, attn_norm_bias, mlp_norm_gain, mlp_norm_bias, dense_bias, down_bias])
    own_x, own_g = tokens[0], out_grad[0]

    shards = [
        jnp.concatenate(
            [
                qkv_weight.astype(B).reshape(part, 2, 3 * size),
                dense_weight.astype(B).transpose(2, 0, 1),
            ],
            axis=2,
        ),
        up_weight.astype(B).reshape(part, 2, hidden),
        down_weight.astype(B).reshape(2, hidden, part).transpose(2, 0, 1),
    ]
    mine = jnp.stack([pick(shard, half, 1)[:, 0] for shard in shards])
    theirs = jnp.stack([pick(shard, 1 - half, 1)[:, 0] for shard in shards])

    seg_other = swap(segment_ids[0], PAIR)
    seg = jnp.stack([segment_ids[0], seg_other])
    seg_col, seg_row = seg[:, :, None], seg[:, None, :]
    qv_here, key_here = pick(qv_bias, half, 0), pick(key_bias, half, 0)
    key_full = jnp.concatenate([key_here, jnp.zeros((heads, size - ROT), F)], axis=1)
    offsets = jnp.stack([qv_here[:, 0], key_full, qv_here[:, 1]], axis=1).reshape(1, 3 * size)
    tables = rope_tables(length)
    up_here = pick(up_bias, half, 0)[None]
    columns = hidden
    half_width = width // 2
    vmem, hbm = pl.BlockSpec(memory_space=pltpu.VMEM), pl.BlockSpec(memory_space=pl.ANY)
    (
        weights,
        _,
        _,
        _,
        x_pair,
        g_pair,
        mlp_in,
        mixed_grad,
        context,
        activation,
        slope,
        attn_send,
        attn_keep,
        mixed_sum,
        bias_sum,
    ) = pl.pallas_call(
        functools.partial(gather_kernel, groups),
        in_specs=[hbm] * 4 + [vmem] * 8,
        out_specs=[hbm] * 13 + [vmem] * 2,
        out_shape=[
            shape((3, width, columns), B),
            shape((3, 3 * part, columns), B),
            shape((length, width), B),
            shape((length, width), B),
            shape((count, width), B),
            shape((count, width), B),
            shape((count, width), B),
            shape((count, 3 * size), B),
            shape((count, size), B),
            shape((count, hidden), B),
            shape((count, hidden), F),
            shape((half_width, columns), B),
            shape((half_width, columns), F),
            shape((1, 3 * size), F),
            shape((1, width), F),
        ],
        scratch_shapes=[
            pltpu.VMEM((3, width, columns), B),
            pltpu.VMEM((2, CHUNK, width), B),
            pltpu.VMEM((2, CHUNK, width), B),
            pltpu.VMEM((length, width), B),
            pltpu.VMEM((length, width), B),
            pltpu.VMEM((count, width), B),
            pltpu.VMEM((length, width), B),
            pltpu.VMEM((width, columns), F),
            pltpu.VMEM((half_width, columns), B),
            pltpu.VMEM((length, size), B),
            pltpu.VMEM((length, size), B),
            pltpu.VMEM((length, size), B),
            pltpu.VMEM((length, size), B),
            pltpu.VMEM((length, size), B),
            pltpu.VMEM((length, 3 * size), B),
            pltpu.VMEM((length, size), F),
            pltpu.VMEM((length, size), F),
            pltpu.VMEM((2, CHUNK, hidden), B),
            pltpu.VMEM((2, CHUNK, hidden), F),
            pltpu.SemaphoreType.DMA((27,)),
            pltpu.SemaphoreType.DMA((27,)),
            pltpu.SemaphoreType.DMA((3, 6)),
            pltpu.SemaphoreType.DMA((3,)),
            pltpu.SemaphoreType.DMA((3,)),
            pltpu.SemaphoreType.DMA((3, 3)),
            pltpu.SemaphoreType.DMA((2, 2)),
            pltpu.SemaphoreType.DMA((3,)),
            pltpu.SemaphoreType.DMA((2, 2)),
            pltpu.SemaphoreType.DMA((2, 5)),
            pltpu.SemaphoreType.DMA((2, 2)),
            pltpu.SemaphoreType.DMA((5,)),
        ],
        compiler_params=pltpu.CompilerParams(
            collective_id=0, has_side_effects=True, vmem_limit_bytes=67043328
        ),
        cost_estimate=pl.CostEstimate(flops=40 * 10**9, bytes_accessed=10**8, transcendentals=10**7),
        name="gather",
    )(mine, theirs, own_x, own_g, vectors, up_here, offsets, *tables, seg_col, seg_row)
    quarter = length // 4
    tall, blocks = 2 * quarter, width // CHUNK
    rows_third = shape((3, part, columns), F)
    dma = pltpu.SemaphoreType.DMA
    block_out, input_grad, near, far, far_two, _, _, _, _, _, _, small = pl.pallas_call(
        functools.partial(scatter_kernel, groups),
        in_specs=[hbm] * 12 + [vmem] * 3,
        out_specs=[hbm] * 11 + [vmem],
        out_shape=[
            shape((length, width), B),
            shape((length, width), B),
            rows_third,
            shape((3, part, columns), B),
            shape((3, part, columns), B),
            shape((3, half_width, columns), B),
            shape((3, half_width // 2, columns), B),
            shape((3, 3 * part, columns), B),
            shape((2, 2, tall, width), B),
            shape((2, 2, quarter, width), B),
            shape((2, quarter, width), B),
            shape((8, width), F),
        ],
        scratch_shapes=[
            pltpu.VMEM((3, width, columns), B),
            pltpu.VMEM((count, hidden), B),
            pltpu.VMEM((count, hidden), B),
            pltpu.VMEM((tall, width), B),
            pltpu.VMEM((2, count, part), B),
            pltpu.VMEM((2, CHUNK, hidden), F),
            pltpu.VMEM((tall, 3 * size), B),
            pltpu.VMEM((count, size), B),
            pltpu.VMEM((2, half_width, columns), F),
            pltpu.VMEM((half_width, columns), B),
            pltpu.VMEM((2, half_width // 2, columns), B),
            pltpu.VMEM((2, part, columns), B),
            pltpu.VMEM((part, columns), B),
            pltpu.VMEM((tall, width), B),
            pltpu.VMEM((2, tall, CHUNK), B),
            pltpu.VMEM((tall, CHUNK), F),
            pltpu.VMEM((2, 2, quarter, width), B),
            pltpu.VMEM((2, 2, quarter, width), F),
            pltpu.VMEM((tall, 128), F),
            pltpu.VMEM((tall, 128), F),
            pltpu.VMEM((1, hidden), F),
            pltpu.VMEM((8, width), F),
            pltpu.VMEM((5, 8, width), F),
            dma((9,)),
            dma((5, 2)),
            dma((3, 4)),
            dma((3, 4)),
            dma((3, 2)),
            dma((3, 2)),
            dma((3, 3)),
            dma((3, 3)),
            dma((3,)),
            dma((3,)),
            dma((3,)),
            dma((2, 2, blocks)),
            dma((2, 2, blocks)),
            dma((2, 2)),
            dma((2, 2)),
            dma((2,)),
            dma((2,)),
            dma((2, 3)),
            dma((2, 3)),
            dma((5,)),
            dma((5,)),
            dma((5,)),
        ],
        compiler_params=pltpu.CompilerParams(
            collective_id=1, has_side_effects=True, vmem_limit_bytes=67043328
        ),
        cost_estimate=pl.CostEstimate(flops=60 * 10**9, bytes_accessed=10**8, transcendentals=10**7),
        name="scatter",
    )(
        attn_send,
        attn_keep,
        weights,
        x_pair,
        g_pair,
        mlp_in,
        mixed_grad,
        context,
        activation,
        slope,
        own_x,
        own_g,
        vectors,
        mixed_sum,
        bias_sum,
    )

    inner = half != (me // (groups // 2)) % 2
    far = far.astype(F) + jnp.where(inner, far_two.astype(F), 0.0)

    def by_half(group, columns=slice(None)):
        mine, theirs = near[group, :, columns], far[group, :, columns]
        return jnp.where(half == 0, jnp.stack([mine, theirs]), jnp.stack([theirs, mine]))

    qkv_shard = by_half(0, slice(0, 3 * size)).transpose(1, 0, 2)
    dense_shard = by_half(0, slice(3 * size, None)).transpose(0, 2, 1)
    up_near, up_far = near[1], far[1]
    up_shard = jnp.where(half == 0, jnp.concatenate([up_near, up_far], 1), jnp.concatenate([up_far, up_near], 1))
    down_shard = by_half(2).transpose(0, 2, 1)
    norms, bias_grad, up_bias_grad = small[0:4], small[4], small[5]
    mixed_bias = small[6].reshape(2, width // 2)[:, : 3 * size].reshape(2, 3, size)
    qv_grad = jnp.stack([mixed_bias[:, 0], mixed_bias[:, 2]], axis=1)
    key_bias_grad = mixed_bias[:, 1, :ROT]

    return (
        block_out[None],
        input_grad[None],
        norms[0],
        norms[1],
        norms[2],
        norms[3],
        qkv_shard.reshape(qkv_weight.shape),
        qv_grad,
        key_bias_grad,
        dense_shard.reshape(dense_weight.shape),
        bias_grad,
        up_shard,
        up_bias_grad,
        down_shard.reshape(down_weight.shape),
        bias_grad,
    )


def solution(mesh):
    placed = (
        P("dp", None, None),
        P("dp", None),
        P("dp", None, None),
        P(),
        P(),
        P(),
        P(),
        P("dp", "tensor", None, None),
        P("tensor", None, None),
        P("tensor", None),
        P("tensor", None, "dp"),
        P(),
        P("dp", "tensor"),
        P("tensor"),
        P("tensor", "dp"),
        P(),
    )

    def whole(*arrays):
        groups, ways = mesh.shape["dp"], mesh.shape["tensor"]
        part = arrays[0].shape[2] // groups
        chosen = body_narrow if part % 128 or groups != 8 else body
        return chosen(*arrays, groups=groups, ways=ways)

    return jax.shard_map(
        whole,
        mesh=mesh,
        in_specs=placed,
        out_specs=(
            P("dp", None, None),
            P("dp", None, None),
            P(),
            P(),
            P(),
            P(),
            P("dp", "tensor", None, None),
            P("tensor", None, None),
            P("tensor", None),
            P("tensor", None, "dp"),
            P(),
            P("dp", "tensor"),
            P("tensor"),
            P("tensor", "dp"),
            P(),
        ),
        check_vma=False,
    )
```

```python
import functools

import jax
import jax.numpy as jnp
from jax import lax
from jax.experimental import pallas as pl
from jax.experimental.pallas import tpu as pltpu
from jax.sharding import PartitionSpec as P

ROT = 64
PAIR = 2
QBLOCK = 256
DOC_MAX = 512
F = jnp.float32
B = jnp.bfloat16


def dot(left, right, dims, kind):
    return lax.dot_general(left, right, (dims, ((), ())), preferred_element_type=F).astype(kind)


def gelu_slope(pre_act):
    cumulative = 0.5 * (1.0 + lax.erf(pre_act * 0.7071067811865476))
    density = jnp.exp(-0.5 * pre_act * pre_act) * 0.3989422804014327
    return cumulative + pre_act * density


def rope_tables(length):
    half = ROT // 2
    frequency = 10000.0 ** (-(jnp.arange(half, dtype=F) * 2.0) / ROT)
    angles = jnp.arange(length, dtype=F)[:, None] * frequency[None, :]
    cosine, sine = jnp.cos(angles), jnp.sin(angles)
    flat = jnp.zeros((length, 128 - ROT), F)
    zero = jnp.zeros_like(sine)
    return (
        jnp.concatenate([cosine, cosine, flat + 1.0], axis=1),
        jnp.concatenate([-sine, zero, flat], axis=1),
        jnp.concatenate([zero, sine, flat], axis=1),
    )


def turn(rows, cosine, from_above, from_below):
    head = rows[:, :128]
    above = pltpu.roll(head, 128 - ROT // 2, 1)
    below = pltpu.roll(head, ROT // 2, 1)
    turned = head * cosine + above * from_above + below * from_below
    return jnp.concatenate([turned, rows[:, 128:]], axis=1)


def block_mask(seg_col_ref, seg_row_ref, first, low, high):
    rows = first + lax.broadcasted_iota(jnp.int32, (QBLOCK, high - low), 0)
    columns = low + lax.broadcasted_iota(jnp.int32, (QBLOCK, high - low), 1)
    same = seg_col_ref[0, first : first + QBLOCK, :] == seg_row_ref[0, :, low:high]
    return (columns <= rows) & same


def key_range(first):
    return max(0, first - DOC_MAX), first + QBLOCK


def attn_forward(mixed_ref, bias_ref, cos_ref, up_ref, down_ref, col_ref, row_ref, q_ref, k_ref, v_ref, ctx_ref, lse_ref):
    size = q_ref.shape[2]
    length = q_ref.shape[1]
    scale = size ** (-0.5)
    tables = (cos_ref[...], up_ref[...], down_ref[...])
    q_ref[0] = turn(mixed_ref[0, :, :size] + bias_ref[:, :size], *tables).astype(B)
    k_ref[0] = turn(mixed_ref[0, :, size : 2 * size] + bias_ref[:, size : 2 * size], *tables).astype(B)
    v_ref[0] = (mixed_ref[0, :, 2 * size :] + bias_ref[:, 2 * size :]).astype(B)
    for first in range(0, length, QBLOCK):
        low, high = key_range(first)
        scores = dot(q_ref[0, first : first + QBLOCK], k_ref[0, low:high], ((1,), (1,)), F) * scale
        scores = jnp.where(block_mask(col_ref, row_ref, first, low, high), scores, -1e30)
        row_max = jnp.max(scores, axis=1, keepdims=True)
        expo = jnp.exp(scores - row_max)
        total = jnp.sum(expo, axis=1, keepdims=True)
        probs = (expo / total).astype(B)
        ctx_ref[0, first : first + QBLOCK] = dot(probs, v_ref[0, low:high], ((1,), (0,)), B)
        lse_ref[0, first : first + QBLOCK] = row_max + jnp.log(total)


def attn_backward(q_ref, k_ref, v_ref, grad_ref, lse_ref, cos_ref, up_ref, down_ref, col_ref, row_ref, mixed_ref, sum_ref, q_acc, k_acc, v_acc):
    size = q_ref.shape[2]
    length = q_ref.shape[1]
    scale = size ** (-0.5)
    k_acc[...] = jnp.zeros_like(k_acc)
    v_acc[...] = jnp.zeros_like(v_acc)
    for first in range(0, length, QBLOCK):
        low, high = key_range(first)
        here = slice(first, first + QBLOCK)
        scores = dot(q_ref[0, here], k_ref[0, low:high], ((1,), (1,)), F) * scale
        scores = jnp.where(block_mask(col_ref, row_ref, first, low, high), scores, -1e30)
        probs = jnp.exp(scores - lse_ref[0, here])
        v_acc[low:high] += dot(probs.astype(B), grad_ref[0, here], ((0,), (0,)), F)
        prob_grad = dot(grad_ref[0, here], v_ref[0, low:high], ((1,), (1,)), F)
        centred = jnp.sum(probs * prob_grad, axis=1, keepdims=True)
        score_grad = (probs * (prob_grad - centred)).astype(B)
        q_acc[here] = dot(score_grad, k_ref[0, low:high], ((1,), (0,)), F) * scale
        k_acc[low:high] += dot(score_grad, q_ref[0, here], ((0,), (0,)), F) * scale
    tables = (cos_ref[...], -up_ref[...], -down_ref[...])
    q_grad = turn(q_acc[...], *tables).astype(B)
    k_grad = turn(k_acc[...], *tables).astype(B)
    v_grad = v_acc[...].astype(B)
    for number, part in enumerate((q_grad, k_grad, v_grad)):
        mixed_ref[0, :, number * size : (number + 1) * size] = part
        sum_ref[0, :, number * size : (number + 1) * size] = jnp.sum(part.astype(F), axis=0, keepdims=True)


def per_seq(rows, columns):
    return pl.BlockSpec((1, rows, columns), lambda seq, *_: (seq, 0, 0))


def shared(rows, columns):
    return pl.BlockSpec((rows, columns), lambda *_: (0, 0))


MESH = pl.DeviceIdType.MESH
CHUNK = 256


def bit_of(index, bit):
    return lax.rem(lax.div(index, bit), 2)


def flip(index, mask):
    bit = 1
    while bit <= mask:
        if mask & bit:
            index = index + bit * (1 - 2 * bit_of(index, bit))
        bit *= 2
    return index


def block_order(groups):
    spread = [bit for bit in (1 << k for k in reversed(range(groups.bit_length() - 1))) if bit != PAIR]
    order = [0, PAIR]
    for bit in spread:
        order = order + [mask | bit for mask in order]
    return spread, order


def stats(rows):
    mean = jnp.mean(rows, axis=1, keepdims=True)
    center = rows - mean
    return mean, lax.rsqrt(jnp.mean(center * center, axis=1, keepdims=True) + 1e-05)


def greet(partners):
    barrier = pltpu.get_barrier_semaphore()
    for axis, index in partners:
        pl.semaphore_signal(barrier, inc=1, device_id={axis: index}, device_id_type=MESH)
    pl.semaphore_wait(barrier, len(partners))


GATHERING = (
    ("x1", "i"),
    ("sh", 0, 1),
    ("pu", 0, "i"),
    ("pu", 0, "o"),
    ("sh", 2, 0),
    ("sh", 0, 0),
    ("hd", 0, "o"),
    ("yo", 2, 0),
    ("yo", 0, 0),
    ("hd", 0, "i"),
    ("st", 0),
    ("x1", "o"),
    ("sh", 1, 1),
    ("sh", 1, 0),
    ("sh", 2, 1),
    ("po", 0, 0),
    ("pu", 1, "o"),
    ("N", 0),
    ("re", 0),
    ("pu", 1, "i"),
    ("hd", 1, "i"),
    ("yo", 1, 0),
    ("yo", 0, 1),
    ("st", 1),
    ("hd", 1, "o"),
    ("po", 0, 1),
    ("g1", "o"),
    ("G", 0),
    ("x2",),
    ("yo", 0, 2),
    ("yo", 0, 3),
    ("po", 0, 2),
    ("g1", "i"),
    ("po", 1, 1),
    ("po", 1, 0),
    ("pu", 2, "o"),
    ("PJ", 0),
    ("re", 1),
    ("CG", 0),
    ("hd", 2, "o"),
    ("pu", 2, "i"),
    ("hd", 2, "i"),
    ("yo", 1, 1),
    ("AT", 0),
    ("g2",),
    ("GR", 0, 0),
    ("po", 1, 2),
    ("x3",),
    ("yo", 1, 2),
    ("GR", 0, 1),
    ("N", 1),
    ("yo", 2, 1),
    ("re", 2),
    ("po", 2, 1),
    ("PJ", 1),
    ("po", 2, 0),
    ("g3",),
    ("yo", 1, 3),
    ("G", 1),
    ("CG", 1),
    ("st", 2),
    ("AT", 1),
    ("yo", 2, 2),
    ("po", 2, 2),
    ("GR", 1, 0),
    ("UP", 0),
    ("yo", 2, 3),
    ("UP", 1),
    ("GR", 1, 1),
)


def gather_kernel(
    groups,
    qkv_ref,
    dense_ref,
    up_ref,
    down_ref,
    seg_ref,
    x_ref,
    g_ref,
    vec_ref,
    up_bias_ref,
    offset_ref,
    cos_ref,
    above_ref,
    below_ref,
    w_out,
    w_relay,
    x_other,
    g_other,
    x_rel,
    g_rel,
    mlp_out,
    mixed_out,
    ctx_out,
    act_out,
    slope_out,
    send_out,
    keep_out,
    sum_ref,
    bias_ref,
    w,
    raw_x,
    raw_g,
    attn_v,
    g_v,
    mlp_v,
    xr_v,
    grad_v,
    send_v,
    q_v,
    k_v,
    v_v,
    cg_v,
    ctx_v,
    mg_v,
    dk_v,
    dv_v,
    act_v,
    slope_v,
    theirs_v,
    seg_v,
    col_v,
    send_sem,
    recv_sem,
    cross_sem,
    two_sem,
    three_sem,
    relay_sem,
    quarter_sem,
    shard_sem,
    seg_sem,
    load_sem,
    rel_sem,
    tile_sem,
    out_sem,
):
    length, width = x_ref.shape
    part = width // groups
    size = q_v.shape[1]
    quarter = length // 4
    me, place = lax.axis_index("dp"), lax.axis_index("tensor")
    core, side = lax.rem(place, 2), lax.div(place, 2)
    pair_to, side_to, core_to = flip(me, PAIR), flip(place, 2), flip(place, 1)
    spread, order = block_order(groups)
    half = bit_of(me, PAIR)
    hidden = slope_v.shape[2]

    def shards(owner, slot):
        at = pl.ds(pl.multiple_of(owner * 3 * size, 128), 3 * size)
        spots = [
            (qkv_ref.at[:, at], grad_v.at[pl.ds(slot * part, part), pl.ds(0, 3 * size)]),
            (dense_ref.at[owner], grad_v.at[pl.ds(2 * part, size), pl.ds(slot * part, part)]),
            (
                up_ref.at[:, pl.ds(pl.multiple_of(owner * hidden, hidden), hidden)],
                grad_v.at[pl.ds((3 + slot) * part, part)],
            ),
        ]
        for number in range(hidden // part):
            at = pl.ds(pl.multiple_of(owner * hidden + number * part, part), part)
            spots.append((down_ref.at[at], slope_v.at[slot, :, pl.ds(number * part, part)]))
        return [
            pltpu.make_async_copy(source, target, shard_sem.at[slot, number])
            for number, (source, target) in enumerate(spots)
        ]

    shard_copies = [shards(half, 0), shards(1 - half, 1)]
    for number in range(3 + hidden // part):
        for slot in (1, 0):
            shard_copies[slot][number].start()

    def shard(group, slot):
        for copy in shard_copies[slot][(0, 2, 3)[group] : (2, 3, None)[group]]:
            copy.wait()

        def put(columns, value):
            if slot:
                theirs_v[group, :, columns] = value.astype(B)
            else:
                w[group, 0:part, columns] = value.astype(B)

        if group == 0:
            put(slice(0, 3 * size), grad_v[slot * part : (slot + 1) * part, : 3 * size])
            put(slice(3 * size, 4 * size), grad_v[2 * part : 2 * part + size, slot * part : (slot + 1) * part].T)
        elif group == 1:
            put(slice(0, hidden), grad_v[(3 + slot) * part : (4 + slot) * part])
        else:
            for number in range(hidden // part):
                at = slice(number * part, (number + 1) * part)
                put(at, slope_v[slot, :, at].T)

    across = PAIR | spread[0]
    inner = bit_of(me, PAIR) != bit_of(me, spread[0])
    greet(
        [("dp", flip(me, mask)) for mask in [PAIR, across] + spread] + [("tensor", side_to), ("tensor", core_to)]
    )
    outer = bit_of(me, PAIR) == bit_of(me, spread[0])
    copies, partial_copies = {}, []

    def remote(key, source, target, axis, index):
        number = len(copies)
        copies[key] = pltpu.make_async_remote_copy(
            src_ref=source,
            dst_ref=target,
            send_sem=send_sem.at[number],
            recv_sem=recv_sem.at[number],
            device_id={axis: index},
            device_id_type=MESH,
        )
        copies[key].start()

    def rows(position):
        return pl.ds(position * part, part)

    def pair_up(group, here=None):
        key = ("w", group, 1)
        if key not in copies:
            number = len(copies)
            copies[key] = pltpu.make_async_remote_copy(
                src_ref=theirs_v.at[group],
                dst_ref=w.at[group, rows(1)],
                send_sem=send_sem.at[number],
                recv_sem=recv_sem.at[number],
                device_id={"dp": pair_to},
                device_id_type=MESH,
            )
        if here is None:
            copies[key].start()
        else:
            pl.when(here)(copies[key].start)

    def onward(group, position, level):
        source = w.at[group, rows(position)]
        far = position + (2 << level)
        remote(("w", group, far), source, w.at[group, rows(far)], "dp", flip(me, spread[level]))

    def partly(here, source, target, send, recv, to):
        copy = pltpu.make_async_remote_copy(
            src_ref=source,
            dst_ref=target,
            send_sem=send,
            recv_sem=recv,
            device_id={"dp": to},
            device_id_type=MESH,
        )
        partial_copies.append((here, copy))
        pl.when(here)(copy.start)
        return copy

    across_to = flip(me, across)

    def straight(group):
        copy = partly(
            inner, theirs_v.at[group], w.at[group, rows(3)], cross_sem.at[group, 0], three_sem.at[group], across_to
        )
        copies[("w", group, 3)] = copy

    def hand(group, here=None):
        source, sem = w.at[group, rows(0)], cross_sem.at[group, 1]
        if here is not inner:
            partly(outer, source, w_relay.at[group, rows(0)], sem, relay_sem.at[group, 0], pair_to)
        if here is not outer:
            partly(inner, source, w_relay.at[group, rows(1)], sem, relay_sem.at[group, 1], across_to)

    def relay(group):
        source = w.at[group, rows(1)]
        partly(
            inner, source, w_relay.at[group, rows(2)], cross_sem.at[group, 2], relay_sem.at[group, 2], across_to
        )

    def pass_on(group, *numbers):
        for number in numbers:
            source, target = w_relay.at[group, rows(number)], 3 if number == 2 else 2
            here = pltpu.make_async_remote_copy(
                src_ref=source,
                dst_ref=source,
                send_sem=relay_sem.at[group, number],
                recv_sem=relay_sem.at[group, number],
                device_id={"dp": pair_to},
                device_id_type=MESH,
            )
            pl.when(inner)(here.wait_recv)
            copy = partly(
                inner,
                source,
                w.at[group, rows(target)],
                cross_sem.at[group, 3 + number],
                (three_sem if target == 3 else two_sem).at[group],
                across_to if number == 0 else pair_to,
            )
            copies[("w", group, target)] = copy

    def to_pair(key, source, target, here):
        if key not in quarters:
            quarters[key] = pltpu.make_async_remote_copy(
                src_ref=source,
                dst_ref=target,
                send_sem=quarter_sem.at[key, 0],
                recv_sem=quarter_sem.at[key, 1],
                device_id={"dp": pair_to},
                device_id_type=MESH,
            )
            partial_copies.append((None, quarters[key]))
        pl.when(here)(quarters[key].start)

    quarters = {}
    arrived = set()

    def arrive(group, position):
        if (group, position) not in arrived:
            arrived.add((group, position))
            copies[("w", group, position)].wait_recv()

    spot = pl.ds(pl.multiple_of(core * (2 * quarter) + side * quarter, quarter), quarter)
    pair_rows = pl.ds(pl.multiple_of(core * (2 * quarter), quarter), 2 * quarter)
    levels = len(spread)
    assert levels == 2

    def over_tiles(source, raw, number, work):
        def load(tile, slot):
            here = pl.ds(pl.multiple_of(tile * CHUNK, CHUNK), CHUNK)
            return pltpu.make_async_copy(source.at[here], raw.at[slot], load_sem.at[number, slot])

        load(0, 0).start()

        def one(tile, carry):
            slot = lax.rem(tile, 2)

            @pl.when(tile + 1 < length // CHUNK)
            def _():
                load(tile + 1, 1 - slot).start()

            load(tile, slot).wait()
            work(tile, slot)
            return carry

        lax.fori_loop(0, length // CHUNK, one, 0)

    outs = {}

    def leave(key, source, target, sem):
        outs[key] = pltpu.make_async_copy(source, target, sem)
        outs[key].start()

    def left(*keys):
        for key in keys:
            outs.pop(key).wait()

    def normalise(seq):
        if seq:
            copies["x3"].wait_recv()
            left(("x", 0))

        def work(tile, slot):
            here = pl.ds(pl.multiple_of(tile * CHUNK, CHUNK), CHUNK)
            both = pl.ds(pl.multiple_of(seq * length + tile * CHUNK, CHUNK), CHUNK)
            mean, inverse = stats(raw_x[slot].astype(F))
            for position, mask in enumerate(order):
                to = slice(position * part, (position + 1) * part)
                there = pl.ds(pl.multiple_of(flip(me, mask) * part, part), part)
                piece = raw_x[slot, :, there]
                normed = (piece.astype(F) - mean) * inverse
                attn_v[here, to] = (normed * vec_ref[0:1, there] + vec_ref[1:2, there]).astype(B)
                mlp_v[both, to] = (normed * vec_ref[2:3, there] + vec_ref[3:4, there]).astype(B)
                xr_v[here, to] = piece

        over_tiles(x_other if seq else x_ref, raw_x, 0, work)
        both = pl.ds(seq * length, length)
        leave(("x", seq), xr_v, x_rel.at[both], rel_sem.at[seq, 0])
        leave(("m", seq), mlp_v.at[both], mlp_out.at[both], rel_sem.at[seq, 2])

    def arrange_grad(seq):
        if seq:
            copies["g3"].wait_recv()
            left(("g", 0))
        else:
            bias_ref[...] = jnp.zeros_like(bias_ref)

        def work(tile, slot):
            here = pl.ds(pl.multiple_of(tile * CHUNK, CHUNK), CHUNK)
            if seq == 0:
                bias_ref[...] += jnp.sum(raw_g[slot].astype(F), axis=0, keepdims=True)
            for position, mask in enumerate(order):
                to = slice(position * part, (position + 1) * part)
                there = pl.ds(pl.multiple_of(flip(me, mask) * part, part), part)
                g_v[here, to] = raw_g[slot, :, there]

        over_tiles(g_other if seq else g_ref, raw_g, 1, work)
        leave(("g", seq), g_v, g_rel.at[pl.ds(seq * length, length)], rel_sem.at[seq, 1])

    def whole_group(group):
        if ("out", group) not in arrived:
            arrived.add(("out", group))
            for position in range(4, 8):
                arrive(group, position)
            leave(("w", group), w.at[group], w_out.at[group], out_sem.at[group])

    def project(seq):
        whole_group(0)

        def one(tile, carry):
            here = pl.ds(pl.multiple_of(tile * CHUNK, CHUNK), CHUNK)
            mixed = dot(attn_v[here], w[0, :, : 3 * size], ((1,), (0,)), F) + offset_ref[...]
            tables = (cos_ref[here], above_ref[here], below_ref[here])
            q_v[here] = turn(mixed[:, :size], *tables).astype(B)
            k_v[here] = turn(mixed[:, size : 2 * size], *tables).astype(B)
            v_v[here] = mixed[:, 2 * size :].astype(B)
            return carry

        lax.fori_loop(0, length // CHUNK, one, 0)

    def project_grad(seq):
        whole_group(0)
        cg_v[...] = dot(g_v[...], w[0, :, 3 * size :], ((1,), (0,)), B)

    def attend(seq):
        if seq:
            seg_copy.wait()
            left(("mg", 0), ("ctx", 0))
        scale = size ** (-0.5)
        ids = seg_ref[...] if seq == 0 else seg_v[...]
        col_v[...] = jnp.broadcast_to(ids.astype(F), (8, length)).T
        dk_v[...] = jnp.zeros_like(dk_v)
        dv_v[...] = jnp.zeros_like(dv_v)
        for first in range(0, length, QBLOCK):
            low, high = key_range(first)
            here, keys = slice(first, first + QBLOCK), slice(low, high)
            scores = dot(q_v[here], k_v[keys], ((1,), (1,)), F) * scale
            row_ids = first + lax.broadcasted_iota(jnp.int32, (QBLOCK, high - low), 0)
            key_ids = low + lax.broadcasted_iota(jnp.int32, (QBLOCK, high - low), 1)
            row = seg_ref[:, keys] if seq == 0 else seg_v[:, keys]
            allowed = (key_ids <= row_ids) & (col_v[here, 0:1] == row.astype(F))
            scores = jnp.where(allowed, scores, -1e30)
            expo = jnp.exp(scores - jnp.max(scores, axis=1, keepdims=True))
            probs = expo / jnp.sum(expo, axis=1, keepdims=True)
            low_probs = probs.astype(B)
            ctx_v[here] = dot(low_probs, v_v[keys], ((1,), (0,)), B)
            dv_v[keys] += dot(low_probs, cg_v[here], ((0,), (0,)), F)
            prob_grad = dot(cg_v[here], v_v[keys], ((1,), (1,)), F)
            centred = jnp.sum(probs * prob_grad, axis=1, keepdims=True)
            score_grad = (probs * (prob_grad - centred)).astype(B)
            q_grad = dot(score_grad, k_v[keys], ((1,), (0,)), F) * scale
            tables = (cos_ref[here], -above_ref[here], -below_ref[here])
            mg_v[here, :size] = turn(q_grad, *tables).astype(B)
            dk_v[keys] += dot(score_grad, q_v[here], ((0,), (0,)), F) * scale
        for first in range(0, length, QBLOCK):
            here = slice(first, first + QBLOCK)
            tables = (cos_ref[here], -above_ref[here], -below_ref[here])
            mg_v[here, size : 2 * size] = turn(dk_v[here], *tables).astype(B)
            mg_v[here, 2 * size :] = dv_v[here].astype(B)
        sums = jnp.sum(mg_v[...].astype(F), axis=0, keepdims=True)
        if seq == 0:
            sum_ref[...] = sums
        else:
            sum_ref[...] += sums
        both = pl.ds(seq * length, length)
        leave(("mg", seq), mg_v, mixed_out.at[both], rel_sem.at[seq, 3])
        leave(("ctx", seq), ctx_v, ctx_out.at[both], rel_sem.at[seq, 4])

    def attn_grads(seq, low, high):
        def one(block, carry):
            here = pl.ds(pl.multiple_of(block * CHUNK, CHUNK), CHUNK)
            qkv = dot(attn_v[:, here], mg_v[...], ((0,), (0,)), F)
            dense = dot(g_v[:, here], ctx_v[...], ((0,), (0,)), F)
            if seq == 0:
                grad_v[here, : 3 * size] = qkv
                grad_v[here, 3 * size :] = dense
            else:
                grad_v[here, : 3 * size] += qkv
                grad_v[here, 3 * size :] += dense
            return carry

        lax.fori_loop(low // CHUNK, high // CHUNK, one, 0)

    def up(low, high):
        def store(tile, slot):
            here = pl.ds(pl.multiple_of(tile * CHUNK, CHUNK), CHUNK)
            return (
                pltpu.make_async_copy(act_v.at[slot], act_out.at[here], tile_sem.at[0, slot]),
                pltpu.make_async_copy(slope_v.at[slot], slope_out.at[here], tile_sem.at[1, slot]),
            )

        def one(tile, carry):
            slot = lax.rem(tile, 2)
            here = pl.ds(pl.multiple_of(tile * CHUNK, CHUNK), CHUNK)
            pre = dot(mlp_v[here], w[1], ((1,), (0,)), F) + up_bias_ref[...]

            @pl.when(tile >= low + 2)
            def _():
                for copy in store(tile - 2, slot):
                    copy.wait()

            cumulative = 0.5 * (1.0 + lax.erf(pre * 0.7071067811865476))
            density = jnp.exp(-0.5 * pre * pre) * 0.3989422804014327
            act_v[slot] = (pre * cumulative).astype(B)
            slope_v[slot] = cumulative + pre * density
            for copy in store(tile, slot):
                copy.start()
            return carry

        lax.fori_loop(low, high, one, 0)
        for tile in (high - 2, high - 1):
            for copy in store(tile, tile % 2):
                copy.wait()

    seg_copy = pltpu.make_async_remote_copy(
        src_ref=seg_ref,
        dst_ref=seg_v,
        send_sem=seg_sem.at[0],
        recv_sem=seg_sem.at[1],
        device_id={"dp": pair_to},
        device_id_type=MESH,
    )
    seg_copy.start()
    kinds = {"o": outer, "i": inner}

    def relay_on(group):
        arrive(group, 1)
        relay(group)

    def send_y(group, position):
        if position:
            arrive(group, position)
        onward(group, position, 1)

    def to_side(name, number, array):
        quarters[number].wait_recv()
        remote(name + "2", array.at[spot], array.at[spot], "tensor", side_to)

    def to_core(name, array):
        copies[name + "2"].wait_recv()
        remote(name + "3", array.at[pair_rows], array.at[pair_rows], "tensor", core_to)

    def gradients(seq, number):
        middle = width // 2
        attn_grads(seq, *((0, middle) if number else (middle, width)))
        if seq and number:
            leave("keep", grad_v.at[pl.ds(0, middle)], keep_out, out_sem.at[4])
        elif seq:
            send_v[...] = grad_v[middle:].astype(B)
            leave("send", send_v, send_out, out_sem.at[3])

    def lift(seq):
        whole_group(1)
        up(seq * length // CHUNK, (seq + 1) * length // CHUNK)

    stages = {
        "sh": shard,
        "pu": lambda group, kind: pair_up(group, kinds[kind]),
        "st": straight,
        "hd": lambda group, kind: hand(group, kinds[kind]),
        "re": relay_on,
        "yo": send_y,
        "po": pass_on,
        "x1": lambda kind: to_pair(0, x_ref.at[spot], x_other.at[spot], kinds[kind]),
        "g1": lambda kind: to_pair(1, g_ref.at[spot], g_other.at[spot], kinds[kind]),
        "x2": lambda: to_side("x", 0, x_other),
        "g2": lambda: to_side("g", 1, g_other),
        "x3": lambda: to_core("x", x_other),
        "g3": lambda: to_core("g", g_other),
        "N": normalise,
        "G": arrange_grad,
        "PJ": project,
        "CG": project_grad,
        "AT": attend,
        "GR": gradients,
        "UP": lift,
    }
    for name, *numbers in GATHERING:
        stages[name](*numbers)
    whole_group(2)
    left(*list(outs))
    for key, copy in copies.items():
        if key[0] != "w" or key[2] not in (2, 3):
            copy.wait_send()
    for here, copy in partial_copies:
        if here is None:
            copy.wait_send()
        else:
            pl.when(here)(copy.wait_send)


SCHEDULE = (
    ("pre", 1),
    ("st", 1, 1),
    ("yf", 0, 3),
    ("kt", 1, 1),
    ("ps", 2),
    ("yf", 0, 2),
    ("st", 0, 1),
    ("yn", 0, 1),
    ("kt", 0, 1),
    ("po", 0, 1),
    ("es", 1),
    ("st", 1, 0),
    ("po", 0, 2),
    ("po", 0, 0),
    ("pk", 2),
    ("kt", 1, 0),
    ("pre", 0),
    ("yf", 2, 3),
    ("st", 0, 0),
    ("yn", 0, 0),
    ("yf", 2, 2),
    ("kt", 0, 0),
    ("sb",),
    ("es", 0),
    ("po", 2, 1),
    ("ps", 1),
    ("se", 0),
    ("zl", 0, 1),
    ("zl", 0, 0),
    ("po", 2, 0),
    ("pk", 1),
    ("yf", 1, 3),
    ("fin", 1),
    ("yn", 2, 0),
    ("se", 1),
    ("yf", 1, 2),
    ("yn", 2, 1),
    ("po", 2, 2),
    ("zl", 2, 1),
    ("fin", 0),
    ("fa", 0),
    ("po", 1, 1),
    ("yn", 1, 0),
    ("po", 1, 2),
    ("yn", 1, 1),
    ("po", 1, 0),
    ("se", 2),
    ("zl", 1, 1),
    ("zl", 1, 0),
    ("fa", 2),
    ("fe", 1),
    ("fe", 0),
    ("zl", 2, 0),
    ("se", 3),
    ("se", 4),
    ("fa", 1),
)

def scatter_kernel(
    groups,
    attn_send,
    attn_keep,
    weights,
    x_rel,
    g_rel,
    mlp_in,
    mixed_grad,
    context,
    activation,
    slope,
    x_ref,
    g_ref,
    vec_ref,
    mixed_sum,
    bias_sum,
    block_out,
    input_grad,
    qkv_out,
    dense_out,
    up_out,
    down_out,
    far_in,
    far_two,
    y_recv,
    z_recv,
    z_relay,
    c_recv,
    x_recv,
    e_recv,
    small_out,
    w,
    act_v,
    pre_v,
    tile_v,
    col_v,
    slope_t,
    mix_t,
    ctx_v,
    keep_v,
    y_send,
    z_send,
    p_send,
    y_stage,
    c_send,
    c_stage,
    r_stage,
    x_send,
    hold_v,
    mean_v,
    inverse_v,
    sum_v,
    small_v,
    small_recv,
    load_sem,
    tile_sem,
    ys_sem,
    yr_sem,
    zs_sem,
    zr_sem,
    zl_sem,
    zf_sem,
    two_sem,
    ps_sem,
    pr_sem,
    cs_sem,
    cr_sem,
    xs_sem,
    xr_sem,
    es_sem,
    er_sem,
    fs_sem,
    fr_sem,
    emit_sem,
    ss_sem,
    sr_sem,
    out_sem,
):
    length, width = x_ref.shape
    part = width // groups
    size = context.shape[1]
    hidden = activation.shape[1]
    quarter = length // 4
    me, place = lax.axis_index("dp"), lax.axis_index("tensor")
    core, side, half = lax.rem(place, 2), lax.div(place, 2), bit_of(me, PAIR)
    pair_to, side_to, core_to = flip(me, PAIR), flip(place, 2), flip(place, 1)
    spread, order = block_order(groups)
    z_to, y_to = [flip(me, bit) for bit in spread]
    across_to = flip(z_to, PAIR)
    inner = bit_of(me, PAIR) != bit_of(me, spread[0])
    outer = bit_of(me, PAIR) == bit_of(me, spread[0])
    greet([("dp", to) for to in (pair_to, z_to, y_to, across_to)] + [("tensor", side_to), ("tensor", core_to)])

    def remote(source, target, send, recv, axis, index):
        return pltpu.make_async_remote_copy(
            src_ref=source, dst_ref=target, send_sem=send, recv_sem=recv, device_id={axis: index}, device_id_type=MESH
        )

    def span(position, count=1):
        return pl.ds(position * part, count * part)

    def step(index, amount):
        return pl.ds(pl.multiple_of(index * amount, amount), amount)

    def y_copy(group, position):
        source = attn_send if group == 0 else y_send
        here = step(position, part) if not isinstance(position, int) else span(position)
        return remote(
            source.at[here], y_recv.at[group, here], ys_sem.at[group, position], yr_sem.at[group, position], "dp", y_to
        )

    slot_of = (0, 0, 1)

    def z_copy(group, position):
        source, sem = z_send.at[slot_of[group], span(position - 2)], zs_sem.at[group, position - 2]
        onward = (
            remote(source, far_two.at[group], sem, two_sem.at[group], "dp", across_to)
            if position == 3
            else remote(source, z_relay.at[group, span(2)], sem, zl_sem.at[group, 2], "dp", across_to)
        )
        aside = remote(
            source, z_relay.at[group, span(position - 2)], sem, zl_sem.at[group, position - 2], "dp", pair_to
        )
        return onward, aside

    def forward(group, number):
        target = 0 if number == 2 else number
        arrived = remote(
            z_relay.at[group, span(number)],
            z_recv.at[group, span(target)],
            zf_sem.at[group, number],
            zl_sem.at[group, number],
            "dp",
            pair_to,
        )
        return arrived, remote(
            z_relay.at[group, span(number)],
            z_recv.at[group, span(target)],
            zf_sem.at[group, number],
            zr_sem.at[group, target],
            "dp",
            pair_to if number == 2 else across_to,
        )

    def pass_on(group, *numbers):
        @pl.when(inner)
        def _():
            for number in numbers:
                arrived, copy = forward(group, number)
                arrived.wait_recv()
                copy.start()

    def z_arrived(group, position):
        return remote(
            z_relay.at[group, span(position)],
            z_recv.at[group, span(position)],
            zf_sem.at[group, position],
            zr_sem.at[group, position],
            "dp",
            pair_to,
        )

    def p_copy(group):
        return remote(
            p_send.at[slot_of[group]], far_in.at[group], ps_sem.at[group], pr_sem.at[group], "dp", pair_to
        )

    emitted = {}

    def emit(group, kind, block, owner):
        copies = []
        for number in range(hidden // part):
            at = pl.ds(number * part, part)
            if group == 2 or (group == 0 and number == 3):
                block[:, at] = block[:, at].T
            if group == 1:
                target = up_out.at[:, pl.ds(pl.multiple_of(owner * hidden + number * part, part), part)]
            elif group == 2:
                target = down_out.at[pl.ds(pl.multiple_of(owner * hidden + number * part, part), part)]
            elif number == 3:
                target = dense_out.at[owner]
            else:
                target = qkv_out.at[:, pl.ds(pl.multiple_of(owner * 3 * size + number * part, part), part)]
            copies.append(pltpu.make_async_copy(block.at[:, at], target, emit_sem.at[group, kind, number]))
            copies[-1].start()
        emitted[(group, kind)] = copies

    def emit_near(group):
        emit(group, 0, keep_v.at[slot_of[group], span(0)], half)

    def emit_far(group):
        block = (
            hold_v.at[1, 1, :, pl.ds(0, hidden)],
            keep_v.at[0, span(1)],
            hold_v.at[1, 1, :, pl.ds(hidden, hidden)],
        )[group]
        p_copy(group).wait_recv()
        staged(far_in.at[group])
        block[...] = y_stage[...].astype(F)

        @pl.when(inner)
        def _():
            remote(
                p_send.at[0], far_two.at[group], two_sem.at[group], two_sem.at[group], "dp", across_to
            ).wait_recv()
            staged(far_two.at[group])
            block[...] += y_stage[...].astype(F)

        emit(group, 1, block, 1 - half)

    def staged(source):
        copy = pltpu.make_async_copy(source, y_stage, load_sem.at[6])
        copy.start()
        copy.wait()

    def y_far(group, position):
        if group == 0:
            need(5)
        y_copy(group, position).wait_recv()
        staged(y_recv.at[group, span(position)])
        total = keep_v[slot_of[group], span(position)] + y_stage[...].astype(F)
        onward, aside = z_copy(group, position)
        if group == 1:
            z_copy(0, position)[0].wait_send()
        z_send[slot_of[group], span(position - 2)] = total.astype(B)
        pl.when(inner)(onward.start)
        pl.when(outer)(aside.start)

    def y_near(group, position):
        if group == 0:
            need(5)
        y_copy(group, position).wait_recv()
        staged(y_recv.at[group, span(position)])
        total = keep_v[slot_of[group], span(position)] + y_stage[...].astype(F)
        keep_v[slot_of[group], span(position)] = total
        if position == 1:
            if group == 1:
                p_copy(0).wait_send()

            @pl.when(outer)
            def _():
                p_send[slot_of[group]] = keep_v[slot_of[group], span(1)].astype(B)
                p_copy(group).start()

    def z_last(group, position):
        def add():
            z_arrived(group, position).wait_recv()
            staged(z_recv.at[group, span(position)])
            return keep_v[slot_of[group], span(position)] + y_stage[...].astype(F)

        if position == 1:

            @pl.when(inner)
            def _():
                p_send[slot_of[group]] = add().astype(B)
                p_copy(group).start()

        else:
            keep_v[slot_of[group], span(0)] = add()
            emit_near(group)

    loads = [
        pltpu.make_async_copy(weights.at[2], w.at[2], load_sem.at[0]),
        pltpu.make_async_copy(weights.at[0], w.at[0], load_sem.at[1]),
        pltpu.make_async_copy(weights.at[1], w.at[1], load_sem.at[2]),
        pltpu.make_async_copy(activation, act_v, load_sem.at[3]),
        pltpu.make_async_copy(context, ctx_v, load_sem.at[4]),
        pltpu.make_async_copy(attn_keep, keep_v.at[0], load_sem.at[5]),
    ]
    for number in (4, 3, 1, 0, 5, 2):
        loads[number].start()
    loaded = set()

    def need(*numbers):
        for number in numbers:
            if number not in loaded:
                loaded.add(number)
                loads[number].wait()

    for position in (3, 2, 1, 0):
        y_copy(0, position).start()

    small_v[...] = jnp.zeros_like(small_v)

    def pre_load(tile, slot):
        here = step(tile, CHUNK)
        return (
            pltpu.make_async_copy(g_rel.at[here], tile_v.at[step(slot, CHUNK)], tile_sem.at[0, slot]),
            pltpu.make_async_copy(slope.at[here], slope_t.at[slot], tile_sem.at[1, slot]),
        )

    sum_v[...] = jnp.zeros_like(sum_v)

    def pre_tiles(seq):
        need(0)
        low, high = seq * length // CHUNK, (seq + 1) * length // CHUNK
        for copy in pre_load(low, 0):
            copy.start()

        def one(tile, carry):
            slot = lax.rem(tile, 2)

            @pl.when(tile + 1 < high)
            def _():
                for copy in pre_load(tile + 1, 1 - slot):
                    copy.start()

            for copy in pre_load(tile, slot):
                copy.wait()
            grad = (dot(tile_v[step(slot, CHUNK)], w[2], ((1,), (0,)), F) * slope_t[slot]).astype(B)
            pre_v[step(tile, CHUNK)] = grad
            sum_v[...] += jnp.sum(grad.astype(F), axis=0, keepdims=True)
            return carry

        lax.fori_loop(low, high, one, 0)

    tall = 2 * quarter
    blocks = width // CHUNK

    def c_copy(which, seq, block):
        here = step(block, CHUNK)
        return remote(
            c_send.at[:, here],
            c_recv.at[which, seq, :, here],
            cs_sem.at[which, seq, block],
            cr_sem.at[which, seq, block],
            "tensor",
            core_to,
        )

    def x_copy(which, seq):
        return remote(
            x_send.at[which, seq], x_recv.at[which, seq], xs_sem.at[which, seq], xr_sem.at[which, seq], "tensor", side_to
        )

    def e_copy(which):
        return remote(x_send.at[which, 1], e_recv.at[which], es_sem.at[which], er_sem.at[which], "dp", pair_to)

    sent_tiles = []

    def send_tile(which, seq):
        begin, block_of = tile_of[which]
        need(*((1, 2) if which == 0 else (0, 1, 3, 4)))
        start = pl.multiple_of(seq * length + (1 - core) * tall, tall)
        begin(start)

        def one(block, carry):
            value = block_of(start, block)
            if sent_tiles:
                c_copy(*sent_tiles[-1], block).wait_send()
            c_send[:, step(block, CHUNK)] = value.astype(B)
            c_copy(which, seq, block).start()
            return carry

        lax.fori_loop(0, blocks, one, 0)
        sent_tiles.append((which, seq))

    def c_load(which, seq, block, slot):
        return pltpu.make_async_copy(c_recv.at[which, seq, :, step(block, CHUNK)], c_stage.at[slot], tile_sem.at[2, slot])

    def keep_tile(which, seq):
        begin, block_of = tile_of[which]
        start = pl.multiple_of(seq * length + core * tall, tall)
        begin(start)
        c_copy(which, seq, 0).wait_recv()
        c_load(which, seq, 0, 0).start()

        def one(block, carry):
            slot = lax.rem(block, 2)
            value = block_of(start, block)

            @pl.when(block + 1 < blocks)
            def _():
                c_copy(which, seq, block + 1).wait_recv()
                c_load(which, seq, block + 1, 1 - slot).start()

            c_load(which, seq, block, slot).wait()
            r_stage[...] = value + c_stage[slot].astype(F)
            here = step(block, CHUNK)
            hold_v[which, seq, :, here] = r_stage[step(side, quarter)]
            x_send[which, seq, :, here] = r_stage[step(1 - side, quarter)].astype(B)
            return carry

        lax.fori_loop(0, blocks, one, 0)
        x_copy(which, seq).start()

    def blend_begin(start):
        copies = (
            pltpu.make_async_copy(x_rel.at[pl.ds(start, tall)], tile_v, tile_sem.at[3, 0]),
            pltpu.make_async_copy(mixed_grad.at[pl.ds(start, tall)], mix_t, tile_sem.at[3, 1]),
        )
        for copy in copies:
            copy.start()
        for copy in copies:
            copy.wait()
        for slot in range(2):
            mean, inverse = stats(tile_v[span_rows(slot)].astype(F))
            mean_v[span_rows(slot)] = jnp.broadcast_to(mean, (CHUNK, 128))
            inverse_v[span_rows(slot)] = jnp.broadcast_to(inverse, (CHUNK, 128))

    def span_rows(slot):
        return pl.ds(slot * CHUNK, CHUNK)

    def natural_block(position):
        result = me
        for level, bit in enumerate([PAIR] + spread):
            flipped = lax.rem(lax.div(position, 1 << level), 2)
            result = result + bit * (1 - 2 * bit_of(me, bit)) * flipped
        return result

    def blend_block(start, block):
        here = step(block, CHUNK)
        there = step(natural_block(block), part)
        attn_grad = dot(mix_t[...], w[0, here, : 3 * size], ((1,), (1,)), F)
        mlp_grad = dot(pre_v[pl.ds(start, tall)], w[1, here, :], ((1,), (1,)), F)
        mean, inverse = mean_v[...], inverse_v[...]
        mean = jnp.concatenate([mean] * (CHUNK // 128), axis=1)
        inverse = jnp.concatenate([inverse] * (CHUNK // 128), axis=1)
        normed = (tile_v[:, here].astype(F) - mean) * inverse
        small_v[0:1, there] += jnp.sum(attn_grad * normed, axis=0, keepdims=True)
        small_v[1:2, there] += jnp.sum(attn_grad, axis=0, keepdims=True)
        small_v[2:3, there] += jnp.sum(mlp_grad * normed, axis=0, keepdims=True)
        small_v[3:4, there] += jnp.sum(mlp_grad, axis=0, keepdims=True)
        return attn_grad * vec_ref[0:1, there] + mlp_grad * vec_ref[2:3, there]

    def product(columns, right, group, positions, sent, old=None):
        count = len(positions)
        base = positions[0]
        sign = positions[1] - positions[0] if count > 1 else 1

        def load(number, slot):
            return pltpu.make_async_copy(
                columns.at[:, step(base + sign * number, part)], col_v.at[slot], tile_sem.at[4, slot]
            )

        load(0, 0).start()

        def one(number, carry):
            slot = lax.rem(number, 2)

            @pl.when(number + 1 < count)
            def _():
                load(number + 1, 1 - slot).start()

            load(number, slot).wait()
            value = dot(col_v[slot], right[...], ((0,), (0,)), F)
            position = base + sign * number
            if sent:
                if old is not None:
                    y_copy(old, position - groups // 2).wait_send()
                y_send[step(position - groups // 2, part)] = value.astype(B)
                y_copy(group, position - groups // 2).start()
            else:
                keep_v[slot_of[group], step(position, part)] = value
            return carry

        lax.fori_loop(0, count, one, 0)

    def small_begin():
        small_v[4:5] = bias_sum[...]
        small_v[5:6, step(half, hidden)] = sum_v[...]
        small_v[6:7, pl.ds(pl.multiple_of(half * (width // 2), width // 2), 3 * size)] = mixed_sum[...]
        small_copy(0).start()

    rounds = [("dp", flip(me, bit)) for bit in [PAIR] + spread] + [("tensor", side_to), ("tensor", core_to)]

    def small_copy(number):
        return remote(small_v, small_recv.at[number], ss_sem.at[number], sr_sem.at[number], *rounds[number])

    def small_end(number):
        small_copy(number).wait()
        if number < 3:
            small_v[...] += small_recv[number]
        else:
            small_v[0:4] += small_recv[number, 0:4]
        if number + 1 < len(rounds):
            small_copy(number + 1).start()

    def branch_begin(start):
        pass

    def branch_block(start, block):
        here, rows = step(block, CHUNK), pl.ds(start, tall)
        return dot(ctx_v[rows], w[0, here, 3 * size :], ((1,), (1,)), F) + dot(
            act_v[rows], w[2, here, :], ((1,), (1,)), F
        )

    def read_stage(source):
        copy = pltpu.make_async_copy(source, tile_v.at[pl.ds(0, quarter)], load_sem.at[6])
        copy.start()
        copy.wait()

    def e_start(which):
        x_copy(which, 1).wait_recv()
        x_copy(which, 1).wait_send()
        read_stage(x_recv.at[which, 1])

        def one(block, carry):
            here = step(block, CHUNK)
            x_send[which, 1, :, here] = (hold_v[which, 1, :, here] + tile_v[0:quarter, here].astype(F)).astype(B)
            return carry

        lax.fori_loop(0, blocks, one, 0)
        e_copy(which).start()

    def gather_own(which):
        x_copy(which, 0).wait_recv()
        read_stage(x_recv.at[which, 0])

        def one(block, carry):
            here = step(block, CHUNK)
            hold_v[which, 0, :, here] += tile_v[0:quarter, here].astype(F)
            return carry

        lax.fori_loop(0, blocks, one, 0)

    def spot(c, s):
        return pl.ds(pl.multiple_of(c * tall + s * quarter, quarter), quarter)

    def position_of(block, shifted=False):
        result = 0
        for level, bit in enumerate([PAIR] + spread):
            mine = bit_of(me, bit)
            if shifted and bit == PAIR:
                mine = 1 - mine
            result = result + (1 << level) * ((1 - mine) if block & bit else mine)
        return result

    def finish(which, out_ref):
        if len(sent_tiles) == 4:
            sent_tiles.append(None)
            for block in range(blocks):
                c_copy(*sent_tiles[3], block).wait_send()
        gather_own(which)
        e_copy(which).wait_recv()
        copies = [
            pltpu.make_async_copy(e_recv.at[which], tile_v.at[pl.ds(0, quarter)], load_sem.at[6]),
            pltpu.make_async_copy(x_ref.at[spot(core, side)], tile_v.at[pl.ds(quarter, quarter)], load_sem.at[7]),
        ]
        if which == 0:
            copies.append(pltpu.make_async_copy(g_ref.at[spot(core, side)], x_send.at[0, 0], load_sem.at[8]))
            x_copy(0, 0).wait_send()
        for copy in copies:
            copy.start()
        for copy in copies:
            copy.wait()
        here = pl.ds(which * quarter, quarter)
        if which == 0:
            total_u, total_un = 0.0, 0.0
            mean, inverse = stats(tile_v[quarter:].astype(F))
            for block in range(groups):
                mine = hold_v[0, 0, :, step(position_of(block), part)]
                theirs = tile_v[0:quarter, step(position_of(block, True), part)].astype(F)
                blend = mine + theirs
                normed = (tile_v[quarter:, block * part : (block + 1) * part].astype(F) - mean) * inverse
                hold_v[0, 1, :, block * part : (block + 1) * part] = blend
                total_u = total_u + jnp.sum(blend, axis=1, keepdims=True)
                total_un = total_un + jnp.sum(blend * normed, axis=1, keepdims=True)
            mean_u, mean_un = total_u * (1.0 / width), total_un * (1.0 / width)
            for block in range(groups):
                at = slice(block * part, (block + 1) * part)
                normed = (tile_v[quarter:, at].astype(F) - mean) * inverse
                inner = (hold_v[0, 1, :, at] - mean_u - normed * mean_un) * inverse
                c_send[here, at] = (x_send[0, 0, :, at].astype(F) + inner).astype(B)
        else:
            for block in range(groups):
                at = slice(block * part, (block + 1) * part)
                mine = hold_v[1, 0, :, step(position_of(block), part)]
                theirs = tile_v[0:quarter, step(position_of(block, True), part)].astype(F)
                bias = vec_ref[4:5, at] + vec_ref[5:6, at]
                c_send[here, at] = (tile_v[quarter:, at].astype(F) + (mine + theirs) + bias).astype(B)
        first = remote(
            c_send.at[here], out_ref.at[spot(core, side)], fs_sem.at[which, 0], fr_sem.at[which, 0], "tensor", side_to
        )
        second = remote(
            c_send.at[here], out_ref.at[spot(core, side)], fs_sem.at[which, 1], fr_sem.at[which, 1], "tensor", core_to
        )
        own = pltpu.make_async_copy(c_send.at[here], out_ref.at[spot(core, side)], out_sem.at[3 + which])
        for copy in (first, second, own):
            copy.start()
        return first, second, own

    def finish_end(which, out_ref, copies):
        first, second, own = copies
        first.wait_recv()
        third = remote(
            out_ref.at[spot(core, 1 - side)],
            out_ref.at[spot(core, 1 - side)],
            fs_sem.at[which, 2],
            fr_sem.at[which, 2],
            "tensor",
            core_to,
        )
        third.start()
        return [first.wait_send, second.wait, third.wait, own.wait]

    tile_of = ((blend_begin, blend_block), (branch_begin, branch_block))
    outs, finished, ends = (input_grad, block_out), {}, []

    def do_product(group, sent):
        columns, right = ((mlp_in, pre_v), (g_rel, act_v))[group - 1]
        if group == 2:
            need(3)
        if group == 1 and not sent:
            for copy in emitted[(0, 0)]:
                copy.wait()
        product(columns, right, group, (7, 6, 5, 4) if sent else (3, 2, 1, 0), sent, 2 if sent and group == 1 else None)

    def do_finish(which):
        finished[which] = finish(which, outs[which])

    def do_end(which):
        ends.extend(finish_end(which, outs[which], finished[which]))

    stages = {
        "pre": pre_tiles,
        "st": send_tile,
        "kt": keep_tile,
        "ps": lambda group: do_product(group, True),
        "pk": lambda group: do_product(group, False),
        "yf": y_far,
        "yn": y_near,
        "po": pass_on,
        "zl": z_last,
        "es": e_start,
        "fin": do_finish,
        "fe": do_end,
        "fa": emit_far,
        "sb": small_begin,
        "se": small_end,
    }
    for name, *numbers in SCHEDULE:
        stages[name](*numbers)
    small_out[...] = small_v[...]
    for end in ends:
        end()
    for group in range(3):
        if group:
            p_copy(group).wait_send()
            for position in (2, 3):
                z_copy(group, position)[0].wait_send()
        for position in range(4):
            if group != 2:
                y_copy(group, position).wait_send()
        for kind in range(2):
            if group or kind:
                for copy in emitted[(group, kind)]:
                    copy.wait()

        @pl.when(inner)
        def _():
            for number in range(3):
                forward(group, number)[1].wait_send()

    for which in range(2):
        e_copy(which).wait_send()
        if which:
            x_copy(which, 0).wait_send()


def body_narrow(
    tokens,
    segment_ids,
    out_grad,
    attn_norm_gain,
    attn_norm_bias,
    mlp_norm_gain,
    mlp_norm_bias,
    qkv_weight,
    qv_bias,
    key_bias,
    dense_weight,
    dense_bias,
    up_weight,
    up_bias,
    down_weight,
    down_bias,
    *,
    groups,
    ways,
):
    length, width = tokens.shape[1:]
    heads, size = qkv_weight.shape[1] // 2, qkv_weight.shape[3]
    part = width // groups
    me = lax.axis_index("dp")
    half = (me // PAIR) % 2
    place = lax.axis_index("tensor")
    core, side = place % 2, place // 2
    spread = [bit for bit in (1 << k for k in reversed(range(groups.bit_length() - 1))) if bit != PAIR]

    def swap(array, bit):
        return lax.ppermute(array, "dp", [(i, i ^ bit) for i in range(groups)])

    def cross(array, bit):
        return lax.ppermute(array, "tensor", [(i, i ^ bit) for i in range(ways)])

    def pick(array, index, axis, count=2):
        rows = array.shape[axis] // count
        return lax.dynamic_slice_in_dim(array, index * rows, rows, axis)

    def join(mine, theirs, index, axis):
        pair = jnp.concatenate([mine, theirs], axis=axis)
        turned = jnp.concatenate([theirs, mine], axis=axis)
        return jnp.where(index == 0, pair, turned)

    order = [0, PAIR]
    for bit in spread:
        order = order + [mask | bit for mask in order]
    inverse = [order.index(mask) for mask in range(groups)]

    def arranged(array):
        return jnp.concatenate(
            [lax.dynamic_slice_in_dim(array, (mask ^ me) * part, part, array.ndim - 1) for mask in order], axis=-1
        )

    def natural(array):
        table = jnp.asarray(inverse, jnp.int32)
        return jnp.concatenate(
            [lax.dynamic_slice_in_dim(array, table[block ^ me] * part, part, array.ndim - 1) for block in range(groups)],
            axis=-1,
        )

    def gather(shard, halves_axis, axis):
        shard = shard.astype(B)
        mine, theirs = pick(shard, half, halves_axis), pick(shard, 1 - half, halves_axis)
        pieces = [jnp.concatenate([mine, swap(theirs, PAIR)], axis=axis)]
        for bit in spread:
            pieces = pieces + [swap(piece, bit) for piece in pieces]
        return jnp.concatenate(pieces, axis=axis)

    def scatter(product, axis, halves_axis):
        count = groups // 2
        sent = swap(product(count, groups, B), spread[-1])
        held = product(0, count, F) + sent.astype(F)
        for bit in reversed(spread[:-1]):
            keep, send = jnp.split(held, 2, axis=axis)
            held = keep + swap(send.astype(B), bit).astype(F)
        keep, send = jnp.split(held, 2, axis=axis)
        return join(keep, swap(send, PAIR), half, halves_axis)

    def share_rows(rows):
        rows = join(rows, cross(rows, 2), side, 0)
        return join(rows, cross(rows, 1), core, 0)

    def own_rows(array, axis):
        return pick(pick(array, core, axis), side, axis)

    def partner_rows(array):
        return share_rows(swap(own_rows(array, 0), PAIR))

    def total_rows(partial):
        held = pick(partial, core, 1).astype(F) + cross(pick(partial, 1 - core, 1), 1).astype(F)
        held = pick(held, side, 1) + cross(pick(held, 1 - side, 1).astype(B), 2).astype(F)
        sent = swap(held[1].astype(B), PAIR).astype(F)
        rows = sent.shape[0]
        sent = jnp.flip(sent.reshape(rows, groups // 2, 2, part), axis=2).reshape(rows, width)
        return held[0] + sent

    own_x, own_g = tokens[0], out_grad[0]
    w_up = gather(up_weight, 1, 0)
    x_other = partner_rows(own_x)
    w_down = gather(down_weight, 0, 1)
    g_other = partner_rows(own_g)
    w_qkv = gather(qkv_weight.reshape(part, 2, -1), 1, 0).reshape(width, -1)
    w_dense = gather(dense_weight.reshape(2 * heads * size, part), 0, 1)

    x_pair = arranged(jnp.concatenate([own_x, x_other], axis=0))
    g_pair = arranged(jnp.concatenate([own_g, g_other], axis=0))
    gains = [arranged(v) for v in (attn_norm_gain, attn_norm_bias, mlp_norm_gain, mlp_norm_bias)]

    def hat(rows):
        rows = rows.astype(F)
        center = rows - jnp.mean(rows, axis=-1, keepdims=True)
        inverse_dev = lax.rsqrt(jnp.mean(center * center, axis=-1, keepdims=True) + 1e-05)
        return center * inverse_dev, inverse_dev

    normed, _ = hat(x_pair)
    attn_in = (normed * gains[0] + gains[1]).astype(B)
    mlp_in = (normed * gains[2] + gains[3]).astype(B)

    up_here = pick(up_bias, half, 0)
    up_pre = dot(mlp_in, w_up, ((1,), (0,)), F) + up_here
    activation = jax.nn.gelu(up_pre, approximate=False).astype(B)
    middle = width // 2

    def columns(array, low, high):
        return array[:, low * part : high * part]

    down_shard = scatter(lambda low, high, kind: dot(activation, columns(g_pair, low, high), ((0,), (0,)), kind), 1, 0)
    pre_grad = (dot(g_pair, w_down, ((1,), (1,)), F) * gelu_slope(up_pre)).astype(B)
    up_shard = scatter(lambda low, high, kind: dot(columns(mlp_in, low, high), pre_grad, ((0,), (0,)), kind), 0, 1)
    up_bias_sum = jnp.sum(pre_grad.astype(F), axis=0)

    seg_other = swap(segment_ids[0], PAIR)
    seg = jnp.stack([segment_ids[0], seg_other])
    seg_col, seg_row = seg[:, :, None], seg[:, None, :]
    qv_here, key_here = pick(qv_bias, half, 0), pick(key_bias, half, 0)
    key_full = jnp.concatenate([key_here, jnp.zeros((heads, size - ROT), F)], axis=1)
    offsets = jnp.stack([qv_here[:, 0], key_full, qv_here[:, 1]], axis=1).reshape(heads, 1, 3 * size)
    mixed = dot(attn_in, w_qkv, ((1,), (0,)), F).reshape(2, length, heads, 3 * size)
    tables = rope_tables(length)
    table_specs = [shared(length, 128)] * 3
    seg_specs = [per_seq(length, 1), per_seq(1, length)]
    context_grad = dot(g_pair, w_dense, ((1,), (1,)), B).reshape(2, length, heads, size)
    contexts, mixed_grads, mixed_sums = [], [], []
    head_shape = jax.ShapeDtypeStruct((2, length, size), B)
    for head in range(heads):
        q, k, v, context, lse = pl.pallas_call(
            attn_forward,
            grid=(2,),
            in_specs=[per_seq(length, 3 * size), shared(1, 3 * size)] + table_specs + seg_specs,
            out_specs=[per_seq(length, size)] * 4 + [per_seq(length, 1)],
            out_shape=[head_shape] * 4 + [jax.ShapeDtypeStruct((2, length, 1), F)],
            name="attn_forward",
        )(mixed[:, :, head], offsets[head], *tables, seg_col, seg_row)
        mixed_grad, mixed_sum = pl.pallas_call(
            attn_backward,
            grid=(2,),
            in_specs=[per_seq(length, size)] * 4 + [per_seq(length, 1)] + table_specs + seg_specs,
            out_specs=[per_seq(length, 3 * size), per_seq(1, 3 * size)],
            out_shape=[
                jax.ShapeDtypeStruct((2, length, 3 * size), B),
                jax.ShapeDtypeStruct((2, 1, 3 * size), F),
            ],
            scratch_shapes=[pltpu.VMEM((length, size), F)] * 3,
            name="attn_backward",
        )(q, k, v, context_grad[:, :, head], lse, *tables, seg_col, seg_row)
        contexts.append(context.reshape(2 * length, size))
        mixed_grads.append(mixed_grad.reshape(2 * length, 3 * size))
        mixed_sums.append(jnp.sum(mixed_sum, axis=(0, 1)))
    context = jnp.concatenate(contexts, axis=1)
    mixed_grad = jnp.concatenate(mixed_grads, axis=1)
    mixed_sum = jnp.stack(mixed_sums).reshape(heads, 3, size)

    qkv_shard = scatter(lambda low, high, kind: dot(columns(attn_in, low, high), mixed_grad, ((0,), (0,)), kind), 0, 1)
    dense_shard = scatter(lambda low, high, kind: dot(context, columns(g_pair, low, high), ((0,), (0,)), kind), 1, 0)

    branch = dot(context, w_dense, ((1,), (0,)), F) + dot(activation, w_down, ((1,), (0,)), F)
    branch_rows = total_rows(branch.astype(B).reshape(2, length, width))
    x_rows, g_rows = own_rows(x_pair[:length], 0), own_rows(g_pair[:length], 0)
    out_rows = (x_rows.astype(F) + branch_rows + arranged(dense_bias) + arranged(down_bias)).astype(B)
    block_out = share_rows(natural(out_rows))

    attn_in_grad = dot(mixed_grad, w_qkv, ((1,), (1,)), F)
    mlp_in_grad = dot(pre_grad, w_up, ((1,), (1,)), F)
    blend = (attn_in_grad * gains[0] + mlp_in_grad * gains[2]).astype(B)
    blend_rows = total_rows(blend.reshape(2, length, width))
    hat_rows, inverse_rows = hat(x_rows)
    inner = (
        blend_rows
        - jnp.mean(blend_rows, axis=-1, keepdims=True)
        - hat_rows * jnp.mean(blend_rows * hat_rows, axis=-1, keepdims=True)
    )
    input_grad = share_rows(natural((g_rows.astype(F) + inner * inverse_rows).astype(B)))

    norm_sums = natural(
        jnp.stack(
            [
                jnp.sum(attn_in_grad * normed, axis=0),
                jnp.sum(attn_in_grad, axis=0),
                jnp.sum(mlp_in_grad * normed, axis=0),
                jnp.sum(mlp_in_grad, axis=0),
            ]
        )
    ).reshape(-1)
    bias_sum = jnp.sum(own_g.astype(F), axis=0)

    def slotted(array):
        zero = jnp.zeros_like(array)
        return join(array, zero, half, 0)

    small = [norm_sums, bias_sum, slotted(up_bias_sum), slotted(mixed_sum).reshape(-1)]
    sizes = [s.shape[0] for s in small]
    flat = jnp.concatenate(small)
    for bit in [1 << k for k in range(groups.bit_length() - 1)]:
        flat = flat + swap(flat, bit)
    ends = [sum(sizes[: i + 1]) for i in range(len(sizes))]
    norms = flat[: ends[0]]
    for bit in [1 << k for k in range(ways.bit_length() - 1)]:
        norms = norms + cross(norms, bit)
    norms = norms.reshape(4, width)
    bias_grad = flat[ends[0] : ends[1]]
    up_bias_grad = flat[ends[1] : ends[2]]
    mixed_bias = flat[ends[2] :].reshape(2 * heads, 3, size)
    qv_grad = jnp.stack([mixed_bias[:, 0], mixed_bias[:, 2]], axis=1)
    key_bias_grad = mixed_bias[:, 1, :ROT]

    return (
        block_out[None],
        input_grad[None],
        norms[0],
        norms[1],
        norms[2],
        norms[3],
        qkv_shard.reshape(qkv_weight.shape),
        qv_grad,
        key_bias_grad,
        dense_shard.reshape(dense_weight.shape),
        bias_grad,
        up_shard,
        up_bias_grad,
        down_shard,
        bias_grad,
    )


def body(
    tokens,
    segment_ids,
    out_grad,
    attn_norm_gain,
    attn_norm_bias,
    mlp_norm_gain,
    mlp_norm_bias,
    qkv_weight,
    qv_bias,
    key_bias,
    dense_weight,
    dense_bias,
    up_weight,
    up_bias,
    down_weight,
    down_bias,
    *,
    groups,
    ways,
):
    length, width = tokens.shape[1:]
    heads, size = qkv_weight.shape[1] // 2, qkv_weight.shape[3]
    assert heads == 1 and ways == 4
    part = width // groups
    hidden = up_weight.shape[1] // 2
    count = 2 * length
    me = lax.axis_index("dp")
    half = (me // PAIR) % 2
    shape = jax.ShapeDtypeStruct

    def pick(array, index, axis):
        rows = array.shape[axis] // 2
        return lax.dynamic_slice_in_dim(array, index * rows, rows, axis)

    vectors = jnp.stack([attn_norm_gain, attn_norm_bias, mlp_norm_gain, mlp_norm_bias, dense_bias, down_bias])
    own_x, own_g = tokens[0], out_grad[0]

    qv_here, key_here = pick(qv_bias, half, 0), pick(key_bias, half, 0)
    key_full = jnp.concatenate([key_here, jnp.zeros((heads, size - ROT), F)], axis=1)
    offsets = jnp.stack([qv_here[:, 0], key_full, qv_here[:, 1]], axis=1).reshape(1, 3 * size)
    tables = rope_tables(length)
    up_here = pick(up_bias, half, 0)[None]
    columns = hidden
    half_width = width // 2
    vmem, hbm = pl.BlockSpec(memory_space=pltpu.VMEM), pl.BlockSpec(memory_space=pl.ANY)
    (
        weights,
        _,
        _,
        _,
        x_pair,
        g_pair,
        mlp_in,
        mixed_grad,
        context,
        activation,
        slope,
        attn_send,
        attn_keep,
        mixed_sum,
        bias_sum,
    ) = pl.pallas_call(
        functools.partial(gather_kernel, groups),
        in_specs=[hbm] * 4 + [vmem] + [hbm] * 2 + [vmem] * 6,
        out_specs=[hbm] * 13 + [vmem] * 2,
        out_shape=[
            shape((3, width, columns), B),
            shape((3, 3 * part, columns), B),
            shape((length, width), B),
            shape((length, width), B),
            shape((count, width), B),
            shape((count, width), B),
            shape((count, width), B),
            shape((count, 3 * size), B),
            shape((count, size), B),
            shape((count, hidden), B),
            shape((count, hidden), F),
            shape((half_width, columns), B),
            shape((half_width, columns), F),
            shape((1, 3 * size), F),
            shape((1, width), F),
        ],
        scratch_shapes=[
            pltpu.VMEM((3, width, columns), B),
            pltpu.VMEM((2, CHUNK, width), B),
            pltpu.VMEM((2, CHUNK, width), B),
            pltpu.VMEM((length, width), B),
            pltpu.VMEM((length, width), B),
            pltpu.VMEM((count, width), B),
            pltpu.VMEM((length, width), B),
            pltpu.VMEM((width, columns), F),
            pltpu.VMEM((half_width, columns), B),
            pltpu.VMEM((length, size), B),
            pltpu.VMEM((length, size), B),
            pltpu.VMEM((length, size), B),
            pltpu.VMEM((length, size), B),
            pltpu.VMEM((length, size), B),
            pltpu.VMEM((length, 3 * size), B),
            pltpu.VMEM((length, size), F),
            pltpu.VMEM((length, size), F),
            pltpu.VMEM((2, CHUNK, hidden), B),
            pltpu.VMEM((2, CHUNK, hidden), F),
            pltpu.VMEM((3, part, columns), B),
            pltpu.VMEM((1, length), jnp.int32),
            pltpu.VMEM((length, 8), F),
            pltpu.SemaphoreType.DMA((27,)),
            pltpu.SemaphoreType.DMA((27,)),
            pltpu.SemaphoreType.DMA((3, 6)),
            pltpu.SemaphoreType.DMA((3,)),
            pltpu.SemaphoreType.DMA((3,)),
            pltpu.SemaphoreType.DMA((3, 3)),
            pltpu.SemaphoreType.DMA((2, 2)),
            pltpu.SemaphoreType.DMA((2, 3 + hidden // part)),
            pltpu.SemaphoreType.DMA((2,)),
            pltpu.SemaphoreType.DMA((2, 2)),
            pltpu.SemaphoreType.DMA((2, 5)),
            pltpu.SemaphoreType.DMA((2, 2)),
            pltpu.SemaphoreType.DMA((5,)),
        ],
        compiler_params=pltpu.CompilerParams(
            collective_id=0, has_side_effects=True, vmem_limit_bytes=67043328
        ),
        cost_estimate=pl.CostEstimate(flops=40 * 10**9, bytes_accessed=10**8, transcendentals=10**7),
        name="gather",
    )(
        qkv_weight.reshape(part, 6 * size),
        dense_weight,
        up_weight,
        down_weight,
        segment_ids,
        own_x,
        own_g,
        vectors,
        up_here,
        offsets,
        *tables,
    )
    quarter = length // 4
    tall, blocks = 2 * quarter, width // CHUNK
    dma = pltpu.SemaphoreType.DMA
    block_out, input_grad, qkv_shard, dense_shard, up_shard, down_shard, _, _, _, _, _, _, _, _, small = pl.pallas_call(
        functools.partial(scatter_kernel, groups),
        in_specs=[hbm] * 12 + [vmem] * 3,
        out_specs=[hbm] * 14 + [vmem],
        out_shape=[
            shape((length, width), B),
            shape((length, width), B),
            shape((part, 6 * size), F),
            shape(dense_weight.shape, F),
            shape(up_weight.shape, F),
            shape(down_weight.shape, F),
            shape((3, part, columns), B),
            shape((3, part, columns), B),
            shape((3, half_width, columns), B),
            shape((3, half_width // 2, columns), B),
            shape((3, 3 * part, columns), B),
            shape((2, 2, tall, width), B),
            shape((2, 2, quarter, width), B),
            shape((2, quarter, width), B),
            shape((8, width), F),
        ],
        scratch_shapes=[
            pltpu.VMEM((3, width, columns), B),
            pltpu.VMEM((count, hidden), B),
            pltpu.VMEM((count, hidden), B),
            pltpu.VMEM((tall, width), B),
            pltpu.VMEM((2, count, part), B),
            pltpu.VMEM((2, CHUNK, hidden), F),
            pltpu.VMEM((tall, 3 * size), B),
            pltpu.VMEM((count, size), B),
            pltpu.VMEM((2, half_width, columns), F),
            pltpu.VMEM((half_width, columns), B),
            pltpu.VMEM((2, half_width // 2, columns), B),
            pltpu.VMEM((2, part, columns), B),
            pltpu.VMEM((part, columns), B),
            pltpu.VMEM((tall, width), B),
            pltpu.VMEM((2, tall, CHUNK), B),
            pltpu.VMEM((tall, CHUNK), F),
            pltpu.VMEM((2, 2, quarter, width), B),
            pltpu.VMEM((2, 2, quarter, width), F),
            pltpu.VMEM((tall, 128), F),
            pltpu.VMEM((tall, 128), F),
            pltpu.VMEM((1, hidden), F),
            pltpu.VMEM((8, width), F),
            pltpu.VMEM((5, 8, width), F),
            dma((9,)),
            dma((5, 2)),
            dma((3, 4)),
            dma((3, 4)),
            dma((3, 2)),
            dma((3, 2)),
            dma((3, 3)),
            dma((3, 3)),
            dma((3,)),
            dma((3,)),
            dma((3,)),
            dma((2, 2, blocks)),
            dma((2, 2, blocks)),
            dma((2, 2)),
            dma((2, 2)),
            dma((2,)),
            dma((2,)),
            dma((2, 3)),
            dma((2, 3)),
            dma((3, 2, hidden // part)),
            dma((5,)),
            dma((5,)),
            dma((5,)),
        ],
        compiler_params=pltpu.CompilerParams(
            collective_id=1, has_side_effects=True, vmem_limit_bytes=67043328
        ),
        cost_estimate=pl.CostEstimate(flops=60 * 10**9, bytes_accessed=10**8, transcendentals=10**7),
        name="scatter",
    )(
        attn_send,
        attn_keep,
        weights,
        x_pair,
        g_pair,
        mlp_in,
        mixed_grad,
        context,
        activation,
        slope,
        own_x,
        own_g,
        vectors,
        mixed_sum,
        bias_sum,
    )

    norms, bias_grad, up_bias_grad = small[0:4], small[4], small[5]
    mixed_bias = small[6].reshape(2, width // 2)[:, : 3 * size].reshape(2, 3, size)
    qv_grad = jnp.stack([mixed_bias[:, 0], mixed_bias[:, 2]], axis=1)
    key_bias_grad = mixed_bias[:, 1, :ROT]

    return (
        block_out[None],
        input_grad[None],
        norms[0],
        norms[1],
        norms[2],
        norms[3],
        qkv_shard.reshape(qkv_weight.shape),
        qv_grad,
        key_bias_grad,
        dense_shard,
        bias_grad,
        up_shard,
        up_bias_grad,
        down_shard,
        bias_grad,
    )


def solution(mesh):
    placed = (
        P("dp", None, None),
        P("dp", None),
        P("dp", None, None),
        P(),
        P(),
        P(),
        P(),
        P("dp", "tensor", None, None),
        P("tensor", None, None),
        P("tensor", None),
        P("tensor", None, "dp"),
        P(),
        P("dp", "tensor"),
        P("tensor"),
        P("tensor", "dp"),
        P(),
    )

    def whole(*arrays):
        groups, ways = mesh.shape["dp"], mesh.shape["tensor"]
        part = arrays[0].shape[2] // groups
        chosen = body_narrow if part % 128 or groups != 8 else body
        return chosen(*arrays, groups=groups, ways=ways)

    return jax.shard_map(
        whole,
        mesh=mesh,
        in_specs=placed,
        out_specs=(
            P("dp", None, None),
            P("dp", None, None),
            P(),
            P(),
            P(),
            P(),
            P("dp", "tensor", None, None),
            P("tensor", None, None),
            P("tensor", None),
            P("tensor", None, "dp"),
            P(),
            P("dp", "tensor"),
            P("tensor"),
            P("tensor", "dp"),
            P(),
        ),
        check_vma=False,
    )
```

```python
import functools

import jax
import jax.numpy as jnp
from jax import lax
from jax.experimental import pallas as pl
from jax.experimental.pallas import tpu as pltpu
from jax.sharding import PartitionSpec as P

ROT = 64
PAIR = 2
QBLOCK = 256
DOC_MAX = 512
F = jnp.float32
B = jnp.bfloat16


def dot(left, right, dims, kind):
    return lax.dot_general(left, right, (dims, ((), ())), preferred_element_type=F).astype(kind)


def gelu_slope(pre_act):
    cumulative = 0.5 * (1.0 + lax.erf(pre_act * 0.7071067811865476))
    density = jnp.exp(-0.5 * pre_act * pre_act) * 0.3989422804014327
    return cumulative + pre_act * density


def rope_tables(length):
    half = ROT // 2
    frequency = 10000.0 ** (-(jnp.arange(half, dtype=F) * 2.0) / ROT)
    angles = jnp.arange(length, dtype=F)[:, None] * frequency[None, :]
    cosine, sine = jnp.cos(angles), jnp.sin(angles)
    flat = jnp.zeros((length, 128 - ROT), F)
    zero = jnp.zeros_like(sine)
    return (
        jnp.concatenate([cosine, cosine, flat + 1.0], axis=1),
        jnp.concatenate([-sine, zero, flat], axis=1),
        jnp.concatenate([zero, sine, flat], axis=1),
    )


def turn(rows, cosine, from_above, from_below):
    head = rows[:, :128]
    above = pltpu.roll(head, 128 - ROT // 2, 1)
    below = pltpu.roll(head, ROT // 2, 1)
    turned = head * cosine + above * from_above + below * from_below
    return jnp.concatenate([turned, rows[:, 128:]], axis=1)


def block_mask(seg_col_ref, seg_row_ref, first, low, high):
    rows = first + lax.broadcasted_iota(jnp.int32, (QBLOCK, high - low), 0)
    columns = low + lax.broadcasted_iota(jnp.int32, (QBLOCK, high - low), 1)
    same = seg_col_ref[0, first : first + QBLOCK, :] == seg_row_ref[0, :, low:high]
    return (columns <= rows) & same


def key_range(first):
    return max(0, first - DOC_MAX), first + QBLOCK


def attn_forward(mixed_ref, bias_ref, cos_ref, up_ref, down_ref, col_ref, row_ref, q_ref, k_ref, v_ref, ctx_ref, lse_ref):
    size = q_ref.shape[2]
    length = q_ref.shape[1]
    scale = size ** (-0.5)
    tables = (cos_ref[...], up_ref[...], down_ref[...])
    q_ref[0] = turn(mixed_ref[0, :, :size] + bias_ref[:, :size], *tables).astype(B)
    k_ref[0] = turn(mixed_ref[0, :, size : 2 * size] + bias_ref[:, size : 2 * size], *tables).astype(B)
    v_ref[0] = (mixed_ref[0, :, 2 * size :] + bias_ref[:, 2 * size :]).astype(B)
    for first in range(0, length, QBLOCK):
        low, high = key_range(first)
        scores = dot(q_ref[0, first : first + QBLOCK], k_ref[0, low:high], ((1,), (1,)), F) * scale
        scores = jnp.where(block_mask(col_ref, row_ref, first, low, high), scores, -1e30)
        row_max = jnp.max(scores, axis=1, keepdims=True)
        expo = jnp.exp(scores - row_max)
        total = jnp.sum(expo, axis=1, keepdims=True)
        probs = (expo / total).astype(B)
        ctx_ref[0, first : first + QBLOCK] = dot(probs, v_ref[0, low:high], ((1,), (0,)), B)
        lse_ref[0, first : first + QBLOCK] = row_max + jnp.log(total)


def attn_backward(q_ref, k_ref, v_ref, grad_ref, lse_ref, cos_ref, up_ref, down_ref, col_ref, row_ref, mixed_ref, sum_ref, q_acc, k_acc, v_acc):
    size = q_ref.shape[2]
    length = q_ref.shape[1]
    scale = size ** (-0.5)
    k_acc[...] = jnp.zeros_like(k_acc)
    v_acc[...] = jnp.zeros_like(v_acc)
    for first in range(0, length, QBLOCK):
        low, high = key_range(first)
        here = slice(first, first + QBLOCK)
        scores = dot(q_ref[0, here], k_ref[0, low:high], ((1,), (1,)), F) * scale
        scores = jnp.where(block_mask(col_ref, row_ref, first, low, high), scores, -1e30)
        probs = jnp.exp(scores - lse_ref[0, here])
        v_acc[low:high] += dot(probs.astype(B), grad_ref[0, here], ((0,), (0,)), F)
        prob_grad = dot(grad_ref[0, here], v_ref[0, low:high], ((1,), (1,)), F)
        centred = jnp.sum(probs * prob_grad, axis=1, keepdims=True)
        score_grad = (probs * (prob_grad - centred)).astype(B)
        q_acc[here] = dot(score_grad, k_ref[0, low:high], ((1,), (0,)), F) * scale
        k_acc[low:high] += dot(score_grad, q_ref[0, here], ((0,), (0,)), F) * scale
    tables = (cos_ref[...], -up_ref[...], -down_ref[...])
    q_grad = turn(q_acc[...], *tables).astype(B)
    k_grad = turn(k_acc[...], *tables).astype(B)
    v_grad = v_acc[...].astype(B)
    for number, part in enumerate((q_grad, k_grad, v_grad)):
        mixed_ref[0, :, number * size : (number + 1) * size] = part
        sum_ref[0, :, number * size : (number + 1) * size] = jnp.sum(part.astype(F), axis=0, keepdims=True)


def per_seq(rows, columns):
    return pl.BlockSpec((1, rows, columns), lambda seq, *_: (seq, 0, 0))


def shared(rows, columns):
    return pl.BlockSpec((rows, columns), lambda *_: (0, 0))


MESH = pl.DeviceIdType.MESH
CHUNK = 256


def bit_of(index, bit):
    return lax.rem(lax.div(index, bit), 2)


def flip(index, mask):
    bit = 1
    while bit <= mask:
        if mask & bit:
            index = index + bit * (1 - 2 * bit_of(index, bit))
        bit *= 2
    return index


def block_order(groups):
    spread = [bit for bit in (1 << k for k in reversed(range(groups.bit_length() - 1))) if bit != PAIR]
    order = [0, PAIR]
    for bit in spread:
        order = order + [mask | bit for mask in order]
    return spread, order


def stats(rows):
    mean = jnp.mean(rows, axis=1, keepdims=True)
    center = rows - mean
    return mean, lax.rsqrt(jnp.mean(center * center, axis=1, keepdims=True) + 1e-05)


def greet(partners):
    barrier = pltpu.get_barrier_semaphore()
    for axis, index in partners:
        pl.semaphore_signal(barrier, inc=1, device_id={axis: index}, device_id_type=MESH)
    pl.semaphore_wait(barrier, len(partners))


STEPS_ONE = (
    ("x1", "i"),
    ("sh", 0, 0),
    ("sh", 0, 1),
    ("pu", 0, "o"),
    ("pu", 0, "i"),
    ("sh", 1, 1),
    ("yo", 0, 0),
    ("gst", 0),
    ("sh", 1, 0),
    ("hd", 0, "o"),
    ("x1", "o"),
    ("yo", 0, 1),
    ("re", 0),
    ("hd", 0, "i"),
    ("gst", 1),
    ("sh", 2, 0),
    ("gpo", 0, 2),
    ("gpo", 0, 0),
    ("pu", 1, "o"),
    ("pu", 1, "i"),
    ("sh", 2, 1),
    ("yo", 0, 3),
    ("x2",),
    ("yo", 2, 0),
    ("N", 0),
    ("g1", "o"),
    ("gpo", 0, 1),
    ("yo", 0, 2),
    ("yo", 1, 0),
    ("hd", 1, "i"),
    ("yo", 1, 1),
    ("g1", "i"),
    ("hd", 2, "o"),
    ("G", 0),
    ("re", 1),
    ("x3",),
    ("hd", 2, "i"),
    ("hd", 1, "o"),
    ("PJ", 0),
    ("CG", 0),
    ("g2",),
    ("pu", 2, "o"),
    ("AT", 0),
    ("gpo", 1, 2),
    ("GR", 0, 0),
    ("gpo", 2, 0),
    ("yo", 1, 3),
    ("pu", 2, "i"),
    ("gpo", 1, 0),
    ("gpo", 1, 1),
    ("GR", 0, 1),
    ("N", 1),
    ("yo", 2, 1),
    ("g3",),
    ("gpo", 2, 1),
    ("re", 2),
    ("gst", 2),
    ("PJ", 1),
    ("G", 1),
    ("CG", 1),
    ("yo", 1, 2),
    ("AT", 1),
    ("gpo", 2, 2),
    ("GR", 1, 0),
    ("yo", 2, 2),
    ("GR", 1, 1),
    ("UP", 0),
    ("yo", 2, 3),
    ("UP", 1),
)

STEPS_TWO = (
    ("ps", 2),
    ("st", 1, 1),
    ("pre", 1),
    ("yf", 0, 3),
    ("kt", 1, 1),
    ("pk", 2),
    ("po", 0, 1),
    ("yf", 0, 2),
    ("st", 0, 1),
    ("yn", 0, 1),
    ("kt", 0, 1),
    ("es", 1),
    ("st", 1, 0),
    ("po", 0, 0),
    ("pre", 0),
    ("yf", 2, 3),
    ("yn", 0, 0),
    ("zl", 0, 1),
    ("kt", 1, 0),
    ("yf", 2, 2),
    ("po", 0, 2),
    ("st", 0, 0),
    ("kt", 0, 0),
    ("po", 2, 1),
    ("sb",),
    ("es", 0),
    ("ps", 1),
    ("se", 0),
    ("zl", 0, 0),
    ("fin", 1),
    ("po", 2, 0),
    ("pk", 1),
    ("yf", 1, 3),
    ("po", 2, 2),
    ("fin", 0),
    ("fa", 0),
    ("yf", 1, 2),
    ("yn", 2, 0),
    ("yn", 2, 1),
    ("zl", 2, 1),
    ("se", 1),
    ("po", 1, 1),
    ("po", 1, 2),
    ("po", 1, 0),
    ("fe", 1),
    ("se", 2),
    ("yn", 1, 1),
    ("yn", 1, 0),
    ("zl", 1, 1),
    ("fe", 0),
    ("se", 3),
    ("zl", 1, 0),
    ("fa", 2),
    ("zl", 2, 0),
    ("se", 4),
    ("fa", 1),
)


def gather_steps(
    groups,
    qkv_ref,
    dense_ref,
    up_ref,
    down_ref,
    seg_ref,
    x_ref,
    g_ref,
    vec_ref,
    up_bias_ref,
    offset_ref,
    tables_ref,
    w_relay,
    x_other,
    g_other,
    x_rel,
    g_rel,
    mlp_out,
    mixed_out,
    ctx_out,
    act_out,
    slope_out,
    send_out,
    keep_out,
    w,
    theirs_v,
    seg_v,
    sum_ref,
    bias_ref,
    send_sem,
    recv_sem,
    cross_sem,
    two_sem,
    three_sem,
    relay_sem,
    quarter_sem,
    shard_sem,
    seg_sem,
    load_sem,
    rel_sem,
    tile_sem,
    out_sem,
):
    length, width = x_ref.shape
    part = width // groups
    size = dense_ref.shape[1]
    quarter = length // 4
    me, place = lax.axis_index("dp"), lax.axis_index("tensor")
    core, side = lax.rem(place, 2), lax.div(place, 2)
    pair_to, side_to, core_to = flip(me, PAIR), flip(place, 2), flip(place, 1)
    spread, order = block_order(groups)
    half = bit_of(me, PAIR)
    hidden = act_out.shape[1]
    raw_x = attn_v = g_v = mlp_v = xr_v = grad_v = send_v = q_v = k_v = v_v = cg_v = ctx_v = mg_v = dk_v = dv_v = act_v = slope_v = col_v = tab_v = None

    def shards(owner, slot):
        at = pl.ds(pl.multiple_of(owner * 3 * size, 128), 3 * size)
        spots = [
            (qkv_ref.at[:, at], grad_v.at[pl.ds(slot * part, part), pl.ds(0, 3 * size)]),
            (dense_ref.at[owner], grad_v.at[pl.ds(2 * part, size), pl.ds(slot * part, part)]),
            (
                up_ref.at[:, pl.ds(pl.multiple_of(owner * hidden, hidden), hidden)],
                grad_v.at[pl.ds((3 + slot) * part, part)],
            ),
        ]
        for number in range(hidden // part):
            at = pl.ds(pl.multiple_of(owner * hidden + number * part, part), part)
            spots.append((down_ref.at[at], slope_v.at[slot, :, pl.ds(number * part, part)]))
        return [
            pltpu.make_async_copy(source, target, shard_sem.at[slot, number])
            for number, (source, target) in enumerate(spots)
        ]

    shard_copies = []

    def shard(group, slot):
        for copy in shard_copies[slot][(0, 2, 3)[group] : (2, 3, None)[group]]:
            copy.wait()

        def put(columns, value):
            if slot:
                theirs_v[group, :, columns] = value.astype(B)
            else:
                w[group, 0:part, columns] = value.astype(B)

        if group == 0:
            put(slice(0, 3 * size), grad_v[slot * part : (slot + 1) * part, : 3 * size])
            put(slice(3 * size, 4 * size), grad_v[2 * part : 2 * part + size, slot * part : (slot + 1) * part].T)
        elif group == 1:
            put(slice(0, hidden), grad_v[(3 + slot) * part : (4 + slot) * part])
        else:
            for number in range(hidden // part):
                at = slice(number * part, (number + 1) * part)
                put(at, slope_v[slot, :, at].T)

    across = PAIR | spread[0]
    inner = bit_of(me, PAIR) != bit_of(me, spread[0])
    outer = bit_of(me, PAIR) == bit_of(me, spread[0])
    copies = {}

    def remote(key, number, source, target, axis, index):
        copies[key] = pltpu.make_async_remote_copy(
            src_ref=source,
            dst_ref=target,
            send_sem=send_sem.at[number],
            recv_sem=recv_sem.at[number],
            device_id={axis: index},
            device_id_type=MESH,
        )
        copies[key].start()

    def rows(position):
        return pl.ds(position * part, part)

    def pair_up(group, here):
        copy = pltpu.make_async_remote_copy(
            src_ref=theirs_v.at[group],
            dst_ref=w.at[group, rows(1)],
            send_sem=send_sem.at[8 * group + 1],
            recv_sem=recv_sem.at[8 * group + 1],
            device_id={"dp": pair_to},
            device_id_type=MESH,
        )
        pl.when(here)(copy.start)

    def onward(group, position, level):
        source = w.at[group, rows(position)]
        far = position + (2 << level)
        remote(("w", far), 8 * group + far, source, w.at[group, rows(far)], "dp", flip(me, spread[level]))

    def partly(here, source, target, send, recv, to):
        copy = pltpu.make_async_remote_copy(
            src_ref=source,
            dst_ref=target,
            send_sem=send,
            recv_sem=recv,
            device_id={"dp": to},
            device_id_type=MESH,
        )
        pl.when(here)(copy.start)

    across_to = flip(me, across)

    def straight(group):
        partly(inner, theirs_v.at[group], w.at[group, rows(3)], cross_sem.at[group, 0], three_sem.at[group], across_to)

    def hand(group, here=None):
        source, sem = w.at[group, rows(0)], cross_sem.at[group, 1]
        if here is not inner:
            partly(outer, source, w_relay.at[group, rows(0)], sem, relay_sem.at[group, 0], pair_to)
        if here is not outer:
            partly(inner, source, w_relay.at[group, rows(1)], sem, relay_sem.at[group, 1], across_to)

    def relay(group):
        source = w.at[group, rows(1)]
        partly(
            inner, source, w_relay.at[group, rows(2)], cross_sem.at[group, 2], relay_sem.at[group, 2], across_to
        )

    def pass_on(group, *numbers):
        for number in numbers:
            source, target = w_relay.at[group, rows(number)], 3 if number == 2 else 2
            here = pltpu.make_async_remote_copy(
                src_ref=source,
                dst_ref=source,
                send_sem=relay_sem.at[group, number],
                recv_sem=relay_sem.at[group, number],
                device_id={"dp": pair_to},
                device_id_type=MESH,
            )
            pl.when(inner)(here.wait_recv)
            partly(
                inner,
                source,
                w.at[group, rows(target)],
                cross_sem.at[group, 3 + number],
                (three_sem if target == 3 else two_sem).at[group],
                across_to if number == 0 else pair_to,
            )

    def to_pair(key, source, target, here):
        if key not in quarters:
            quarters[key] = pltpu.make_async_remote_copy(
                src_ref=source,
                dst_ref=target,
                send_sem=quarter_sem.at[key, 0],
                recv_sem=quarter_sem.at[key, 1],
                device_id={"dp": pair_to},
                device_id_type=MESH,
            )
        pl.when(here)(quarters[key].start)

    quarters = {}
    arrived = set()

    def arrive(group, position):
        if (group, position) not in arrived:
            arrived.add((group, position))
            sem = {2: two_sem.at[group], 3: three_sem.at[group]}.get(position, recv_sem.at[8 * group + position])
            pltpu.make_async_remote_copy(
                src_ref=w.at[group, rows(position)],
                dst_ref=w.at[group, rows(position)],
                send_sem=sem,
                recv_sem=sem,
                device_id={"dp": pair_to},
                device_id_type=MESH,
            ).wait_recv()

    spot = pl.ds(pl.multiple_of(core * (2 * quarter) + side * quarter, quarter), quarter)
    pair_rows = pl.ds(pl.multiple_of(core * (2 * quarter), quarter), 2 * quarter)
    levels = len(spread)
    assert levels == 2

    def over_tiles(source, raw, number, work):
        def load(tile, slot):
            here = pl.ds(pl.multiple_of(tile * CHUNK, CHUNK), CHUNK)
            return pltpu.make_async_copy(source.at[here], raw.at[slot], load_sem.at[number, slot])

        load(0, 0).start()

        def one(tile, carry):
            slot = lax.rem(tile, 2)

            @pl.when(tile + 1 < length // CHUNK)
            def _():
                load(tile + 1, 1 - slot).start()

            load(tile, slot).wait()
            work(tile, slot)
            return carry

        lax.fori_loop(0, length // CHUNK, one, 0)

    outs = {}

    def leave(key, source, target, sem):
        outs[key] = pltpu.make_async_copy(source, target, sem)
        outs[key].start()

    def left(*keys):
        for key in keys:
            outs.pop(key).wait()

    def normalise(seq):
        if seq:
            copies["x3"].wait_recv()
            left(("x", 0))

        def work(tile, slot):
            here = pl.ds(pl.multiple_of(tile * CHUNK, CHUNK), CHUNK)
            both = pl.ds(pl.multiple_of(seq * length + tile * CHUNK, CHUNK), CHUNK)
            mean, inverse = stats(raw_x[slot].astype(F))
            for position, mask in enumerate(order):
                to = slice(position * part, (position + 1) * part)
                there = pl.ds(pl.multiple_of(flip(me, mask) * part, part), part)
                piece = raw_x[slot, :, there]
                normed = (piece.astype(F) - mean) * inverse
                attn_v[here, to] = (normed * vec_ref[0:1, there] + vec_ref[1:2, there]).astype(B)
                mlp_v[both, to] = (normed * vec_ref[2:3, there] + vec_ref[3:4, there]).astype(B)
                xr_v[here, to] = piece

        over_tiles(x_other if seq else x_ref, raw_x, 0, work)
        both = pl.ds(seq * length, length)
        leave(("x", seq), xr_v, x_rel.at[both], rel_sem.at[seq, 0])
        leave(("m", seq), mlp_v.at[both], mlp_out.at[both], rel_sem.at[seq, 2])

    def arrange_grad(seq):
        if seq:
            copies["g3"].wait_recv()
            left(("g", 0))
        else:
            bias_ref[...] = jnp.zeros_like(bias_ref)

        def work(tile, slot):
            here = pl.ds(pl.multiple_of(tile * CHUNK, CHUNK), CHUNK)
            if seq == 0:
                bias_ref[...] += jnp.sum(raw_x[slot].astype(F), axis=0, keepdims=True)
            for position, mask in enumerate(order):
                to = slice(position * part, (position + 1) * part)
                there = pl.ds(pl.multiple_of(flip(me, mask) * part, part), part)
                g_v[here, to] = raw_x[slot, :, there]

        over_tiles(g_other if seq else g_ref, raw_x, 1, work)
        leave(("g", seq), g_v, g_rel.at[pl.ds(seq * length, length)], rel_sem.at[seq, 1])

    def whole_group(group):
        if ("out", group) not in arrived:
            arrived.add(("out", group))
            for position in range(1, 8):
                arrive(group, position)

    def project(seq):
        whole_group(0)
        if seq == 0:
            left("tables")

        def one(tile, carry):
            here = pl.ds(pl.multiple_of(tile * CHUNK, CHUNK), CHUNK)
            mixed = dot(attn_v[here], w[0, :, : 3 * size], ((1,), (0,)), F) + offset_ref[...]
            tables = (tab_v[0, here], tab_v[1, here], tab_v[2, here])
            q_v[here] = turn(mixed[:, :size], *tables).astype(B)
            k_v[here] = turn(mixed[:, size : 2 * size], *tables).astype(B)
            v_v[here] = mixed[:, 2 * size :].astype(B)
            return carry

        lax.fori_loop(0, length // CHUNK, one, 0)

    def project_grad(seq):
        whole_group(0)
        cg_v[...] = dot(g_v[...], w[0, :, 3 * size :], ((1,), (0,)), B)

    def attend(seq):
        if seq:
            copies["seg"].wait()
            left(("mg", 0), ("ctx", 0))
        scale = size ** (-0.5)
        ids = seg_ref[...] if seq == 0 else seg_v[...]
        col_v[...] = jnp.broadcast_to(ids.astype(F), (8, length)).T
        dk_v[...] = jnp.zeros_like(dk_v)
        dv_v[...] = jnp.zeros_like(dv_v)
        for first in range(0, length, QBLOCK):
            low, high = key_range(first)
            here, keys = slice(first, first + QBLOCK), slice(low, high)
            scores = dot(q_v[here], k_v[keys], ((1,), (1,)), F) * scale
            row_ids = first + lax.broadcasted_iota(jnp.int32, (QBLOCK, high - low), 0)
            key_ids = low + lax.broadcasted_iota(jnp.int32, (QBLOCK, high - low), 1)
            row = seg_ref[:, keys] if seq == 0 else seg_v[:, keys]
            allowed = (key_ids <= row_ids) & (col_v[here, 0:1] == row.astype(F))
            scores = jnp.where(allowed, scores, -1e30)
            expo = jnp.exp(scores - jnp.max(scores, axis=1, keepdims=True))
            probs = expo / jnp.sum(expo, axis=1, keepdims=True)
            low_probs = probs.astype(B)
            ctx_v[here] = dot(low_probs, v_v[keys], ((1,), (0,)), B)
            dv_v[keys] += dot(low_probs, cg_v[here], ((0,), (0,)), F)
            prob_grad = dot(cg_v[here], v_v[keys], ((1,), (1,)), F)
            centred = jnp.sum(probs * prob_grad, axis=1, keepdims=True)
            score_grad = (probs * (prob_grad - centred)).astype(B)
            q_grad = dot(score_grad, k_v[keys], ((1,), (0,)), F) * scale
            tables = (tab_v[0, here], -tab_v[1, here], -tab_v[2, here])
            mg_v[here, :size] = turn(q_grad, *tables).astype(B)
            dk_v[keys] += dot(score_grad, q_v[here], ((0,), (0,)), F) * scale
        for first in range(0, length, QBLOCK):
            here = slice(first, first + QBLOCK)
            tables = (tab_v[0, here], -tab_v[1, here], -tab_v[2, here])
            mg_v[here, size : 2 * size] = turn(dk_v[here], *tables).astype(B)
            mg_v[here, 2 * size :] = dv_v[here].astype(B)
        sums = jnp.sum(mg_v[...].astype(F), axis=0, keepdims=True)
        if seq == 0:
            sum_ref[...] = sums
        else:
            sum_ref[...] += sums
        both = pl.ds(seq * length, length)
        leave(("mg", seq), mg_v, mixed_out.at[both], rel_sem.at[seq, 3])
        leave(("ctx", seq), ctx_v, ctx_out.at[both], rel_sem.at[seq, 4])

    def attn_grads(seq, low, high):
        def one(block, carry):
            here = pl.ds(pl.multiple_of(block * CHUNK, CHUNK), CHUNK)
            qkv = dot(attn_v[:, here], mg_v[...], ((0,), (0,)), F)
            dense = dot(g_v[:, here], ctx_v[...], ((0,), (0,)), F)
            if seq == 0:
                grad_v[here, : 3 * size] = qkv
                grad_v[here, 3 * size :] = dense
            else:
                grad_v[here, : 3 * size] += qkv
                grad_v[here, 3 * size :] += dense
            return carry

        lax.fori_loop(low // CHUNK, high // CHUNK, one, 0)

    def up(low, high):
        def store(tile, slot):
            here = pl.ds(pl.multiple_of(tile * CHUNK, CHUNK), CHUNK)
            return (
                pltpu.make_async_copy(act_v.at[slot], act_out.at[here], tile_sem.at[0, slot]),
                pltpu.make_async_copy(slope_v.at[slot], slope_out.at[here], tile_sem.at[1, slot]),
            )

        def one(tile, carry):
            slot = lax.rem(tile, 2)
            here = pl.ds(pl.multiple_of(tile * CHUNK, CHUNK), CHUNK)
            pre = dot(mlp_v[here], w[1], ((1,), (0,)), F) + up_bias_ref[...]

            @pl.when(tile >= low + 2)
            def _():
                for copy in store(tile - 2, slot):
                    copy.wait()

            cumulative = 0.5 * (1.0 + lax.erf(pre * 0.7071067811865476))
            density = jnp.exp(-0.5 * pre * pre) * 0.3989422804014327
            act_v[slot] = (pre * cumulative).astype(B)
            slope_v[slot] = cumulative + pre * density
            for copy in store(tile, slot):
                copy.start()
            return carry

        lax.fori_loop(low, high, one, 0)
        for tile in (high - 2, high - 1):
            for copy in store(tile, tile % 2):
                copy.wait()

    kinds = {"o": outer, "i": inner}

    def relay_on(group):
        arrive(group, 1)
        relay(group)

    def send_y(group, position):
        if position:
            arrive(group, position)
        onward(group, position, 1)

    def to_side(name, number, array):
        quarters[number].wait_recv()
        remote(name + "2", 24 + number, array.at[spot], array.at[spot], "tensor", side_to)

    def to_core(name, array):
        copies[name + "2"].wait_recv()
        remote(name + "3", 26 + (name == "g"), array.at[pair_rows], array.at[pair_rows], "tensor", core_to)

    def gradients(seq, number):
        middle = width // 2
        attn_grads(seq, *((0, middle) if number else (middle, width)))
        if seq and number:
            leave("keep", grad_v.at[pl.ds(0, middle)], keep_out, out_sem.at[4])
        elif seq:
            send_v[...] = grad_v[middle:].astype(B)
            leave("send", send_v, send_out, out_sem.at[3])

    def lift(seq):
        whole_group(1)
        up(seq * length // CHUNK, (seq + 1) * length // CHUNK)

    stages = {
        "sh": shard,
        "pu": lambda group, kind: pair_up(group, kinds[kind]),
        "gst": straight,
        "hd": lambda group, kind: hand(group, kinds[kind]),
        "re": relay_on,
        "yo": send_y,
        "gpo": pass_on,
        "x1": lambda kind: to_pair(0, x_ref.at[spot], x_other.at[spot], kinds[kind]),
        "g1": lambda kind: to_pair(1, g_ref.at[spot], g_other.at[spot], kinds[kind]),
        "x2": lambda: to_side("x", 0, x_other),
        "g2": lambda: to_side("g", 1, g_other),
        "x3": lambda: to_core("x", x_other),
        "g3": lambda: to_core("g", g_other),
        "N": normalise,
        "G": arrange_grad,
        "PJ": project,
        "CG": project_grad,
        "AT": attend,
        "GR": gradients,
        "UP": lift,
    }
    def begin(*private):
        nonlocal raw_x, attn_v, g_v, mlp_v, xr_v, grad_v, send_v, q_v, k_v
        nonlocal v_v, cg_v, ctx_v, mg_v, dk_v, dv_v, act_v, slope_v, col_v, tab_v
        (
            raw_x,
            attn_v,
            g_v,
            mlp_v,
            xr_v,
            grad_v,
            send_v,
            q_v,
            k_v,
            v_v,
            cg_v,
            ctx_v,
            mg_v,
            dk_v,
            dv_v,
            act_v,
            slope_v,
            col_v,
            tab_v,
        ) = private
        shard_copies.extend([shards(half, 0), shards(1 - half, 1)])
        for number in range(3 + hidden // part):
            for slot in (1, 0):
                shard_copies[slot][number].start()
        leave("tables", tables_ref, tab_v, out_sem.at[0])
        greet(
            [("dp", flip(me, mask)) for mask in [PAIR, across] + spread] + [("tensor", side_to), ("tensor", core_to)]
        )
        copies["seg"] = pltpu.make_async_remote_copy(
            src_ref=seg_ref,
            dst_ref=seg_v,
            send_sem=seg_sem.at[0],
            recv_sem=seg_sem.at[1],
            device_id={"dp": pair_to},
            device_id_type=MESH,
        )
        copies["seg"].start()

    def close():
        left(*list(outs))
        for name in ("x2", "x3", "g2", "g3"):
            copies[name].wait_send()
        for key in (0, 1):
            quarters[key].wait_send()

    def finish():
        def gone(sem):
            pltpu.make_async_remote_copy(
                src_ref=w.at[0, rows(0)],
                dst_ref=w.at[0, rows(0)],
                send_sem=sem,
                recv_sem=sem,
                device_id={"dp": pair_to},
                device_id_type=MESH,
            ).wait_send()

        for group in range(3):
            for position in (1, 4, 5, 6, 7):
                gone(send_sem.at[8 * group + position])
            gone(cross_sem.at[group, 1])

            @pl.when(inner)
            def _():
                for number in (0, 2, 3, 4, 5):
                    gone(cross_sem.at[group, number])

    return begin, stages, whole_group, close, finish


def scatter_steps(
    groups,
    steps,
    earlier,
    whole_group,
    attn_send,
    attn_keep,
    x_rel,
    g_rel,
    mlp_in,
    mixed_grad,
    context,
    activation,
    slope,
    x_ref,
    g_ref,
    vec_ref,
    mixed_sum,
    bias_sum,
    block_out,
    input_grad,
    qkv_out,
    dense_out,
    up_out,
    down_out,
    far_in,
    far_two,
    y_recv,
    z_recv,
    z_relay,
    c_recv,
    x_recv,
    e_recv,
    small_out,
    w,
    small_recv,
    load_sem,
    tile_sem,
    ys_sem,
    yr_sem,
    zs_sem,
    zr_sem,
    zl_sem,
    zf_sem,
    two_sem,
    ps_sem,
    pr_sem,
    cs_sem,
    cr_sem,
    xs_sem,
    xr_sem,
    es_sem,
    er_sem,
    fs_sem,
    fr_sem,
    emit_sem,
    ss_sem,
    sr_sem,
    out_sem,
    act_v,
    pre_v,
    tile_v,
    col_v,
    slope_t,
    mix_t,
    ctx_v,
    keep_v,
    y_send,
    z_send,
    p_send,
    y_stage,
    c_send,
    c_stage,
    r_stage,
    x_send,
    hold_v,
    mean_v,
    inverse_v,
    sum_v,
    small_v,
):
    length, width = x_ref.shape
    part = width // groups
    size = context.shape[1]
    hidden = activation.shape[1]
    quarter = length // 4
    me, place = lax.axis_index("dp"), lax.axis_index("tensor")
    core, side, half = lax.rem(place, 2), lax.div(place, 2), bit_of(me, PAIR)
    pair_to, side_to, core_to = flip(me, PAIR), flip(place, 2), flip(place, 1)
    spread, order = block_order(groups)
    z_to, y_to = [flip(me, bit) for bit in spread]
    across_to = flip(z_to, PAIR)
    inner = bit_of(me, PAIR) != bit_of(me, spread[0])
    outer = bit_of(me, PAIR) == bit_of(me, spread[0])

    def remote(source, target, send, recv, axis, index):
        return pltpu.make_async_remote_copy(
            src_ref=source, dst_ref=target, send_sem=send, recv_sem=recv, device_id={axis: index}, device_id_type=MESH
        )

    def span(position, count=1):
        return pl.ds(position * part, count * part)

    def step(index, amount):
        return pl.ds(pl.multiple_of(index * amount, amount), amount)

    def y_copy(group, position):
        source = attn_send if group == 0 else y_send
        here = step(position, part) if not isinstance(position, int) else span(position)
        return remote(
            source.at[here], y_recv.at[group, here], ys_sem.at[group, position], yr_sem.at[group, position], "dp", y_to
        )

    slot_of = (0, 0, 1)

    def z_copy(group, position):
        source, sem = z_send.at[slot_of[group], span(position - 2)], zs_sem.at[group, position - 2]
        onward = (
            remote(source, far_two.at[group], sem, two_sem.at[group], "dp", across_to)
            if position == 3
            else remote(source, z_relay.at[group, span(2)], sem, zl_sem.at[group, 2], "dp", across_to)
        )
        aside = remote(
            source, z_relay.at[group, span(position - 2)], sem, zl_sem.at[group, position - 2], "dp", pair_to
        )
        return onward, aside

    def forward(group, number):
        target = 0 if number == 2 else number
        arrived = remote(
            z_relay.at[group, span(number)],
            z_recv.at[group, span(target)],
            zf_sem.at[group, number],
            zl_sem.at[group, number],
            "dp",
            pair_to,
        )
        return arrived, remote(
            z_relay.at[group, span(number)],
            z_recv.at[group, span(target)],
            zf_sem.at[group, number],
            zr_sem.at[group, target],
            "dp",
            pair_to if number == 2 else across_to,
        )

    def pass_on(group, *numbers):
        @pl.when(inner)
        def _():
            for number in numbers:
                arrived, copy = forward(group, number)
                arrived.wait_recv()
                copy.start()

    def z_arrived(group, position):
        return remote(
            z_relay.at[group, span(position)],
            z_recv.at[group, span(position)],
            zf_sem.at[group, position],
            zr_sem.at[group, position],
            "dp",
            pair_to,
        )

    def p_copy(group):
        return remote(
            p_send.at[slot_of[group]], far_in.at[group], ps_sem.at[group], pr_sem.at[group], "dp", pair_to
        )

    emitted = {}

    def emit(group, kind, block, owner):
        copies = []
        for number in range(hidden // part):
            at = pl.ds(number * part, part)
            if group == 2 or (group == 0 and number == 3):
                block[:, at] = block[:, at].T
            if group == 1:
                target = up_out.at[:, pl.ds(pl.multiple_of(owner * hidden + number * part, part), part)]
            elif group == 2:
                target = down_out.at[pl.ds(pl.multiple_of(owner * hidden + number * part, part), part)]
            elif number == 3:
                target = dense_out.at[owner]
            else:
                target = qkv_out.at[:, pl.ds(pl.multiple_of(owner * 3 * size + number * part, part), part)]
            copies.append(pltpu.make_async_copy(block.at[:, at], target, emit_sem.at[group, kind, number]))
            copies[-1].start()
        emitted[(group, kind)] = copies

    def emit_near(group):
        emit(group, 0, keep_v.at[slot_of[group], span(0)], half)

    def emit_far(group):
        block = (
            hold_v.at[1, 1, :, pl.ds(0, hidden)],
            keep_v.at[0, span(1)],
            hold_v.at[1, 1, :, pl.ds(hidden, hidden)],
        )[group]
        p_copy(group).wait_recv()
        staged(far_in.at[group])
        block[...] = y_stage[...].astype(F)

        @pl.when(inner)
        def _():
            remote(
                p_send.at[0], far_two.at[group], two_sem.at[group], two_sem.at[group], "dp", across_to
            ).wait_recv()
            staged(far_two.at[group])
            block[...] += y_stage[...].astype(F)

        emit(group, 1, block, 1 - half)

    def staged(source):
        copy = pltpu.make_async_copy(source, y_stage, load_sem.at[6])
        copy.start()
        copy.wait()

    def y_far(group, position):
        if group == 0:
            need(5)
        y_copy(group, position).wait_recv()
        staged(y_recv.at[group, span(position)])
        total = keep_v[slot_of[group], span(position)] + y_stage[...].astype(F)
        onward, aside = z_copy(group, position)
        if group == 1:
            z_copy(0, position)[0].wait_send()
        z_send[slot_of[group], span(position - 2)] = total.astype(B)
        pl.when(inner)(onward.start)
        pl.when(outer)(aside.start)

    def y_near(group, position):
        if group == 0:
            need(5)
        y_copy(group, position).wait_recv()
        staged(y_recv.at[group, span(position)])
        total = keep_v[slot_of[group], span(position)] + y_stage[...].astype(F)
        keep_v[slot_of[group], span(position)] = total
        if position == 1:
            if group == 1:
                p_copy(0).wait_send()

            @pl.when(outer)
            def _():
                p_send[slot_of[group]] = keep_v[slot_of[group], span(1)].astype(B)
                p_copy(group).start()

    def z_last(group, position):
        def add():
            z_arrived(group, position).wait_recv()
            staged(z_recv.at[group, span(position)])
            return keep_v[slot_of[group], span(position)] + y_stage[...].astype(F)

        if position == 1:

            @pl.when(inner)
            def _():
                p_send[slot_of[group]] = add().astype(B)
                p_copy(group).start()

        else:
            keep_v[slot_of[group], span(0)] = add()
            emit_near(group)

    loads = [
        None,
        None,
        None,
        pltpu.make_async_copy(activation, act_v, load_sem.at[3]),
        pltpu.make_async_copy(context, ctx_v, load_sem.at[4]),
        pltpu.make_async_copy(attn_keep, keep_v.at[0], load_sem.at[5]),
    ]
    for number in (3, 5, 4):
        loads[number].start()
    loaded = set()

    def need(*numbers):
        for number in numbers:
            if number not in loaded:
                loaded.add(number)
                loads[number].wait()

    for position in (3, 2, 1, 0):
        y_copy(0, position).start()

    small_v[...] = jnp.zeros_like(small_v)

    def pre_load(tile, slot):
        here = step(tile, CHUNK)
        return (
            pltpu.make_async_copy(g_rel.at[here], tile_v.at[step(slot, CHUNK)], tile_sem.at[0, slot]),
            pltpu.make_async_copy(slope.at[here], slope_t.at[slot], tile_sem.at[1, slot]),
        )

    sum_v[...] = jnp.zeros_like(sum_v)

    def pre_tiles(seq):
        whole_group(2)
        low, high = seq * length // CHUNK, (seq + 1) * length // CHUNK
        for copy in pre_load(low, 0):
            copy.start()

        def one(tile, carry):
            slot = lax.rem(tile, 2)

            @pl.when(tile + 1 < high)
            def _():
                for copy in pre_load(tile + 1, 1 - slot):
                    copy.start()

            for copy in pre_load(tile, slot):
                copy.wait()
            grad = (dot(tile_v[step(slot, CHUNK)], w[2], ((1,), (0,)), F) * slope_t[slot]).astype(B)
            pre_v[step(tile, CHUNK)] = grad
            sum_v[...] += jnp.sum(grad.astype(F), axis=0, keepdims=True)
            return carry

        lax.fori_loop(low, high, one, 0)

    tall = 2 * quarter
    blocks = width // CHUNK

    def c_copy(which, seq, block):
        here = step(block, CHUNK)
        return remote(
            c_send.at[:, here],
            c_recv.at[which, seq, :, here],
            cs_sem.at[which, seq, block],
            cr_sem.at[which, seq, block],
            "tensor",
            core_to,
        )

    def x_copy(which, seq):
        return remote(
            x_send.at[which, seq], x_recv.at[which, seq], xs_sem.at[which, seq], xr_sem.at[which, seq], "tensor", side_to
        )

    def e_copy(which):
        return remote(x_send.at[which, 1], e_recv.at[which], es_sem.at[which], er_sem.at[which], "dp", pair_to)

    sent_tiles = []

    def send_tile(which, seq):
        begin, block_of = tile_of[which]
        whole_group(2)
        if which:
            need(3, 4)
        start = pl.multiple_of(seq * length + (1 - core) * tall, tall)
        begin(start)

        def one(block, carry):
            value = block_of(start, block)
            if sent_tiles:
                c_copy(*sent_tiles[-1], block).wait_send()
            c_send[:, step(block, CHUNK)] = value.astype(B)
            c_copy(which, seq, block).start()
            return carry

        lax.fori_loop(0, blocks, one, 0)
        sent_tiles.append((which, seq))

    def c_load(which, seq, block, slot):
        return pltpu.make_async_copy(c_recv.at[which, seq, :, step(block, CHUNK)], c_stage.at[slot], tile_sem.at[2, slot])

    def keep_tile(which, seq):
        begin, block_of = tile_of[which]
        start = pl.multiple_of(seq * length + core * tall, tall)
        begin(start)
        c_copy(which, seq, 0).wait_recv()
        c_load(which, seq, 0, 0).start()

        def one(block, carry):
            slot = lax.rem(block, 2)
            value = block_of(start, block)

            @pl.when(block + 1 < blocks)
            def _():
                c_copy(which, seq, block + 1).wait_recv()
                c_load(which, seq, block + 1, 1 - slot).start()

            c_load(which, seq, block, slot).wait()
            r_stage[...] = value + c_stage[slot].astype(F)
            here = step(block, CHUNK)
            hold_v[which, seq, :, here] = r_stage[step(side, quarter)]
            x_send[which, seq, :, here] = r_stage[step(1 - side, quarter)].astype(B)
            return carry

        lax.fori_loop(0, blocks, one, 0)
        x_copy(which, seq).start()

    def blend_begin(start):
        copies = (
            pltpu.make_async_copy(x_rel.at[pl.ds(start, tall)], tile_v, tile_sem.at[3, 0]),
            pltpu.make_async_copy(mixed_grad.at[pl.ds(start, tall)], mix_t, tile_sem.at[3, 1]),
        )
        for copy in copies:
            copy.start()
        for copy in copies:
            copy.wait()
        for slot in range(2):
            mean, inverse = stats(tile_v[span_rows(slot)].astype(F))
            mean_v[span_rows(slot)] = jnp.broadcast_to(mean, (CHUNK, 128))
            inverse_v[span_rows(slot)] = jnp.broadcast_to(inverse, (CHUNK, 128))

    def span_rows(slot):
        return pl.ds(slot * CHUNK, CHUNK)

    def natural_block(position):
        result = me
        for level, bit in enumerate([PAIR] + spread):
            flipped = lax.rem(lax.div(position, 1 << level), 2)
            result = result + bit * (1 - 2 * bit_of(me, bit)) * flipped
        return result

    def blend_block(start, block):
        here = step(block, CHUNK)
        there = step(natural_block(block), part)
        attn_grad = dot(mix_t[...], w[0, here, : 3 * size], ((1,), (1,)), F)
        mlp_grad = dot(pre_v[pl.ds(start, tall)], w[1, here, :], ((1,), (1,)), F)
        mean, inverse = mean_v[...], inverse_v[...]
        mean = jnp.concatenate([mean] * (CHUNK // 128), axis=1)
        inverse = jnp.concatenate([inverse] * (CHUNK // 128), axis=1)
        normed = (tile_v[:, here].astype(F) - mean) * inverse
        small_v[0:1, there] += jnp.sum(attn_grad * normed, axis=0, keepdims=True)
        small_v[1:2, there] += jnp.sum(attn_grad, axis=0, keepdims=True)
        small_v[2:3, there] += jnp.sum(mlp_grad * normed, axis=0, keepdims=True)
        small_v[3:4, there] += jnp.sum(mlp_grad, axis=0, keepdims=True)
        return attn_grad * vec_ref[0:1, there] + mlp_grad * vec_ref[2:3, there]

    def product(columns, right, group, positions, sent, old=None):
        count = len(positions)
        base = positions[0]
        sign = positions[1] - positions[0] if count > 1 else 1

        def load(number, slot):
            return pltpu.make_async_copy(
                columns.at[:, step(base + sign * number, part)], col_v.at[slot], tile_sem.at[4, slot]
            )

        load(0, 0).start()

        def one(number, carry):
            slot = lax.rem(number, 2)

            @pl.when(number + 1 < count)
            def _():
                load(number + 1, 1 - slot).start()

            load(number, slot).wait()
            value = dot(col_v[slot], right[...], ((0,), (0,)), F)
            position = base + sign * number
            if sent:
                if old is not None:
                    y_copy(old, position - groups // 2).wait_send()
                y_send[step(position - groups // 2, part)] = value.astype(B)
                y_copy(group, position - groups // 2).start()
            else:
                keep_v[slot_of[group], step(position, part)] = value
            return carry

        lax.fori_loop(0, count, one, 0)

    def small_begin():
        small_v[4:5] = bias_sum[...]
        small_v[5:6, step(half, hidden)] = sum_v[...]
        small_v[6:7, pl.ds(pl.multiple_of(half * (width // 2), width // 2), 3 * size)] = mixed_sum[...]
        small_copy(0).start()

    rounds = [("dp", flip(me, bit)) for bit in [PAIR] + spread] + [("tensor", side_to), ("tensor", core_to)]

    def small_copy(number):
        return remote(small_v, small_recv.at[number], ss_sem.at[number], sr_sem.at[number], *rounds[number])

    def small_end(number):
        small_copy(number).wait()
        if number < 3:
            small_v[...] += small_recv[number]
        else:
            small_v[0:4] += small_recv[number, 0:4]
        if number + 1 < len(rounds):
            small_copy(number + 1).start()

    def branch_begin(start):
        pass

    def branch_block(start, block):
        here, rows = step(block, CHUNK), pl.ds(start, tall)
        return dot(ctx_v[rows], w[0, here, 3 * size :], ((1,), (1,)), F) + dot(
            act_v[rows], w[2, here, :], ((1,), (1,)), F
        )

    def read_stage(source):
        copy = pltpu.make_async_copy(source, tile_v.at[pl.ds(0, quarter)], load_sem.at[6])
        copy.start()
        copy.wait()

    def e_start(which):
        x_copy(which, 1).wait_recv()
        x_copy(which, 1).wait_send()
        read_stage(x_recv.at[which, 1])

        def one(block, carry):
            here = step(block, CHUNK)
            x_send[which, 1, :, here] = (hold_v[which, 1, :, here] + tile_v[0:quarter, here].astype(F)).astype(B)
            return carry

        lax.fori_loop(0, blocks, one, 0)
        e_copy(which).start()

    def gather_own(which):
        x_copy(which, 0).wait_recv()
        read_stage(x_recv.at[which, 0])

        def one(block, carry):
            here = step(block, CHUNK)
            hold_v[which, 0, :, here] += tile_v[0:quarter, here].astype(F)
            return carry

        lax.fori_loop(0, blocks, one, 0)

    def spot(c, s):
        return pl.ds(pl.multiple_of(c * tall + s * quarter, quarter), quarter)

    def position_of(block, shifted=False):
        result = 0
        for level, bit in enumerate([PAIR] + spread):
            mine = bit_of(me, bit)
            if shifted and bit == PAIR:
                mine = 1 - mine
            result = result + (1 << level) * ((1 - mine) if block & bit else mine)
        return result

    def finish(which, out_ref):
        if len(sent_tiles) == 4:
            sent_tiles.append(None)
            for block in range(blocks):
                c_copy(*sent_tiles[3], block).wait_send()
        gather_own(which)
        e_copy(which).wait_recv()
        copies = [
            pltpu.make_async_copy(e_recv.at[which], tile_v.at[pl.ds(0, quarter)], load_sem.at[6]),
            pltpu.make_async_copy(x_ref.at[spot(core, side)], tile_v.at[pl.ds(quarter, quarter)], load_sem.at[7]),
        ]
        if which == 0:
            copies.append(pltpu.make_async_copy(g_ref.at[spot(core, side)], x_send.at[0, 0], load_sem.at[8]))
            x_copy(0, 0).wait_send()
        for copy in copies:
            copy.start()
        for copy in copies:
            copy.wait()
        here = pl.ds(which * quarter, quarter)
        if which == 0:
            total_u, total_un = 0.0, 0.0
            mean, inverse = stats(tile_v[quarter:].astype(F))
            for block in range(groups):
                mine = hold_v[0, 0, :, step(position_of(block), part)]
                theirs = tile_v[0:quarter, step(position_of(block, True), part)].astype(F)
                blend = mine + theirs
                normed = (tile_v[quarter:, block * part : (block + 1) * part].astype(F) - mean) * inverse
                hold_v[0, 1, :, block * part : (block + 1) * part] = blend
                total_u = total_u + jnp.sum(blend, axis=1, keepdims=True)
                total_un = total_un + jnp.sum(blend * normed, axis=1, keepdims=True)
            mean_u, mean_un = total_u * (1.0 / width), total_un * (1.0 / width)
            for block in range(groups):
                at = slice(block * part, (block + 1) * part)
                normed = (tile_v[quarter:, at].astype(F) - mean) * inverse
                inner = (hold_v[0, 1, :, at] - mean_u - normed * mean_un) * inverse
                c_send[here, at] = (x_send[0, 0, :, at].astype(F) + inner).astype(B)
        else:
            for block in range(groups):
                at = slice(block * part, (block + 1) * part)
                mine = hold_v[1, 0, :, step(position_of(block), part)]
                theirs = tile_v[0:quarter, step(position_of(block, True), part)].astype(F)
                bias = vec_ref[4:5, at] + vec_ref[5:6, at]
                c_send[here, at] = (tile_v[quarter:, at].astype(F) + (mine + theirs) + bias).astype(B)
        first = remote(
            c_send.at[here], out_ref.at[spot(core, side)], fs_sem.at[which, 0], fr_sem.at[which, 0], "tensor", side_to
        )
        second = remote(
            c_send.at[here], out_ref.at[spot(core, side)], fs_sem.at[which, 1], fr_sem.at[which, 1], "tensor", core_to
        )
        own = pltpu.make_async_copy(c_send.at[here], out_ref.at[spot(core, side)], out_sem.at[3 + which])
        for copy in (first, second, own):
            copy.start()
        return first, second, own

    def finish_end(which, out_ref, copies):
        first, second, own = copies
        first.wait_recv()
        third = remote(
            out_ref.at[spot(core, 1 - side)],
            out_ref.at[spot(core, 1 - side)],
            fs_sem.at[which, 2],
            fr_sem.at[which, 2],
            "tensor",
            core_to,
        )
        third.start()
        return [first.wait_send, second.wait, third.wait, own.wait]

    tile_of = ((blend_begin, blend_block), (branch_begin, branch_block))
    outs, finished, ends = (input_grad, block_out), {}, []

    def do_product(group, sent):
        columns, right = ((mlp_in, pre_v), (g_rel, act_v))[group - 1]
        if group == 2:
            need(3)
        if group == 1 and not sent:
            for copy in emitted[(0, 0)]:
                copy.wait()
        product(columns, right, group, (7, 6, 5, 4) if sent else (3, 2, 1, 0), sent, 2 if sent and group == 1 else None)

    def do_finish(which):
        finished[which] = finish(which, outs[which])

    def do_end(which):
        ends.extend(finish_end(which, outs[which], finished[which]))

    stages = {
        "pre": pre_tiles,
        "st": send_tile,
        "kt": keep_tile,
        "ps": lambda group: do_product(group, True),
        "pk": lambda group: do_product(group, False),
        "yf": y_far,
        "yn": y_near,
        "po": pass_on,
        "zl": z_last,
        "es": e_start,
        "fin": do_finish,
        "fe": do_end,
        "fa": emit_far,
        "sb": small_begin,
        "se": small_end,
    }
    for name, *numbers in steps:
        (stages if name in stages else earlier)[name](*numbers)
    small_out[...] = small_v[...]
    for end in ends:
        end()
    for group in range(3):
        if group:
            p_copy(group).wait_send()
            for position in (2, 3):
                z_copy(group, position)[0].wait_send()
        for position in range(4):
            if group != 2:
                y_copy(group, position).wait_send()
        for kind in range(2):
            if group or kind:
                for copy in emitted[(group, kind)]:
                    copy.wait()

        @pl.when(inner)
        def _():
            for number in range(3):
                forward(group, number)[1].wait_send()

    for which in range(2):
        e_copy(which).wait_send()
        if which:
            x_copy(which, 0).wait_send()


def layer_kernel(
    groups,
    scoped_one,
    scoped_two,
    qkv_ref,
    dense_ref,
    up_ref,
    down_ref,
    seg_ref,
    x_ref,
    g_ref,
    vec_ref,
    up_bias_ref,
    offset_ref,
    tables_ref,
    block_out,
    input_grad,
    qkv_out,
    dense_out,
    up_out,
    down_out,
    w_relay,
    x_other,
    g_other,
    x_rel,
    g_rel,
    mlp_out,
    mixed_out,
    ctx_out,
    act_out,
    slope_out,
    send_out,
    keep_out,
    far_in,
    far_two,
    y_recv,
    z_recv,
    z_relay,
    c_recv,
    x_recv,
    e_recv,
    small_out,
    w,
    theirs_v,
    seg_v,
    sum_ref,
    bias_ref,
    small_recv,
    send_sem,
    recv_sem,
    cross_sem,
    two_sem,
    three_sem,
    relay_sem,
    quarter_sem,
    shard_sem,
    seg_sem,
    load_sem,
    rel_sem,
    tile_sem,
    out_sem,
    s_load_sem,
    s_tile_sem,
    s_ys_sem,
    s_yr_sem,
    s_zs_sem,
    s_zr_sem,
    s_zl_sem,
    s_zf_sem,
    s_two_sem,
    s_ps_sem,
    s_pr_sem,
    s_cs_sem,
    s_cr_sem,
    s_xs_sem,
    s_xr_sem,
    s_es_sem,
    s_er_sem,
    s_fs_sem,
    s_fr_sem,
    s_emit_sem,
    s_ss_sem,
    s_sr_sem,
    s_out_sem,
):
    begin, earlier, whole_group, close, finish = gather_steps(
        groups,
        qkv_ref,
        dense_ref,
        up_ref,
        down_ref,
        seg_ref,
        x_ref,
        g_ref,
        vec_ref,
        up_bias_ref,
        offset_ref,
        tables_ref,
        w_relay,
        x_other,
        g_other,
        x_rel,
        g_rel,
        mlp_out,
        mixed_out,
        ctx_out,
        act_out,
        slope_out,
        send_out,
        keep_out,
        w,
        theirs_v,
        seg_v,
        sum_ref,
        bias_ref,
        send_sem,
        recv_sem,
        cross_sem,
        two_sem,
        three_sem,
        relay_sem,
        quarter_sem,
        shard_sem,
        seg_sem,
        load_sem,
        rel_sem,
        tile_sem,
        out_sem,
    )

    def first(*private):
        begin(*private)
        for name, *numbers in STEPS_ONE:
            earlier[name](*numbers)
        close()

    def second(*private):
        scatter_steps(
            groups,
            STEPS_TWO,
            earlier,
            whole_group,
            send_out,
            keep_out,
            x_rel,
            g_rel,
            mlp_out,
            mixed_out,
            ctx_out,
            act_out,
            slope_out,
            x_ref,
            g_ref,
            vec_ref,
            sum_ref,
            bias_ref,
            block_out,
            input_grad,
            qkv_out,
            dense_out,
            up_out,
            down_out,
            far_in,
            far_two,
            y_recv,
            z_recv,
            z_relay,
            c_recv,
            x_recv,
            e_recv,
            small_out,
            w,
            small_recv,
            s_load_sem,
            s_tile_sem,
            s_ys_sem,
            s_yr_sem,
            s_zs_sem,
            s_zr_sem,
            s_zl_sem,
            s_zf_sem,
            s_two_sem,
            s_ps_sem,
            s_pr_sem,
            s_cs_sem,
            s_cr_sem,
            s_xs_sem,
            s_xr_sem,
            s_es_sem,
            s_er_sem,
            s_fs_sem,
            s_fr_sem,
            s_emit_sem,
            s_ss_sem,
            s_sr_sem,
            s_out_sem,
            *private,
        )
        finish()

    pl.run_scoped(first, *scoped_one)
    pl.run_scoped(second, *scoped_two)


def body_narrow(
    tokens,
    segment_ids,
    out_grad,
    attn_norm_gain,
    attn_norm_bias,
    mlp_norm_gain,
    mlp_norm_bias,
    qkv_weight,
    qv_bias,
    key_bias,
    dense_weight,
    dense_bias,
    up_weight,
    up_bias,
    down_weight,
    down_bias,
    *,
    groups,
    ways,
):
    length, width = tokens.shape[1:]
    heads, size = qkv_weight.shape[1] // 2, qkv_weight.shape[3]
    part = width // groups
    me = lax.axis_index("dp")
    half = (me // PAIR) % 2
    place = lax.axis_index("tensor")
    core, side = place % 2, place // 2
    spread = [bit for bit in (1 << k for k in reversed(range(groups.bit_length() - 1))) if bit != PAIR]

    def swap(array, bit):
        return lax.ppermute(array, "dp", [(i, i ^ bit) for i in range(groups)])

    def cross(array, bit):
        return lax.ppermute(array, "tensor", [(i, i ^ bit) for i in range(ways)])

    def pick(array, index, axis, count=2):
        rows = array.shape[axis] // count
        return lax.dynamic_slice_in_dim(array, index * rows, rows, axis)

    def join(mine, theirs, index, axis):
        pair = jnp.concatenate([mine, theirs], axis=axis)
        turned = jnp.concatenate([theirs, mine], axis=axis)
        return jnp.where(index == 0, pair, turned)

    order = [0, PAIR]
    for bit in spread:
        order = order + [mask | bit for mask in order]
    inverse = [order.index(mask) for mask in range(groups)]

    def arranged(array):
        return jnp.concatenate(
            [lax.dynamic_slice_in_dim(array, (mask ^ me) * part, part, array.ndim - 1) for mask in order], axis=-1
        )

    def natural(array):
        table = jnp.asarray(inverse, jnp.int32)
        return jnp.concatenate(
            [lax.dynamic_slice_in_dim(array, table[block ^ me] * part, part, array.ndim - 1) for block in range(groups)],
            axis=-1,
        )

    def gather(shard, halves_axis, axis):
        shard = shard.astype(B)
        mine, theirs = pick(shard, half, halves_axis), pick(shard, 1 - half, halves_axis)
        pieces = [jnp.concatenate([mine, swap(theirs, PAIR)], axis=axis)]
        for bit in spread:
            pieces = pieces + [swap(piece, bit) for piece in pieces]
        return jnp.concatenate(pieces, axis=axis)

    def scatter(product, axis, halves_axis):
        count = groups // 2
        sent = swap(product(count, groups, B), spread[-1])
        held = product(0, count, F) + sent.astype(F)
        for bit in reversed(spread[:-1]):
            keep, send = jnp.split(held, 2, axis=axis)
            held = keep + swap(send.astype(B), bit).astype(F)
        keep, send = jnp.split(held, 2, axis=axis)
        return join(keep, swap(send, PAIR), half, halves_axis)

    def share_rows(rows):
        rows = join(rows, cross(rows, 2), side, 0)
        return join(rows, cross(rows, 1), core, 0)

    def own_rows(array, axis):
        return pick(pick(array, core, axis), side, axis)

    def partner_rows(array):
        return share_rows(swap(own_rows(array, 0), PAIR))

    def total_rows(partial):
        held = pick(partial, core, 1).astype(F) + cross(pick(partial, 1 - core, 1), 1).astype(F)
        held = pick(held, side, 1) + cross(pick(held, 1 - side, 1).astype(B), 2).astype(F)
        sent = swap(held[1].astype(B), PAIR).astype(F)
        rows = sent.shape[0]
        sent = jnp.flip(sent.reshape(rows, groups // 2, 2, part), axis=2).reshape(rows, width)
        return held[0] + sent

    own_x, own_g = tokens[0], out_grad[0]
    w_up = gather(up_weight, 1, 0)
    x_other = partner_rows(own_x)
    w_down = gather(down_weight, 0, 1)
    g_other = partner_rows(own_g)
    w_qkv = gather(qkv_weight.reshape(part, 2, -1), 1, 0).reshape(width, -1)
    w_dense = gather(dense_weight.reshape(2 * heads * size, part), 0, 1)

    x_pair = arranged(jnp.concatenate([own_x, x_other], axis=0))
    g_pair = arranged(jnp.concatenate([own_g, g_other], axis=0))
    gains = [arranged(v) for v in (attn_norm_gain, attn_norm_bias, mlp_norm_gain, mlp_norm_bias)]

    def hat(rows):
        rows = rows.astype(F)
        center = rows - jnp.mean(rows, axis=-1, keepdims=True)
        inverse_dev = lax.rsqrt(jnp.mean(center * center, axis=-1, keepdims=True) + 1e-05)
        return center * inverse_dev, inverse_dev

    normed, _ = hat(x_pair)
    attn_in = (normed * gains[0] + gains[1]).astype(B)
    mlp_in = (normed * gains[2] + gains[3]).astype(B)

    up_here = pick(up_bias, half, 0)
    up_pre = dot(mlp_in, w_up, ((1,), (0,)), F) + up_here
    activation = jax.nn.gelu(up_pre, approximate=False).astype(B)
    middle = width // 2

    def columns(array, low, high):
        return array[:, low * part : high * part]

    down_shard = scatter(lambda low, high, kind: dot(activation, columns(g_pair, low, high), ((0,), (0,)), kind), 1, 0)
    pre_grad = (dot(g_pair, w_down, ((1,), (1,)), F) * gelu_slope(up_pre)).astype(B)
    up_shard = scatter(lambda low, high, kind: dot(columns(mlp_in, low, high), pre_grad, ((0,), (0,)), kind), 0, 1)
    up_bias_sum = jnp.sum(pre_grad.astype(F), axis=0)

    seg_other = swap(segment_ids[0], PAIR)
    seg = jnp.stack([segment_ids[0], seg_other])
    seg_col, seg_row = seg[:, :, None], seg[:, None, :]
    qv_here, key_here = pick(qv_bias, half, 0), pick(key_bias, half, 0)
    key_full = jnp.concatenate([key_here, jnp.zeros((heads, size - ROT), F)], axis=1)
    offsets = jnp.stack([qv_here[:, 0], key_full, qv_here[:, 1]], axis=1).reshape(heads, 1, 3 * size)
    mixed = dot(attn_in, w_qkv, ((1,), (0,)), F).reshape(2, length, heads, 3 * size)
    tables = rope_tables(length)
    table_specs = [shared(length, 128)] * 3
    seg_specs = [per_seq(length, 1), per_seq(1, length)]
    context_grad = dot(g_pair, w_dense, ((1,), (1,)), B).reshape(2, length, heads, size)
    contexts, mixed_grads, mixed_sums = [], [], []
    head_shape = jax.ShapeDtypeStruct((2, length, size), B)
    for head in range(heads):
        q, k, v, context, lse = pl.pallas_call(
            attn_forward,
            grid=(2,),
            in_specs=[per_seq(length, 3 * size), shared(1, 3 * size)] + table_specs + seg_specs,
            out_specs=[per_seq(length, size)] * 4 + [per_seq(length, 1)],
            out_shape=[head_shape] * 4 + [jax.ShapeDtypeStruct((2, length, 1), F)],
            name="attn_forward",
        )(mixed[:, :, head], offsets[head], *tables, seg_col, seg_row)
        mixed_grad, mixed_sum = pl.pallas_call(
            attn_backward,
            grid=(2,),
            in_specs=[per_seq(length, size)] * 4 + [per_seq(length, 1)] + table_specs + seg_specs,
            out_specs=[per_seq(length, 3 * size), per_seq(1, 3 * size)],
            out_shape=[
                jax.ShapeDtypeStruct((2, length, 3 * size), B),
                jax.ShapeDtypeStruct((2, 1, 3 * size), F),
            ],
            scratch_shapes=[pltpu.VMEM((length, size), F)] * 3,
            name="attn_backward",
        )(q, k, v, context_grad[:, :, head], lse, *tables, seg_col, seg_row)
        contexts.append(context.reshape(2 * length, size))
        mixed_grads.append(mixed_grad.reshape(2 * length, 3 * size))
        mixed_sums.append(jnp.sum(mixed_sum, axis=(0, 1)))
    context = jnp.concatenate(contexts, axis=1)
    mixed_grad = jnp.concatenate(mixed_grads, axis=1)
    mixed_sum = jnp.stack(mixed_sums).reshape(heads, 3, size)

    qkv_shard = scatter(lambda low, high, kind: dot(columns(attn_in, low, high), mixed_grad, ((0,), (0,)), kind), 0, 1)
    dense_shard = scatter(lambda low, high, kind: dot(context, columns(g_pair, low, high), ((0,), (0,)), kind), 1, 0)

    branch = dot(context, w_dense, ((1,), (0,)), F) + dot(activation, w_down, ((1,), (0,)), F)
    branch_rows = total_rows(branch.astype(B).reshape(2, length, width))
    x_rows, g_rows = own_rows(x_pair[:length], 0), own_rows(g_pair[:length], 0)
    out_rows = (x_rows.astype(F) + branch_rows + arranged(dense_bias) + arranged(down_bias)).astype(B)
    block_out = share_rows(natural(out_rows))

    attn_in_grad = dot(mixed_grad, w_qkv, ((1,), (1,)), F)
    mlp_in_grad = dot(pre_grad, w_up, ((1,), (1,)), F)
    blend = (attn_in_grad * gains[0] + mlp_in_grad * gains[2]).astype(B)
    blend_rows = total_rows(blend.reshape(2, length, width))
    hat_rows, inverse_rows = hat(x_rows)
    inner = (
        blend_rows
        - jnp.mean(blend_rows, axis=-1, keepdims=True)
        - hat_rows * jnp.mean(blend_rows * hat_rows, axis=-1, keepdims=True)
    )
    input_grad = share_rows(natural((g_rows.astype(F) + inner * inverse_rows).astype(B)))

    norm_sums = natural(
        jnp.stack(
            [
                jnp.sum(attn_in_grad * normed, axis=0),
                jnp.sum(attn_in_grad, axis=0),
                jnp.sum(mlp_in_grad * normed, axis=0),
                jnp.sum(mlp_in_grad, axis=0),
            ]
        )
    ).reshape(-1)
    bias_sum = jnp.sum(own_g.astype(F), axis=0)

    def slotted(array):
        zero = jnp.zeros_like(array)
        return join(array, zero, half, 0)

    small = [norm_sums, bias_sum, slotted(up_bias_sum), slotted(mixed_sum).reshape(-1)]
    sizes = [s.shape[0] for s in small]
    flat = jnp.concatenate(small)
    for bit in [1 << k for k in range(groups.bit_length() - 1)]:
        flat = flat + swap(flat, bit)
    ends = [sum(sizes[: i + 1]) for i in range(len(sizes))]
    norms = flat[: ends[0]]
    for bit in [1 << k for k in range(ways.bit_length() - 1)]:
        norms = norms + cross(norms, bit)
    norms = norms.reshape(4, width)
    bias_grad = flat[ends[0] : ends[1]]
    up_bias_grad = flat[ends[1] : ends[2]]
    mixed_bias = flat[ends[2] :].reshape(2 * heads, 3, size)
    qv_grad = jnp.stack([mixed_bias[:, 0], mixed_bias[:, 2]], axis=1)
    key_bias_grad = mixed_bias[:, 1, :ROT]

    return (
        block_out[None],
        input_grad[None],
        norms[0],
        norms[1],
        norms[2],
        norms[3],
        qkv_shard.reshape(qkv_weight.shape),
        qv_grad,
        key_bias_grad,
        dense_shard.reshape(dense_weight.shape),
        bias_grad,
        up_shard,
        up_bias_grad,
        down_shard,
        bias_grad,
    )


def body(
    tokens,
    segment_ids,
    out_grad,
    attn_norm_gain,
    attn_norm_bias,
    mlp_norm_gain,
    mlp_norm_bias,
    qkv_weight,
    qv_bias,
    key_bias,
    dense_weight,
    dense_bias,
    up_weight,
    up_bias,
    down_weight,
    down_bias,
    *,
    groups,
    ways,
):
    length, width = tokens.shape[1:]
    heads, size = qkv_weight.shape[1] // 2, qkv_weight.shape[3]
    assert heads == 1 and ways == 4
    part = width // groups
    hidden = up_weight.shape[1] // 2
    count = 2 * length
    me = lax.axis_index("dp")
    half = (me // PAIR) % 2
    shape = jax.ShapeDtypeStruct

    def pick(array, index, axis):
        rows = array.shape[axis] // 2
        return lax.dynamic_slice_in_dim(array, index * rows, rows, axis)

    vectors = jnp.stack([attn_norm_gain, attn_norm_bias, mlp_norm_gain, mlp_norm_bias, dense_bias, down_bias])
    own_x, own_g = tokens[0], out_grad[0]

    qv_here, key_here = pick(qv_bias, half, 0), pick(key_bias, half, 0)
    key_full = jnp.concatenate([key_here, jnp.zeros((heads, size - ROT), F)], axis=1)
    offsets = jnp.stack([qv_here[:, 0], key_full, qv_here[:, 1]], axis=1).reshape(1, 3 * size)
    tables = rope_tables(length)
    up_here = pick(up_bias, half, 0)[None]
    columns = hidden
    half_width = width // 2
    vmem, hbm = pl.BlockSpec(memory_space=pltpu.VMEM), pl.BlockSpec(memory_space=pl.ANY)
    quarter = length // 4
    tall, blocks = 2 * quarter, width // CHUNK
    dma = pltpu.SemaphoreType.DMA
    scoped_one = [
        pltpu.VMEM((2, CHUNK, width), B),
        pltpu.VMEM((length, width), B),
        pltpu.VMEM((length, width), B),
        pltpu.VMEM((count, width), B),
        pltpu.VMEM((length, width), B),
        pltpu.VMEM((width, columns), F),
        pltpu.VMEM((half_width, columns), B),
        pltpu.VMEM((length, size), B),
        pltpu.VMEM((length, size), B),
        pltpu.VMEM((length, size), B),
        pltpu.VMEM((length, size), B),
        pltpu.VMEM((length, size), B),
        pltpu.VMEM((length, 3 * size), B),
        pltpu.VMEM((length, size), F),
        pltpu.VMEM((length, size), F),
        pltpu.VMEM((2, CHUNK, hidden), B),
        pltpu.VMEM((2, CHUNK, hidden), F),
        pltpu.VMEM((length, 8), F),
        pltpu.VMEM((3, length, 128), F),
    ]
    scoped_two = [
        pltpu.VMEM((count, hidden), B),
        pltpu.VMEM((count, hidden), B),
        pltpu.VMEM((tall, width), B),
        pltpu.VMEM((2, count, part), B),
        pltpu.VMEM((2, CHUNK, hidden), F),
        pltpu.VMEM((tall, 3 * size), B),
        pltpu.VMEM((count, size), B),
        pltpu.VMEM((2, half_width, columns), F),
        pltpu.VMEM((half_width, columns), B),
        pltpu.VMEM((2, half_width // 2, columns), B),
        pltpu.VMEM((2, part, columns), B),
        pltpu.VMEM((part, columns), B),
        pltpu.VMEM((tall, width), B),
        pltpu.VMEM((2, tall, CHUNK), B),
        pltpu.VMEM((tall, CHUNK), F),
        pltpu.VMEM((2, 2, quarter, width), B),
        pltpu.VMEM((2, 2, quarter, width), F),
        pltpu.VMEM((tall, 128), F),
        pltpu.VMEM((tall, 128), F),
        pltpu.VMEM((1, hidden), F),
        pltpu.VMEM((8, width), F),
    ]
    block_out, input_grad, qkv_shard, dense_shard, up_shard, down_shard, *_, small = pl.pallas_call(
        functools.partial(layer_kernel, groups, scoped_one, scoped_two),
        in_specs=[hbm] * 4 + [vmem] + [hbm] * 2 + [vmem] * 3 + [hbm],
        out_specs=[hbm] * 26 + [vmem],
        out_shape=[
            shape((length, width), B),
            shape((length, width), B),
            shape((part, 6 * size), F),
            shape(dense_weight.shape, F),
            shape(up_weight.shape, F),
            shape(down_weight.shape, F),
            shape((3, 3 * part, columns), B),
            shape((length, width), B),
            shape((length, width), B),
            shape((count, width), B),
            shape((count, width), B),
            shape((count, width), B),
            shape((count, 3 * size), B),
            shape((count, size), B),
            shape((count, hidden), B),
            shape((count, hidden), F),
            shape((half_width, columns), B),
            shape((half_width, columns), F),
            shape((3, part, columns), B),
            shape((3, part, columns), B),
            shape((3, half_width, columns), B),
            shape((3, half_width // 2, columns), B),
            shape((3, 3 * part, columns), B),
            shape((2, 2, tall, width), B),
            shape((2, 2, quarter, width), B),
            shape((2, quarter, width), B),
            shape((8, width), F),
        ],
        scratch_shapes=[
            pltpu.VMEM((3, width, columns), B),
            pltpu.VMEM((3, part, columns), B),
            pltpu.VMEM((1, length), jnp.int32),
            pltpu.VMEM((1, 3 * size), F),
            pltpu.VMEM((1, width), F),
            pltpu.VMEM((5, 8, width), F),
            dma((28,)),
            dma((28,)),
            dma((3, 6)),
            dma((3,)),
            dma((3,)),
            dma((3, 3)),
            dma((2, 2)),
            dma((2, 3 + hidden // part)),
            dma((2,)),
            dma((2, 2)),
            dma((2, 5)),
            dma((2, 2)),
            dma((5,)),
            dma((9,)),
            dma((5, 2)),
            dma((3, 4)),
            dma((3, 4)),
            dma((3, 2)),
            dma((3, 2)),
            dma((3, 3)),
            dma((3, 3)),
            dma((3,)),
            dma((3,)),
            dma((3,)),
            dma((2, 2, blocks)),
            dma((2, 2, blocks)),
            dma((2, 2)),
            dma((2, 2)),
            dma((2,)),
            dma((2,)),
            dma((2, 3)),
            dma((2, 3)),
            dma((3, 2, hidden // part)),
            dma((5,)),
            dma((5,)),
            dma((5,)),
        ],
        compiler_params=pltpu.CompilerParams(
            collective_id=0, has_side_effects=True, vmem_limit_bytes=67043328
        ),
        cost_estimate=pl.CostEstimate(flops=100 * 10**9, bytes_accessed=2 * 10**8, transcendentals=10**7),
        name="layer",
    )(
        qkv_weight.reshape(part, 6 * size),
        dense_weight,
        up_weight,
        down_weight,
        segment_ids,
        own_x,
        own_g,
        vectors,
        up_here,
        offsets,
        jnp.stack(tables),
    )

    norms, bias_grad, up_bias_grad = small[0:4], small[4], small[5]
    mixed_bias = small[6].reshape(2, width // 2)[:, : 3 * size].reshape(2, 3, size)
    qv_grad = jnp.stack([mixed_bias[:, 0], mixed_bias[:, 2]], axis=1)
    key_bias_grad = mixed_bias[:, 1, :ROT]

    return (
        block_out[None],
        input_grad[None],
        norms[0],
        norms[1],
        norms[2],
        norms[3],
        qkv_shard.reshape(qkv_weight.shape),
        qv_grad,
        key_bias_grad,
        dense_shard,
        bias_grad,
        up_shard,
        up_bias_grad,
        down_shard,
        bias_grad,
    )


def solution(mesh):
    placed = (
        P("dp", None, None),
        P("dp", None),
        P("dp", None, None),
        P(),
        P(),
        P(),
        P(),
        P("dp", "tensor", None, None),
        P("tensor", None, None),
        P("tensor", None),
        P("tensor", None, "dp"),
        P(),
        P("dp", "tensor"),
        P("tensor"),
        P("tensor", "dp"),
        P(),
    )

    def whole(*arrays):
        groups, ways = mesh.shape["dp"], mesh.shape["tensor"]
        part = arrays[0].shape[2] // groups
        chosen = body_narrow if part % 128 or groups != 8 else body
        return chosen(*arrays, groups=groups, ways=ways)

    return jax.shard_map(
        whole,
        mesh=mesh,
        in_specs=placed,
        out_specs=(
            P("dp", None, None),
            P("dp", None, None),
            P(),
            P(),
            P(),
            P(),
            P("dp", "tensor", None, None),
            P("tensor", None, None),
            P("tensor", None),
            P("tensor", None, "dp"),
            P(),
            P("dp", "tensor"),
            P("tensor"),
            P("tensor", "dp"),
            P(),
        ),
        check_vma=False,
    )
```

```python
import functools

import jax
import jax.numpy as jnp
from jax import lax
from jax.experimental import pallas as pl
from jax.experimental.pallas import tpu as pltpu
from jax.sharding import PartitionSpec as P

ROT = 64
PAIR = 2
QBLOCK = 256
DOC_MAX = 512
F = jnp.float32
B = jnp.bfloat16


def dot(left, right, dims, kind):
    return lax.dot_general(left, right, (dims, ((), ())), preferred_element_type=F).astype(kind)


def gelu_slope(pre_act):
    cumulative = 0.5 * (1.0 + lax.erf(pre_act * 0.7071067811865476))
    density = jnp.exp(-0.5 * pre_act * pre_act) * 0.3989422804014327
    return cumulative + pre_act * density


def rope_tables(length):
    half = ROT // 2
    frequency = 10000.0 ** (-(jnp.arange(half, dtype=F) * 2.0) / ROT)
    angles = jnp.arange(length, dtype=F)[:, None] * frequency[None, :]
    cosine, sine = jnp.cos(angles), jnp.sin(angles)
    flat = jnp.zeros((length, 128 - ROT), F)
    zero = jnp.zeros_like(sine)
    return (
        jnp.concatenate([cosine, cosine, flat + 1.0], axis=1),
        jnp.concatenate([-sine, zero, flat], axis=1),
        jnp.concatenate([zero, sine, flat], axis=1),
    )


def turn(rows, cosine, from_above, from_below):
    head = rows[:, :128]
    above = pltpu.roll(head, 128 - ROT // 2, 1)
    below = pltpu.roll(head, ROT // 2, 1)
    turned = head * cosine + above * from_above + below * from_below
    return jnp.concatenate([turned, rows[:, 128:]], axis=1)


def block_mask(seg_col_ref, seg_row_ref, first, low, high):
    rows = first + lax.broadcasted_iota(jnp.int32, (QBLOCK, high - low), 0)
    columns = low + lax.broadcasted_iota(jnp.int32, (QBLOCK, high - low), 1)
    same = seg_col_ref[0, first : first + QBLOCK, :] == seg_row_ref[0, :, low:high]
    return (columns <= rows) & same


def key_range(first):
    return max(0, first - DOC_MAX), first + QBLOCK


def attn_forward(mixed_ref, bias_ref, cos_ref, up_ref, down_ref, col_ref, row_ref, q_ref, k_ref, v_ref, ctx_ref, lse_ref):
    size = q_ref.shape[2]
    length = q_ref.shape[1]
    scale = size ** (-0.5)
    tables = (cos_ref[...], up_ref[...], down_ref[...])
    q_ref[0] = turn(mixed_ref[0, :, :size] + bias_ref[:, :size], *tables).astype(B)
    k_ref[0] = turn(mixed_ref[0, :, size : 2 * size] + bias_ref[:, size : 2 * size], *tables).astype(B)
    v_ref[0] = (mixed_ref[0, :, 2 * size :] + bias_ref[:, 2 * size :]).astype(B)
    for first in range(0, length, QBLOCK):
        low, high = key_range(first)
        scores = dot(q_ref[0, first : first + QBLOCK], k_ref[0, low:high], ((1,), (1,)), F) * scale
        scores = jnp.where(block_mask(col_ref, row_ref, first, low, high), scores, -1e30)
        row_max = jnp.max(scores, axis=1, keepdims=True)
        expo = jnp.exp(scores - row_max)
        total = jnp.sum(expo, axis=1, keepdims=True)
        probs = (expo / total).astype(B)
        ctx_ref[0, first : first + QBLOCK] = dot(probs, v_ref[0, low:high], ((1,), (0,)), B)
        lse_ref[0, first : first + QBLOCK] = row_max + jnp.log(total)


def attn_backward(q_ref, k_ref, v_ref, grad_ref, lse_ref, cos_ref, up_ref, down_ref, col_ref, row_ref, mixed_ref, sum_ref, q_acc, k_acc, v_acc):
    size = q_ref.shape[2]
    length = q_ref.shape[1]
    scale = size ** (-0.5)
    k_acc[...] = jnp.zeros_like(k_acc)
    v_acc[...] = jnp.zeros_like(v_acc)
    for first in range(0, length, QBLOCK):
        low, high = key_range(first)
        here = slice(first, first + QBLOCK)
        scores = dot(q_ref[0, here], k_ref[0, low:high], ((1,), (1,)), F) * scale
        scores = jnp.where(block_mask(col_ref, row_ref, first, low, high), scores, -1e30)
        probs = jnp.exp(scores - lse_ref[0, here])
        v_acc[low:high] += dot(probs.astype(B), grad_ref[0, here], ((0,), (0,)), F)
        prob_grad = dot(grad_ref[0, here], v_ref[0, low:high], ((1,), (1,)), F)
        centred = jnp.sum(probs * prob_grad, axis=1, keepdims=True)
        score_grad = (probs * (prob_grad - centred)).astype(B)
        q_acc[here] = dot(score_grad, k_ref[0, low:high], ((1,), (0,)), F) * scale
        k_acc[low:high] += dot(score_grad, q_ref[0, here], ((0,), (0,)), F) * scale
    tables = (cos_ref[...], -up_ref[...], -down_ref[...])
    q_grad = turn(q_acc[...], *tables).astype(B)
    k_grad = turn(k_acc[...], *tables).astype(B)
    v_grad = v_acc[...].astype(B)
    for number, part in enumerate((q_grad, k_grad, v_grad)):
        mixed_ref[0, :, number * size : (number + 1) * size] = part
        sum_ref[0, :, number * size : (number + 1) * size] = jnp.sum(part.astype(F), axis=0, keepdims=True)


def per_seq(rows, columns):
    return pl.BlockSpec((1, rows, columns), lambda seq, *_: (seq, 0, 0))


def shared(rows, columns):
    return pl.BlockSpec((rows, columns), lambda *_: (0, 0))


MESH = pl.DeviceIdType.MESH
CHUNK = 256


def by_rows(count, work, rows=64):
    def one(number, carry):
        work(pl.ds(pl.multiple_of(number * rows, rows), rows))
        return carry

    lax.fori_loop(0, count // rows, one, 0)


def bit_of(index, bit):
    return lax.rem(lax.div(index, bit), 2)


def flip(index, mask):
    bit = 1
    while bit <= mask:
        if mask & bit:
            index = index + bit * (1 - 2 * bit_of(index, bit))
        bit *= 2
    return index


def block_order(groups):
    spread = [bit for bit in (1 << k for k in reversed(range(groups.bit_length() - 1))) if bit != PAIR]
    order = [0, PAIR]
    for bit in spread:
        order = order + [mask | bit for mask in order]
    return spread, order


def stats(rows):
    mean = jnp.mean(rows, axis=1, keepdims=True)
    center = rows - mean
    return mean, lax.rsqrt(jnp.mean(center * center, axis=1, keepdims=True) + 1e-05)


def greet(partners):
    barrier = pltpu.get_barrier_semaphore()
    for axis, index in partners:
        pl.semaphore_signal(barrier, inc=1, device_id={axis: index}, device_id_type=MESH)
    pl.semaphore_wait(barrier, len(partners))


STEPS_ONE = (
    ("x1", "i"),
    ("sh", 0, 0),
    ("sh", 0, 1),
    ("pu", 0, "o"),
    ("pu", 0, "i"),
    ("sh", 1, 1),
    ("yo", 0, 0),
    ("gst", 0),
    ("sh", 1, 0),
    ("hd", 0, "o"),
    ("x1", "o"),
    ("yo", 0, 1),
    ("re", 0),
    ("hd", 0, "i"),
    ("gst", 1),
    ("sh", 2, 0),
    ("gpo", 0, 2),
    ("gpo", 0, 0),
    ("pu", 1, "o"),
    ("pu", 1, "i"),
    ("sh", 2, 1),
    ("yo", 0, 3),
    ("x2",),
    ("yo", 2, 0),
    ("N", 0),
    ("g1", "o"),
    ("gpo", 0, 1),
    ("yo", 0, 2),
    ("yo", 1, 0),
    ("hd", 1, "i"),
    ("yo", 1, 1),
    ("g1", "i"),
    ("hd", 2, "o"),
    ("G", 0),
    ("re", 1),
    ("x3",),
    ("hd", 2, "i"),
    ("hd", 1, "o"),
    ("PJ", 0),
    ("CG", 0),
    ("g2",),
    ("pu", 2, "o"),
    ("AT", 0),
    ("gpo", 1, 2),
    ("GR", 0, 0),
    ("gpo", 2, 0),
    ("yo", 1, 3),
    ("pu", 2, "i"),
    ("gpo", 1, 0),
    ("gpo", 1, 1),
    ("GR", 0, 1),
    ("N", 1),
    ("yo", 2, 1),
    ("g3",),
    ("gpo", 2, 1),
    ("re", 2),
    ("gst", 2),
    ("PJ", 1),
    ("G", 1),
    ("CG", 1),
    ("yo", 1, 2),
    ("AT", 1),
    ("gpo", 2, 2),
    ("GR", 1, 0),
    ("yo", 2, 2),
    ("GR", 1, 1),
    ("UP", 0),
    ("yo", 2, 3),
    ("UP", 1),
)

STEPS_TWO = (
    ("ps", 2),
    ("st", 1, 1),
    ("pre", 1),
    ("yf", 0, 3),
    ("kt", 1, 1),
    ("pk", 2),
    ("po", 0, 1),
    ("yf", 0, 2),
    ("st", 0, 1),
    ("yn", 0, 1),
    ("kt", 0, 1),
    ("es", 1),
    ("st", 1, 0),
    ("po", 0, 0),
    ("pre", 0),
    ("yf", 2, 3),
    ("yn", 0, 0),
    ("zl", 0, 1),
    ("kt", 1, 0),
    ("yf", 2, 2),
    ("po", 0, 2),
    ("st", 0, 0),
    ("kt", 0, 0),
    ("po", 2, 1),
    ("sb",),
    ("es", 0),
    ("ps", 1),
    ("se", 0),
    ("zl", 0, 0),
    ("fin", 1),
    ("po", 2, 0),
    ("pk", 1),
    ("yf", 1, 3),
    ("po", 2, 2),
    ("fin", 0),
    ("fa", 0),
    ("yf", 1, 2),
    ("yn", 2, 0),
    ("yn", 2, 1),
    ("zl", 2, 1),
    ("se", 1),
    ("po", 1, 1),
    ("po", 1, 2),
    ("po", 1, 0),
    ("fe", 1),
    ("se", 2),
    ("yn", 1, 1),
    ("yn", 1, 0),
    ("zl", 1, 1),
    ("fe", 0),
    ("se", 3),
    ("zl", 1, 0),
    ("fa", 2),
    ("zl", 2, 0),
    ("se", 4),
    ("fa", 1),
)


def gather_steps(
    groups,
    qkv_ref,
    dense_ref,
    up_ref,
    down_ref,
    seg_ref,
    x_ref,
    g_ref,
    vec_ref,
    up_bias_ref,
    qv_ref,
    key_ref,
    tables_ref,
    w_relay,
    x_other,
    g_other,
    x_rel,
    g_rel,
    mlp_out,
    mixed_out,
    ctx_out,
    act_out,
    slope_out,
    send_out,
    keep_out,
    w,
    theirs_v,
    seg_v,
    sum_ref,
    bias_ref,
    send_sem,
    recv_sem,
    cross_sem,
    two_sem,
    three_sem,
    relay_sem,
    quarter_sem,
    shard_sem,
    seg_sem,
    load_sem,
    rel_sem,
    tile_sem,
    out_sem,
):
    length, width = x_ref.shape
    part = width // groups
    size = dense_ref.shape[1]
    quarter = length // 4
    me, place = lax.axis_index("dp"), lax.axis_index("tensor")
    core, side = lax.rem(place, 2), lax.div(place, 2)
    pair_to, side_to, core_to = flip(me, PAIR), flip(place, 2), flip(place, 1)
    spread, order = block_order(groups)
    half = bit_of(me, PAIR)
    hidden = act_out.shape[1]
    raw_x = attn_v = g_v = mlp_v = xr_v = grad_v = send_v = q_v = k_v = v_v = cg_v = ctx_v = mg_v = dk_v = dv_v = act_v = slope_v = col_v = tab_v = None

    def shards(owner, slot):
        at = pl.ds(pl.multiple_of(owner * 3 * size, 128), 3 * size)
        spots = [
            (qkv_ref.at[:, at], grad_v.at[pl.ds(slot * part, part), pl.ds(0, 3 * size)]),
            (dense_ref.at[owner], grad_v.at[pl.ds(2 * part, size), pl.ds(slot * part, part)]),
            (
                up_ref.at[:, pl.ds(pl.multiple_of(owner * hidden, hidden), hidden)],
                grad_v.at[pl.ds((3 + slot) * part, part)],
            ),
        ]
        for number in range(hidden // part):
            at = pl.ds(pl.multiple_of(owner * hidden + number * part, part), part)
            spots.append((down_ref.at[at], slope_v.at[slot, :, pl.ds(number * part, part)]))
        return [
            pltpu.make_async_copy(source, target, shard_sem.at[slot, number])
            for number, (source, target) in enumerate(spots)
        ]

    shard_copies = []

    def shard(group, slot):
        for copy in shard_copies[slot][(0, 2, 3)[group] : (2, 3, None)[group]]:
            copy.wait()

        def put(columns, value):
            if slot:
                theirs_v[group, :, columns] = value.astype(B)
            else:
                w[group, 0:part, columns] = value.astype(B)

        if group == 0:
            put(slice(0, 3 * size), grad_v[slot * part : (slot + 1) * part, : 3 * size])
            put(slice(3 * size, 4 * size), grad_v[2 * part : 2 * part + size, slot * part : (slot + 1) * part].T)
        elif group == 1:
            put(slice(0, hidden), grad_v[(3 + slot) * part : (4 + slot) * part])
        else:
            for number in range(hidden // part):
                at = slice(number * part, (number + 1) * part)
                put(at, slope_v[slot, :, at].T)

    across = PAIR | spread[0]
    inner = bit_of(me, PAIR) != bit_of(me, spread[0])
    outer = bit_of(me, PAIR) == bit_of(me, spread[0])
    copies = {}

    def remote(key, number, source, target, axis, index):
        copies[key] = pltpu.make_async_remote_copy(
            src_ref=source,
            dst_ref=target,
            send_sem=send_sem.at[number],
            recv_sem=recv_sem.at[number],
            device_id={axis: index},
            device_id_type=MESH,
        )
        copies[key].start()

    def rows(position):
        return pl.ds(position * part, part)

    def pair_up(group, here):
        copy = pltpu.make_async_remote_copy(
            src_ref=theirs_v.at[group],
            dst_ref=w.at[group, rows(1)],
            send_sem=send_sem.at[8 * group + 1],
            recv_sem=recv_sem.at[8 * group + 1],
            device_id={"dp": pair_to},
            device_id_type=MESH,
        )
        pl.when(here)(copy.start)

    def onward(group, position, level):
        source = w.at[group, rows(position)]
        far = position + (2 << level)
        remote(("w", far), 8 * group + far, source, w.at[group, rows(far)], "dp", flip(me, spread[level]))

    def partly(here, source, target, send, recv, to):
        copy = pltpu.make_async_remote_copy(
            src_ref=source,
            dst_ref=target,
            send_sem=send,
            recv_sem=recv,
            device_id={"dp": to},
            device_id_type=MESH,
        )
        pl.when(here)(copy.start)

    across_to = flip(me, across)

    def straight(group):
        partly(inner, theirs_v.at[group], w.at[group, rows(3)], cross_sem.at[group, 0], three_sem.at[group], across_to)

    def hand(group, here=None):
        source, sem = w.at[group, rows(0)], cross_sem.at[group, 1]
        if here is not inner:
            partly(outer, source, w_relay.at[group, rows(0)], sem, relay_sem.at[group, 0], pair_to)
        if here is not outer:
            partly(inner, source, w_relay.at[group, rows(1)], sem, relay_sem.at[group, 1], across_to)

    def relay(group):
        source = w.at[group, rows(1)]
        partly(
            inner, source, w_relay.at[group, rows(2)], cross_sem.at[group, 2], relay_sem.at[group, 2], across_to
        )

    def pass_on(group, *numbers):
        for number in numbers:
            source, target = w_relay.at[group, rows(number)], 3 if number == 2 else 2
            here = pltpu.make_async_remote_copy(
                src_ref=source,
                dst_ref=source,
                send_sem=relay_sem.at[group, number],
                recv_sem=relay_sem.at[group, number],
                device_id={"dp": pair_to},
                device_id_type=MESH,
            )
            pl.when(inner)(here.wait_recv)
            partly(
                inner,
                source,
                w.at[group, rows(target)],
                cross_sem.at[group, 3 + number],
                (three_sem if target == 3 else two_sem).at[group],
                across_to if number == 0 else pair_to,
            )

    def to_pair(key, source, target, here):
        if key not in quarters:
            quarters[key] = pltpu.make_async_remote_copy(
                src_ref=source,
                dst_ref=target,
                send_sem=quarter_sem.at[key, 0],
                recv_sem=quarter_sem.at[key, 1],
                device_id={"dp": pair_to},
                device_id_type=MESH,
            )
        pl.when(here)(quarters[key].start)

    quarters = {}
    arrived = set()

    def arrive(group, position):
        if (group, position) not in arrived:
            arrived.add((group, position))
            sem = {2: two_sem.at[group], 3: three_sem.at[group]}.get(position, recv_sem.at[8 * group + position])
            pltpu.make_async_remote_copy(
                src_ref=w.at[group, rows(position)],
                dst_ref=w.at[group, rows(position)],
                send_sem=sem,
                recv_sem=sem,
                device_id={"dp": pair_to},
                device_id_type=MESH,
            ).wait_recv()

    spot = pl.ds(pl.multiple_of(core * (2 * quarter) + side * quarter, quarter), quarter)
    pair_rows = pl.ds(pl.multiple_of(core * (2 * quarter), quarter), 2 * quarter)
    levels = len(spread)
    assert levels == 2

    def over_tiles(source, raw, number, work):
        def load(tile, slot):
            here = pl.ds(pl.multiple_of(tile * CHUNK, CHUNK), CHUNK)
            return pltpu.make_async_copy(source.at[here], raw.at[slot], load_sem.at[number, slot])

        load(0, 0).start()

        def one(tile, carry):
            slot = lax.rem(tile, 2)

            @pl.when(tile + 1 < length // CHUNK)
            def _():
                load(tile + 1, 1 - slot).start()

            load(tile, slot).wait()
            work(tile, slot)
            return carry

        lax.fori_loop(0, length // CHUNK, one, 0)

    outs = {}

    def leave(key, source, target, sem):
        outs[key] = pltpu.make_async_copy(source, target, sem)
        outs[key].start()

    def left(*keys):
        for key in keys:
            outs.pop(key).wait()

    def normalise(seq):
        if seq:
            copies["x3"].wait_recv()
            left(("x", 0))

        def work(tile, slot):
            here = pl.ds(pl.multiple_of(tile * CHUNK, CHUNK), CHUNK)
            both = pl.ds(pl.multiple_of(seq * length + tile * CHUNK, CHUNK), CHUNK)
            raw, attn_to, mlp_to, x_to = raw_x.at[slot], attn_v.at[here], mlp_v.at[both], xr_v.at[here]

            def some(at):
                mean, inverse = stats(raw[at].astype(F))
                for position, mask in enumerate(order):
                    to = slice(position * part, (position + 1) * part)
                    there = pl.ds(pl.multiple_of(flip(me, mask) * part, part), part)
                    piece = raw[at, there]
                    normed = (piece.astype(F) - mean) * inverse
                    attn_to[at, to] = (normed * vec_ref[0:1, there] + vec_ref[1:2, there]).astype(B)
                    mlp_to[at, to] = (normed * vec_ref[2:3, there] + vec_ref[3:4, there]).astype(B)
                    x_to[at, to] = piece

            by_rows(CHUNK, some)

        over_tiles(x_other if seq else x_ref, raw_x, 0, work)
        both = pl.ds(seq * length, length)
        leave(("x", seq), xr_v, x_rel.at[both], rel_sem.at[seq, 0])
        leave(("m", seq), mlp_v.at[both], mlp_out.at[both], rel_sem.at[seq, 2])

    def arrange_grad(seq):
        if seq:
            copies["g3"].wait_recv()
            left(("g", 0))
        else:
            bias_ref[...] = jnp.zeros_like(bias_ref)

        def work(tile, slot):
            here = pl.ds(pl.multiple_of(tile * CHUNK, CHUNK), CHUNK)
            raw, g_to = raw_x.at[slot], g_v.at[here]

            def some(at):
                if seq == 0:
                    bias_ref[...] += jnp.sum(raw[at].astype(F), axis=0, keepdims=True)
                for position, mask in enumerate(order):
                    to = slice(position * part, (position + 1) * part)
                    there = pl.ds(pl.multiple_of(flip(me, mask) * part, part), part)
                    g_to[at, to] = raw[at, there]

            by_rows(CHUNK, some, 32)

        over_tiles(g_other if seq else g_ref, raw_x, 1, work)
        leave(("g", seq), g_v, g_rel.at[pl.ds(seq * length, length)], rel_sem.at[seq, 1])

    def whole_group(group):
        if ("out", group) not in arrived:
            arrived.add(("out", group))
            for position in range(1, 8):
                arrive(group, position)

    def project(seq):
        whole_group(0)
        key_row = jnp.concatenate([key_ref[pl.ds(half, 1)], jnp.zeros((1, size - ROT), F)], axis=1)
        offsets = (qv_ref[half, 0:1], key_row, qv_ref[half, 1:2])
        if seq == 0:
            left("tables")

        def one(tile, carry):
            here = pl.ds(pl.multiple_of(tile * CHUNK, CHUNK), CHUNK)
            mixed = dot(attn_v[here], w[0, :, : 3 * size], ((1,), (0,)), F)
            tables = (tab_v[0, here], tab_v[1, here], tab_v[2, here])
            q_v[here] = turn(mixed[:, :size] + offsets[0], *tables).astype(B)
            k_v[here] = turn(mixed[:, size : 2 * size] + offsets[1], *tables).astype(B)
            v_v[here] = (mixed[:, 2 * size :] + offsets[2]).astype(B)
            return carry

        lax.fori_loop(0, length // CHUNK, one, 0)

    def project_grad(seq):
        whole_group(0)

        def some(at):
            cg_v[at] = dot(g_v[at], w[0, :, 3 * size :], ((1,), (0,)), B)

        by_rows(length, some, CHUNK)

    def attend(seq):
        if seq:
            copies["seg"].wait()
            left(("mg", 0), ("ctx", 0))
        scale = size ** (-0.5)
        ids = seg_ref[...] if seq == 0 else seg_v[...]
        col_v[...] = jnp.broadcast_to(ids.astype(F), (8, length)).T

        def clear(here):
            dk_v[here] = jnp.zeros((128, size), F)
            dv_v[here] = jnp.zeros((128, size), F)

        by_rows(length, clear, 128)
        def queries(first, low, reach):
            here, keys = pl.ds(first, QBLOCK), pl.ds(low, reach)
            scores = dot(q_v[here], k_v[keys], ((1,), (1,)), F) * scale
            row_ids = first + lax.broadcasted_iota(jnp.int32, (QBLOCK, reach), 0)
            key_ids = low + lax.broadcasted_iota(jnp.int32, (QBLOCK, reach), 1)
            row = seg_ref[:, keys] if seq == 0 else seg_v[:, keys]
            allowed = (key_ids <= row_ids) & (col_v[here, 0:1] == row.astype(F))
            scores = jnp.where(allowed, scores, -1e30)
            expo = jnp.exp(scores - jnp.max(scores, axis=1, keepdims=True))
            probs = expo / jnp.sum(expo, axis=1, keepdims=True)
            low_probs = probs.astype(B)
            ctx_v[here] = dot(low_probs, v_v[keys], ((1,), (0,)), B)
            dv_v[keys] += dot(low_probs, cg_v[here], ((0,), (0,)), F)
            prob_grad = dot(cg_v[here], v_v[keys], ((1,), (1,)), F)
            centred = jnp.sum(probs * prob_grad, axis=1, keepdims=True)
            score_grad = (probs * (prob_grad - centred)).astype(B)
            q_grad = dot(score_grad, k_v[keys], ((1,), (0,)), F) * scale
            tables = (tab_v[0, here], -tab_v[1, here], -tab_v[2, here])
            mg_v[here, :size] = turn(q_grad, *tables).astype(B)
            dk_v[keys] += dot(score_grad, q_v[here], ((0,), (0,)), F) * scale

        for first in range(0, DOC_MAX, QBLOCK):
            queries(first, 0, first + QBLOCK)

        def later(number, carry):
            low = pl.multiple_of(number * QBLOCK - DOC_MAX, QBLOCK)
            queries(pl.multiple_of(number * QBLOCK, QBLOCK), low, DOC_MAX + QBLOCK)
            return carry

        lax.fori_loop(DOC_MAX // QBLOCK, length // QBLOCK, later, 0)

        def turn_back(here):
            tables = (tab_v[0, here], -tab_v[1, here], -tab_v[2, here])
            mg_v[here, size : 2 * size] = turn(dk_v[here], *tables).astype(B)
            mg_v[here, 2 * size :] = dv_v[here].astype(B)

        by_rows(length, turn_back)
        if seq == 0:
            sum_ref[...] = jnp.zeros_like(sum_ref)

        def add_sums(here):
            sum_ref[...] += jnp.sum(mg_v[here].astype(F), axis=0, keepdims=True)

        by_rows(length, add_sums, 128)
        both = pl.ds(seq * length, length)
        leave(("mg", seq), mg_v, mixed_out.at[both], rel_sem.at[seq, 3])
        leave(("ctx", seq), ctx_v, ctx_out.at[both], rel_sem.at[seq, 4])

    def attn_grads(seq, low, high):
        def one(block, carry):
            here = pl.ds(pl.multiple_of(block * CHUNK, CHUNK), CHUNK)
            qkv = dot(attn_v[:, here], mg_v[...], ((0,), (0,)), F)
            dense = dot(g_v[:, here], ctx_v[...], ((0,), (0,)), F)
            if seq == 0:
                grad_v[here, : 3 * size] = qkv
                grad_v[here, 3 * size :] = dense
            else:
                grad_v[here, : 3 * size] += qkv
                grad_v[here, 3 * size :] += dense
            return carry

        lax.fori_loop(low // CHUNK, high // CHUNK, one, 0)

    def up(low, high):
        def store(tile, slot):
            here = pl.ds(pl.multiple_of(tile * CHUNK, CHUNK), CHUNK)
            return (
                pltpu.make_async_copy(act_v.at[slot], act_out.at[here], tile_sem.at[0, slot]),
                pltpu.make_async_copy(slope_v.at[slot], slope_out.at[here], tile_sem.at[1, slot]),
            )

        def one(tile, carry):
            slot = lax.rem(tile, 2)
            here = pl.ds(pl.multiple_of(tile * CHUNK, CHUNK), CHUNK)
            pre = dot(mlp_v[here], w[1], ((1,), (0,)), F) + up_bias_ref[:, pl.ds(pl.multiple_of(half * hidden, hidden), hidden)]

            @pl.when(tile >= low + 2)
            def _():
                for copy in store(tile - 2, slot):
                    copy.wait()

            slope_v[slot] = pre
            act_to, slope_to = act_v.at[slot], slope_v.at[slot]

            def some(at):
                pre = slope_to[at]
                cumulative = 0.5 * (1.0 + lax.erf(pre * 0.7071067811865476))
                density = jnp.exp(-0.5 * pre * pre) * 0.3989422804014327
                act_to[at] = (pre * cumulative).astype(B)
                slope_to[at] = cumulative + pre * density

            by_rows(CHUNK, some)
            for copy in store(tile, slot):
                copy.start()
            return carry

        lax.fori_loop(low, high, one, 0)
        for tile in (high - 2, high - 1):
            for copy in store(tile, tile % 2):
                copy.wait()

    kinds = {"o": outer, "i": inner}

    def relay_on(group):
        arrive(group, 1)
        relay(group)

    def send_y(group, position):
        if position:
            arrive(group, position)
        onward(group, position, 1)

    def to_side(name, number, array):
        quarters[number].wait_recv()
        remote(name + "2", 24 + number, array.at[spot], array.at[spot], "tensor", side_to)

    def to_core(name, array):
        copies[name + "2"].wait_recv()
        remote(name + "3", 26 + (name == "g"), array.at[pair_rows], array.at[pair_rows], "tensor", core_to)

    def gradients(seq, number):
        middle = width // 2
        attn_grads(seq, *((0, middle) if number else (middle, width)))
        if seq and number:
            leave("keep", grad_v.at[pl.ds(0, middle)], keep_out, out_sem.at[4])
        elif seq:
            def narrow(at):
                send_v[at] = grad_v.at[pl.ds(middle, middle)][at].astype(B)

            by_rows(middle, narrow, 128)
            leave("send", send_v, send_out, out_sem.at[3])

    def lift(seq):
        whole_group(1)
        up(seq * length // CHUNK, (seq + 1) * length // CHUNK)

    stages = {
        "sh": shard,
        "pu": lambda group, kind: pair_up(group, kinds[kind]),
        "gst": straight,
        "hd": lambda group, kind: hand(group, kinds[kind]),
        "re": relay_on,
        "yo": send_y,
        "gpo": pass_on,
        "x1": lambda kind: to_pair(0, x_ref.at[spot], x_other.at[spot], kinds[kind]),
        "g1": lambda kind: to_pair(1, g_ref.at[spot], g_other.at[spot], kinds[kind]),
        "x2": lambda: to_side("x", 0, x_other),
        "g2": lambda: to_side("g", 1, g_other),
        "x3": lambda: to_core("x", x_other),
        "g3": lambda: to_core("g", g_other),
        "N": normalise,
        "G": arrange_grad,
        "PJ": project,
        "CG": project_grad,
        "AT": attend,
        "GR": gradients,
        "UP": lift,
    }
    def begin(*private):
        nonlocal raw_x, attn_v, g_v, mlp_v, xr_v, grad_v, send_v, q_v, k_v
        nonlocal v_v, cg_v, ctx_v, mg_v, dk_v, dv_v, act_v, slope_v, col_v, tab_v
        (
            raw_x,
            attn_v,
            g_v,
            mlp_v,
            xr_v,
            grad_v,
            send_v,
            q_v,
            k_v,
            v_v,
            cg_v,
            ctx_v,
            mg_v,
            dk_v,
            dv_v,
            act_v,
            slope_v,
            col_v,
            tab_v,
        ) = private
        shard_copies.extend([shards(half, 0), shards(1 - half, 1)])
        for number in range(3 + hidden // part):
            for slot in (1, 0):
                shard_copies[slot][number].start()
        leave("tables", tables_ref, tab_v, out_sem.at[0])
        greet(
            [("dp", flip(me, mask)) for mask in [PAIR, across] + spread] + [("tensor", side_to), ("tensor", core_to)]
        )
        copies["seg"] = pltpu.make_async_remote_copy(
            src_ref=seg_ref,
            dst_ref=seg_v,
            send_sem=seg_sem.at[0],
            recv_sem=seg_sem.at[1],
            device_id={"dp": pair_to},
            device_id_type=MESH,
        )
        copies["seg"].start()

    def close():
        left(*list(outs))
        for name in ("x2", "x3", "g2", "g3"):
            copies[name].wait_send()
        for key in (0, 1):
            quarters[key].wait_send()

    def finish():
        def gone(sem):
            pltpu.make_async_remote_copy(
                src_ref=w.at[0, rows(0)],
                dst_ref=w.at[0, rows(0)],
                send_sem=sem,
                recv_sem=sem,
                device_id={"dp": pair_to},
                device_id_type=MESH,
            ).wait_send()

        for group in range(3):
            for position in (1, 4, 5, 6, 7):
                gone(send_sem.at[8 * group + position])
            gone(cross_sem.at[group, 1])

            @pl.when(inner)
            def _():
                for number in (0, 2, 3, 4, 5):
                    gone(cross_sem.at[group, number])

    return begin, stages, whole_group, close, finish


def scatter_steps(
    groups,
    steps,
    earlier,
    whole_group,
    attn_send,
    attn_keep,
    x_rel,
    g_rel,
    mlp_in,
    mixed_grad,
    context,
    activation,
    slope,
    x_ref,
    g_ref,
    vec_ref,
    mixed_sum,
    bias_sum,
    block_out,
    input_grad,
    qkv_out,
    dense_out,
    up_out,
    down_out,
    far_in,
    far_two,
    y_recv,
    z_recv,
    z_relay,
    c_recv,
    x_recv,
    e_recv,
    small_out,
    w,
    small_recv,
    load_sem,
    tile_sem,
    ys_sem,
    yr_sem,
    zs_sem,
    zr_sem,
    zl_sem,
    zf_sem,
    two_sem,
    ps_sem,
    pr_sem,
    cs_sem,
    cr_sem,
    xs_sem,
    xr_sem,
    es_sem,
    er_sem,
    fs_sem,
    fr_sem,
    emit_sem,
    ss_sem,
    sr_sem,
    out_sem,
    act_v,
    pre_v,
    tile_v,
    col_v,
    slope_t,
    mix_t,
    ctx_v,
    keep_v,
    y_send,
    z_send,
    p_send,
    y_stage,
    c_send,
    c_stage,
    r_stage,
    x_send,
    hold_v,
    mean_v,
    inverse_v,
    sum_v,
    small_v,
):
    length, width = x_ref.shape
    part = width // groups
    size = context.shape[1]
    hidden = activation.shape[1]
    quarter = length // 4
    me, place = lax.axis_index("dp"), lax.axis_index("tensor")
    core, side, half = lax.rem(place, 2), lax.div(place, 2), bit_of(me, PAIR)
    pair_to, side_to, core_to = flip(me, PAIR), flip(place, 2), flip(place, 1)
    spread, order = block_order(groups)
    z_to, y_to = [flip(me, bit) for bit in spread]
    across_to = flip(z_to, PAIR)
    inner = bit_of(me, PAIR) != bit_of(me, spread[0])
    outer = bit_of(me, PAIR) == bit_of(me, spread[0])

    def remote(source, target, send, recv, axis, index):
        return pltpu.make_async_remote_copy(
            src_ref=source, dst_ref=target, send_sem=send, recv_sem=recv, device_id={axis: index}, device_id_type=MESH
        )

    def span(position, count=1):
        return pl.ds(position * part, count * part)

    def step(index, amount):
        return pl.ds(pl.multiple_of(index * amount, amount), amount)

    def y_copy(group, position):
        source = attn_send if group == 0 else y_send
        here = step(position, part) if not isinstance(position, int) else span(position)
        return remote(
            source.at[here], y_recv.at[group, here], ys_sem.at[group, position], yr_sem.at[group, position], "dp", y_to
        )

    slot_of = (0, 0, 1)

    def z_copy(group, position):
        source, sem = z_send.at[slot_of[group], span(position - 2)], zs_sem.at[group, position - 2]
        onward = (
            remote(source, far_two.at[group], sem, two_sem.at[group], "dp", across_to)
            if position == 3
            else remote(source, z_relay.at[group, span(2)], sem, zl_sem.at[group, 2], "dp", across_to)
        )
        aside = remote(
            source, z_relay.at[group, span(position - 2)], sem, zl_sem.at[group, position - 2], "dp", pair_to
        )
        return onward, aside

    def forward(group, number):
        target = 0 if number == 2 else number
        arrived = remote(
            z_relay.at[group, span(number)],
            z_recv.at[group, span(target)],
            zf_sem.at[group, number],
            zl_sem.at[group, number],
            "dp",
            pair_to,
        )
        return arrived, remote(
            z_relay.at[group, span(number)],
            z_recv.at[group, span(target)],
            zf_sem.at[group, number],
            zr_sem.at[group, target],
            "dp",
            pair_to if number == 2 else across_to,
        )

    def pass_on(group, *numbers):
        @pl.when(inner)
        def _():
            for number in numbers:
                arrived, copy = forward(group, number)
                arrived.wait_recv()
                copy.start()

    def z_arrived(group, position):
        return remote(
            z_relay.at[group, span(position)],
            z_recv.at[group, span(position)],
            zf_sem.at[group, position],
            zr_sem.at[group, position],
            "dp",
            pair_to,
        )

    def p_copy(group):
        return remote(
            p_send.at[slot_of[group]], far_in.at[group], ps_sem.at[group], pr_sem.at[group], "dp", pair_to
        )

    emitted = {}

    def emit(group, kind, block, owner):
        copies = []
        for number in range(hidden // part):
            at = pl.ds(number * part, part)
            if group == 2 or (group == 0 and number == 3):
                block[:, at] = block[:, at].T
            if group == 1:
                target = up_out.at[:, pl.ds(pl.multiple_of(owner * hidden + number * part, part), part)]
            elif group == 2:
                target = down_out.at[pl.ds(pl.multiple_of(owner * hidden + number * part, part), part)]
            elif number == 3:
                target = dense_out.at[owner]
            else:
                target = qkv_out.at[:, pl.ds(pl.multiple_of(owner * 3 * size + number * part, part), part)]
            copies.append(pltpu.make_async_copy(block.at[:, at], target, emit_sem.at[group, kind, number]))
            copies[-1].start()
        emitted[(group, kind)] = copies

    def emit_near(group):
        emit(group, 0, keep_v.at[slot_of[group], span(0)], half)

    def emit_far(group):
        block = (
            hold_v.at[1, 1, :, pl.ds(0, hidden)],
            keep_v.at[0, span(1)],
            hold_v.at[1, 1, :, pl.ds(hidden, hidden)],
        )[group]
        p_copy(group).wait_recv()
        staged(far_in.at[group])

        def widen(at):
            block[at] = y_stage[at].astype(F)

        def add(at):
            block[at] += y_stage[at].astype(F)

        by_rows(part, widen)

        @pl.when(inner)
        def _():
            remote(
                p_send.at[0], far_two.at[group], two_sem.at[group], two_sem.at[group], "dp", across_to
            ).wait_recv()
            staged(far_two.at[group])
            by_rows(part, add)

        emit(group, 1, block, 1 - half)

    def staged(source):
        copy = pltpu.make_async_copy(source, y_stage, load_sem.at[6])
        copy.start()
        copy.wait()

    def y_far(group, position):
        if group == 0:
            need(5)
        y_copy(group, position).wait_recv()
        staged(y_recv.at[group, span(position)])
        onward, aside = z_copy(group, position)
        if group == 1:
            z_copy(0, position)[0].wait_send()
        kept, target = keep_v.at[slot_of[group], span(position)], z_send.at[slot_of[group], span(position - 2)]

        def add(at):
            target[at] = (kept[at] + y_stage[at].astype(F)).astype(B)

        by_rows(part, add)
        pl.when(inner)(onward.start)
        pl.when(outer)(aside.start)

    def y_near(group, position):
        if group == 0:
            need(5)
        y_copy(group, position).wait_recv()
        staged(y_recv.at[group, span(position)])
        kept, target = keep_v.at[slot_of[group], span(position)], p_send.at[slot_of[group]]
        if position == 1 and group == 1:
            p_copy(0).wait_send()

        def add(at):
            total = kept[at] + y_stage[at].astype(F)
            kept[at] = total
            if position == 1:
                target[at] = total.astype(B)

        by_rows(part, add)
        if position == 1:
            pl.when(outer)(p_copy(group).start)

    def z_last(group, position):
        kept, target = keep_v.at[slot_of[group], span(position)], p_send.at[slot_of[group]]

        def add(at):
            total = kept[at] + y_stage[at].astype(F)
            if position == 1:
                target[at] = total.astype(B)
            else:
                kept[at] = total

        def add_all():
            z_arrived(group, position).wait_recv()
            staged(z_recv.at[group, span(position)])
            by_rows(part, add)

        if position == 1:

            @pl.when(inner)
            def _():
                add_all()
                p_copy(group).start()

        else:
            add_all()
            emit_near(group)

    loads = [
        None,
        None,
        None,
        pltpu.make_async_copy(activation, act_v, load_sem.at[3]),
        pltpu.make_async_copy(context, ctx_v, load_sem.at[4]),
        pltpu.make_async_copy(attn_keep, keep_v.at[0], load_sem.at[5]),
    ]
    for number in (3, 5, 4):
        loads[number].start()
    loaded = set()

    def need(*numbers):
        for number in numbers:
            if number not in loaded:
                loaded.add(number)
                loads[number].wait()

    for position in (3, 2, 1, 0):
        y_copy(0, position).start()

    small_v[...] = jnp.zeros_like(small_v)

    def pre_load(tile, slot):
        here = step(tile, CHUNK)
        return (
            pltpu.make_async_copy(g_rel.at[here], tile_v.at[step(slot, CHUNK)], tile_sem.at[0, slot]),
            pltpu.make_async_copy(slope.at[here], slope_t.at[slot], tile_sem.at[1, slot]),
        )

    sum_v[...] = jnp.zeros_like(sum_v)

    def pre_tiles(seq):
        whole_group(2)
        low, high = seq * length // CHUNK, (seq + 1) * length // CHUNK
        for copy in pre_load(low, 0):
            copy.start()

        def one(tile, carry):
            slot = lax.rem(tile, 2)

            @pl.when(tile + 1 < high)
            def _():
                for copy in pre_load(tile + 1, 1 - slot):
                    copy.start()

            for copy in pre_load(tile, slot):
                copy.wait()
            grad = (dot(tile_v[step(slot, CHUNK)], w[2], ((1,), (0,)), F) * slope_t[slot]).astype(B)
            pre_v[step(tile, CHUNK)] = grad
            sum_v[...] += jnp.sum(grad.astype(F), axis=0, keepdims=True)
            return carry

        lax.fori_loop(low, high, one, 0)

    tall = 2 * quarter
    blocks = width // CHUNK

    def c_copy(which, seq, block):
        here = step(block, CHUNK)
        return remote(
            c_send.at[:, here],
            c_recv.at[which, seq, :, here],
            cs_sem.at[which, seq, block],
            cr_sem.at[which, seq, block],
            "tensor",
            core_to,
        )

    def x_copy(which, seq):
        return remote(
            x_send.at[which, seq], x_recv.at[which, seq], xs_sem.at[which, seq], xr_sem.at[which, seq], "tensor", side_to
        )

    def e_copy(which):
        return remote(x_send.at[which, 1], e_recv.at[which], es_sem.at[which], er_sem.at[which], "dp", pair_to)

    sent_tiles = []

    def send_tile(which, seq):
        begin, block_of = tile_of[which]
        whole_group(2)
        if which:
            need(3, 4)
        start = pl.multiple_of(seq * length + (1 - core) * tall, tall)
        begin(start)

        def one(block, carry):
            value = block_of(start, block)
            if sent_tiles:
                c_copy(*sent_tiles[-1], block).wait_send()
            c_send[:, step(block, CHUNK)] = value.astype(B)
            c_copy(which, seq, block).start()
            return carry

        lax.fori_loop(0, blocks, one, 0)
        sent_tiles.append((which, seq))

    def c_load(which, seq, block, slot):
        return pltpu.make_async_copy(c_recv.at[which, seq, :, step(block, CHUNK)], c_stage.at[slot], tile_sem.at[2, slot])

    def keep_tile(which, seq):
        begin, block_of = tile_of[which]
        start = pl.multiple_of(seq * length + core * tall, tall)
        begin(start)
        c_copy(which, seq, 0).wait_recv()
        c_load(which, seq, 0, 0).start()

        def one(block, carry):
            slot = lax.rem(block, 2)
            value = block_of(start, block)

            @pl.when(block + 1 < blocks)
            def _():
                c_copy(which, seq, block + 1).wait_recv()
                c_load(which, seq, block + 1, 1 - slot).start()

            c_load(which, seq, block, slot).wait()
            r_stage[...] = value + c_stage[slot].astype(F)
            here = step(block, CHUNK)
            hold_v[which, seq, :, here] = r_stage[step(side, quarter)]
            x_send[which, seq, :, here] = r_stage[step(1 - side, quarter)].astype(B)
            return carry

        lax.fori_loop(0, blocks, one, 0)
        x_copy(which, seq).start()

    def blend_begin(start):
        copies = (
            pltpu.make_async_copy(x_rel.at[pl.ds(start, tall)], tile_v, tile_sem.at[3, 0]),
            pltpu.make_async_copy(mixed_grad.at[pl.ds(start, tall)], mix_t, tile_sem.at[3, 1]),
        )
        for copy in copies:
            copy.start()
        for copy in copies:
            copy.wait()
        for slot in range(2):
            mean, inverse = stats(tile_v[span_rows(slot)].astype(F))
            mean_v[span_rows(slot)] = jnp.broadcast_to(mean, (CHUNK, 128))
            inverse_v[span_rows(slot)] = jnp.broadcast_to(inverse, (CHUNK, 128))

    def span_rows(slot):
        return pl.ds(slot * CHUNK, CHUNK)

    def natural_block(position):
        result = me
        for level, bit in enumerate([PAIR] + spread):
            flipped = lax.rem(lax.div(position, 1 << level), 2)
            result = result + bit * (1 - 2 * bit_of(me, bit)) * flipped
        return result

    def blend_block(start, block):
        here = step(block, CHUNK)
        there = step(natural_block(block), part)
        attn_grad = dot(mix_t[...], w[0, here, : 3 * size], ((1,), (1,)), F)
        mlp_grad = dot(pre_v[pl.ds(start, tall)], w[1, here, :], ((1,), (1,)), F)
        mean, inverse = mean_v[...], inverse_v[...]
        mean = jnp.concatenate([mean] * (CHUNK // 128), axis=1)
        inverse = jnp.concatenate([inverse] * (CHUNK // 128), axis=1)
        normed = (tile_v[:, here].astype(F) - mean) * inverse
        small_v[0:1, there] += jnp.sum(attn_grad * normed, axis=0, keepdims=True)
        small_v[1:2, there] += jnp.sum(attn_grad, axis=0, keepdims=True)
        small_v[2:3, there] += jnp.sum(mlp_grad * normed, axis=0, keepdims=True)
        small_v[3:4, there] += jnp.sum(mlp_grad, axis=0, keepdims=True)
        return attn_grad * vec_ref[0:1, there] + mlp_grad * vec_ref[2:3, there]

    def product(columns, right, group, positions, sent, old=None):
        count = len(positions)
        base = positions[0]
        sign = positions[1] - positions[0] if count > 1 else 1

        def load(number, slot):
            return pltpu.make_async_copy(
                columns.at[:, step(base + sign * number, part)], col_v.at[slot], tile_sem.at[4, slot]
            )

        load(0, 0).start()

        def one(number, carry):
            slot = lax.rem(number, 2)

            @pl.when(number + 1 < count)
            def _():
                load(number + 1, 1 - slot).start()

            load(number, slot).wait()
            value = dot(col_v[slot], right[...], ((0,), (0,)), F)
            position = base + sign * number
            if sent:
                if old is not None:
                    y_copy(old, position - groups // 2).wait_send()
                y_send[step(position - groups // 2, part)] = value.astype(B)
                y_copy(group, position - groups // 2).start()
            else:
                keep_v[slot_of[group], step(position, part)] = value
            return carry

        lax.fori_loop(0, count, one, 0)

    def small_begin():
        small_v[4:5] = bias_sum[...]
        small_v[5:6, step(half, hidden)] = sum_v[...]
        small_v[6:7, pl.ds(pl.multiple_of(half * (width // 2), width // 2), 3 * size)] = mixed_sum[...]
        small_copy(0).start()

    rounds = [("dp", flip(me, bit)) for bit in [PAIR] + spread] + [("tensor", side_to), ("tensor", core_to)]

    def small_copy(number):
        return remote(small_v, small_recv.at[number], ss_sem.at[number], sr_sem.at[number], *rounds[number])

    def small_end(number):
        small_copy(number).wait()
        if number < 3:
            small_v[...] += small_recv[number]
        else:
            small_v[0:4] += small_recv[number, 0:4]
        if number + 1 < len(rounds):
            small_copy(number + 1).start()

    def branch_begin(start):
        pass

    def branch_block(start, block):
        here, rows = step(block, CHUNK), pl.ds(start, tall)
        return dot(ctx_v[rows], w[0, here, 3 * size :], ((1,), (1,)), F) + dot(
            act_v[rows], w[2, here, :], ((1,), (1,)), F
        )

    def read_stage(source):
        copy = pltpu.make_async_copy(source, tile_v.at[pl.ds(0, quarter)], load_sem.at[6])
        copy.start()
        copy.wait()

    def e_start(which):
        x_copy(which, 1).wait_recv()
        x_copy(which, 1).wait_send()
        read_stage(x_recv.at[which, 1])

        def one(block, carry):
            here = step(block, CHUNK)
            x_send[which, 1, :, here] = (hold_v[which, 1, :, here] + tile_v[0:quarter, here].astype(F)).astype(B)
            return carry

        lax.fori_loop(0, blocks, one, 0)
        e_copy(which).start()

    def gather_own(which):
        x_copy(which, 0).wait_recv()
        read_stage(x_recv.at[which, 0])

        def one(block, carry):
            here = step(block, CHUNK)
            hold_v[which, 0, :, here] += tile_v[0:quarter, here].astype(F)
            return carry

        lax.fori_loop(0, blocks, one, 0)

    def spot(c, s):
        return pl.ds(pl.multiple_of(c * tall + s * quarter, quarter), quarter)

    def position_of(block, shifted=False):
        result = 0
        for level, bit in enumerate([PAIR] + spread):
            mine = bit_of(me, bit)
            if shifted and bit == PAIR:
                mine = 1 - mine
            result = result + (1 << level) * ((1 - mine) if block & bit else mine)
        return result

    def finish(which, out_ref):
        if len(sent_tiles) == 4:
            sent_tiles.append(None)
            for block in range(blocks):
                c_copy(*sent_tiles[3], block).wait_send()
        gather_own(which)
        e_copy(which).wait_recv()
        copies = [
            pltpu.make_async_copy(e_recv.at[which], tile_v.at[pl.ds(0, quarter)], load_sem.at[6]),
            pltpu.make_async_copy(x_ref.at[spot(core, side)], tile_v.at[pl.ds(quarter, quarter)], load_sem.at[7]),
        ]
        if which == 0:
            copies.append(pltpu.make_async_copy(g_ref.at[spot(core, side)], x_send.at[0, 0], load_sem.at[8]))
            x_copy(0, 0).wait_send()
        for copy in copies:
            copy.start()
        for copy in copies:
            copy.wait()
        here = pl.ds(which * quarter, quarter)
        held, sent, own_x, g_rows = hold_v.at[which, 0], tile_v, tile_v.at[pl.ds(quarter, quarter)], x_send.at[0, 0]
        target = c_send.at[here]

        def total(at, block):
            mine = held[at, step(position_of(block), part)]
            return mine + sent[at, step(position_of(block, True), part)].astype(F)

        def some_grad(at):
            rows = own_x[at].astype(F)
            mean, inverse = stats(rows)
            normed = (rows - mean) * inverse
            blend = jnp.concatenate([total(at, block) for block in range(groups)], axis=1)
            inner_grad = (
                blend
                - jnp.mean(blend, axis=1, keepdims=True)
                - normed * jnp.mean(blend * normed, axis=1, keepdims=True)
            )
            target[at] = (g_rows[at].astype(F) + inner_grad * inverse).astype(B)

        def some_out(at):
            for block in range(groups):
                cut = slice(block * part, (block + 1) * part)
                bias = vec_ref[4:5, cut] + vec_ref[5:6, cut]
                target[at, cut] = (own_x[at, cut].astype(F) + total(at, block) + bias).astype(B)

        by_rows(quarter, some_out if which else some_grad)
        first = remote(
            c_send.at[here], out_ref.at[spot(core, side)], fs_sem.at[which, 0], fr_sem.at[which, 0], "tensor", side_to
        )
        second = remote(
            c_send.at[here], out_ref.at[spot(core, side)], fs_sem.at[which, 1], fr_sem.at[which, 1], "tensor", core_to
        )
        own = pltpu.make_async_copy(c_send.at[here], out_ref.at[spot(core, side)], out_sem.at[3 + which])
        for copy in (first, second, own):
            copy.start()
        return first, second, own

    def finish_end(which, out_ref, copies):
        first, second, own = copies
        first.wait_recv()
        third = remote(
            out_ref.at[spot(core, 1 - side)],
            out_ref.at[spot(core, 1 - side)],
            fs_sem.at[which, 2],
            fr_sem.at[which, 2],
            "tensor",
            core_to,
        )
        third.start()
        return [first.wait_send, second.wait, third.wait, own.wait]

    tile_of = ((blend_begin, blend_block), (branch_begin, branch_block))
    outs, finished, ends = (input_grad, block_out), {}, []

    def do_product(group, sent):
        columns, right = ((mlp_in, pre_v), (g_rel, act_v))[group - 1]
        if group == 2:
            need(3)
        if group == 1 and not sent:
            for copy in emitted[(0, 0)]:
                copy.wait()
        product(columns, right, group, (7, 6, 5, 4) if sent else (3, 2, 1, 0), sent, 2 if sent and group == 1 else None)

    def do_finish(which):
        finished[which] = finish(which, outs[which])

    def do_end(which):
        ends.extend(finish_end(which, outs[which], finished[which]))

    stages = {
        "pre": pre_tiles,
        "st": send_tile,
        "kt": keep_tile,
        "ps": lambda group: do_product(group, True),
        "pk": lambda group: do_product(group, False),
        "yf": y_far,
        "yn": y_near,
        "po": pass_on,
        "zl": z_last,
        "es": e_start,
        "fin": do_finish,
        "fe": do_end,
        "fa": emit_far,
        "sb": small_begin,
        "se": small_end,
    }
    for name, *numbers in steps:
        (stages if name in stages else earlier)[name](*numbers)
    small_out[...] = small_v[...]
    for end in ends:
        end()
    for group in range(3):
        if group:
            p_copy(group).wait_send()
            for position in (2, 3):
                z_copy(group, position)[0].wait_send()
        for position in range(4):
            if group != 2:
                y_copy(group, position).wait_send()
        for kind in range(2):
            if group or kind:
                for copy in emitted[(group, kind)]:
                    copy.wait()

        @pl.when(inner)
        def _():
            for number in range(3):
                forward(group, number)[1].wait_send()

    for which in range(2):
        e_copy(which).wait_send()
        if which:
            x_copy(which, 0).wait_send()


def layer_kernel(
    groups,
    scoped_one,
    scoped_two,
    qkv_ref,
    dense_ref,
    up_ref,
    down_ref,
    seg_ref,
    x_ref,
    g_ref,
    vec_ref,
    up_bias_ref,
    qv_ref,
    key_ref,
    tables_ref,
    block_out,
    input_grad,
    qkv_out,
    dense_out,
    up_out,
    down_out,
    w_relay,
    x_other,
    g_other,
    x_rel,
    g_rel,
    mlp_out,
    mixed_out,
    ctx_out,
    act_out,
    slope_out,
    send_out,
    keep_out,
    far_in,
    far_two,
    y_recv,
    z_recv,
    z_relay,
    c_recv,
    x_recv,
    e_recv,
    small_out,
    w,
    theirs_v,
    seg_v,
    sum_ref,
    bias_ref,
    small_recv,
    send_sem,
    recv_sem,
    cross_sem,
    two_sem,
    three_sem,
    relay_sem,
    quarter_sem,
    shard_sem,
    seg_sem,
    load_sem,
    rel_sem,
    tile_sem,
    out_sem,
    s_load_sem,
    s_tile_sem,
    s_ys_sem,
    s_yr_sem,
    s_zs_sem,
    s_zr_sem,
    s_zl_sem,
    s_zf_sem,
    s_two_sem,
    s_ps_sem,
    s_pr_sem,
    s_cs_sem,
    s_cr_sem,
    s_xs_sem,
    s_xr_sem,
    s_es_sem,
    s_er_sem,
    s_fs_sem,
    s_fr_sem,
    s_emit_sem,
    s_ss_sem,
    s_sr_sem,
    s_out_sem,
):
    begin, earlier, whole_group, close, finish = gather_steps(
        groups,
        qkv_ref,
        dense_ref,
        up_ref,
        down_ref,
        seg_ref,
        x_ref,
        g_ref,
        vec_ref,
        up_bias_ref,
        qv_ref,
        key_ref,
        tables_ref,
        w_relay,
        x_other,
        g_other,
        x_rel,
        g_rel,
        mlp_out,
        mixed_out,
        ctx_out,
        act_out,
        slope_out,
        send_out,
        keep_out,
        w,
        theirs_v,
        seg_v,
        sum_ref,
        bias_ref,
        send_sem,
        recv_sem,
        cross_sem,
        two_sem,
        three_sem,
        relay_sem,
        quarter_sem,
        shard_sem,
        seg_sem,
        load_sem,
        rel_sem,
        tile_sem,
        out_sem,
    )

    def first(*private):
        begin(*private)
        for name, *numbers in STEPS_ONE:
            earlier[name](*numbers)
        close()

    def second(*private):
        scatter_steps(
            groups,
            STEPS_TWO,
            earlier,
            whole_group,
            send_out,
            keep_out,
            x_rel,
            g_rel,
            mlp_out,
            mixed_out,
            ctx_out,
            act_out,
            slope_out,
            x_ref,
            g_ref,
            vec_ref,
            sum_ref,
            bias_ref,
            block_out,
            input_grad,
            qkv_out,
            dense_out,
            up_out,
            down_out,
            far_in,
            far_two,
            y_recv,
            z_recv,
            z_relay,
            c_recv,
            x_recv,
            e_recv,
            small_out,
            w,
            small_recv,
            s_load_sem,
            s_tile_sem,
            s_ys_sem,
            s_yr_sem,
            s_zs_sem,
            s_zr_sem,
            s_zl_sem,
            s_zf_sem,
            s_two_sem,
            s_ps_sem,
            s_pr_sem,
            s_cs_sem,
            s_cr_sem,
            s_xs_sem,
            s_xr_sem,
            s_es_sem,
            s_er_sem,
            s_fs_sem,
            s_fr_sem,
            s_emit_sem,
            s_ss_sem,
            s_sr_sem,
            s_out_sem,
            *private,
        )
        finish()

    pl.run_scoped(first, *scoped_one)
    pl.run_scoped(second, *scoped_two)


def body_narrow(
    tokens,
    segment_ids,
    out_grad,
    attn_norm_gain,
    attn_norm_bias,
    mlp_norm_gain,
    mlp_norm_bias,
    qkv_weight,
    qv_bias,
    key_bias,
    dense_weight,
    dense_bias,
    up_weight,
    up_bias,
    down_weight,
    down_bias,
    *,
    groups,
    ways,
):
    length, width = tokens.shape[1:]
    heads, size = qkv_weight.shape[1] // 2, qkv_weight.shape[3]
    part = width // groups
    me = lax.axis_index("dp")
    half = (me // PAIR) % 2
    place = lax.axis_index("tensor")
    core, side = place % 2, place // 2
    spread = [bit for bit in (1 << k for k in reversed(range(groups.bit_length() - 1))) if bit != PAIR]

    def swap(array, bit):
        return lax.ppermute(array, "dp", [(i, i ^ bit) for i in range(groups)])

    def cross(array, bit):
        return lax.ppermute(array, "tensor", [(i, i ^ bit) for i in range(ways)])

    def pick(array, index, axis, count=2):
        rows = array.shape[axis] // count
        return lax.dynamic_slice_in_dim(array, index * rows, rows, axis)

    def join(mine, theirs, index, axis):
        pair = jnp.concatenate([mine, theirs], axis=axis)
        turned = jnp.concatenate([theirs, mine], axis=axis)
        return jnp.where(index == 0, pair, turned)

    order = [0, PAIR]
    for bit in spread:
        order = order + [mask | bit for mask in order]
    inverse = [order.index(mask) for mask in range(groups)]

    def arranged(array):
        return jnp.concatenate(
            [lax.dynamic_slice_in_dim(array, (mask ^ me) * part, part, array.ndim - 1) for mask in order], axis=-1
        )

    def natural(array):
        table = jnp.asarray(inverse, jnp.int32)
        return jnp.concatenate(
            [lax.dynamic_slice_in_dim(array, table[block ^ me] * part, part, array.ndim - 1) for block in range(groups)],
            axis=-1,
        )

    def gather(shard, halves_axis, axis):
        shard = shard.astype(B)
        mine, theirs = pick(shard, half, halves_axis), pick(shard, 1 - half, halves_axis)
        pieces = [jnp.concatenate([mine, swap(theirs, PAIR)], axis=axis)]
        for bit in spread:
            pieces = pieces + [swap(piece, bit) for piece in pieces]
        return jnp.concatenate(pieces, axis=axis)

    def scatter(product, axis, halves_axis):
        count = groups // 2
        sent = swap(product(count, groups, B), spread[-1])
        held = product(0, count, F) + sent.astype(F)
        for bit in reversed(spread[:-1]):
            keep, send = jnp.split(held, 2, axis=axis)
            held = keep + swap(send.astype(B), bit).astype(F)
        keep, send = jnp.split(held, 2, axis=axis)
        return join(keep, swap(send, PAIR), half, halves_axis)

    def share_rows(rows):
        rows = join(rows, cross(rows, 2), side, 0)
        return join(rows, cross(rows, 1), core, 0)

    def own_rows(array, axis):
        return pick(pick(array, core, axis), side, axis)

    def partner_rows(array):
        return share_rows(swap(own_rows(array, 0), PAIR))

    def total_rows(partial):
        held = pick(partial, core, 1).astype(F) + cross(pick(partial, 1 - core, 1), 1).astype(F)
        held = pick(held, side, 1) + cross(pick(held, 1 - side, 1).astype(B), 2).astype(F)
        sent = swap(held[1].astype(B), PAIR).astype(F)
        rows = sent.shape[0]
        sent = jnp.flip(sent.reshape(rows, groups // 2, 2, part), axis=2).reshape(rows, width)
        return held[0] + sent

    own_x, own_g = tokens[0], out_grad[0]
    w_up = gather(up_weight, 1, 0)
    x_other = partner_rows(own_x)
    w_down = gather(down_weight, 0, 1)
    g_other = partner_rows(own_g)
    w_qkv = gather(qkv_weight.reshape(part, 2, -1), 1, 0).reshape(width, -1)
    w_dense = gather(dense_weight.reshape(2 * heads * size, part), 0, 1)

    x_pair = arranged(jnp.concatenate([own_x, x_other], axis=0))
    g_pair = arranged(jnp.concatenate([own_g, g_other], axis=0))
    gains = [arranged(v) for v in (attn_norm_gain, attn_norm_bias, mlp_norm_gain, mlp_norm_bias)]

    def hat(rows):
        rows = rows.astype(F)
        center = rows - jnp.mean(rows, axis=-1, keepdims=True)
        inverse_dev = lax.rsqrt(jnp.mean(center * center, axis=-1, keepdims=True) + 1e-05)
        return center * inverse_dev, inverse_dev

    normed, _ = hat(x_pair)
    attn_in = (normed * gains[0] + gains[1]).astype(B)
    mlp_in = (normed * gains[2] + gains[3]).astype(B)

    up_here = pick(up_bias, half, 0)
    up_pre = dot(mlp_in, w_up, ((1,), (0,)), F) + up_here
    activation = jax.nn.gelu(up_pre, approximate=False).astype(B)
    middle = width // 2

    def columns(array, low, high):
        return array[:, low * part : high * part]

    down_shard = scatter(lambda low, high, kind: dot(activation, columns(g_pair, low, high), ((0,), (0,)), kind), 1, 0)
    pre_grad = (dot(g_pair, w_down, ((1,), (1,)), F) * gelu_slope(up_pre)).astype(B)
    up_shard = scatter(lambda low, high, kind: dot(columns(mlp_in, low, high), pre_grad, ((0,), (0,)), kind), 0, 1)
    up_bias_sum = jnp.sum(pre_grad.astype(F), axis=0)

    seg_other = swap(segment_ids[0], PAIR)
    seg = jnp.stack([segment_ids[0], seg_other])
    seg_col, seg_row = seg[:, :, None], seg[:, None, :]
    qv_here, key_here = pick(qv_bias, half, 0), pick(key_bias, half, 0)
    key_full = jnp.concatenate([key_here, jnp.zeros((heads, size - ROT), F)], axis=1)
    offsets = jnp.stack([qv_here[:, 0], key_full, qv_here[:, 1]], axis=1).reshape(heads, 1, 3 * size)
    mixed = dot(attn_in, w_qkv, ((1,), (0,)), F).reshape(2, length, heads, 3 * size)
    tables = rope_tables(length)
    table_specs = [shared(length, 128)] * 3
    seg_specs = [per_seq(length, 1), per_seq(1, length)]
    context_grad = dot(g_pair, w_dense, ((1,), (1,)), B).reshape(2, length, heads, size)
    contexts, mixed_grads, mixed_sums = [], [], []
    head_shape = jax.ShapeDtypeStruct((2, length, size), B)
    for head in range(heads):
        q, k, v, context, lse = pl.pallas_call(
            attn_forward,
            grid=(2,),
            in_specs=[per_seq(length, 3 * size), shared(1, 3 * size)] + table_specs + seg_specs,
            out_specs=[per_seq(length, size)] * 4 + [per_seq(length, 1)],
            out_shape=[head_shape] * 4 + [jax.ShapeDtypeStruct((2, length, 1), F)],
            name="attn_forward",
        )(mixed[:, :, head], offsets[head], *tables, seg_col, seg_row)
        mixed_grad, mixed_sum = pl.pallas_call(
            attn_backward,
            grid=(2,),
            in_specs=[per_seq(length, size)] * 4 + [per_seq(length, 1)] + table_specs + seg_specs,
            out_specs=[per_seq(length, 3 * size), per_seq(1, 3 * size)],
            out_shape=[
                jax.ShapeDtypeStruct((2, length, 3 * size), B),
                jax.ShapeDtypeStruct((2, 1, 3 * size), F),
            ],
            scratch_shapes=[pltpu.VMEM((length, size), F)] * 3,
            name="attn_backward",
        )(q, k, v, context_grad[:, :, head], lse, *tables, seg_col, seg_row)
        contexts.append(context.reshape(2 * length, size))
        mixed_grads.append(mixed_grad.reshape(2 * length, 3 * size))
        mixed_sums.append(jnp.sum(mixed_sum, axis=(0, 1)))
    context = jnp.concatenate(contexts, axis=1)
    mixed_grad = jnp.concatenate(mixed_grads, axis=1)
    mixed_sum = jnp.stack(mixed_sums).reshape(heads, 3, size)

    qkv_shard = scatter(lambda low, high, kind: dot(columns(attn_in, low, high), mixed_grad, ((0,), (0,)), kind), 0, 1)
    dense_shard = scatter(lambda low, high, kind: dot(context, columns(g_pair, low, high), ((0,), (0,)), kind), 1, 0)

    branch = dot(context, w_dense, ((1,), (0,)), F) + dot(activation, w_down, ((1,), (0,)), F)
    branch_rows = total_rows(branch.astype(B).reshape(2, length, width))
    x_rows, g_rows = own_rows(x_pair[:length], 0), own_rows(g_pair[:length], 0)
    out_rows = (x_rows.astype(F) + branch_rows + arranged(dense_bias) + arranged(down_bias)).astype(B)
    block_out = share_rows(natural(out_rows))

    attn_in_grad = dot(mixed_grad, w_qkv, ((1,), (1,)), F)
    mlp_in_grad = dot(pre_grad, w_up, ((1,), (1,)), F)
    blend = (attn_in_grad * gains[0] + mlp_in_grad * gains[2]).astype(B)
    blend_rows = total_rows(blend.reshape(2, length, width))
    hat_rows, inverse_rows = hat(x_rows)
    inner = (
        blend_rows
        - jnp.mean(blend_rows, axis=-1, keepdims=True)
        - hat_rows * jnp.mean(blend_rows * hat_rows, axis=-1, keepdims=True)
    )
    input_grad = share_rows(natural((g_rows.astype(F) + inner * inverse_rows).astype(B)))

    norm_sums = natural(
        jnp.stack(
            [
                jnp.sum(attn_in_grad * normed, axis=0),
                jnp.sum(attn_in_grad, axis=0),
                jnp.sum(mlp_in_grad * normed, axis=0),
                jnp.sum(mlp_in_grad, axis=0),
            ]
        )
    ).reshape(-1)
    bias_sum = jnp.sum(own_g.astype(F), axis=0)

    def slotted(array):
        zero = jnp.zeros_like(array)
        return join(array, zero, half, 0)

    small = [norm_sums, bias_sum, slotted(up_bias_sum), slotted(mixed_sum).reshape(-1)]
    sizes = [s.shape[0] for s in small]
    flat = jnp.concatenate(small)
    for bit in [1 << k for k in range(groups.bit_length() - 1)]:
        flat = flat + swap(flat, bit)
    ends = [sum(sizes[: i + 1]) for i in range(len(sizes))]
    norms = flat[: ends[0]]
    for bit in [1 << k for k in range(ways.bit_length() - 1)]:
        norms = norms + cross(norms, bit)
    norms = norms.reshape(4, width)
    bias_grad = flat[ends[0] : ends[1]]
    up_bias_grad = flat[ends[1] : ends[2]]
    mixed_bias = flat[ends[2] :].reshape(2 * heads, 3, size)
    qv_grad = jnp.stack([mixed_bias[:, 0], mixed_bias[:, 2]], axis=1)
    key_bias_grad = mixed_bias[:, 1, :ROT]

    return (
        block_out[None],
        input_grad[None],
        norms[0],
        norms[1],
        norms[2],
        norms[3],
        qkv_shard.reshape(qkv_weight.shape),
        qv_grad,
        key_bias_grad,
        dense_shard.reshape(dense_weight.shape),
        bias_grad,
        up_shard,
        up_bias_grad,
        down_shard,
        bias_grad,
    )


def body(
    tokens,
    segment_ids,
    out_grad,
    attn_norm_gain,
    attn_norm_bias,
    mlp_norm_gain,
    mlp_norm_bias,
    qkv_weight,
    qv_bias,
    key_bias,
    dense_weight,
    dense_bias,
    up_weight,
    up_bias,
    down_weight,
    down_bias,
    *,
    groups,
    ways,
):
    length, width = tokens.shape[1:]
    heads, size = qkv_weight.shape[1] // 2, qkv_weight.shape[3]
    assert heads == 1 and ways == 4
    part = width // groups
    hidden = up_weight.shape[1] // 2
    count = 2 * length
    me = lax.axis_index("dp")
    half = (me // PAIR) % 2
    shape = jax.ShapeDtypeStruct

    def pick(array, index, axis):
        rows = array.shape[axis] // 2
        return lax.dynamic_slice_in_dim(array, index * rows, rows, axis)

    vectors = jnp.stack([attn_norm_gain, attn_norm_bias, mlp_norm_gain, mlp_norm_bias, dense_bias, down_bias])
    own_x, own_g = tokens[0], out_grad[0]

    tables = rope_tables(length)
    columns = hidden
    half_width = width // 2
    vmem, hbm = pl.BlockSpec(memory_space=pltpu.VMEM), pl.BlockSpec(memory_space=pl.ANY)
    quarter = length // 4
    tall, blocks = 2 * quarter, width // CHUNK
    dma = pltpu.SemaphoreType.DMA
    scoped_one = [
        pltpu.VMEM((2, CHUNK, width), B),
        pltpu.VMEM((length, width), B),
        pltpu.VMEM((length, width), B),
        pltpu.VMEM((count, width), B),
        pltpu.VMEM((length, width), B),
        pltpu.VMEM((width, columns), F),
        pltpu.VMEM((half_width, columns), B),
        pltpu.VMEM((length, size), B),
        pltpu.VMEM((length, size), B),
        pltpu.VMEM((length, size), B),
        pltpu.VMEM((length, size), B),
        pltpu.VMEM((length, size), B),
        pltpu.VMEM((length, 3 * size), B),
        pltpu.VMEM((length, size), F),
        pltpu.VMEM((length, size), F),
        pltpu.VMEM((2, CHUNK, hidden), B),
        pltpu.VMEM((2, CHUNK, hidden), F),
        pltpu.VMEM((length, 8), F),
        pltpu.VMEM((3, length, 128), F),
    ]
    scoped_two = [
        pltpu.VMEM((count, hidden), B),
        pltpu.VMEM((count, hidden), B),
        pltpu.VMEM((tall, width), B),
        pltpu.VMEM((2, count, part), B),
        pltpu.VMEM((2, CHUNK, hidden), F),
        pltpu.VMEM((tall, 3 * size), B),
        pltpu.VMEM((count, size), B),
        pltpu.VMEM((2, half_width, columns), F),
        pltpu.VMEM((half_width, columns), B),
        pltpu.VMEM((2, half_width // 2, columns), B),
        pltpu.VMEM((2, part, columns), B),
        pltpu.VMEM((part, columns), B),
        pltpu.VMEM((tall, width), B),
        pltpu.VMEM((2, tall, CHUNK), B),
        pltpu.VMEM((tall, CHUNK), F),
        pltpu.VMEM((2, 2, quarter, width), B),
        pltpu.VMEM((2, 2, quarter, width), F),
        pltpu.VMEM((tall, 128), F),
        pltpu.VMEM((tall, 128), F),
        pltpu.VMEM((1, hidden), F),
        pltpu.VMEM((8, width), F),
    ]
    block_out, input_grad, qkv_shard, dense_shard, up_shard, down_shard, *_, small = pl.pallas_call(
        functools.partial(layer_kernel, groups, scoped_one, scoped_two),
        in_specs=[hbm] * 4 + [vmem] + [hbm] * 2 + [vmem] * 4 + [hbm],
        out_specs=[hbm] * 26 + [vmem],
        out_shape=[
            shape((length, width), B),
            shape((length, width), B),
            shape((part, 6 * size), F),
            shape(dense_weight.shape, F),
            shape(up_weight.shape, F),
            shape(down_weight.shape, F),
            shape((3, 3 * part, columns), B),
            shape((length, width), B),
            shape((length, width), B),
            shape((count, width), B),
            shape((count, width), B),
            shape((count, width), B),
            shape((count, 3 * size), B),
            shape((count, size), B),
            shape((count, hidden), B),
            shape((count, hidden), F),
            shape((half_width, columns), B),
            shape((half_width, columns), F),
            shape((3, part, columns), B),
            shape((3, part, columns), B),
            shape((3, half_width, columns), B),
            shape((3, half_width // 2, columns), B),
            shape((3, 3 * part, columns), B),
            shape((2, 2, tall, width), B),
            shape((2, 2, quarter, width), B),
            shape((2, quarter, width), B),
            shape((8, width), F),
        ],
        scratch_shapes=[
            pltpu.VMEM((3, width, columns), B),
            pltpu.VMEM((3, part, columns), B),
            pltpu.VMEM((1, length), jnp.int32),
            pltpu.VMEM((1, 3 * size), F),
            pltpu.VMEM((1, width), F),
            pltpu.VMEM((5, 8, width), F),
            dma((28,)),
            dma((28,)),
            dma((3, 6)),
            dma((3,)),
            dma((3,)),
            dma((3, 3)),
            dma((2, 2)),
            dma((2, 3 + hidden // part)),
            dma((2,)),
            dma((2, 2)),
            dma((2, 5)),
            dma((2, 2)),
            dma((5,)),
            dma((9,)),
            dma((5, 2)),
            dma((3, 4)),
            dma((3, 4)),
            dma((3, 2)),
            dma((3, 2)),
            dma((3, 3)),
            dma((3, 3)),
            dma((3,)),
            dma((3,)),
            dma((3,)),
            dma((2, 2, blocks)),
            dma((2, 2, blocks)),
            dma((2, 2)),
            dma((2, 2)),
            dma((2,)),
            dma((2,)),
            dma((2, 3)),
            dma((2, 3)),
            dma((3, 2, hidden // part)),
            dma((5,)),
            dma((5,)),
            dma((5,)),
        ],
        compiler_params=pltpu.CompilerParams(
            collective_id=0, has_side_effects=True, vmem_limit_bytes=67043328
        ),
        cost_estimate=pl.CostEstimate(flops=100 * 10**9, bytes_accessed=2 * 10**8, transcendentals=10**7),
        name="layer",
    )(
        qkv_weight.reshape(part, 6 * size),
        dense_weight,
        up_weight,
        down_weight,
        segment_ids,
        own_x,
        own_g,
        vectors,
        up_bias.reshape(1, 2 * hidden),
        qv_bias,
        key_bias,
        jnp.stack(tables),
    )

    norms, bias_grad, up_bias_grad = small[0:4], small[4], small[5]
    mixed_bias = small[6].reshape(2, width // 2)[:, : 3 * size].reshape(2, 3, size)
    qv_grad = jnp.stack([mixed_bias[:, 0], mixed_bias[:, 2]], axis=1)
    key_bias_grad = mixed_bias[:, 1, :ROT]

    return (
        block_out[None],
        input_grad[None],
        norms[0],
        norms[1],
        norms[2],
        norms[3],
        qkv_shard.reshape(qkv_weight.shape),
        qv_grad,
        key_bias_grad,
        dense_shard,
        bias_grad,
        up_shard,
        up_bias_grad,
        down_shard,
        bias_grad,
    )


def solution(mesh):
    placed = (
        P("dp", None, None),
        P("dp", None),
        P("dp", None, None),
        P(),
        P(),
        P(),
        P(),
        P("dp", "tensor", None, None),
        P("tensor", None, None),
        P("tensor", None),
        P("tensor", None, "dp"),
        P(),
        P("dp", "tensor"),
        P("tensor"),
        P("tensor", "dp"),
        P(),
    )

    def whole(*arrays):
        groups, ways = mesh.shape["dp"], mesh.shape["tensor"]
        part = arrays[0].shape[2] // groups
        chosen = body_narrow if part % 128 or groups != 8 else body
        return chosen(*arrays, groups=groups, ways=ways)

    return jax.shard_map(
        whole,
        mesh=mesh,
        in_specs=placed,
        out_specs=(
            P("dp", None, None),
            P("dp", None, None),
            P(),
            P(),
            P(),
            P(),
            P("dp", "tensor", None, None),
            P("tensor", None, None),
            P("tensor", None),
            P("tensor", None, "dp"),
            P(),
            P("dp", "tensor"),
            P("tensor"),
            P("tensor", "dp"),
            P(),
        ),
        check_vma=False,
    )
```

```python
import functools

import jax
import jax.numpy as jnp
from jax import lax
from jax.experimental import pallas as pl
from jax.experimental.pallas import tpu as pltpu
from jax.sharding import PartitionSpec as P

ROT = 64
PAIR = 2
QBLOCK = 256
DOC_MAX = 512
F = jnp.float32
B = jnp.bfloat16


def dot(left, right, dims, kind):
    return lax.dot_general(left, right, (dims, ((), ())), preferred_element_type=F).astype(kind)


def gelu_slope(pre_act):
    cumulative = 0.5 * (1.0 + lax.erf(pre_act * 0.7071067811865476))
    density = jnp.exp(-0.5 * pre_act * pre_act) * 0.3989422804014327
    return cumulative + pre_act * density


def rope_tables(length):
    half = ROT // 2
    frequency = 10000.0 ** (-(jnp.arange(half, dtype=F) * 2.0) / ROT)
    angles = jnp.arange(length, dtype=F)[:, None] * frequency[None, :]
    cosine, sine = jnp.cos(angles), jnp.sin(angles)
    flat = jnp.zeros((length, 128 - ROT), F)
    zero = jnp.zeros_like(sine)
    return (
        jnp.concatenate([cosine, cosine, flat + 1.0], axis=1),
        jnp.concatenate([-sine, zero, flat], axis=1),
        jnp.concatenate([zero, sine, flat], axis=1),
    )


def turn(rows, cosine, from_above, from_below):
    head = rows[:, :128]
    above = pltpu.roll(head, 128 - ROT // 2, 1)
    below = pltpu.roll(head, ROT // 2, 1)
    turned = head * cosine + above * from_above + below * from_below
    return jnp.concatenate([turned, rows[:, 128:]], axis=1)


def block_mask(seg_col_ref, seg_row_ref, first, low, high):
    rows = first + lax.broadcasted_iota(jnp.int32, (QBLOCK, high - low), 0)
    columns = low + lax.broadcasted_iota(jnp.int32, (QBLOCK, high - low), 1)
    same = seg_col_ref[0, first : first + QBLOCK, :] == seg_row_ref[0, :, low:high]
    return (columns <= rows) & same


def key_range(first):
    return max(0, first - DOC_MAX), first + QBLOCK


def attn_forward(mixed_ref, bias_ref, cos_ref, up_ref, down_ref, col_ref, row_ref, q_ref, k_ref, v_ref, ctx_ref, lse_ref):
    size = q_ref.shape[2]
    length = q_ref.shape[1]
    scale = size ** (-0.5)
    tables = (cos_ref[...], up_ref[...], down_ref[...])
    q_ref[0] = turn(mixed_ref[0, :, :size] + bias_ref[:, :size], *tables).astype(B)
    k_ref[0] = turn(mixed_ref[0, :, size : 2 * size] + bias_ref[:, size : 2 * size], *tables).astype(B)
    v_ref[0] = (mixed_ref[0, :, 2 * size :] + bias_ref[:, 2 * size :]).astype(B)
    for first in range(0, length, QBLOCK):
        low, high = key_range(first)
        scores = dot(q_ref[0, first : first + QBLOCK], k_ref[0, low:high], ((1,), (1,)), F) * scale
        scores = jnp.where(block_mask(col_ref, row_ref, first, low, high), scores, -1e30)
        row_max = jnp.max(scores, axis=1, keepdims=True)
        expo = jnp.exp(scores - row_max)
        total = jnp.sum(expo, axis=1, keepdims=True)
        probs = (expo / total).astype(B)
        ctx_ref[0, first : first + QBLOCK] = dot(probs, v_ref[0, low:high], ((1,), (0,)), B)
        lse_ref[0, first : first + QBLOCK] = row_max + jnp.log(total)


def attn_backward(q_ref, k_ref, v_ref, grad_ref, lse_ref, cos_ref, up_ref, down_ref, col_ref, row_ref, mixed_ref, sum_ref, q_acc, k_acc, v_acc):
    size = q_ref.shape[2]
    length = q_ref.shape[1]
    scale = size ** (-0.5)
    k_acc[...] = jnp.zeros_like(k_acc)
    v_acc[...] = jnp.zeros_like(v_acc)
    for first in range(0, length, QBLOCK):
        low, high = key_range(first)
        here = slice(first, first + QBLOCK)
        scores = dot(q_ref[0, here], k_ref[0, low:high], ((1,), (1,)), F) * scale
        scores = jnp.where(block_mask(col_ref, row_ref, first, low, high), scores, -1e30)
        probs = jnp.exp(scores - lse_ref[0, here])
        v_acc[low:high] += dot(probs.astype(B), grad_ref[0, here], ((0,), (0,)), F)
        prob_grad = dot(grad_ref[0, here], v_ref[0, low:high], ((1,), (1,)), F)
        centred = jnp.sum(probs * prob_grad, axis=1, keepdims=True)
        score_grad = (probs * (prob_grad - centred)).astype(B)
        q_acc[here] = dot(score_grad, k_ref[0, low:high], ((1,), (0,)), F) * scale
        k_acc[low:high] += dot(score_grad, q_ref[0, here], ((0,), (0,)), F) * scale
    tables = (cos_ref[...], -up_ref[...], -down_ref[...])
    q_grad = turn(q_acc[...], *tables).astype(B)
    k_grad = turn(k_acc[...], *tables).astype(B)
    v_grad = v_acc[...].astype(B)
    for number, part in enumerate((q_grad, k_grad, v_grad)):
        mixed_ref[0, :, number * size : (number + 1) * size] = part
        sum_ref[0, :, number * size : (number + 1) * size] = jnp.sum(part.astype(F), axis=0, keepdims=True)


def per_seq(rows, columns):
    return pl.BlockSpec((1, rows, columns), lambda seq, *_: (seq, 0, 0))


def shared(rows, columns):
    return pl.BlockSpec((rows, columns), lambda *_: (0, 0))


MESH = pl.DeviceIdType.MESH
CHUNK = 256


def by_rows(count, work, rows=64):
    def one(number, carry):
        work(pl.ds(pl.multiple_of(number * rows, rows), rows))
        return carry

    lax.fori_loop(0, count // rows, one, 0)


def bit_of(index, bit):
    return lax.rem(lax.div(index, bit), 2)


def flip(index, mask):
    bit = 1
    while bit <= mask:
        if mask & bit:
            index = index + bit * (1 - 2 * bit_of(index, bit))
        bit *= 2
    return index


def block_order(groups):
    spread = [bit for bit in (1 << k for k in reversed(range(groups.bit_length() - 1))) if bit != PAIR]
    order = [0, PAIR]
    for bit in spread:
        order = order + [mask | bit for mask in order]
    return spread, order


def stats(rows):
    mean = jnp.mean(rows, axis=1, keepdims=True)
    center = rows - mean
    return mean, lax.rsqrt(jnp.mean(center * center, axis=1, keepdims=True) + 1e-05)


def greet(partners):
    barrier = pltpu.get_barrier_semaphore()
    for axis, index in partners:
        pl.semaphore_signal(barrier, inc=1, device_id={axis: index}, device_id_type=MESH)
    pl.semaphore_wait(barrier, len(partners))


STEPS_ONE = (
    ("x1", "i"),
    ("sh", 0, 0),
    ("sh", 0, 1),
    ("pu", 0, "o"),
    ("pu", 0, "i"),
    ("sh", 1, 1),
    ("yo", 0, 0),
    ("gst", 0),
    ("sh", 1, 0),
    ("hd", 0, "o"),
    ("x1", "o"),
    ("yo", 0, 1),
    ("re", 0),
    ("hd", 0, "i"),
    ("gst", 1),
    ("sh", 2, 0),
    ("gpo", 0, 2),
    ("gpo", 0, 0),
    ("pu", 1, "o"),
    ("pu", 1, "i"),
    ("sh", 2, 1),
    ("yo", 0, 3),
    ("x2",),
    ("yo", 2, 0),
    ("N", 0),
    ("g1", "o"),
    ("gpo", 0, 1),
    ("yo", 0, 2),
    ("yo", 1, 0),
    ("hd", 1, "i"),
    ("yo", 1, 1),
    ("g1", "i"),
    ("hd", 2, "o"),
    ("G", 0),
    ("re", 1),
    ("x3",),
    ("hd", 2, "i"),
    ("hd", 1, "o"),
    ("PJ", 0),
    ("CG", 0),
    ("g2",),
    ("pu", 2, "o"),
    ("AT", 0),
    ("gpo", 1, 2),
    ("GR", 0, 0),
    ("gpo", 2, 0),
    ("yo", 1, 3),
    ("pu", 2, "i"),
    ("gpo", 1, 0),
    ("gpo", 1, 1),
    ("GR", 0, 1),
    ("N", 1),
    ("yo", 2, 1),
    ("g3",),
    ("gpo", 2, 1),
    ("re", 2),
    ("gst", 2),
    ("PJ", 1),
    ("G", 1),
    ("CG", 1),
    ("yo", 1, 2),
    ("AT", 1),
    ("gpo", 2, 2),
    ("GR", 1, 0),
    ("yo", 2, 2),
    ("GR", 1, 1),
    ("UP", 0),
    ("yo", 2, 3),
    ("UP", 1),
)

STEPS_TWO = (
    ("ps", 2),
    ("st", 1, 1),
    ("pre", 1),
    ("yf", 0, 3),
    ("kt", 1, 1),
    ("pk", 2),
    ("po", 0, 1),
    ("yf", 0, 2),
    ("st", 0, 1),
    ("yn", 0, 1),
    ("kt", 0, 1),
    ("es", 1),
    ("st", 1, 0),
    ("po", 0, 0),
    ("pre", 0),
    ("yf", 2, 3),
    ("yn", 0, 0),
    ("zl", 0, 1),
    ("kt", 1, 0),
    ("yf", 2, 2),
    ("po", 0, 2),
    ("st", 0, 0),
    ("kt", 0, 0),
    ("po", 2, 1),
    ("sb",),
    ("es", 0),
    ("ps", 1),
    ("se", 0),
    ("zl", 0, 0),
    ("fin", 1),
    ("po", 2, 0),
    ("pk", 1),
    ("yf", 1, 3),
    ("po", 2, 2),
    ("fin", 0),
    ("fa", 0),
    ("yf", 1, 2),
    ("yn", 2, 0),
    ("yn", 2, 1),
    ("zl", 2, 1),
    ("se", 1),
    ("po", 1, 1),
    ("po", 1, 2),
    ("po", 1, 0),
    ("fe", 1),
    ("se", 2),
    ("yn", 1, 1),
    ("yn", 1, 0),
    ("zl", 1, 1),
    ("fe", 0),
    ("se", 3),
    ("zl", 1, 0),
    ("fa", 2),
    ("zl", 2, 0),
    ("se", 4),
    ("fa", 1),
)


def gather_steps(
    groups,
    qkv_ref,
    dense_ref,
    up_ref,
    down_ref,
    seg_ref,
    x_ref,
    g_ref,
    vec_ref,
    up_bias_ref,
    qv_ref,
    key_ref,
    tables_ref,
    w_relay,
    x_other,
    g_other,
    x_rel,
    g_rel,
    mlp_out,
    mixed_out,
    ctx_out,
    act_out,
    slope_out,
    send_out,
    keep_out,
    w,
    theirs_v,
    seg_v,
    sum_ref,
    bias_ref,
    send_sem,
    recv_sem,
    cross_sem,
    two_sem,
    three_sem,
    relay_sem,
    quarter_sem,
    shard_sem,
    seg_sem,
    load_sem,
    rel_sem,
    tile_sem,
    out_sem,
):
    length, width = x_ref.shape
    part = width // groups
    size = dense_ref.shape[1]
    quarter = length // 4
    me, place = lax.axis_index("dp"), lax.axis_index("tensor")
    core, side = lax.rem(place, 2), lax.div(place, 2)
    pair_to, side_to, core_to = flip(me, PAIR), flip(place, 2), flip(place, 1)
    spread, order = block_order(groups)
    half = bit_of(me, PAIR)
    hidden = act_out.shape[1]
    raw_x = attn_v = g_v = mlp_v = xr_v = grad_v = send_v = q_v = k_v = v_v = cg_v = ctx_v = mg_v = dk_v = dv_v = act_v = slope_v = col_v = tab_v = None

    def shards(owner, slot):
        at = pl.ds(pl.multiple_of(owner * 3 * size, 128), 3 * size)
        spots = [
            (qkv_ref.at[:, at], grad_v.at[pl.ds(slot * part, part), pl.ds(0, 3 * size)]),
            (dense_ref.at[owner], grad_v.at[pl.ds(2 * part, size), pl.ds(slot * part, part)]),
            (
                up_ref.at[:, pl.ds(pl.multiple_of(owner * hidden, hidden), hidden)],
                grad_v.at[pl.ds((3 + slot) * part, part)],
            ),
        ]
        for number in range(hidden // part):
            at = pl.ds(pl.multiple_of(owner * hidden + number * part, part), part)
            spots.append((down_ref.at[at], slope_v.at[slot, :, pl.ds(number * part, part)]))
        return [
            pltpu.make_async_copy(source, target, shard_sem.at[slot, number])
            for number, (source, target) in enumerate(spots)
        ]

    shard_copies = []

    def shard(group, slot):
        for copy in shard_copies[slot][(0, 2, 3)[group] : (2, 3, None)[group]]:
            copy.wait()

        def put(columns, value):
            if slot:
                theirs_v[group, :, columns] = value.astype(B)
            else:
                w[group, 0:part, columns] = value.astype(B)

        if group == 0:
            put(slice(0, 3 * size), grad_v[slot * part : (slot + 1) * part, : 3 * size])
            put(slice(3 * size, 4 * size), grad_v[2 * part : 2 * part + size, slot * part : (slot + 1) * part].T)
        elif group == 1:
            put(slice(0, hidden), grad_v[(3 + slot) * part : (4 + slot) * part])
        else:
            for number in range(hidden // part):
                at = slice(number * part, (number + 1) * part)
                put(at, slope_v[slot, :, at].T)

    across = PAIR | spread[0]
    inner = bit_of(me, PAIR) != bit_of(me, spread[0])
    outer = bit_of(me, PAIR) == bit_of(me, spread[0])
    copies = {}

    def remote(key, number, source, target, axis, index):
        copies[key] = pltpu.make_async_remote_copy(
            src_ref=source,
            dst_ref=target,
            send_sem=send_sem.at[number],
            recv_sem=recv_sem.at[number],
            device_id={axis: index},
            device_id_type=MESH,
        )
        copies[key].start()

    def rows(position):
        return pl.ds(position * part, part)

    def pair_up(group, here):
        copy = pltpu.make_async_remote_copy(
            src_ref=theirs_v.at[group],
            dst_ref=w.at[group, rows(1)],
            send_sem=send_sem.at[8 * group + 1],
            recv_sem=recv_sem.at[8 * group + 1],
            device_id={"dp": pair_to},
            device_id_type=MESH,
        )
        pl.when(here)(copy.start)

    def onward(group, position, level):
        source = w.at[group, rows(position)]
        far = position + (2 << level)
        remote(("w", far), 8 * group + far, source, w.at[group, rows(far)], "dp", flip(me, spread[level]))

    def partly(here, source, target, send, recv, to):
        copy = pltpu.make_async_remote_copy(
            src_ref=source,
            dst_ref=target,
            send_sem=send,
            recv_sem=recv,
            device_id={"dp": to},
            device_id_type=MESH,
        )
        pl.when(here)(copy.start)

    across_to = flip(me, across)

    def straight(group):
        partly(inner, theirs_v.at[group], w.at[group, rows(3)], cross_sem.at[group, 0], three_sem.at[group], across_to)

    def hand(group, here=None):
        source, sem = w.at[group, rows(0)], cross_sem.at[group, 1]
        if here is not inner:
            partly(outer, source, w_relay.at[group, rows(0)], sem, relay_sem.at[group, 0], pair_to)
        if here is not outer:
            partly(inner, source, w_relay.at[group, rows(1)], sem, relay_sem.at[group, 1], across_to)

    def relay(group):
        source = w.at[group, rows(1)]
        partly(
            inner, source, w_relay.at[group, rows(2)], cross_sem.at[group, 2], relay_sem.at[group, 2], across_to
        )

    def pass_on(group, *numbers):
        for number in numbers:
            source, target = w_relay.at[group, rows(number)], 3 if number == 2 else 2
            here = pltpu.make_async_remote_copy(
                src_ref=source,
                dst_ref=source,
                send_sem=relay_sem.at[group, number],
                recv_sem=relay_sem.at[group, number],
                device_id={"dp": pair_to},
                device_id_type=MESH,
            )
            pl.when(inner)(here.wait_recv)
            partly(
                inner,
                source,
                w.at[group, rows(target)],
                cross_sem.at[group, 3 + number],
                (three_sem if target == 3 else two_sem).at[group],
                across_to if number == 0 else pair_to,
            )

    def to_pair(key, source, target, here):
        if key not in quarters:
            quarters[key] = pltpu.make_async_remote_copy(
                src_ref=source,
                dst_ref=target,
                send_sem=quarter_sem.at[key, 0],
                recv_sem=quarter_sem.at[key, 1],
                device_id={"dp": pair_to},
                device_id_type=MESH,
            )
        pl.when(here)(quarters[key].start)

    quarters = {}
    arrived = set()

    def arrive(group, position):
        if (group, position) not in arrived:
            arrived.add((group, position))
            sem = {2: two_sem.at[group], 3: three_sem.at[group]}.get(position, recv_sem.at[8 * group + position])
            pltpu.make_async_remote_copy(
                src_ref=w.at[group, rows(position)],
                dst_ref=w.at[group, rows(position)],
                send_sem=sem,
                recv_sem=sem,
                device_id={"dp": pair_to},
                device_id_type=MESH,
            ).wait_recv()

    spot = pl.ds(pl.multiple_of(core * (2 * quarter) + side * quarter, quarter), quarter)
    pair_rows = pl.ds(pl.multiple_of(core * (2 * quarter), quarter), 2 * quarter)
    levels = len(spread)
    assert levels == 2

    def over_tiles(source, raw, number, work):
        def load(tile, slot):
            here = pl.ds(pl.multiple_of(tile * CHUNK, CHUNK), CHUNK)
            return pltpu.make_async_copy(source.at[here], raw.at[slot], load_sem.at[number, slot])

        load(0, 0).start()

        def one(tile, carry):
            slot = lax.rem(tile, 2)

            @pl.when(tile + 1 < length // CHUNK)
            def _():
                load(tile + 1, 1 - slot).start()

            load(tile, slot).wait()
            work(tile, slot)
            return carry

        lax.fori_loop(0, length // CHUNK, one, 0)

    outs = {}

    def leave(key, source, target, sem):
        outs[key] = pltpu.make_async_copy(source, target, sem)
        outs[key].start()

    def left(*keys):
        for key in keys:
            outs.pop(key).wait()

    def normalise(seq):
        if seq:
            copies["x3"].wait_recv()
            left(("x", 0))

        def work(tile, slot):
            here = pl.ds(pl.multiple_of(tile * CHUNK, CHUNK), CHUNK)
            both = pl.ds(pl.multiple_of(seq * length + tile * CHUNK, CHUNK), CHUNK)
            raw, attn_to, mlp_to, x_to = raw_x.at[slot], attn_v.at[here], mlp_v.at[both], xr_v.at[here]

            def some(at):
                mean, inverse = stats(raw[at].astype(F))
                for position, mask in enumerate(order):
                    to = slice(position * part, (position + 1) * part)
                    there = pl.ds(pl.multiple_of(flip(me, mask) * part, part), part)
                    piece = raw[at, there]
                    normed = (piece.astype(F) - mean) * inverse
                    attn_to[at, to] = (normed * vec_ref[0:1, there] + vec_ref[1:2, there]).astype(B)
                    mlp_to[at, to] = (normed * vec_ref[2:3, there] + vec_ref[3:4, there]).astype(B)
                    x_to[at, to] = piece

            by_rows(CHUNK, some)

        over_tiles(x_other if seq else x_ref, raw_x, 0, work)
        both = pl.ds(seq * length, length)
        leave(("x", seq), xr_v, x_rel.at[both], rel_sem.at[seq, 0])
        leave(("m", seq), mlp_v.at[both], mlp_out.at[both], rel_sem.at[seq, 2])

    def arrange_grad(seq):
        if seq:
            copies["g3"].wait_recv()
            left(("g", 0))
        else:
            bias_ref[...] = jnp.zeros_like(bias_ref)

        def work(tile, slot):
            here = pl.ds(pl.multiple_of(tile * CHUNK, CHUNK), CHUNK)
            raw, g_to = raw_x.at[slot], g_v.at[here]

            def some(at):
                if seq == 0:
                    bias_ref[...] += jnp.sum(raw[at].astype(F), axis=0, keepdims=True)
                for position, mask in enumerate(order):
                    to = slice(position * part, (position + 1) * part)
                    there = pl.ds(pl.multiple_of(flip(me, mask) * part, part), part)
                    g_to[at, to] = raw[at, there]

            by_rows(CHUNK, some, 32)

        over_tiles(g_other if seq else g_ref, raw_x, 1, work)
        leave(("g", seq), g_v, g_rel.at[pl.ds(seq * length, length)], rel_sem.at[seq, 1])

    def whole_group(group):
        if ("out", group) not in arrived:
            arrived.add(("out", group))
            for position in range(1, 8):
                arrive(group, position)

    def project(seq):
        whole_group(0)
        key_row = jnp.concatenate([key_ref[pl.ds(half, 1)], jnp.zeros((1, size - ROT), F)], axis=1)
        offsets = (qv_ref[half, 0:1], key_row, qv_ref[half, 1:2])
        if seq == 0:
            left("tables")

        def one(tile, carry):
            here = pl.ds(pl.multiple_of(tile * CHUNK, CHUNK), CHUNK)
            mixed = dot(attn_v[here], w[0, :, : 3 * size], ((1,), (0,)), F)
            tables = (tab_v[0, here], tab_v[1, here], tab_v[2, here])
            q_v[here] = turn(mixed[:, :size] + offsets[0], *tables).astype(B)
            k_v[here] = turn(mixed[:, size : 2 * size] + offsets[1], *tables).astype(B)
            v_v[here] = (mixed[:, 2 * size :] + offsets[2]).astype(B)
            return carry

        lax.fori_loop(0, length // CHUNK, one, 0)

    def project_grad(seq):
        whole_group(0)

        def some(at):
            cg_v[at] = dot(g_v[at], w[0, :, 3 * size :], ((1,), (0,)), B)

        by_rows(length, some, CHUNK)

    def attend(seq):
        if seq:
            copies["seg"].wait()
            left(("mg", 0), ("ctx", 0))
        scale = size ** (-0.5)
        ids = seg_ref[...] if seq == 0 else seg_v[...]
        col_v[...] = jnp.broadcast_to(ids.astype(F), (8, length)).T

        def clear(here):
            dk_v[here] = jnp.zeros((128, size), F)
            dv_v[here] = jnp.zeros((128, size), F)

        by_rows(length, clear, 128)
        def queries(first, low, reach):
            here, keys = pl.ds(first, QBLOCK), pl.ds(low, reach)
            scores = dot(q_v[here], k_v[keys], ((1,), (1,)), F) * scale
            row_ids = first + lax.broadcasted_iota(jnp.int32, (QBLOCK, reach), 0)
            key_ids = low + lax.broadcasted_iota(jnp.int32, (QBLOCK, reach), 1)
            row = seg_ref[:, keys] if seq == 0 else seg_v[:, keys]
            allowed = (key_ids <= row_ids) & (col_v[here, 0:1] == row.astype(F))
            scores = jnp.where(allowed, scores, -1e30)
            expo = jnp.exp(scores - jnp.max(scores, axis=1, keepdims=True))
            probs = expo / jnp.sum(expo, axis=1, keepdims=True)
            low_probs = probs.astype(B)
            ctx_v[here] = dot(low_probs, v_v[keys], ((1,), (0,)), B)
            dv_v[keys] += dot(low_probs, cg_v[here], ((0,), (0,)), F)
            prob_grad = dot(cg_v[here], v_v[keys], ((1,), (1,)), F)
            centred = jnp.sum(probs * prob_grad, axis=1, keepdims=True)
            score_grad = (probs * (prob_grad - centred)).astype(B)
            q_grad = dot(score_grad, k_v[keys], ((1,), (0,)), F) * scale
            tables = (tab_v[0, here], -tab_v[1, here], -tab_v[2, here])
            mg_v[here, :size] = turn(q_grad, *tables).astype(B)
            dk_v[keys] += dot(score_grad, q_v[here], ((0,), (0,)), F) * scale

        for first in range(0, DOC_MAX, QBLOCK):
            queries(first, 0, first + QBLOCK)

        def later(number, carry):
            low = pl.multiple_of(number * QBLOCK - DOC_MAX, QBLOCK)
            queries(pl.multiple_of(number * QBLOCK, QBLOCK), low, DOC_MAX + QBLOCK)
            return carry

        lax.fori_loop(DOC_MAX // QBLOCK, length // QBLOCK, later, 0)

        def turn_back(here):
            tables = (tab_v[0, here], -tab_v[1, here], -tab_v[2, here])
            mg_v[here, size : 2 * size] = turn(dk_v[here], *tables).astype(B)
            mg_v[here, 2 * size :] = dv_v[here].astype(B)

        by_rows(length, turn_back)
        if seq == 0:
            sum_ref[...] = jnp.zeros_like(sum_ref)

        def add_sums(here):
            sum_ref[...] += jnp.sum(mg_v[here].astype(F), axis=0, keepdims=True)

        by_rows(length, add_sums, 128)
        both = pl.ds(seq * length, length)
        leave(("mg", seq), mg_v, mixed_out.at[both], rel_sem.at[seq, 3])
        leave(("ctx", seq), ctx_v, ctx_out.at[both], rel_sem.at[seq, 4])

    def attn_grads(seq, low, high):
        def one(block, carry):
            here = pl.ds(pl.multiple_of(block * CHUNK, CHUNK), CHUNK)
            qkv = dot(attn_v[:, here], mg_v[...], ((0,), (0,)), F)
            dense = dot(g_v[:, here], ctx_v[...], ((0,), (0,)), F)
            if seq == 0:
                grad_v[here, : 3 * size] = qkv
                grad_v[here, 3 * size :] = dense
            else:
                grad_v[here, : 3 * size] += qkv
                grad_v[here, 3 * size :] += dense
            return carry

        lax.fori_loop(low // CHUNK, high // CHUNK, one, 0)

    def up(low, high):
        def store(tile, slot):
            here = pl.ds(pl.multiple_of(tile * CHUNK, CHUNK), CHUNK)
            return (
                pltpu.make_async_copy(act_v.at[slot], act_out.at[here], tile_sem.at[0, slot]),
                pltpu.make_async_copy(slope_v.at[slot], slope_out.at[here], tile_sem.at[1, slot]),
            )

        def one(tile, carry):
            slot = lax.rem(tile, 2)
            here = pl.ds(pl.multiple_of(tile * CHUNK, CHUNK), CHUNK)
            pre = dot(mlp_v[here], w[1], ((1,), (0,)), F) + up_bias_ref[:, pl.ds(pl.multiple_of(half * hidden, hidden), hidden)]

            @pl.when(tile >= low + 2)
            def _():
                for copy in store(tile - 2, slot):
                    copy.wait()

            slope_v[slot] = pre
            act_to, slope_to = act_v.at[slot], slope_v.at[slot]

            def some(at):
                pre = slope_to[at]
                cumulative = 0.5 * (1.0 + lax.erf(pre * 0.7071067811865476))
                density = jnp.exp(-0.5 * pre * pre) * 0.3989422804014327
                act_to[at] = (pre * cumulative).astype(B)
                slope_to[at] = cumulative + pre * density

            by_rows(CHUNK, some)
            for copy in store(tile, slot):
                copy.start()
            return carry

        lax.fori_loop(low, high, one, 0)
        for tile in (high - 2, high - 1):
            for copy in store(tile, tile % 2):
                copy.wait()

    kinds = {"o": outer, "i": inner}

    def relay_on(group):
        arrive(group, 1)
        relay(group)

    def send_y(group, position):
        if position:
            arrive(group, position)
        onward(group, position, 1)

    def to_side(name, number, array):
        quarters[number].wait_recv()
        remote(name + "2", 24 + number, array.at[spot], array.at[spot], "tensor", side_to)

    def to_core(name, array):
        copies[name + "2"].wait_recv()
        remote(name + "3", 26 + (name == "g"), array.at[pair_rows], array.at[pair_rows], "tensor", core_to)

    def gradients(seq, number):
        middle = width // 2
        attn_grads(seq, *((0, middle) if number else (middle, width)))
        if seq and number:
            leave("keep", grad_v.at[pl.ds(0, middle)], keep_out, out_sem.at[4])
        elif seq:
            def narrow(at):
                send_v[at] = grad_v.at[pl.ds(middle, middle)][at].astype(B)

            by_rows(middle, narrow, 128)
            leave("send", send_v, send_out, out_sem.at[3])

    def lift(seq):
        whole_group(1)
        up(seq * length // CHUNK, (seq + 1) * length // CHUNK)

    stages = {
        "sh": shard,
        "pu": lambda group, kind: pair_up(group, kinds[kind]),
        "gst": straight,
        "hd": lambda group, kind: hand(group, kinds[kind]),
        "re": relay_on,
        "yo": send_y,
        "gpo": pass_on,
        "x1": lambda kind: to_pair(0, x_ref.at[spot], x_other.at[spot], kinds[kind]),
        "g1": lambda kind: to_pair(1, g_ref.at[spot], g_other.at[spot], kinds[kind]),
        "x2": lambda: to_side("x", 0, x_other),
        "g2": lambda: to_side("g", 1, g_other),
        "x3": lambda: to_core("x", x_other),
        "g3": lambda: to_core("g", g_other),
        "N": normalise,
        "G": arrange_grad,
        "PJ": project,
        "CG": project_grad,
        "AT": attend,
        "GR": gradients,
        "UP": lift,
    }
    def begin(*private):
        nonlocal raw_x, attn_v, g_v, mlp_v, xr_v, grad_v, send_v, q_v, k_v
        nonlocal v_v, cg_v, ctx_v, mg_v, dk_v, dv_v, act_v, slope_v, col_v, tab_v
        (
            raw_x,
            attn_v,
            g_v,
            mlp_v,
            xr_v,
            grad_v,
            send_v,
            q_v,
            k_v,
            v_v,
            cg_v,
            ctx_v,
            mg_v,
            dk_v,
            dv_v,
            act_v,
            slope_v,
            col_v,
            tab_v,
        ) = private
        shard_copies.extend([shards(half, 0), shards(1 - half, 1)])
        for number in range(3 + hidden // part):
            for slot in (1, 0):
                shard_copies[slot][number].start()
        leave("tables", tables_ref, tab_v, out_sem.at[0])
        greet(
            [("dp", flip(me, mask)) for mask in [PAIR, across] + spread] + [("tensor", side_to), ("tensor", core_to)]
        )
        copies["seg"] = pltpu.make_async_remote_copy(
            src_ref=seg_ref,
            dst_ref=seg_v,
            send_sem=seg_sem.at[0],
            recv_sem=seg_sem.at[1],
            device_id={"dp": pair_to},
            device_id_type=MESH,
        )
        copies["seg"].start()

    def close():
        left(*list(outs))
        for name in ("x2", "x3", "g2", "g3"):
            copies[name].wait_send()
        for key in (0, 1):
            quarters[key].wait_send()

    def finish():
        def gone(sem):
            pltpu.make_async_remote_copy(
                src_ref=w.at[0, rows(0)],
                dst_ref=w.at[0, rows(0)],
                send_sem=sem,
                recv_sem=sem,
                device_id={"dp": pair_to},
                device_id_type=MESH,
            ).wait_send()

        for group in range(3):
            for position in (1, 4, 5, 6, 7):
                gone(send_sem.at[8 * group + position])
            gone(cross_sem.at[group, 1])

            @pl.when(inner)
            def _():
                for number in (0, 2, 3, 4, 5):
                    gone(cross_sem.at[group, number])

    return begin, stages, whole_group, close, finish


def scatter_steps(
    groups,
    steps,
    earlier,
    whole_group,
    attn_send,
    attn_keep,
    x_rel,
    g_rel,
    mlp_in,
    mixed_grad,
    context,
    activation,
    slope,
    x_ref,
    g_ref,
    vec_ref,
    mixed_sum,
    bias_sum,
    block_out,
    input_grad,
    qkv_out,
    dense_out,
    up_out,
    down_out,
    far_in,
    far_two,
    y_recv,
    z_recv,
    z_relay,
    c_recv,
    x_recv,
    e_recv,
    small_out,
    w,
    small_recv,
    load_sem,
    tile_sem,
    ys_sem,
    yr_sem,
    zs_sem,
    zr_sem,
    zl_sem,
    zf_sem,
    two_sem,
    ps_sem,
    pr_sem,
    cs_sem,
    cr_sem,
    xs_sem,
    xr_sem,
    es_sem,
    er_sem,
    fs_sem,
    fr_sem,
    emit_sem,
    ss_sem,
    sr_sem,
    out_sem,
    act_v,
    pre_v,
    tile_v,
    col_v,
    slope_t,
    mix_t,
    ctx_v,
    keep_v,
    y_send,
    z_send,
    p_send,
    y_stage,
    c_send,
    c_stage,
    r_stage,
    x_send,
    hold_v,
    mean_v,
    inverse_v,
    sum_v,
    small_v,
):
    length, width = x_ref.shape
    part = width // groups
    size = context.shape[1]
    hidden = activation.shape[1]
    quarter = length // 4
    me, place = lax.axis_index("dp"), lax.axis_index("tensor")
    core, side, half = lax.rem(place, 2), lax.div(place, 2), bit_of(me, PAIR)
    pair_to, side_to, core_to = flip(me, PAIR), flip(place, 2), flip(place, 1)
    spread, order = block_order(groups)
    z_to, y_to = [flip(me, bit) for bit in spread]
    across_to = flip(z_to, PAIR)
    inner = bit_of(me, PAIR) != bit_of(me, spread[0])
    outer = bit_of(me, PAIR) == bit_of(me, spread[0])

    def remote(source, target, send, recv, axis, index):
        return pltpu.make_async_remote_copy(
            src_ref=source, dst_ref=target, send_sem=send, recv_sem=recv, device_id={axis: index}, device_id_type=MESH
        )

    def span(position, count=1):
        return pl.ds(position * part, count * part)

    def step(index, amount):
        return pl.ds(pl.multiple_of(index * amount, amount), amount)

    def y_copy(group, position):
        source = attn_send if group == 0 else y_send
        here = step(position, part) if not isinstance(position, int) else span(position)
        return remote(
            source.at[here], y_recv.at[group, here], ys_sem.at[group, position], yr_sem.at[group, position], "dp", y_to
        )

    slot_of = (0, 0, 1)

    def z_copy(group, position):
        source, sem = z_send.at[slot_of[group], span(position - 2)], zs_sem.at[group, position - 2]
        onward = (
            remote(source, far_two.at[group], sem, two_sem.at[group], "dp", across_to)
            if position == 3
            else remote(source, z_relay.at[group, span(2)], sem, zl_sem.at[group, 2], "dp", across_to)
        )
        aside = remote(
            source, z_relay.at[group, span(position - 2)], sem, zl_sem.at[group, position - 2], "dp", pair_to
        )
        return onward, aside

    def forward(group, number):
        target = 0 if number == 2 else number
        arrived = remote(
            z_relay.at[group, span(number)],
            z_recv.at[group, span(target)],
            zf_sem.at[group, number],
            zl_sem.at[group, number],
            "dp",
            pair_to,
        )
        return arrived, remote(
            z_relay.at[group, span(number)],
            z_recv.at[group, span(target)],
            zf_sem.at[group, number],
            zr_sem.at[group, target],
            "dp",
            pair_to if number == 2 else across_to,
        )

    def pass_on(group, *numbers):
        @pl.when(inner)
        def _():
            for number in numbers:
                arrived, copy = forward(group, number)
                arrived.wait_recv()
                copy.start()

    def z_arrived(group, position):
        return remote(
            z_relay.at[group, span(position)],
            z_recv.at[group, span(position)],
            zf_sem.at[group, position],
            zr_sem.at[group, position],
            "dp",
            pair_to,
        )

    def p_copy(group):
        return remote(
            p_send.at[slot_of[group]], far_in.at[group], ps_sem.at[group], pr_sem.at[group], "dp", pair_to
        )

    emitted = {}

    def emit(group, kind, block, owner):
        copies = []
        for number in range(hidden // part):
            at = pl.ds(number * part, part)
            if group == 2 or (group == 0 and number == 3):
                block[:, at] = block[:, at].T
            if group == 1:
                target = up_out.at[:, pl.ds(pl.multiple_of(owner * hidden + number * part, part), part)]
            elif group == 2:
                target = down_out.at[pl.ds(pl.multiple_of(owner * hidden + number * part, part), part)]
            elif number == 3:
                target = dense_out.at[owner]
            else:
                target = qkv_out.at[:, pl.ds(pl.multiple_of(owner * 3 * size + number * part, part), part)]
            copies.append(pltpu.make_async_copy(block.at[:, at], target, emit_sem.at[group, kind, number]))
            copies[-1].start()
        emitted[(group, kind)] = copies

    def emit_near(group):
        emit(group, 0, keep_v.at[slot_of[group], span(0)], half)

    def emit_far(group):
        block = (
            hold_v.at[1, 1, :, pl.ds(0, hidden)],
            keep_v.at[0, span(1)],
            hold_v.at[1, 1, :, pl.ds(hidden, hidden)],
        )[group]
        p_copy(group).wait_recv()
        staged(far_in.at[group])

        def widen(at):
            block[at] = y_stage[at].astype(F)

        def add(at):
            block[at] += y_stage[at].astype(F)

        by_rows(part, widen)

        @pl.when(inner)
        def _():
            remote(
                p_send.at[0], far_two.at[group], two_sem.at[group], two_sem.at[group], "dp", across_to
            ).wait_recv()
            staged(far_two.at[group])
            by_rows(part, add)

        emit(group, 1, block, 1 - half)

    def staged(source):
        copy = pltpu.make_async_copy(source, y_stage, load_sem.at[6])
        copy.start()
        copy.wait()

    def y_far(group, position):
        if group == 0:
            need(5)
        y_copy(group, position).wait_recv()
        staged(y_recv.at[group, span(position)])
        onward, aside = z_copy(group, position)
        if group == 1:
            z_copy(0, position)[0].wait_send()
        kept, target = keep_v.at[slot_of[group], span(position)], z_send.at[slot_of[group], span(position - 2)]

        def add(at):
            target[at] = (kept[at] + y_stage[at].astype(F)).astype(B)

        by_rows(part, add)
        pl.when(inner)(onward.start)
        pl.when(outer)(aside.start)

    def y_near(group, position):
        if group == 0:
            need(5)
        y_copy(group, position).wait_recv()
        staged(y_recv.at[group, span(position)])
        kept, target = keep_v.at[slot_of[group], span(position)], p_send.at[slot_of[group]]
        if position == 1 and group == 1:
            p_copy(0).wait_send()

        def add(at):
            total = kept[at] + y_stage[at].astype(F)
            kept[at] = total
            if position == 1:
                target[at] = total.astype(B)

        by_rows(part, add)
        if position == 1:
            pl.when(outer)(p_copy(group).start)

    def z_last(group, position):
        kept, target = keep_v.at[slot_of[group], span(position)], p_send.at[slot_of[group]]

        def add(at):
            total = kept[at] + y_stage[at].astype(F)
            if position == 1:
                target[at] = total.astype(B)
            else:
                kept[at] = total

        def add_all():
            z_arrived(group, position).wait_recv()
            staged(z_recv.at[group, span(position)])
            by_rows(part, add)

        if position == 1:

            @pl.when(inner)
            def _():
                add_all()
                p_copy(group).start()

        else:
            add_all()
            emit_near(group)

    loads = [
        None,
        None,
        None,
        pltpu.make_async_copy(activation, act_v, load_sem.at[3]),
        pltpu.make_async_copy(context, ctx_v, load_sem.at[4]),
        pltpu.make_async_copy(attn_keep, keep_v.at[0], load_sem.at[5]),
    ]
    for number in (3, 5, 4):
        loads[number].start()
    loaded = set()

    def need(*numbers):
        for number in numbers:
            if number not in loaded:
                loaded.add(number)
                loads[number].wait()

    for position in (3, 2, 1, 0):
        y_copy(0, position).start()

    small_v[...] = jnp.zeros_like(small_v)

    def pre_load(tile, slot):
        here = step(tile, CHUNK)
        return (
            pltpu.make_async_copy(g_rel.at[here], tile_v.at[step(slot, CHUNK)], tile_sem.at[0, slot]),
            pltpu.make_async_copy(slope.at[here], slope_t.at[slot], tile_sem.at[1, slot]),
        )

    sum_v[...] = jnp.zeros_like(sum_v)

    def pre_tiles(seq):
        whole_group(2)
        low, high = seq * length // CHUNK, (seq + 1) * length // CHUNK
        for copy in pre_load(low, 0):
            copy.start()

        def one(tile, carry):
            slot = lax.rem(tile, 2)

            @pl.when(tile + 1 < high)
            def _():
                for copy in pre_load(tile + 1, 1 - slot):
                    copy.start()

            for copy in pre_load(tile, slot):
                copy.wait()
            grad = (dot(tile_v[step(slot, CHUNK)], w[2], ((1,), (0,)), F) * slope_t[slot]).astype(B)
            pre_v[step(tile, CHUNK)] = grad
            sum_v[...] += jnp.sum(grad.astype(F), axis=0, keepdims=True)
            return carry

        lax.fori_loop(low, high, one, 0)

    tall = 2 * quarter
    blocks = width // CHUNK

    def c_copy(which, seq, block):
        here = step(block, CHUNK)
        return remote(
            c_send.at[:, here],
            c_recv.at[which, seq, :, here],
            cs_sem.at[which, seq, block],
            cr_sem.at[which, seq, block],
            "tensor",
            core_to,
        )

    def x_copy(which, seq):
        return remote(
            x_send.at[which, seq], x_recv.at[which, seq], xs_sem.at[which, seq], xr_sem.at[which, seq], "tensor", side_to
        )

    def e_copy(which):
        return remote(x_send.at[which, 1], e_recv.at[which], es_sem.at[which], er_sem.at[which], "dp", pair_to)

    sent_tiles = []

    def send_tile(which, seq):
        begin, block_of = tile_of[which]
        whole_group(2)
        if which:
            need(3, 4)
        start = pl.multiple_of(seq * length + (1 - core) * tall, tall)
        begin(start)

        def one(block, carry):
            value = block_of(start, block)
            if sent_tiles:
                c_copy(*sent_tiles[-1], block).wait_send()
            c_send[:, step(block, CHUNK)] = value.astype(B)
            c_copy(which, seq, block).start()
            return carry

        lax.fori_loop(0, blocks, one, 0)
        sent_tiles.append((which, seq))

    def c_load(which, seq, block, slot):
        return pltpu.make_async_copy(c_recv.at[which, seq, :, step(block, CHUNK)], c_stage.at[slot], tile_sem.at[2, slot])

    def keep_tile(which, seq):
        begin, block_of = tile_of[which]
        start = pl.multiple_of(seq * length + core * tall, tall)
        begin(start)
        c_copy(which, seq, 0).wait_recv()
        c_load(which, seq, 0, 0).start()

        def one(block, carry):
            slot = lax.rem(block, 2)
            value = block_of(start, block)

            @pl.when(block + 1 < blocks)
            def _():
                c_copy(which, seq, block + 1).wait_recv()
                c_load(which, seq, block + 1, 1 - slot).start()

            c_load(which, seq, block, slot).wait()
            r_stage[...] = value + c_stage[slot].astype(F)
            here = step(block, CHUNK)
            hold_v[which, seq, :, here] = r_stage[step(side, quarter)]
            x_send[which, seq, :, here] = r_stage[step(1 - side, quarter)].astype(B)
            return carry

        lax.fori_loop(0, blocks, one, 0)
        x_copy(which, seq).start()

    def blend_begin(start):
        copies = (
            pltpu.make_async_copy(x_rel.at[pl.ds(start, tall)], tile_v, tile_sem.at[3, 0]),
            pltpu.make_async_copy(mixed_grad.at[pl.ds(start, tall)], mix_t, tile_sem.at[3, 1]),
        )
        for copy in copies:
            copy.start()
        for copy in copies:
            copy.wait()
        for slot in range(2):
            mean, inverse = stats(tile_v[span_rows(slot)].astype(F))
            mean_v[span_rows(slot)] = jnp.broadcast_to(mean, (CHUNK, 128))
            inverse_v[span_rows(slot)] = jnp.broadcast_to(inverse, (CHUNK, 128))

    def span_rows(slot):
        return pl.ds(slot * CHUNK, CHUNK)

    def natural_block(position):
        result = me
        for level, bit in enumerate([PAIR] + spread):
            flipped = lax.rem(lax.div(position, 1 << level), 2)
            result = result + bit * (1 - 2 * bit_of(me, bit)) * flipped
        return result

    def blend_block(start, block):
        here = step(block, CHUNK)
        there = step(natural_block(block), part)
        attn_grad = dot(mix_t[...], w[0, here, : 3 * size], ((1,), (1,)), F)
        mlp_grad = dot(pre_v[pl.ds(start, tall)], w[1, here, :], ((1,), (1,)), F)
        mean, inverse = mean_v[...], inverse_v[...]
        mean = jnp.concatenate([mean] * (CHUNK // 128), axis=1)
        inverse = jnp.concatenate([inverse] * (CHUNK // 128), axis=1)
        normed = (tile_v[:, here].astype(F) - mean) * inverse
        small_v[0:1, there] += jnp.sum(attn_grad * normed, axis=0, keepdims=True)
        small_v[1:2, there] += jnp.sum(attn_grad, axis=0, keepdims=True)
        small_v[2:3, there] += jnp.sum(mlp_grad * normed, axis=0, keepdims=True)
        small_v[3:4, there] += jnp.sum(mlp_grad, axis=0, keepdims=True)
        return attn_grad * vec_ref[0:1, there] + mlp_grad * vec_ref[2:3, there]

    def product(columns, right, group, positions, sent, old=None):
        count = len(positions)
        base = positions[0]
        sign = positions[1] - positions[0] if count > 1 else 1

        def load(number, slot):
            return pltpu.make_async_copy(
                columns.at[:, step(base + sign * number, part)], col_v.at[slot], tile_sem.at[4, slot]
            )

        load(0, 0).start()

        def one(number, carry):
            slot = lax.rem(number, 2)

            @pl.when(number + 1 < count)
            def _():
                load(number + 1, 1 - slot).start()

            load(number, slot).wait()
            value = dot(col_v[slot], right[...], ((0,), (0,)), F)
            position = base + sign * number
            if sent:
                if old is not None:
                    y_copy(old, position - groups // 2).wait_send()
                y_send[step(position - groups // 2, part)] = value.astype(B)
                y_copy(group, position - groups // 2).start()
            else:
                keep_v[slot_of[group], step(position, part)] = value
            return carry

        lax.fori_loop(0, count, one, 0)

    def small_begin():
        small_v[4:5] = bias_sum[...]
        small_v[5:6, step(half, hidden)] = sum_v[...]
        small_v[6:7, pl.ds(pl.multiple_of(half * (width // 2), width // 2), 3 * size)] = mixed_sum[...]
        small_copy(0).start()

    rounds = [("dp", flip(me, bit)) for bit in [PAIR] + spread] + [("tensor", side_to), ("tensor", core_to)]

    def small_copy(number):
        return remote(small_v, small_recv.at[number], ss_sem.at[number], sr_sem.at[number], *rounds[number])

    def small_end(number):
        small_copy(number).wait()
        if number < 3:
            small_v[...] += small_recv[number]
        else:
            small_v[0:4] += small_recv[number, 0:4]
        if number + 1 < len(rounds):
            small_copy(number + 1).start()

    def branch_begin(start):
        pass

    def branch_block(start, block):
        here, rows = step(block, CHUNK), pl.ds(start, tall)
        return dot(ctx_v[rows], w[0, here, 3 * size :], ((1,), (1,)), F) + dot(
            act_v[rows], w[2, here, :], ((1,), (1,)), F
        )

    def read_stage(source):
        copy = pltpu.make_async_copy(source, tile_v.at[pl.ds(0, quarter)], load_sem.at[6])
        copy.start()
        copy.wait()

    def e_start(which):
        x_copy(which, 1).wait_recv()
        x_copy(which, 1).wait_send()
        read_stage(x_recv.at[which, 1])

        def one(block, carry):
            here = step(block, CHUNK)
            x_send[which, 1, :, here] = (hold_v[which, 1, :, here] + tile_v[0:quarter, here].astype(F)).astype(B)
            return carry

        lax.fori_loop(0, blocks, one, 0)
        e_copy(which).start()

    def gather_own(which):
        x_copy(which, 0).wait_recv()
        read_stage(x_recv.at[which, 0])

        def one(block, carry):
            here = step(block, CHUNK)
            hold_v[which, 0, :, here] += tile_v[0:quarter, here].astype(F)
            return carry

        lax.fori_loop(0, blocks, one, 0)

    def spot(c, s):
        return pl.ds(pl.multiple_of(c * tall + s * quarter, quarter), quarter)

    def position_of(block, shifted=False):
        result = 0
        for level, bit in enumerate([PAIR] + spread):
            mine = bit_of(me, bit)
            if shifted and bit == PAIR:
                mine = 1 - mine
            result = result + (1 << level) * ((1 - mine) if block & bit else mine)
        return result

    def finish(which, out_ref):
        if len(sent_tiles) == 4:
            sent_tiles.append(None)
            for block in range(blocks):
                c_copy(*sent_tiles[3], block).wait_send()
        gather_own(which)
        e_copy(which).wait_recv()
        copies = [
            pltpu.make_async_copy(e_recv.at[which], tile_v.at[pl.ds(0, quarter)], load_sem.at[6]),
            pltpu.make_async_copy(x_ref.at[spot(core, side)], tile_v.at[pl.ds(quarter, quarter)], load_sem.at[7]),
        ]
        if which == 0:
            copies.append(pltpu.make_async_copy(g_ref.at[spot(core, side)], x_send.at[0, 0], load_sem.at[8]))
            x_copy(0, 0).wait_send()
        for copy in copies:
            copy.start()
        for copy in copies:
            copy.wait()
        here = pl.ds(which * quarter, quarter)
        held, sent, own_x, g_rows = hold_v.at[which, 0], tile_v, tile_v.at[pl.ds(quarter, quarter)], x_send.at[0, 0]
        target = c_send.at[here]

        def total(at, block):
            mine = held[at, step(position_of(block), part)]
            return mine + sent[at, step(position_of(block, True), part)].astype(F)

        def some_grad(at):
            rows = own_x[at].astype(F)
            mean, inverse = stats(rows)
            normed = (rows - mean) * inverse
            blend = jnp.concatenate([total(at, block) for block in range(groups)], axis=1)
            inner_grad = (
                blend
                - jnp.mean(blend, axis=1, keepdims=True)
                - normed * jnp.mean(blend * normed, axis=1, keepdims=True)
            )
            target[at] = (g_rows[at].astype(F) + inner_grad * inverse).astype(B)

        def some_out(at):
            for block in range(groups):
                cut = slice(block * part, (block + 1) * part)
                bias = vec_ref[4:5, cut] + vec_ref[5:6, cut]
                target[at, cut] = (own_x[at, cut].astype(F) + total(at, block) + bias).astype(B)

        by_rows(quarter, some_out if which else some_grad)
        first = remote(
            c_send.at[here], out_ref.at[spot(core, side)], fs_sem.at[which, 0], fr_sem.at[which, 0], "tensor", side_to
        )
        second = remote(
            c_send.at[here], out_ref.at[spot(core, side)], fs_sem.at[which, 1], fr_sem.at[which, 1], "tensor", core_to
        )
        own = pltpu.make_async_copy(c_send.at[here], out_ref.at[spot(core, side)], out_sem.at[3 + which])
        for copy in (first, second, own):
            copy.start()
        return first, second, own

    def finish_end(which, out_ref, copies):
        first, second, own = copies
        first.wait_recv()
        third = remote(
            out_ref.at[spot(core, 1 - side)],
            out_ref.at[spot(core, 1 - side)],
            fs_sem.at[which, 2],
            fr_sem.at[which, 2],
            "tensor",
            core_to,
        )
        third.start()
        return [first.wait_send, second.wait, third.wait, own.wait]

    tile_of = ((blend_begin, blend_block), (branch_begin, branch_block))
    outs, finished, ends = (input_grad, block_out), {}, []

    def do_product(group, sent):
        columns, right = ((mlp_in, pre_v), (g_rel, act_v))[group - 1]
        if group == 2:
            need(3)
        if group == 1 and not sent:
            for copy in emitted[(0, 0)]:
                copy.wait()
        product(columns, right, group, (7, 6, 5, 4) if sent else (3, 2, 1, 0), sent, 2 if sent and group == 1 else None)

    def do_finish(which):
        finished[which] = finish(which, outs[which])

    def do_end(which):
        ends.extend(finish_end(which, outs[which], finished[which]))

    stages = {
        "pre": pre_tiles,
        "st": send_tile,
        "kt": keep_tile,
        "ps": lambda group: do_product(group, True),
        "pk": lambda group: do_product(group, False),
        "yf": y_far,
        "yn": y_near,
        "po": pass_on,
        "zl": z_last,
        "es": e_start,
        "fin": do_finish,
        "fe": do_end,
        "fa": emit_far,
        "sb": small_begin,
        "se": small_end,
    }
    for name, *numbers in steps:
        (stages if name in stages else earlier)[name](*numbers)
    small_out[...] = small_v[...]
    for end in ends:
        end()
    for group in range(3):
        if group:
            p_copy(group).wait_send()
            for position in (2, 3):
                z_copy(group, position)[0].wait_send()
        for position in range(4):
            if group != 2:
                y_copy(group, position).wait_send()
        for kind in range(2):
            if group or kind:
                for copy in emitted[(group, kind)]:
                    copy.wait()

        @pl.when(inner)
        def _():
            for number in range(3):
                forward(group, number)[1].wait_send()

    for which in range(2):
        e_copy(which).wait_send()
        if which:
            x_copy(which, 0).wait_send()


def layer_kernel(
    groups,
    scoped_one,
    scoped_two,
    qkv_ref,
    dense_ref,
    up_ref,
    down_ref,
    seg_ref,
    x_ref,
    g_ref,
    vec_ref,
    up_bias_ref,
    qv_ref,
    key_ref,
    tables_ref,
    block_out,
    input_grad,
    qkv_out,
    dense_out,
    up_out,
    down_out,
    w_relay,
    x_other,
    g_other,
    x_rel,
    g_rel,
    mlp_out,
    mixed_out,
    ctx_out,
    act_out,
    slope_out,
    send_out,
    keep_out,
    far_in,
    far_two,
    y_recv,
    z_recv,
    z_relay,
    c_recv,
    x_recv,
    e_recv,
    small_out,
    w,
    theirs_v,
    seg_v,
    sum_ref,
    bias_ref,
    small_recv,
    send_sem,
    recv_sem,
    cross_sem,
    two_sem,
    three_sem,
    relay_sem,
    quarter_sem,
    shard_sem,
    seg_sem,
    load_sem,
    rel_sem,
    tile_sem,
    out_sem,
    s_load_sem,
    s_tile_sem,
    s_ys_sem,
    s_yr_sem,
    s_zs_sem,
    s_zr_sem,
    s_zl_sem,
    s_zf_sem,
    s_two_sem,
    s_ps_sem,
    s_pr_sem,
    s_cs_sem,
    s_cr_sem,
    s_xs_sem,
    s_xr_sem,
    s_es_sem,
    s_er_sem,
    s_fs_sem,
    s_fr_sem,
    s_emit_sem,
    s_ss_sem,
    s_sr_sem,
    s_out_sem,
):
    begin, earlier, whole_group, close, finish = gather_steps(
        groups,
        qkv_ref,
        dense_ref,
        up_ref,
        down_ref,
        seg_ref,
        x_ref,
        g_ref,
        vec_ref,
        up_bias_ref,
        qv_ref,
        key_ref,
        tables_ref,
        w_relay,
        x_other,
        g_other,
        x_rel,
        g_rel,
        mlp_out,
        mixed_out,
        ctx_out,
        act_out,
        slope_out,
        send_out,
        keep_out,
        w,
        theirs_v,
        seg_v,
        sum_ref,
        bias_ref,
        send_sem,
        recv_sem,
        cross_sem,
        two_sem,
        three_sem,
        relay_sem,
        quarter_sem,
        shard_sem,
        seg_sem,
        load_sem,
        rel_sem,
        tile_sem,
        out_sem,
    )

    def first(*private):
        begin(*private)
        for name, *numbers in STEPS_ONE:
            earlier[name](*numbers)
        close()

    def second(*private):
        scatter_steps(
            groups,
            STEPS_TWO,
            earlier,
            whole_group,
            send_out,
            keep_out,
            x_rel,
            g_rel,
            mlp_out,
            mixed_out,
            ctx_out,
            act_out,
            slope_out,
            x_ref,
            g_ref,
            vec_ref,
            sum_ref,
            bias_ref,
            block_out,
            input_grad,
            qkv_out,
            dense_out,
            up_out,
            down_out,
            far_in,
            far_two,
            y_recv,
            z_recv,
            z_relay,
            c_recv,
            x_recv,
            e_recv,
            small_out,
            w,
            small_recv,
            s_load_sem,
            s_tile_sem,
            s_ys_sem,
            s_yr_sem,
            s_zs_sem,
            s_zr_sem,
            s_zl_sem,
            s_zf_sem,
            s_two_sem,
            s_ps_sem,
            s_pr_sem,
            s_cs_sem,
            s_cr_sem,
            s_xs_sem,
            s_xr_sem,
            s_es_sem,
            s_er_sem,
            s_fs_sem,
            s_fr_sem,
            s_emit_sem,
            s_ss_sem,
            s_sr_sem,
            s_out_sem,
            *private,
        )
        finish()

    pl.run_scoped(first, *scoped_one)
    pl.run_scoped(second, *scoped_two)


def place_kernel(*refs):
    count = (len(refs) - 2) // 3
    sources, targets, staging = refs[:count], refs[count : 2 * count], refs[2 * count : 3 * count]
    in_sem, out_sem = refs[3 * count :]
    pieces = []
    for number, (source, target, stage) in enumerate(zip(sources, targets, staging)):
        rows = source.shape[0] // 2
        for part in range(2):
            at = pl.ds(part * rows, rows)
            pieces.append(
                (
                    pltpu.make_async_copy(source.at[at], stage.at[at], in_sem.at[number, part]),
                    pltpu.make_async_copy(stage.at[at], target.at[at], out_sem.at[number, part]),
                )
            )
    for load, _ in pieces:
        load.start()
    for load, store in pieces:
        load.wait()
        store.start()
    for _, store in pieces:
        store.wait()


def body_narrow(
    tokens,
    segment_ids,
    out_grad,
    attn_norm_gain,
    attn_norm_bias,
    mlp_norm_gain,
    mlp_norm_bias,
    qkv_weight,
    qv_bias,
    key_bias,
    dense_weight,
    dense_bias,
    up_weight,
    up_bias,
    down_weight,
    down_bias,
    *,
    groups,
    ways,
):
    length, width = tokens.shape[1:]
    heads, size = qkv_weight.shape[1] // 2, qkv_weight.shape[3]
    part = width // groups
    me = lax.axis_index("dp")
    half = (me // PAIR) % 2
    place = lax.axis_index("tensor")
    core, side = place % 2, place // 2
    spread = [bit for bit in (1 << k for k in reversed(range(groups.bit_length() - 1))) if bit != PAIR]

    def swap(array, bit):
        return lax.ppermute(array, "dp", [(i, i ^ bit) for i in range(groups)])

    def cross(array, bit):
        return lax.ppermute(array, "tensor", [(i, i ^ bit) for i in range(ways)])

    def pick(array, index, axis, count=2):
        rows = array.shape[axis] // count
        return lax.dynamic_slice_in_dim(array, index * rows, rows, axis)

    def join(mine, theirs, index, axis):
        pair = jnp.concatenate([mine, theirs], axis=axis)
        turned = jnp.concatenate([theirs, mine], axis=axis)
        return jnp.where(index == 0, pair, turned)

    order = [0, PAIR]
    for bit in spread:
        order = order + [mask | bit for mask in order]
    inverse = [order.index(mask) for mask in range(groups)]

    def arranged(array):
        return jnp.concatenate(
            [lax.dynamic_slice_in_dim(array, (mask ^ me) * part, part, array.ndim - 1) for mask in order], axis=-1
        )

    def natural(array):
        table = jnp.asarray(inverse, jnp.int32)
        return jnp.concatenate(
            [lax.dynamic_slice_in_dim(array, table[block ^ me] * part, part, array.ndim - 1) for block in range(groups)],
            axis=-1,
        )

    def gather(shard, halves_axis, axis):
        shard = shard.astype(B)
        mine, theirs = pick(shard, half, halves_axis), pick(shard, 1 - half, halves_axis)
        pieces = [jnp.concatenate([mine, swap(theirs, PAIR)], axis=axis)]
        for bit in spread:
            pieces = pieces + [swap(piece, bit) for piece in pieces]
        return jnp.concatenate(pieces, axis=axis)

    def scatter(product, axis, halves_axis):
        count = groups // 2
        sent = swap(product(count, groups, B), spread[-1])
        held = product(0, count, F) + sent.astype(F)
        for bit in reversed(spread[:-1]):
            keep, send = jnp.split(held, 2, axis=axis)
            held = keep + swap(send.astype(B), bit).astype(F)
        keep, send = jnp.split(held, 2, axis=axis)
        return join(keep, swap(send, PAIR), half, halves_axis)

    def share_rows(rows):
        rows = join(rows, cross(rows, 2), side, 0)
        return join(rows, cross(rows, 1), core, 0)

    def own_rows(array, axis):
        return pick(pick(array, core, axis), side, axis)

    def partner_rows(array):
        return share_rows(swap(own_rows(array, 0), PAIR))

    def total_rows(partial):
        held = pick(partial, core, 1).astype(F) + cross(pick(partial, 1 - core, 1), 1).astype(F)
        held = pick(held, side, 1) + cross(pick(held, 1 - side, 1).astype(B), 2).astype(F)
        sent = swap(held[1].astype(B), PAIR).astype(F)
        rows = sent.shape[0]
        sent = jnp.flip(sent.reshape(rows, groups // 2, 2, part), axis=2).reshape(rows, width)
        return held[0] + sent

    own_x, own_g = tokens[0], out_grad[0]
    w_up = gather(up_weight, 1, 0)
    x_other = partner_rows(own_x)
    w_down = gather(down_weight, 0, 1)
    g_other = partner_rows(own_g)
    w_qkv = gather(qkv_weight.reshape(part, 2, -1), 1, 0).reshape(width, -1)
    w_dense = gather(dense_weight.reshape(2 * heads * size, part), 0, 1)

    x_pair = arranged(jnp.concatenate([own_x, x_other], axis=0))
    g_pair = arranged(jnp.concatenate([own_g, g_other], axis=0))
    gains = [arranged(v) for v in (attn_norm_gain, attn_norm_bias, mlp_norm_gain, mlp_norm_bias)]

    def hat(rows):
        rows = rows.astype(F)
        center = rows - jnp.mean(rows, axis=-1, keepdims=True)
        inverse_dev = lax.rsqrt(jnp.mean(center * center, axis=-1, keepdims=True) + 1e-05)
        return center * inverse_dev, inverse_dev

    normed, _ = hat(x_pair)
    attn_in = (normed * gains[0] + gains[1]).astype(B)
    mlp_in = (normed * gains[2] + gains[3]).astype(B)

    up_here = pick(up_bias, half, 0)
    up_pre = dot(mlp_in, w_up, ((1,), (0,)), F) + up_here
    activation = jax.nn.gelu(up_pre, approximate=False).astype(B)
    middle = width // 2

    def columns(array, low, high):
        return array[:, low * part : high * part]

    down_shard = scatter(lambda low, high, kind: dot(activation, columns(g_pair, low, high), ((0,), (0,)), kind), 1, 0)
    pre_grad = (dot(g_pair, w_down, ((1,), (1,)), F) * gelu_slope(up_pre)).astype(B)
    up_shard = scatter(lambda low, high, kind: dot(columns(mlp_in, low, high), pre_grad, ((0,), (0,)), kind), 0, 1)
    up_bias_sum = jnp.sum(pre_grad.astype(F), axis=0)

    seg_other = swap(segment_ids[0], PAIR)
    seg = jnp.stack([segment_ids[0], seg_other])
    seg_col, seg_row = seg[:, :, None], seg[:, None, :]
    qv_here, key_here = pick(qv_bias, half, 0), pick(key_bias, half, 0)
    key_full = jnp.concatenate([key_here, jnp.zeros((heads, size - ROT), F)], axis=1)
    offsets = jnp.stack([qv_here[:, 0], key_full, qv_here[:, 1]], axis=1).reshape(heads, 1, 3 * size)
    mixed = dot(attn_in, w_qkv, ((1,), (0,)), F).reshape(2, length, heads, 3 * size)
    tables = rope_tables(length)
    table_specs = [shared(length, 128)] * 3
    seg_specs = [per_seq(length, 1), per_seq(1, length)]
    context_grad = dot(g_pair, w_dense, ((1,), (1,)), B).reshape(2, length, heads, size)
    contexts, mixed_grads, mixed_sums = [], [], []
    head_shape = jax.ShapeDtypeStruct((2, length, size), B)
    for head in range(heads):
        q, k, v, context, lse = pl.pallas_call(
            attn_forward,
            grid=(2,),
            in_specs=[per_seq(length, 3 * size), shared(1, 3 * size)] + table_specs + seg_specs,
            out_specs=[per_seq(length, size)] * 4 + [per_seq(length, 1)],
            out_shape=[head_shape] * 4 + [jax.ShapeDtypeStruct((2, length, 1), F)],
            name="attn_forward",
        )(mixed[:, :, head], offsets[head], *tables, seg_col, seg_row)
        mixed_grad, mixed_sum = pl.pallas_call(
            attn_backward,
            grid=(2,),
            in_specs=[per_seq(length, size)] * 4 + [per_seq(length, 1)] + table_specs + seg_specs,
            out_specs=[per_seq(length, 3 * size), per_seq(1, 3 * size)],
            out_shape=[
                jax.ShapeDtypeStruct((2, length, 3 * size), B),
                jax.ShapeDtypeStruct((2, 1, 3 * size), F),
            ],
            scratch_shapes=[pltpu.VMEM((length, size), F)] * 3,
            name="attn_backward",
        )(q, k, v, context_grad[:, :, head], lse, *tables, seg_col, seg_row)
        contexts.append(context.reshape(2 * length, size))
        mixed_grads.append(mixed_grad.reshape(2 * length, 3 * size))
        mixed_sums.append(jnp.sum(mixed_sum, axis=(0, 1)))
    context = jnp.concatenate(contexts, axis=1)
    mixed_grad = jnp.concatenate(mixed_grads, axis=1)
    mixed_sum = jnp.stack(mixed_sums).reshape(heads, 3, size)

    qkv_shard = scatter(lambda low, high, kind: dot(columns(attn_in, low, high), mixed_grad, ((0,), (0,)), kind), 0, 1)
    dense_shard = scatter(lambda low, high, kind: dot(context, columns(g_pair, low, high), ((0,), (0,)), kind), 1, 0)

    branch = dot(context, w_dense, ((1,), (0,)), F) + dot(activation, w_down, ((1,), (0,)), F)
    branch_rows = total_rows(branch.astype(B).reshape(2, length, width))
    x_rows, g_rows = own_rows(x_pair[:length], 0), own_rows(g_pair[:length], 0)
    out_rows = (x_rows.astype(F) + branch_rows + arranged(dense_bias) + arranged(down_bias)).astype(B)
    block_out = share_rows(natural(out_rows))

    attn_in_grad = dot(mixed_grad, w_qkv, ((1,), (1,)), F)
    mlp_in_grad = dot(pre_grad, w_up, ((1,), (1,)), F)
    blend = (attn_in_grad * gains[0] + mlp_in_grad * gains[2]).astype(B)
    blend_rows = total_rows(blend.reshape(2, length, width))
    hat_rows, inverse_rows = hat(x_rows)
    inner = (
        blend_rows
        - jnp.mean(blend_rows, axis=-1, keepdims=True)
        - hat_rows * jnp.mean(blend_rows * hat_rows, axis=-1, keepdims=True)
    )
    input_grad = share_rows(natural((g_rows.astype(F) + inner * inverse_rows).astype(B)))

    norm_sums = natural(
        jnp.stack(
            [
                jnp.sum(attn_in_grad * normed, axis=0),
                jnp.sum(attn_in_grad, axis=0),
                jnp.sum(mlp_in_grad * normed, axis=0),
                jnp.sum(mlp_in_grad, axis=0),
            ]
        )
    ).reshape(-1)
    bias_sum = jnp.sum(own_g.astype(F), axis=0)

    def slotted(array):
        zero = jnp.zeros_like(array)
        return join(array, zero, half, 0)

    small = [norm_sums, bias_sum, slotted(up_bias_sum), slotted(mixed_sum).reshape(-1)]
    sizes = [s.shape[0] for s in small]
    flat = jnp.concatenate(small)
    for bit in [1 << k for k in range(groups.bit_length() - 1)]:
        flat = flat + swap(flat, bit)
    ends = [sum(sizes[: i + 1]) for i in range(len(sizes))]
    norms = flat[: ends[0]]
    for bit in [1 << k for k in range(ways.bit_length() - 1)]:
        norms = norms + cross(norms, bit)
    norms = norms.reshape(4, width)
    bias_grad = flat[ends[0] : ends[1]]
    up_bias_grad = flat[ends[1] : ends[2]]
    mixed_bias = flat[ends[2] :].reshape(2 * heads, 3, size)
    qv_grad = jnp.stack([mixed_bias[:, 0], mixed_bias[:, 2]], axis=1)
    key_bias_grad = mixed_bias[:, 1, :ROT]

    return (
        block_out[None],
        input_grad[None],
        norms[0],
        norms[1],
        norms[2],
        norms[3],
        qkv_shard.reshape(qkv_weight.shape),
        qv_grad,
        key_bias_grad,
        dense_shard.reshape(dense_weight.shape),
        bias_grad,
        up_shard,
        up_bias_grad,
        down_shard,
        bias_grad,
    )


def body(
    tokens,
    segment_ids,
    out_grad,
    attn_norm_gain,
    attn_norm_bias,
    mlp_norm_gain,
    mlp_norm_bias,
    qkv_weight,
    qv_bias,
    key_bias,
    dense_weight,
    dense_bias,
    up_weight,
    up_bias,
    down_weight,
    down_bias,
    *,
    groups,
    ways,
):
    length, width = tokens.shape[1:]
    heads, size = qkv_weight.shape[1] // 2, qkv_weight.shape[3]
    assert heads == 1 and ways == 4
    part = width // groups
    hidden = up_weight.shape[1] // 2
    count = 2 * length
    me = lax.axis_index("dp")
    half = (me // PAIR) % 2
    shape = jax.ShapeDtypeStruct

    def pick(array, index, axis):
        rows = array.shape[axis] // 2
        return lax.dynamic_slice_in_dim(array, index * rows, rows, axis)

    vectors = jnp.stack([attn_norm_gain, attn_norm_bias, mlp_norm_gain, mlp_norm_bias, dense_bias, down_bias])
    own_x, own_g = tokens[0], out_grad[0]

    tables = rope_tables(length)
    columns = hidden
    half_width = width // 2
    vmem, hbm = pl.BlockSpec(memory_space=pltpu.VMEM), pl.BlockSpec(memory_space=pl.ANY)
    quarter = length // 4
    tall, blocks = 2 * quarter, width // CHUNK
    dma = pltpu.SemaphoreType.DMA
    scoped_one = [
        pltpu.VMEM((2, CHUNK, width), B),
        pltpu.VMEM((length, width), B),
        pltpu.VMEM((length, width), B),
        pltpu.VMEM((count, width), B),
        pltpu.VMEM((length, width), B),
        pltpu.VMEM((width, columns), F),
        pltpu.VMEM((half_width, columns), B),
        pltpu.VMEM((length, size), B),
        pltpu.VMEM((length, size), B),
        pltpu.VMEM((length, size), B),
        pltpu.VMEM((length, size), B),
        pltpu.VMEM((length, size), B),
        pltpu.VMEM((length, 3 * size), B),
        pltpu.VMEM((length, size), F),
        pltpu.VMEM((length, size), F),
        pltpu.VMEM((2, CHUNK, hidden), B),
        pltpu.VMEM((2, CHUNK, hidden), F),
        pltpu.VMEM((length, 8), F),
        pltpu.VMEM((3, length, 128), F),
    ]
    scoped_two = [
        pltpu.VMEM((count, hidden), B),
        pltpu.VMEM((count, hidden), B),
        pltpu.VMEM((tall, width), B),
        pltpu.VMEM((2, count, part), B),
        pltpu.VMEM((2, CHUNK, hidden), F),
        pltpu.VMEM((tall, 3 * size), B),
        pltpu.VMEM((count, size), B),
        pltpu.VMEM((2, half_width, columns), F),
        pltpu.VMEM((half_width, columns), B),
        pltpu.VMEM((2, half_width // 2, columns), B),
        pltpu.VMEM((2, part, columns), B),
        pltpu.VMEM((part, columns), B),
        pltpu.VMEM((tall, width), B),
        pltpu.VMEM((2, tall, CHUNK), B),
        pltpu.VMEM((tall, CHUNK), F),
        pltpu.VMEM((2, 2, quarter, width), B),
        pltpu.VMEM((2, 2, quarter, width), F),
        pltpu.VMEM((tall, 128), F),
        pltpu.VMEM((tall, 128), F),
        pltpu.VMEM((1, hidden), F),
        pltpu.VMEM((8, width), F),
    ]
    block_out, input_grad, qkv_shard, dense_shard, up_shard, down_shard, *_, small = pl.pallas_call(
        functools.partial(layer_kernel, groups, scoped_one, scoped_two),
        in_specs=[hbm] * 4 + [vmem] + [hbm] * 2 + [vmem] * 4 + [hbm],
        out_specs=[hbm] * 26 + [vmem],
        out_shape=[
            shape((length, width), B),
            shape((length, width), B),
            shape((part, 6 * size), F),
            shape(dense_weight.shape, F),
            shape(up_weight.shape, F),
            shape(down_weight.shape, F),
            shape((3, 3 * part, columns), B),
            shape((length, width), B),
            shape((length, width), B),
            shape((count, width), B),
            shape((count, width), B),
            shape((count, width), B),
            shape((count, 3 * size), B),
            shape((count, size), B),
            shape((count, hidden), B),
            shape((count, hidden), F),
            shape((half_width, columns), B),
            shape((half_width, columns), F),
            shape((3, part, columns), B),
            shape((3, part, columns), B),
            shape((3, half_width, columns), B),
            shape((3, half_width // 2, columns), B),
            shape((3, 3 * part, columns), B),
            shape((2, 2, tall, width), B),
            shape((2, 2, quarter, width), B),
            shape((2, quarter, width), B),
            shape((8, width), F),
        ],
        scratch_shapes=[
            pltpu.VMEM((3, width, columns), B),
            pltpu.VMEM((3, part, columns), B),
            pltpu.VMEM((1, length), jnp.int32),
            pltpu.VMEM((1, 3 * size), F),
            pltpu.VMEM((1, width), F),
            pltpu.VMEM((5, 8, width), F),
            dma((28,)),
            dma((28,)),
            dma((3, 6)),
            dma((3,)),
            dma((3,)),
            dma((3, 3)),
            dma((2, 2)),
            dma((2, 3 + hidden // part)),
            dma((2,)),
            dma((2, 2)),
            dma((2, 5)),
            dma((2, 2)),
            dma((5,)),
            dma((9,)),
            dma((5, 2)),
            dma((3, 4)),
            dma((3, 4)),
            dma((3, 2)),
            dma((3, 2)),
            dma((3, 3)),
            dma((3, 3)),
            dma((3,)),
            dma((3,)),
            dma((3,)),
            dma((2, 2, blocks)),
            dma((2, 2, blocks)),
            dma((2, 2)),
            dma((2, 2)),
            dma((2,)),
            dma((2,)),
            dma((2, 3)),
            dma((2, 3)),
            dma((3, 2, hidden // part)),
            dma((5,)),
            dma((5,)),
            dma((5,)),
        ],
        compiler_params=pltpu.CompilerParams(
            collective_id=0, has_side_effects=True, vmem_limit_bytes=67043328
        ),
        cost_estimate=pl.CostEstimate(flops=100 * 10**9, bytes_accessed=2 * 10**8, transcendentals=10**7),
        name="layer",
    )(
        qkv_weight.reshape(part, 6 * size),
        dense_weight,
        up_weight,
        down_weight,
        segment_ids,
        own_x,
        own_g,
        vectors,
        up_bias.reshape(1, 2 * hidden),
        qv_bias,
        key_bias,
        jnp.stack(tables),
    )

    made = [block_out, input_grad, dense_shard, up_shard, down_shard]
    block_out, input_grad, dense_shard, up_shard, down_shard = pl.pallas_call(
        place_kernel,
        in_specs=[hbm] * len(made),
        out_specs=[hbm] * len(made),
        out_shape=[shape(a.shape, a.dtype) for a in made],
        scratch_shapes=[pltpu.VMEM(a.shape, a.dtype) for a in made] + [dma((len(made), 2)), dma((len(made), 2))],
        compiler_params=pltpu.CompilerParams(vmem_limit_bytes=67043328),
        cost_estimate=pl.CostEstimate(flops=0, bytes_accessed=28 * 10**6, transcendentals=0),
        name="place",
    )(*made)
    norms, bias_grad, up_bias_grad = small[0:4], small[4], small[5]
    mixed_bias = small[6].reshape(2, width // 2)[:, : 3 * size].reshape(2, 3, size)
    qv_grad = jnp.stack([mixed_bias[:, 0], mixed_bias[:, 2]], axis=1)
    key_bias_grad = mixed_bias[:, 1, :ROT]

    return (
        block_out[None],
        input_grad[None],
        norms[0],
        norms[1],
        norms[2],
        norms[3],
        qkv_shard.reshape(qkv_weight.shape),
        qv_grad,
        key_bias_grad,
        dense_shard,
        bias_grad,
        up_shard,
        up_bias_grad,
        down_shard,
        bias_grad,
    )


def solution(mesh):
    placed = (
        P("dp", None, None),
        P("dp", None),
        P("dp", None, None),
        P(),
        P(),
        P(),
        P(),
        P("dp", "tensor", None, None),
        P("tensor", None, None),
        P("tensor", None),
        P("tensor", None, "dp"),
        P(),
        P("dp", "tensor"),
        P("tensor"),
        P("tensor", "dp"),
        P(),
    )

    def whole(*arrays):
        groups, ways = mesh.shape["dp"], mesh.shape["tensor"]
        part = arrays[0].shape[2] // groups
        chosen = body_narrow if part % 128 or groups != 8 else body
        return chosen(*arrays, groups=groups, ways=ways)

    return jax.shard_map(
        whole,
        mesh=mesh,
        in_specs=placed,
        out_specs=(
            P("dp", None, None),
            P("dp", None, None),
            P(),
            P(),
            P(),
            P(),
            P("dp", "tensor", None, None),
            P("tensor", None, None),
            P("tensor", None),
            P("tensor", None, "dp"),
            P(),
            P("dp", "tensor"),
            P("tensor"),
            P("tensor", "dp"),
            P(),
        ),
        check_vma=False,
    )
```
